32 devices in a mesh: dp: 8 (over z, y), fsdp: 4 (over x, core).
Axes of the slice: x: 2, y: 2, z: 4, core: 2. Of those that a mesh axis runs over, the one named last changes fastest.
Arguments:
- inputs: bfloat16 [4096, 1024], P(('dp', 'fsdp')), may hold values from -6 to 6
- lengths: int32 [32, 1], P(('dp', 'fsdp')), may hold values from 0 to 128, as said below
- w_values: bfloat16 [1024, 2048], P(('dp', 'fsdp')), may hold values from -0.1875 to 0.1875
- w_mix: bfloat16 [1024, 4224], P(('dp', 'fsdp')), may hold values from -0.1875 to 0.1875
- w_out: bfloat16 [2048, 1024], P(('dp', 'fsdp')), may hold values from -0.25 to 0.25
- w_expand: bfloat16 [1024, 4096], P(('dp', 'fsdp')), may hold values from -0.1875 to 0.1875
- w_reduce: bfloat16 [4096, 1024], P(('dp', 'fsdp')), may hold values from -0.09375 to 0.09375
- ema_params: bfloat16 [1024, 64], P(('dp', 'fsdp')), may hold values from -2.5 to 2.5
- norm_gains: bfloat16 [3, 1024], P(None, ('dp', 'fsdp')), may hold values from 0.25 to 1.75
- norm_biases: bfloat16 [2, 1024], P(None, ('dp', 'fsdp')), may hold values from -2 to 2
- head_gains: bfloat16 [2, 128], replicated, may hold values from 0.25 to 1.75
- query_bias: bfloat16 [128], replicated, may hold values from -3 to 3
- position_bias: bfloat16 [128], replicated, may hold values from -3 to 3
- cotangent: bfloat16 [4096, 1024], P(('dp', 'fsdp')), may hold values from -6 to 6
Outputs:
- output: bfloat16 [4096, 1024], P(('dp', 'fsdp'))
- grad_inputs: float32 [4096, 1024], P(('dp', 'fsdp'))
- grad_w_values: float32 [1024, 2048], P(('dp', 'fsdp'))
- grad_w_mix: float32 [1024, 4224], P(('dp', 'fsdp'))
- grad_w_out: float32 [2048, 1024], P(('dp', 'fsdp'))
- grad_w_expand: float32 [1024, 4096], P(('dp', 'fsdp'))
- grad_w_reduce: float32 [4096, 1024], P(('dp', 'fsdp'))
- grad_ema_params: float32 [1024, 64], P(('dp', 'fsdp'))
- grad_norm_gains: float32 [3, 1024], P(None, ('dp', 'fsdp'))
- grad_norm_biases: float32 [2, 1024], P(None, ('dp', 'fsdp'))
- grad_head_gains: float32 [2, 128], replicated
- grad_query_bias: float32 [128], replicated
- grad_position_bias: float32 [128], replicated
- rms: float32 [3], replicated
The draws below stay inside these ranges and needn't reach their ends.
Inputs may be any that keep to these rules, and one draw needn't show every extreme that they name: Every length is a multiple of 128, zero for an unused slot; each device's lengths sum to exactly 128: it holds a single row of 128 tokens starting at its first slot.
All inputs are finite; a program needn't handle non-finite values.
Results may differ from the reference program's by a relative error of at most 0.014.
The reference program's roundings to bfloat16 on the way count: a program that leaves them out, or rounds other values in their place, can miss the bound.
Values may be sent and summed in bfloat16 or wider, within the bound.
A program may use at most 192 MiB of HBM per device.

```python
import jax
import jax.numpy as jnp
from jax import lax

D = 1024
Z = 128
VALS = 2048
EMA_N = 16
FF = 4096
BLOCK = 128
TOK_DEV = 128
ROWS_DEV = 1
GROUPS = 32
TOKENS = 4096
MIXW = 4224


def draw_lengths(key, part):
    fill_key, weight_key, whole_key = jax.random.split(jax.random.fold_in(key, 17), 3)
    filled = jax.random.randint(fill_key, (GROUPS, 1), 1, ROWS_DEV + 1)
    base = jax.random.randint(weight_key, (GROUPS, ROWS_DEV), 1, 9)
    weights = base * base * base
    bounds = jnp.cumsum(weights, axis=1)
    marks = filled * bounds // bounds[:, -1:]
    counts = marks - jnp.concatenate([jnp.zeros((GROUPS, 1), jnp.int32), marks[:, :-1]], axis=1)
    chosen = jax.random.randint(whole_key, (), 0, GROUPS)
    single = jnp.where(jnp.arange(ROWS_DEV) == 0, ROWS_DEV, 0).astype(jnp.int32)
    counts = jnp.where((jnp.arange(GROUPS) == chosen)[:, None], single[None, :], counts)
    return (counts * BLOCK).astype(jnp.int32)


def steps_of(stream_key, extent, shards, low, top_value):
    def one(position, shards_of):
        steps = jax.random.uniform(jax.random.fold_in(jax.random.fold_in(stream_key, 6), position), (shards_of,), jnp.float32, low / len(shards), top_value / len(shards))
        return jnp.repeat(jnp.exp(steps), extent[position] // shards_of).reshape((-1,) + (1,) * (len(extent) - position - 1))

    factor_of = one(*shards[0])
    for cut in shards[1:]:
        factor_of = factor_of * one(*cut)
    return factor_of


def noise(stream_key, shape, scale, reach, pieces=(), held_as=jnp.bfloat16):
    level = steps_of(stream_key, shape, pieces, -0.22, 0.18) if pieces else 1.0
    values = jax.random.normal(stream_key, shape, jnp.float32) * scale * level
    return jnp.minimum(jnp.maximum(values, -reach), reach).astype(held_as)


def setup_inputs(seed: int = 0) -> dict:
    arg_keys = jax.random.split(jax.random.key(seed), 15)
    inputs = noise(arg_keys[0], (TOKENS, D), 1.0, 6.0, ((0, 32),))
    lengths = draw_lengths(jax.random.fold_in(arg_keys[14], 71), 0)
    w_values = noise(arg_keys[2], (D, VALS), D ** -0.5, 0.1875, ((0, 32),))
    w_mix = noise(arg_keys[3], (D, MIXW), D ** -0.5, 0.1875, ((0, 32),))
    w_out = noise(arg_keys[4], (VALS, D), (VALS // 4) ** -0.5, 0.25, ((0, 32),))
    w_expand = noise(arg_keys[5], (D, FF), D ** -0.5, 0.1875, ((0, 32),))
    w_reduce = noise(arg_keys[6], (FF, D), FF ** -0.5, 0.09375, ((0, 32),))
    ema_params = noise(arg_keys[7], (D, 4 * EMA_N), 0.6, 2.5, ((0, 32),))
    norm_gains = jnp.clip(1.0 + 0.15 * jax.random.normal(arg_keys[8], (3, D), jnp.float32), 0.25, 1.75).astype(jnp.bfloat16)
    norm_biases = noise(arg_keys[9], (2, D), 0.3, 2.0, ((1, 32),))
    head_gains = jnp.clip(1.0 + 0.15 * jax.random.normal(arg_keys[10], (2, Z), jnp.float32), 0.25, 1.75).astype(jnp.bfloat16)
    query_bias = noise(arg_keys[11], (Z,), 0.5, 3.0)
    position_bias = noise(arg_keys[12], (BLOCK,), 0.5, 3.0)
    cotangent = noise(arg_keys[13], (TOKENS, D), 1.0, 6.0, ((0, 32),))
    return {"inputs": inputs, "lengths": lengths, "w_values": w_values, "w_mix": w_mix, "w_out": w_out, "w_expand": w_expand, "w_reduce": w_reduce, "ema_params": ema_params, "norm_gains": norm_gains, "norm_biases": norm_biases, "head_gains": head_gains, "query_bias": query_bias, "position_bias": position_bias, "cotangent": cotangent}


@jax.custom_vjp
def low(v):
    return lax.optimization_barrier(v.astype(jnp.bfloat16)).astype(jnp.float32)

@jax.custom_vjp
def low_back(v):
    return v

def low_keep(v):
    return (low(v), None)

def low_pass(kept, grad):
    return (grad,)

def back_keep(v):
    return (v, None)

def back_low(kept, grad):
    return (low(grad),)
low.defvjp(low_keep, low_pass)
low_back.defvjp(back_keep, back_low)
EPS = 1e-05
NEG = -1e+30

def silu(value):
    return value * jax.nn.sigmoid(value)

def layer_norm(value, gain, shift):
    centre = lax.optimization_barrier(jnp.mean(value, axis=-1, keepdims=True))
    centered = value - centre
    spread = lax.optimization_barrier(jnp.mean(centered * centered, axis=-1, keepdims=True))
    return centered * lax.rsqrt(spread + EPS) * gain + shift

def product(left, right):
    return jnp.dot(left, right, precision=lax.Precision.HIGHEST, preferred_element_type=jnp.float32)

def ema_mix(normed, keep, ema_params):
    count = ema_params.shape[1] // 4
    damping = jax.nn.sigmoid(ema_params[:, :count]).T
    mixing = jax.nn.sigmoid(ema_params[:, count:2 * count]).T
    expand = ema_params[:, 2 * count:3 * count].T
    project = ema_params[:, 3 * count:].T
    factor = 1.0 - mixing * damping
    inflow = mixing * expand

    def advance(state, item):
        column, flag = item
        state = factor * state * flag[:, None, None] + inflow * column[:, None, :]
        return (state, 0.25 * lax.optimization_barrier(jnp.sum(project * state, axis=1)))
    start = jnp.zeros((normed.shape[0], count, normed.shape[2]), jnp.float32)
    _, smooth = lax.scan(advance, start, (jnp.swapaxes(normed, 0, 1), jnp.swapaxes(keep, 0, 1)))
    return jnp.swapaxes(smooth, 0, 1)

def layout(lengths, rows):
    ends = jnp.cumsum(lengths, axis=1)
    starts = ends - lengths
    filled = ends[:, -1:]
    place = lax.broadcasted_iota(jnp.int32, (lengths.shape[0], rows), 1)
    begin = jnp.any(place[:, :, None] == starts[:, None, :], axis=2) | (place == filled)
    keep = jnp.where(begin, 0.0, 1.0).astype(jnp.float32)
    valid = jnp.where(place < filled, 1.0, 0.0).astype(jnp.float32)
    return (keep, valid)

def attend(query, key, value, position_bias):
    span = query.shape[1]
    row = lax.broadcasted_iota(jnp.int32, (span, span), 0)
    col = lax.broadcasted_iota(jnp.int32, (span, span), 1)
    table = position_bias[jnp.clip(row - col, 0, span - 1)]
    scale = query.shape[2] ** (-0.5)
    scores = jnp.einsum('kiz,kjz->kij', query, key, precision=lax.Precision.HIGHEST) * scale + table
    scores = low_back(jnp.where(row >= col, scores, NEG))
    log_total = jax.nn.logsumexp(scores, axis=-1, keepdims=True)
    probs = low(jnp.exp(scores - log_total))
    return low_back(jnp.einsum('kij,kjv->kiv', probs, value, precision=lax.Precision.HIGHEST))

def run_layer(params, stream, keep, valid):
    w_values, w_mix, w_out, w_expand, w_reduce, ema_params, norm_gains, norm_biases, head_gains, query_bias, position_bias = params
    width = stream.shape[2]
    key_width = head_gains.shape[1]
    value_width = w_values.shape[1]
    span = position_bias.shape[0]
    normed = layer_norm(stream, norm_gains[0], norm_biases[0])
    smooth = ema_mix(normed, keep, ema_params)
    mixed = silu(smooth + norm_gains[1] * normed)
    flat = stream.reshape(-1, width)
    normed_low = low(normed.reshape(-1, width))
    mixed_low = low(mixed.reshape(-1, width))
    value_pre = low_back(product(normed_low, w_values))
    value_low = low(silu(value_pre))
    mixture = low_back(product(mixed_low, w_mix))
    lower = width
    middle = width + key_width
    upper = middle + value_width
    update = jax.nn.sigmoid(mixture[:, :lower])
    zeta = silu(mixture[:, lower:middle])
    reset = silu(mixture[:, middle:upper])
    candidate = mixture[:, upper:]
    query_low = low(zeta * head_gains[0] + query_bias)
    key_low = low(zeta * head_gains[1])
    attended = attend(query_low.reshape(-1, span, key_width), key_low.reshape(-1, span, key_width), value_low.reshape(-1, span, value_width), position_bias).reshape(-1, value_width)
    gated_low = low(attended * reset)
    hidden = silu(candidate + low_back(product(gated_low, w_out)))
    attn_branch = update * (hidden - flat)
    first = flat + attn_branch
    normed_two = low(layer_norm(first, norm_gains[2], norm_biases[1]))
    expand_pre = low_back(product(normed_two, w_expand))
    expand_low = low(silu(expand_pre))
    branch = low_back(product(expand_low, w_reduce))
    mask = valid.reshape(-1, 1)
    result = (first + branch) * mask
    stats = jnp.stack([jnp.sum(mask * flat * flat), jnp.sum(mask * attn_branch * attn_branch), jnp.sum(mask * branch * branch), jnp.sum(valid)])
    return (result.reshape(stream.shape), stats)

def reference(inputs, lengths, w_values, w_mix, w_out, w_expand, w_reduce, ema_params, norm_gains, norm_biases, head_gains, query_bias, position_bias, cotangent):
    weights = tuple((item.astype(jnp.float32) for item in (w_values, w_mix, w_out, w_expand, w_reduce, ema_params, norm_gains, norm_biases, head_gains, query_bias, position_bias)))
    per_step = 1
    for _ in range(12):
        if per_step * 2 * TOK_DEV <= 4096 and GROUPS % (per_step * 2) == 0:
            per_step = per_step * 2
    steps = GROUPS // per_step
    stream_blocks = inputs.astype(jnp.float32).reshape(steps, per_step, TOK_DEV, D)
    back_blocks = cotangent.astype(jnp.float32).reshape(steps, per_step, TOK_DEV, D)
    length_blocks = lengths.reshape(steps, per_step, ROWS_DEV)

    def visit(carry, item):
        stream, grad_in, lens = item
        keep, valid = layout(lens, TOK_DEV)

        def forward(params, source):
            return run_layer(params, source, keep, valid)
        result, back, stats = jax.vjp(forward, weights, stream, has_aux=True)
        grad_weights, grad_source = back(grad_in)
        totals, sums = carry
        totals = jax.tree.map(lambda left, right: left + right, totals, grad_weights)
        return ((totals, sums + stats), (result.astype(jnp.bfloat16), grad_source))
    start = (jax.tree.map(jnp.zeros_like, weights), jnp.zeros((4,), jnp.float32))
    (grads, sums), (results, grad_sources) = lax.scan(visit, start, (stream_blocks, back_blocks, length_blocks))
    rms = jnp.sqrt(sums[:3] / (sums[3] * D))
    return (results.reshape(TOKENS, D), grad_sources.reshape(TOKENS, D), grads[0], grads[1], grads[2], grads[3], grads[4], grads[5], grads[6], grads[7], grads[8], grads[9], grads[10], rms)
```

```python
import functools

import jax
import jax.numpy as jnp
from jax import lax
from jax.experimental import pallas as pl
from jax.experimental.pallas import tpu as pltpu
from jax.sharding import PartitionSpec as P

EPS = 1e-05
NEG = -1e30
F32 = jnp.float32
LOW = jnp.bfloat16
MESH = pl.DeviceIdType.MESH
LINES = 96
STATES = 16


def silu(value):
    return value * jax.nn.sigmoid(value)


def silu_slope(value):
    sigma = jax.nn.sigmoid(value)
    return sigma * (1.0 + value * (1.0 - sigma))


def here():
    dp = lax.axis_index("dp")
    f = lax.axis_index("fsdp")
    return dp // 2, dp % 2, f // 2, f % 2


def device(z, y, x, c):
    return (z * 2 + y, x * 2 + c)


def slot_of(y, x, c):
    return y * 4 + x * 2 + c


def plane_peers(y, x, c):
    peers = []
    for mask in range(1, 8):
        peers.append(
            (
                1 - y if mask & 4 else y,
                1 - x if mask & 2 else x,
                1 - c if mask & 1 else c,
            )
        )
    return peers


def line_peers(z):
    return [z + 1 - 2 * (z % 2), 3 - z, (z + 2) % 4]


def greet(across=True):
    z, y, x, c = here()
    barrier = pltpu.get_barrier_semaphore()
    count = 7
    for peer in plane_peers(y, x, c):
        pl.semaphore_signal(barrier, inc=1, device_id=device(z, *peer), device_id_type=MESH)
    if across:
        count = 10
        for other in line_peers(z):
            pl.semaphore_signal(barrier, inc=1, device_id=device(other, y, x, c), device_id_type=MESH)
    pl.semaphore_wait(barrier, count)


class Net:
    def __init__(self, send, recv):
        self.send = send
        self.recv = recv
        self.used = 0

    def copy(self, src, dst, target):
        line = self.used
        self.used += 1
        made = pltpu.make_async_remote_copy(
            src_ref=src,
            dst_ref=dst,
            send_sem=self.send.at[line],
            recv_sem=self.recv.at[line],
            device_id=target,
            device_id_type=MESH,
        )
        made.start()
        return made


def neighbours(y, x):
    return [(y, 1 - x), (1 - y, x), (1 - y, 1 - x)]


def gather_plane(net, src, dst):
    z, y, x, c = here()
    me = slot_of(y, x, c)
    near = [net.copy(src, dst.at[me], device(z, yy, xx, c)) for yy, xx in neighbours(y, x)]
    twin = [net.copy(src, dst.at[me], device(z, y, x, 1 - c))]
    dst[me] = src[...]
    yield
    for copy, (yy, xx) in zip(near, neighbours(y, x)):
        copy.wait_recv()
        block = dst.at[slot_of(yy, xx, c)]
        twin.append(net.copy(block, block, device(z, y, x, 1 - c)))
    yield
    for copy in twin:
        copy.wait()
    for copy in near:
        copy.wait_send()


def spread_plane(net, src, dst):
    z, y, x, c = here()
    me = slot_of(y, x, c)
    copies = [net.copy(src, dst.at[me], device(z, *peer)) for peer in plane_peers(y, x, c)]
    dst[me] = src[...]
    yield
    for copy in copies:
        copy.wait()


def swap_plane(net, src, dst):
    z, y, x, c = here()
    me = slot_of(y, x, c)
    copies = []
    for peer in plane_peers(y, x, c):
        copies.append(net.copy(src.at[slot_of(*peer)], dst.at[me], device(z, *peer)))
    dst[me] = src[me]
    yield
    for copy in copies:
        copy.wait()


def sum_plane(net, src, got, sent, far, out):
    z, y, x, c = here()
    chips = [(y, x)] + neighbours(y, x)
    first = []
    for k in (3, 1, 2, 0):
        yy, xx = chips[k]
        first.append((k, net.copy(src.at[slot_of(yy, xx, 1 - c)], got.at[k], device(z, y, x, 1 - c))))
    yield
    second = []
    for k, copy in first:
        copy.wait_recv()
        yy, xx = chips[k]
        pair = src[slot_of(yy, xx, c)].astype(F32) + got[k].astype(F32)
        if k == 0:
            out[...] = pair
        else:
            sent[k - 1] = pair.astype(LOW)
            second.append(net.copy(sent.at[k - 1], far.at[k - 1], device(z, yy, xx, c)))
    yield
    for k, copy in first:
        copy.wait_send()
    for copy in second:
        copy.wait()
    out[...] = out[...] + far[0].astype(F32) + far[1].astype(F32) + far[2].astype(F32)


def gather_line(net, bufs):
    z, y, x, c = here()
    near, mirror, _ = line_peers(z)
    waits = []
    for buf in bufs:
        waits.append(net.copy(buf.at[z], buf.at[z], device(near, y, x, c)))
        waits.append(net.copy(buf.at[z], buf.at[z], device(mirror, y, x, c)))
    yield
    relayed = (2 * z) % 3 + 3 * (z // 3)
    target = (3 * z + 2) % 5
    more = []
    for k, buf in enumerate(bufs):
        waits[2 * k].wait_recv()
        waits[2 * k + 1].wait_recv()
        more.append(net.copy(buf.at[relayed], buf.at[relayed], device(target, y, x, c)))
    yield
    for copy in waits:
        copy.wait_send()
    for copy in more:
        copy.wait()


def spread_line(net, buf):
    z, y, x, c = here()
    copies = [net.copy(buf.at[z], buf.at[z], device(other, y, x, c)) for other in line_peers(z)]
    yield
    for copy in copies:
        copy.wait()


def sum_line(net, bufs, gots, outs):
    z, y, x, c = here()
    near, mirror, across = line_peers(z)
    target = (2 * z + 1) % 5
    relayed = (2 * z) % 3 + 3 * (z // 3)
    first = []
    for buf, got in zip(bufs, gots):
        first.append(net.copy(buf.at[across], got.at[0], device(target, y, x, c)))
    yield
    second = []
    for copy, buf, got in zip(first, bufs, gots):
        copy.wait_recv()
        buf[relayed] = (buf[relayed].astype(F32) + got[0].astype(F32)).astype(LOW)
        second.append(net.copy(buf.at[near], got.at[1], device(near, y, x, c)))
        second.append(net.copy(buf.at[mirror], got.at[2], device(mirror, y, x, c)))
    yield
    for copy in first:
        copy.wait_send()
    for copy in second:
        copy.wait()
    for buf, got, out in zip(bufs, gots, outs):
        out[...] = (buf[z].astype(F32) + got[1].astype(F32) + got[2].astype(F32)).astype(out.dtype)


def drive(*stages):
    live = list(stages)
    while live:
        live = [stage for stage in live if advance(stage)]


def advance(stage):
    for _ in stage:
        return True
    return False


VMEM = pl.BlockSpec(memory_space=pltpu.VMEM)


def exchange(kernel, name, outs, scratch, number, *operands, smem=()):
    specs = [
        pl.BlockSpec(memory_space=pltpu.SMEM) if index in smem else VMEM
        for index in range(len(operands))
    ]
    return pl.pallas_call(
        kernel,
        name=name,
        out_shape=[jax.ShapeDtypeStruct(shape, dtype) for shape, dtype in outs],
        in_specs=specs,
        out_specs=[VMEM] * len(outs),
        scratch_shapes=[pltpu.VMEM(shape, dtype) for shape, dtype in scratch]
        + [pltpu.SemaphoreType.DMA((LINES,)), pltpu.SemaphoreType.DMA((LINES,))],
        compiler_params=pltpu.CompilerParams(
            collective_id=number, has_side_effects=True, vmem_limit_bytes=58 << 20
        ),
    )(*operands)


def lanes_to_rows(wide, tall):
    for s in range(8):
        tall[:, s, :] = wide[:, s * 128 : (s + 1) * 128]


def pick_halves(arr, base, slot, pair):
    one = base + ((2 * pair * 8 + slot) // 2) * 128
    two = base + (((2 * pair + 1) * 8 + slot) // 2) * 128
    left = arr[:, one : one + 128].astype(F32)
    right = arr[:, two : two + 128].astype(F32)
    lane = lax.broadcasted_iota(jnp.int32, left.shape, 1)
    if slot % 2 == 0:
        return jnp.where(lane < 64, left, pltpu.roll(right, 64, 1)).astype(LOW)
    return jnp.where(lane < 64, pltpu.roll(left, 64, 1), right).astype(LOW)


def ema_forward(factor, gain, source, out):
    steps = source.shape[0]

    def step(t, states):
        column = source[t]
        new = []
        terms = []
        for j in range(STATES):
            state = factor[j] * states[j] + column
            new.append(state)
            terms.append(gain[j] * state)
        while len(terms) > 1:
            terms = [terms[i] + terms[i + 1] for i in range(0, len(terms), 2)]
        out[t] = terms[0]
        return tuple(new)

    zero = jnp.zeros(source.shape[1:], F32)
    lax.fori_loop(0, steps, step, (zero,) * STATES)


def front_kernel(
    x_ref, small_ref, wv_ref, wm_ref, wo_ref, cot_ref, lens_ref,
    wa_ref, wo_all, normed_all, mixed_all, cot_all, prm_ref, fac_ref, gain_ref, nrm_ref, pre_ref,
    blocks, small_all, turned, smooth, own_normed, own_mixed, own_cot, send, recv,
):
    net = Net(send, recv)
    z, y, x, c = here()
    greet()
    small_plane = spread_plane(net, small_ref, small_all.at[z])
    advance(small_plane)
    for s in range(8):
        for pair in range(2):
            blocks[s, :, pair * 128 : (pair + 1) * 128] = pick_halves(wv_ref, 0, s, pair)
            blocks[s, :, 512 + pair * 128 : 640 + pair * 128] = pick_halves(wm_ref, 1152, s, pair)
        blocks[s, :, 256:384] = wm_ref[:, s * 128 : (s + 1) * 128]
        blocks[s, :, 384:512] = wm_ref[:, 1024:1152]
        blocks[s, :, 768:896] = wm_ref[:, 3200 + s * 128 : 3328 + s * 128]
    weights_plane = swap_plane(net, blocks, wa_ref.at[z])
    advance(weights_plane)
    advance(small_plane)
    small_line = spread_line(net, small_all)
    advance(small_line)
    wo_all[z] = wo_ref[...]
    out_line = gather_line(net, [wo_all])
    advance(out_line)
    stream = x_ref[...].astype(F32)
    centered = stream - jnp.mean(stream, axis=-1, keepdims=True)
    spread = jnp.mean(centered * centered, axis=-1, keepdims=True)
    xhat = centered * lax.rsqrt(spread + EPS)
    pre_ref[...] = xhat
    row = lax.broadcasted_iota(jnp.int32, cot_ref.shape, 0)
    own_cot[...] = jnp.where(row < lens_ref[0, 0], cot_ref[...].astype(F32), 0.0).astype(LOW)
    advance(weights_plane)
    weights_line = gather_line(net, [wa_ref])
    advance(weights_line)
    advance(small_line)
    turned[...] = small_all[...].reshape(1024, 128).astype(F32).T
    damping = jax.nn.sigmoid(turned[0:16])
    mixing = jax.nn.sigmoid(turned[16:32])
    factor = 1.0 - mixing * damping
    gain = 0.25 * turned[48:64] * (mixing * turned[32:48])
    lanes_to_rows(factor, fac_ref)
    lanes_to_rows(gain, gain_ref)
    prm_ref[...] = turned[64:72]
    normed = pre_ref[...] * turned[64:65] + turned[67:68]
    own_normed[...] = normed.astype(LOW)
    normed_plane = gather_plane(net, own_normed, normed_all)
    advance(normed_plane)
    lanes_to_rows(normed, nrm_ref)
    pre_ref[...] = turned[65:66] * normed
    ema_forward(fac_ref, gain_ref, nrm_ref, smooth)
    for s in range(8):
        cols = slice(s * 128, (s + 1) * 128)
        pre_ref[:, cols] = pre_ref[:, cols] + smooth[:, s, :]
    own_mixed[...] = silu(pre_ref[...]).astype(LOW)
    mixed_plane = gather_plane(net, own_mixed, mixed_all)
    advance(mixed_plane)
    cot_plane = gather_plane(net, own_cot, cot_all)
    drive(normed_plane, mixed_plane, weights_line, out_line, cot_plane)


def front(inputs, small, w_values, w_mix, w_out, cotangent, lengths):
    rows, width = inputs.shape
    return exchange(
        front_kernel, "front",
        [
            ((4, 8, 32, 896), LOW), ((4, 64, 1024), LOW),
            ((8, rows, width), LOW), ((8, rows, width), LOW), ((8, rows, width), LOW),
            ((8, width), F32), ((16, 8, 128), F32), ((16, 8, 128), F32),
            ((rows, 8, 128), F32), ((rows, width), F32),
        ],
        [
            ((8, 32, 896), LOW), ((4, 8, 32, 128), LOW), ((128, 1024), F32), ((rows, 8, 128), F32),
            ((rows, width), LOW), ((rows, width), LOW), ((rows, width), LOW),
        ],
        1,
        inputs, small, w_values, w_mix, w_out, cotangent, lengths, smem=(6,),
    )


def hidden_kernel(
    part_ref, upd_ref, we_ref, wr_ref,
    out_ref, upd_all, we_all, wr_all,
    blocks, got, sent, far, send, recv,
):
    net = Net(send, recv)
    z, y, x, c = here()
    greet()
    total = sum_plane(net, part_ref, got, sent, far, out_ref)
    advance(total)
    wr_all[z] = wr_ref[...]
    reduce_line = gather_line(net, [wr_all])
    advance(reduce_line)
    update = swap_plane(net, upd_ref, upd_all)
    advance(update)
    for s in range(8):
        for zz in range(4):
            blocks[s, :, zz * 128 : (zz + 1) * 128] = we_ref[:, (zz * 8 + s) * 128 : (zz * 8 + s + 1) * 128]
    weights = swap_plane(net, blocks, we_all.at[z])
    advance(weights)
    advance(total)
    advance(update)
    advance(weights)
    expand_line = gather_line(net, [we_all])
    drive(reduce_line, expand_line, total)


def join_hidden(part, update, w_expand, w_reduce):
    return exchange(
        hidden_kernel, "join_hidden",
        [((128, 1024), F32), ((8, 128, 128), LOW), ((4, 8, 32, 512), LOW), ((4, 128, 1024), LOW)],
        [((8, 32, 512), LOW), ((4, 128, 1024), LOW), ((3, 128, 1024), LOW), ((3, 128, 1024), LOW)],
        2,
        part, update, w_expand, w_reduce,
    )


def tokens_kernel(src, dst, send, recv):
    greet(False)
    drive(gather_plane(Net(send, recv), src, dst))


def all_tokens(value, number):
    return exchange(tokens_kernel, "all_tokens", [((8,) + value.shape, LOW)], [], number, value)[0]


def ffn_kernel(
    normed_part, branch_part, ge_ref, gr_ref,
    normed_out, branch_out, ge_out, gr_out,
    got, sent, far, got_b, sent_b, far_b, ge, gr, ge_got, gr_got, send, recv,
):
    net = Net(send, recv)
    greet()
    normed = sum_plane(net, normed_part, got, sent, far, normed_out)
    advance(normed)
    ge[...] = ge_ref[...]
    gr[...] = gr_ref[...]
    line = sum_line(net, [gr, ge], [gr_got, ge_got], [gr_out, ge_out])
    branch = sum_plane(net, branch_part, got_b, sent_b, far_b, branch_out)
    drive(line, normed, branch)


def join_ffn(normed_part, branch_part, grad_expand, grad_reduce):
    plane = [((4, 128, 1024), LOW), ((3, 128, 1024), LOW), ((3, 128, 1024), LOW)]
    return exchange(
        ffn_kernel, "join_ffn",
        [((128, 1024), F32), ((128, 1024), F32), ((256, 512), LOW), ((128, 1024), F32)],
        plane + plane
        + [((4, 256, 512), LOW), ((4, 128, 1024), LOW), ((3, 256, 512), LOW), ((3, 128, 1024), LOW)],
        4,
        normed_part, branch_part, grad_expand, grad_reduce,
    )


def back_kernel(src, upd, dst, upd_all, send, recv):
    net = Net(send, recv)
    greet(False)
    drive(gather_plane(net, src, dst), swap_plane(net, upd, upd_all))


def back_tokens(grad_hidden, grad_update):
    return exchange(
        back_kernel, "back_tokens",
        [((8, 128, 1024), LOW), ((8, 128, 128), LOW)], [], 5, grad_hidden, grad_update,
    )


def swap_kernel(src, dst, send, recv):
    greet(False)
    drive(swap_plane(Net(send, recv), src, dst))


def swap_blocks(value, number):
    return exchange(swap_kernel, "swap_blocks", [(value.shape, value.dtype)], [], number, value)[0]


def mixed_kernel(
    zeta_ref, normed_part, mixed_part, ga_ref, go_ref, ge_ref,
    zeta_all, normed_out, mixed_out, ga_out, go_out, ge_out,
    got, sent, far, got_b, sent_b, far_b, ga, go, ga_got, go_got, send, recv,
):
    net = Net(send, recv)
    greet()
    zeta = spread_plane(net, zeta_ref, zeta_all)
    mixed = sum_plane(net, mixed_part, got, sent, far, mixed_out)
    advance(zeta)
    advance(mixed)
    ga[...] = ga_ref[...]
    go[...] = go_ref[...]
    line = sum_line(net, [go, ga], [go_got, ga_got], [go_out, ga_out])
    normed = sum_plane(net, normed_part, got_b, sent_b, far_b, normed_out)
    drive(line, mixed, normed, zeta, swap_plane(net, ge_ref, ge_out))


def join_mixed(zeta, normed_part, mixed_part, grad_a, grad_o, grad_e):
    plane = [((4, 128, 1024), LOW), ((3, 128, 1024), LOW), ((3, 128, 1024), LOW)]
    return exchange(
        mixed_kernel, "join_mixed",
        [
            ((8, 128, 128), LOW), ((128, 1024), F32), ((128, 1024), F32),
            ((256, 768), LOW), ((64, 1024), F32), ((8, 32, 512), LOW),
        ],
        plane + plane
        + [((4, 256, 768), LOW), ((4, 64, 1024), LOW), ((3, 256, 768), LOW), ((3, 64, 1024), LOW)],
        7,
        zeta, normed_part, mixed_part, grad_a, grad_o, grad_e,
    )


def last_kernel(
    ga_ref, gz_ref, sums_ref,
    ga_out, gz_out, sums_out,
    blocks, parts, line_parts, cols, send, recv,
):
    net = Net(send, recv)
    z, y, x, c = here()
    greet()
    for s in range(8):
        blocks[s] = sums_ref[:, s * 128 : (s + 1) * 128]
    small = swap_plane(net, blocks, parts)
    advance(small)
    weights = swap_plane(net, ga_ref, ga_out)
    advance(weights)
    zeta = swap_line(net, gz_ref, gz_out)
    advance(zeta)
    advance(small)
    total = parts[0]
    for s in range(1, 8):
        total = total + parts[s]
    line_parts[z] = total
    drive(spread_line(net, line_parts))
    cols[...] = (line_parts[0] + line_parts[1]) + (line_parts[2] + line_parts[3])
    drive(spread_plane(net, cols, sums_out), weights, zeta)


def swap_line(net, src, dst):
    z, y, x, c = here()
    copies = [net.copy(src.at[other], dst.at[z], device(other, y, x, c)) for other in line_peers(z)]
    dst[z] = src[z]
    yield
    for copy in copies:
        copy.wait()


def last_sums(grad_a, grad_z, sums):
    rows = sums.shape[0]
    return exchange(
        last_kernel, "last_sums",
        [((8, 32, 768), LOW), ((4, 32, 128), F32), ((8, rows, 128), F32)],
        [((8, rows, 128), F32), ((8, rows, 128), F32), ((4, rows, 128), F32), ((rows, 128), F32)],
        8,
        grad_a, grad_z, sums,
    )


def ema_back_kernel(fac, gain, nrm, gm, factor_sum, gain_sum, grad_nrm):
    steps = nrm.shape[0]
    zero = jnp.zeros(nrm.shape[1:], F32)
    group = 4
    for base in range(0, STATES, group):

        def step(t, carry):
            column = nrm[t]
            pull = gm[t]
            new = []
            for k in range(group):
                state, slope, by_factor, by_gain = carry[4 * k : 4 * k + 4]
                f = fac[base + k]
                slope = f * slope + state
                state = f * state + column
                new += [state, slope, by_factor + pull * slope, by_gain + pull * state]
            return tuple(new)

        done = lax.fori_loop(0, steps, step, (zero,) * (4 * group))
        for k in range(group):
            factor_sum[base + k] = done[4 * k + 2]
            gain_sum[base + k] = done[4 * k + 3]

    def turn(t, states):
        at = steps - 1 - t
        pull = gm[at]
        new = []
        terms = []
        for j in range(STATES):
            state = fac[j] * states[j] + pull
            new.append(state)
            terms.append(gain[j] * state)
        while len(terms) > 1:
            terms = [terms[i] + terms[i + 1] for i in range(0, len(terms), 2)]
        grad_nrm[at] = terms[0]
        return tuple(new)

    lax.fori_loop(0, steps, turn, (zero,) * STATES)


def ema_back(fac, gain, nrm, gm):
    return pl.pallas_call(
        ema_back_kernel,
        name="ema_back",
        out_shape=[
            jax.ShapeDtypeStruct(fac.shape, F32),
            jax.ShapeDtypeStruct(fac.shape, F32),
            jax.ShapeDtypeStruct(nrm.shape, F32),
        ],
        in_specs=[VMEM] * 4,
        out_specs=[VMEM] * 3,
    )(fac, gain, nrm, gm)


def layer_norm(value, gain, shift):
    centre = jnp.mean(value, axis=-1, keepdims=True)
    centered = value - centre
    spread = jnp.mean(centered * centered, axis=-1, keepdims=True)
    return centered * lax.rsqrt(spread + EPS) * gain + shift


def ema_mix(normed, keep, ema_params):
    count = ema_params.shape[1] // 4
    damping = jax.nn.sigmoid(ema_params[:, :count]).T
    mixing = jax.nn.sigmoid(ema_params[:, count : 2 * count]).T
    expand = ema_params[:, 2 * count : 3 * count].T
    project = ema_params[:, 3 * count :].T
    factor = 1.0 - mixing * damping
    inflow = mixing * expand

    def advance(state, item):
        column, flag = item
        state = factor * state * flag[:, None, None] + inflow * column[:, None, :]
        return (state, 0.25 * jnp.sum(project * state, axis=1))

    start = jnp.zeros((normed.shape[0], count, normed.shape[2]), jnp.float32)
    _, smooth = lax.scan(advance, start, (jnp.swapaxes(normed, 0, 1), jnp.swapaxes(keep, 0, 1)))
    return jnp.swapaxes(smooth, 0, 1)


def layout(lengths, rows):
    ends = jnp.cumsum(lengths, axis=1)
    starts = ends - lengths
    place = lax.broadcasted_iota(jnp.int32, (lengths.shape[0], rows), 1)
    begin = jnp.any(place[:, :, None] == starts[:, None, :], axis=2) | (place == ends)
    keep = jnp.where(begin, 0.0, 1.0).astype(jnp.float32)
    valid = jnp.where(place < ends, 1.0, 0.0).astype(jnp.float32)
    return (keep, valid)


def dot_rows(left, right):
    return lax.dot_general(
        left, right, (((0,), (0,)), ((), ())), preferred_element_type=jnp.float32
    )


def dot_cols(left, right):
    return lax.dot_general(
        left, right, (((1,), (1,)), ((), ())), preferred_element_type=jnp.float32
    )


def block_scores(query_low, key_low, position, scale):
    span = query_low.shape[1]
    row = lax.broadcasted_iota(jnp.int32, (span, span), 0)
    col = lax.broadcasted_iota(jnp.int32, (span, span), 1)
    table = position[jnp.clip(row - col, 0, span - 1)]
    scores = (
        jnp.einsum("kiz,kjz->kij", query_low, key_low, preferred_element_type=jnp.float32) * scale
        + table
    )
    return jnp.where(row >= col, scores, NEG)


def diagonal_sums(grid):
    size = grid.shape[0]
    flipped = grid[:, ::-1]
    padded = jnp.pad(flipped, ((0, 0), (0, size)))
    skewed = padded.reshape(-1)[: size * (2 * size - 1)].reshape(size, 2 * size - 1)
    return jnp.sum(skewed, axis=0)[size - 1 :]


def group_rows(value):
    return lax.all_gather(value, "fsdp", axis=0, tiled=True)


def group_total(value):
    return lax.psum_scatter(value, "fsdp", scatter_dimension=0, tiled=True)


def owner_layout(grad, owners):
    return grad.reshape(owners * 8, -1)


def owner_shard(piece, columns):
    return piece.reshape(-1, columns)


def on_device(
    inputs,
    lengths,
    w_values,
    w_mix,
    w_out,
    w_expand,
    w_reduce,
    ema_params,
    norm_gains,
    norm_biases,
    head_gains,
    query_bias,
    position_bias,
    cotangent,
):
    rows, width = inputs.shape
    span = position_bias.shape[0]
    blocks = rows // span
    key_width = head_gains.shape[1]
    scale = key_width ** (-0.5)
    keep, valid = layout(lengths, rows)
    mask = valid[0][:, None]
    gathered = (
        lax.all_gather(w_values, ("dp", "fsdp"), axis=0, tiled=True),
        lax.all_gather(w_mix, ("dp", "fsdp"), axis=0, tiled=True),
        lax.all_gather(w_out, ("dp", "fsdp"), axis=0, tiled=True),
        lax.all_gather(ema_params, ("dp", "fsdp"), axis=0, tiled=True),
        lax.all_gather(norm_gains, ("dp", "fsdp"), axis=1, tiled=True),
        lax.all_gather(norm_biases, ("dp", "fsdp"), axis=1, tiled=True),
    )
    values_full, mix_full, out_full, ema_full, gains_full, biases_full = gathered
    value_width = values_full.shape[1]
    group_size = lax.axis_size("fsdp")
    data_size = lax.axis_size("dp")
    owners = group_size * data_size
    shard_rows = w_expand.shape[0]
    hidden_units = w_expand.shape[1]
    unit_block = hidden_units // (group_size * data_size)
    pieces = w_expand.reshape(shard_rows, data_size, group_size, unit_block)
    swapped = lax.all_to_all(pieces, "fsdp", split_axis=2, concat_axis=0, tiled=True)
    expand_quarter, reduce_use = (
        lax.all_gather(swapped, "dp", axis=0, tiled=True),
        lax.all_gather(w_reduce, "dp", axis=0, tiled=True),
    )
    expand_use = expand_quarter.reshape(expand_quarter.shape[0], data_size * unit_block)
    gains_f = gains_full.astype(jnp.float32)
    biases_f = biases_full.astype(jnp.float32)
    heads_f = head_gains.astype(jnp.float32)
    query_shift = query_bias.astype(jnp.float32)
    position_f = position_bias.astype(jnp.float32)
    stream = inputs.astype(jnp.float32)

    def front(source, gain, shift, omega, params):
        normed_part = layer_norm(source, gain, shift)
        smooth = ema_mix(normed_part[None], keep, params)[0]
        return (normed_part, silu(smooth + omega * normed_part))

    (normed, mixed), front_back = jax.vjp(
        front, stream, gains_f[0], biases_f[0], gains_f[1], ema_full.astype(jnp.float32)
    )
    normed_low = normed.astype(jnp.bfloat16)
    mixed_low = mixed.astype(jnp.bfloat16)
    value_pre = jnp.dot(normed_low, values_full, preferred_element_type=jnp.float32)
    value_low = silu(value_pre).astype(jnp.bfloat16)
    mixture = jnp.dot(mixed_low, mix_full, preferred_element_type=jnp.float32)
    middle = width + key_width
    upper = middle + value_width
    update = jax.nn.sigmoid(mixture[:, :width])
    zeta_pre = mixture[:, width:middle]
    zeta = silu(zeta_pre)
    reset_pre = mixture[:, middle:upper]
    reset = silu(reset_pre)
    candidate = mixture[:, upper:]
    query_low = (
        (zeta * heads_f[0] + query_shift).astype(jnp.bfloat16).reshape(blocks, span, key_width)
    )
    key_low = (zeta * heads_f[1]).astype(jnp.bfloat16).reshape(blocks, span, key_width)
    value_blocks = value_low.reshape(blocks, span, value_width)
    scores = block_scores(query_low, key_low, position_f, scale)
    log_total = jax.nn.logsumexp(scores, axis=-1, keepdims=True)
    weights_low = jnp.exp(scores - log_total).astype(jnp.bfloat16)
    attended = jnp.einsum(
        "kij,kjv->kiv", weights_low, value_blocks, preferred_element_type=jnp.float32
    ).reshape(rows, value_width)
    gated_low = (attended * reset).astype(jnp.bfloat16)
    hidden_pre = candidate + jnp.dot(gated_low, out_full, preferred_element_type=jnp.float32)
    hidden = silu(hidden_pre)
    attn_branch = update * (hidden - stream)
    first = stream + attn_branch
    normed_two, norm_back = jax.vjp(layer_norm, first, gains_f[2], biases_f[1])
    normed_two_low = normed_two.astype(jnp.bfloat16)
    ffn_rows = group_rows(normed_two_low)
    expand_pre = jnp.dot(ffn_rows, expand_use, preferred_element_type=jnp.float32)
    expand_low = silu(expand_pre).astype(jnp.bfloat16)
    branch_part = jnp.dot(expand_low, reduce_use, preferred_element_type=jnp.float32)
    branch = group_total(branch_part)
    output = ((first + branch) * mask).astype(jnp.bfloat16)
    values_back, mix_back, out_back = (
        lax.all_gather(w_values, ("dp", "fsdp"), axis=0, tiled=True),
        lax.all_gather(w_mix, ("dp", "fsdp"), axis=0, tiled=True),
        lax.all_gather(w_out, ("dp", "fsdp"), axis=0, tiled=True),
    )
    grad_out = cotangent.astype(jnp.float32) * mask
    grad_branch = grad_out.astype(jnp.bfloat16)
    grad_rows = group_rows(grad_branch)
    grad_reduce = dot_rows(expand_low, grad_rows)
    grad_expand_out = dot_cols(grad_rows, reduce_use)
    grad_expand_pre = (grad_expand_out * silu_slope(expand_pre)).astype(jnp.bfloat16)
    grad_expand = dot_rows(ffn_rows, grad_expand_pre)
    normed_two_part = dot_cols(grad_expand_pre, expand_use)
    grad_normed_two = group_total(normed_two_part)
    grad_first_norm, grad_gain_two, grad_shift_two = norm_back(grad_normed_two)
    grad_first = grad_out + grad_first_norm
    grad_direct = grad_first * (1.0 - update)
    grad_update = grad_first * (hidden - stream)
    grad_hidden_pre = grad_first * update * silu_slope(hidden_pre)
    grad_hidden_low = grad_hidden_pre.astype(jnp.bfloat16)
    grad_out_proj = dot_rows(gated_low, grad_hidden_low)
    grad_gated = dot_cols(grad_hidden_low, out_back)
    grad_attended = (grad_gated * reset).astype(jnp.bfloat16).reshape(blocks, span, value_width)
    grad_reset = grad_gated * attended
    scores_again = block_scores(query_low, key_low, position_f, scale)
    probs = jnp.exp(scores_again - log_total)
    probs_low = probs.astype(jnp.bfloat16)
    grad_weights = jnp.einsum(
        "kiv,kjv->kij", grad_attended, value_blocks, preferred_element_type=jnp.float32
    )
    grad_value = jnp.einsum(
        "kij,kiv->kjv", probs_low, grad_attended, preferred_element_type=jnp.float32
    ).reshape(rows, value_width)
    inner = jnp.sum(probs * grad_weights, axis=-1, keepdims=True)
    grad_scores = (probs * (grad_weights - inner)).astype(jnp.bfloat16)
    grad_position = diagonal_sums(jnp.sum(grad_scores.astype(jnp.float32), axis=0))
    grad_query = (
        jnp.einsum(
            "kij,kjz->kiz", grad_scores, key_low, preferred_element_type=jnp.float32
        ).reshape(rows, key_width)
        * scale
    )
    grad_key = (
        jnp.einsum(
            "kij,kiz->kjz", grad_scores, query_low, preferred_element_type=jnp.float32
        ).reshape(rows, key_width)
        * scale
    )
    grad_value_pre = (grad_value * silu_slope(value_pre)).astype(jnp.bfloat16)
    grad_values = dot_rows(normed_low, grad_value_pre)
    grad_normed = dot_cols(grad_value_pre, values_back)
    grad_zeta = grad_query * heads_f[0] + grad_key * heads_f[1]
    grad_heads = jnp.stack([jnp.sum(grad_query * zeta, axis=0), jnp.sum(grad_key * zeta, axis=0)])
    grad_query_shift = jnp.sum(grad_query, axis=0)
    grad_mixture = jnp.concatenate(
        [
            grad_update * update * (1.0 - update),
            grad_zeta * silu_slope(zeta_pre),
            grad_reset * silu_slope(reset_pre),
            grad_hidden_pre,
        ],
        axis=1,
    ).astype(jnp.bfloat16)
    grad_mix = dot_rows(mixed_low, grad_mixture)
    grad_mixed = dot_cols(grad_mixture, mix_back)
    grad_source, grad_gain_one, grad_shift_one, grad_omega, grad_ema = front_back(
        (grad_normed, grad_mixed)
    )
    grad_inputs = grad_direct + grad_source
    grad_gains = jnp.stack([grad_gain_one, grad_omega, grad_gain_two])
    grad_shifts = jnp.stack([grad_shift_one, grad_shift_two])
    summed_expand, grad_reduce_dev = (
        lax.psum_scatter(grad_expand, "dp", scatter_dimension=0, tiled=True),
        lax.psum_scatter(grad_reduce, "dp", scatter_dimension=0, tiled=True),
    )
    summed_pieces = summed_expand.reshape(group_size * shard_rows, data_size, 1, unit_block)
    owned = lax.all_to_all(summed_pieces, "fsdp", split_axis=0, concat_axis=2, tiled=True)
    grad_expand_dev = owned.reshape(shard_rows, hidden_units)
    summed_block = (
        lax.psum_scatter(
            owner_layout(grad_values, owners), ("dp", "fsdp"), scatter_dimension=0, tiled=True
        ),
        lax.psum_scatter(
            owner_layout(grad_mix, owners), ("dp", "fsdp"), scatter_dimension=0, tiled=True
        ),
        lax.psum_scatter(grad_out_proj, ("dp", "fsdp"), scatter_dimension=0, tiled=True),
        lax.psum_scatter(
            owner_layout(grad_ema, owners), ("dp", "fsdp"), scatter_dimension=0, tiled=True
        ),
        lax.psum_scatter(grad_gains, ("dp", "fsdp"), scatter_dimension=1, tiled=True),
        lax.psum_scatter(grad_shifts, ("dp", "fsdp"), scatter_dimension=1, tiled=True),
    )
    values_flat, mix_flat, grad_out_dev, ema_flat, grad_gains_dev, grad_shifts_dev = summed_block
    grad_values_dev = owner_shard(values_flat, grad_values.shape[1])
    grad_mix_dev = owner_shard(mix_flat, grad_mix.shape[1])
    grad_ema_dev = owner_shard(ema_flat, grad_ema.shape[1])
    squares = jnp.stack(
        [
            jnp.sum(mask * stream * stream),
            jnp.sum(mask * attn_branch * attn_branch),
            jnp.sum(mask * branch * branch),
        ]
    )
    square_sums, tokens_seen, heads_total, shift_total, position_total = lax.psum(
        (squares, jnp.sum(valid), grad_heads, grad_query_shift, grad_position), ("dp", "fsdp")
    )
    rms = jnp.sqrt(square_sums / (tokens_seen * width))
    return (
        output,
        grad_inputs,
        grad_values_dev,
        grad_mix_dev,
        grad_out_dev,
        grad_expand_dev,
        grad_reduce_dev,
        grad_ema_dev,
        grad_gains_dev,
        grad_shifts_dev,
        heads_total,
        shift_total,
        position_total,
        rms,
    )


def table_kernel(pos_ref, out_ref):
    wide = jnp.broadcast_to(pos_ref[...], out_ref.shape)
    out_ref[...] = pltpu.roll(wide, 1, 1, stride=1, stride_axis=0)


def distance_table(position):
    span = position.shape[0]
    return pl.pallas_call(
        table_kernel, name="distance_table", out_shape=jax.ShapeDtypeStruct((span, span), F32)
    )(position[::-1][None])


def distance_sums_kernel(grid_ref, out_ref):
    row = lax.broadcasted_iota(jnp.int32, grid_ref.shape, 0)
    col = lax.broadcasted_iota(jnp.int32, grid_ref.shape, 1)
    mirror = jnp.where(row + col == grid_ref.shape[0] - 1, 1.0, 0.0).astype(LOW)
    turned = jnp.dot(grid_ref[...], mirror, preferred_element_type=F32)
    out_ref[...] = jnp.sum(pltpu.roll(turned, 1, 1, stride=1, stride_axis=0), axis=0, keepdims=True)


def distance_sums(grid):
    return pl.pallas_call(
        distance_sums_kernel, name="distance_sums", out_shape=jax.ShapeDtypeStruct((1, grid.shape[1]), F32)
    )(grid)[0]


def rows_dot(left, right):
    return lax.dot_general(left, right, (((0,), (0,)), ((), ())), preferred_element_type=F32)


def cols_dot(left, right):
    return lax.dot_general(left, right, (((1,), (1,)), ((), ())), preferred_element_type=F32)


def halves_to_columns(blocks):
    rows = blocks.shape[1]
    return blocks.reshape(8, rows, 4, 64).transpose(1, 2, 0, 3).reshape(rows, 2048)


def on_plane(
    inputs, lengths, w_values, w_mix, w_out, w_expand, w_reduce, ema_params,
    norm_gains, norm_biases, head_gains, query_bias, position_bias, cotangent,
):
    rows, width = inputs.shape
    scale = head_gains.shape[1] ** (-0.5)
    dp = lax.axis_index("dp")
    f = lax.axis_index("fsdp")
    me = (dp % 2) * 4 + f
    owner = dp * 4 + f
    heads_f = head_gains.astype(F32)
    query_shift = query_bias.astype(F32)
    table = distance_table(position_bias.astype(F32))
    valid = (lax.broadcasted_iota(jnp.int32, (rows, 1), 0) < lengths[0, 0]).astype(F32)
    small = jnp.concatenate(
        [ema_params, norm_gains.T, norm_biases.T, jnp.zeros((32, 59), LOW)], axis=1
    )
    (
        wa, wo, normed_all, mixed_all, cot_all, prm, factor, gain, nrm, pre,
    ) = front(inputs, small, w_values, w_mix, w_out, cotangent, lengths)
    wa = wa.reshape(1024, 896)
    wo = wo.reshape(256, 1024)
    tokens = 8 * rows
    normed_rows = normed_all.reshape(tokens, width)
    mixed_rows = mixed_all.reshape(tokens, width)
    cot_rows = cot_all.reshape(tokens, width)
    stream = inputs.astype(F32)

    value_pre = jnp.dot(normed_rows, wa[:, :256], preferred_element_type=F32)
    value_low = silu(value_pre).astype(LOW)
    mixture = jnp.dot(mixed_rows, wa[:, 256:], preferred_element_type=F32)
    zeta_pre = mixture[:, 128:256]
    zeta = silu(zeta_pre)
    reset_pre = mixture[:, 256:512]
    reset = silu(reset_pre)
    query_low = (zeta * heads_f[0] + query_shift).astype(LOW).reshape(8, rows, 128)
    key_low = (zeta * heads_f[1]).astype(LOW).reshape(8, rows, 128)
    row = lax.broadcasted_iota(jnp.int32, (rows, rows), 0)
    col = lax.broadcasted_iota(jnp.int32, (rows, rows), 1)
    scores = jnp.einsum("kiz,kjz->kij", query_low, key_low, preferred_element_type=F32) * scale + table
    scores = jnp.where(row >= col, scores, NEG)
    log_total = jax.nn.logsumexp(scores, axis=-1, keepdims=True)
    probs = jnp.exp(scores - log_total)
    weights_low = probs.astype(LOW)
    value_blocks = value_low.reshape(8, rows, 256)
    attended = jnp.einsum("kij,kjv->kiv", weights_low, value_blocks, preferred_element_type=F32).reshape(tokens, 256)
    gated_low = (attended * reset).astype(LOW)
    part = jnp.dot(gated_low, wo, preferred_element_type=F32)
    spread_cols = (jnp.arange(8)[:, None] == me).astype(F32)
    part = (part.reshape(tokens, 8, 128) + mixture[:, None, 512:640] * spread_cols[None]).reshape(8, rows, width)
    hidden_pre, update_all, we, wr = join_hidden(
        part.astype(LOW), mixture[:, :128].reshape(8, rows, 128).astype(LOW), w_expand, w_reduce
    )
    we = we.reshape(1024, 512)
    wr = wr.reshape(512, 1024)

    update = jax.nn.sigmoid(update_all.astype(F32).transpose(1, 0, 2).reshape(rows, width))
    hidden = silu(hidden_pre)
    attn_branch = update * (hidden - stream)
    first = stream + attn_branch
    centred = first - jnp.mean(first, axis=-1, keepdims=True)
    inverse = lax.rsqrt(jnp.mean(centred * centred, axis=-1, keepdims=True) + EPS)
    xhat = centred * inverse
    normed_two_low = (xhat * prm[2] + prm[4]).astype(LOW)
    ffn_rows = all_tokens(normed_two_low, 3).reshape(tokens, width)

    expand_pre = jnp.dot(ffn_rows, we, preferred_element_type=F32)
    expand_low = silu(expand_pre).astype(LOW)
    branch_part = jnp.dot(expand_low, wr, preferred_element_type=F32).astype(LOW)
    grad_expand_out = cols_dot(cot_rows, wr)
    grad_expand_pre = (grad_expand_out * silu_slope(expand_pre)).astype(LOW)
    normed_two_part = cols_dot(grad_expand_pre, we).astype(LOW)
    grad_reduce = rows_dot(expand_low, cot_rows).astype(LOW)
    grad_expand = rows_dot(ffn_rows, grad_expand_pre).astype(LOW)
    grad_normed_two, branch, grad_expand_sum, grad_reduce_dev = join_ffn(
        normed_two_part.reshape(8, rows, width), branch_part.reshape(8, rows, width),
        grad_expand.reshape(4, 256, 512), grad_reduce.reshape(4, 128, 1024),
    )

    output = ((first + branch) * valid).astype(LOW)
    grad_out = cotangent.astype(F32) * valid
    gh = grad_normed_two * prm[2]
    grad_first = grad_out + inverse * (
        gh - jnp.mean(gh, axis=-1, keepdims=True) - xhat * jnp.mean(gh * xhat, axis=-1, keepdims=True)
    )
    grad_direct = grad_first * (1.0 - update)
    grad_update = grad_first * (hidden - stream)
    grad_hidden_low = (grad_first * update * silu_slope(hidden_pre)).astype(LOW)
    grad_update_low = (grad_update * update * (1.0 - update)).astype(LOW)
    hid_all, upd_all = back_tokens(
        grad_hidden_low, grad_update_low.reshape(rows, 8, 128).transpose(1, 0, 2)
    )
    hid_rows = hid_all.reshape(tokens, width)
    upd_rows = upd_all.reshape(tokens, 128)

    grad_gated = cols_dot(hid_rows, wo)
    grad_attended = (grad_gated * reset).astype(LOW)
    grad_reset = grad_gated * attended
    attended_blocks = grad_attended.reshape(8, rows, 256)
    grad_weights = jnp.einsum("kiv,kjv->kij", attended_blocks, value_blocks, preferred_element_type=F32)
    grad_weights_all = swap_blocks(grad_weights, 6)
    grad_value = jnp.einsum("kij,kiv->kjv", weights_low, attended_blocks, preferred_element_type=F32).reshape(tokens, 256)
    grad_value_pre = (grad_value * silu_slope(value_pre)).astype(LOW)
    grad_reset_low = (grad_reset * silu_slope(reset_pre)).astype(LOW)
    cand_rows = lax.dynamic_slice_in_dim(hid_rows, me * 128, 128, 1)
    grad_mixture = jnp.concatenate([upd_rows, grad_reset_low, cand_rows], axis=1)
    wa_mix = jnp.concatenate([wa[:, 256:384], wa[:, 512:896]], axis=1)
    normed_part = cols_dot(grad_value_pre, wa[:, :256]).astype(LOW)
    mixed_part = cols_dot(grad_mixture, wa_mix).astype(LOW)
    grad_out_part = rows_dot(gated_low, hid_rows).astype(LOW)
    grad_a = jnp.concatenate(
        [rows_dot(normed_rows, grad_value_pre), rows_dot(mixed_rows, grad_mixture)], axis=1
    ).astype(LOW)

    def own(value):
        return lax.dynamic_index_in_dim(value, me, 0, keepdims=False)

    own_probs = own(probs)
    own_zeta_pre = own(zeta_pre.reshape(8, rows, 128))
    own_zeta = silu(own_zeta_pre)
    grad_weights_own = jnp.sum(grad_weights_all, axis=0)
    inner = jnp.sum(own_probs * grad_weights_own, axis=-1, keepdims=True)
    grad_scores = (own_probs * (grad_weights_own - inner)).astype(LOW)
    grad_position = distance_sums(grad_scores)
    grad_query = jnp.dot(grad_scores, own(key_low), preferred_element_type=F32) * scale
    grad_key = rows_dot(grad_scores, own(query_low)) * scale
    grad_zeta = grad_query * heads_f[0] + grad_key * heads_f[1]
    grad_heads = jnp.stack([jnp.sum(grad_query * own_zeta, axis=0), jnp.sum(grad_key * own_zeta, axis=0)])
    grad_query_shift = jnp.sum(grad_query, axis=0)
    grad_zeta_low = (grad_zeta * silu_slope(own_zeta_pre)).astype(LOW)
    zeta_all, grad_normed, grad_mixed, grad_a_sum, grad_out_dev, grad_expand_swapped = join_mixed(
        grad_zeta_low, normed_part.reshape(8, rows, width), mixed_part.reshape(8, rows, width),
        grad_a.reshape(4, 256, 768), grad_out_part.reshape(4, 64, 1024),
        grad_expand_sum.reshape(8, 32, 512),
    )
    grad_z = rows_dot(mixed_rows, zeta_all.reshape(tokens, 128))
    grad_mixed = grad_mixed + cols_dot(grad_zeta_low, wa[:, 384:512])

    gm = grad_mixed * silu_slope(pre)
    factor_sum, gain_sum, grad_nrm = ema_back(factor, gain, nrm, gm.reshape(rows, 8, 128))
    normed = nrm.reshape(rows, width)
    grad_normed_all = grad_normed + gm * prm[1] + grad_nrm.reshape(rows, width)
    centre_one = stream - jnp.mean(stream, axis=-1, keepdims=True)
    inverse_one = lax.rsqrt(jnp.mean(centre_one * centre_one, axis=-1, keepdims=True) + EPS)
    xhat_one = centre_one * inverse_one
    gh_one = grad_normed_all * prm[0]
    grad_inputs = grad_direct + inverse_one * (
        gh_one - jnp.mean(gh_one, axis=-1, keepdims=True) - xhat_one * jnp.mean(gh_one * xhat_one, axis=-1, keepdims=True)
    )
    misc = jnp.concatenate(
        [
            grad_heads.reshape(-1), grad_query_shift, grad_position,
            jnp.stack(
                [
                    jnp.sum(valid * stream * stream), jnp.sum(valid * attn_branch * attn_branch),
                    jnp.sum(valid * branch * branch), jnp.sum(valid),
                ]
            ),
            jnp.zeros((width - 516,), F32),
        ]
    )
    vectors = jnp.stack(
        [
            jnp.sum(grad_normed_all * xhat_one, axis=0), jnp.sum(gm * normed, axis=0),
            jnp.sum(grad_normed_two * xhat, axis=0), jnp.sum(grad_normed_all, axis=0),
            jnp.sum(grad_normed_two, axis=0), misc, jnp.zeros_like(misc), jnp.zeros_like(misc),
        ]
    )
    sums = jnp.concatenate([factor_sum.reshape(16, width), gain_sum.reshape(16, width), vectors])
    grad_a_all, grad_z_all, sums_all = last_sums(
        grad_a_sum.reshape(8, 32, 768), lax.dynamic_index_in_dim(grad_z.reshape(4, 8, 32, 128), me, 1, keepdims=False), sums
    )
    sums_all = sums_all.transpose(1, 0, 2).reshape(40, width)
    mine = lax.dynamic_slice_in_dim(sums_all, owner * 32, 32, 1)
    raw = ema_params.astype(F32)
    damping = jax.nn.sigmoid(raw[:, :16])
    mixing = jax.nn.sigmoid(raw[:, 16:32])
    expand = raw[:, 32:48]
    project = raw[:, 48:64]
    by_factor = mine[:16].T * (0.25 * project * mixing * expand)
    by_gain = mine[16:32].T
    by_inflow = 0.25 * project * by_gain
    grad_ema = jnp.concatenate(
        [
            -by_factor * mixing * damping * (1.0 - damping),
            (by_inflow * expand - by_factor * damping) * mixing * (1.0 - mixing),
            by_inflow * mixing,
            0.25 * mixing * expand * by_gain,
        ],
        axis=1,
    )
    full = grad_a_all.astype(F32)
    grad_values_dev = halves_to_columns(full[:, :, :256])
    grad_mix_dev = jnp.concatenate(
        [
            full[:, :, 256:384].transpose(1, 0, 2).reshape(32, 1024),
            jnp.sum(grad_z_all, axis=0),
            halves_to_columns(full[:, :, 384:640]),
            full[:, :, 640:768].transpose(1, 0, 2).reshape(32, 1024),
        ],
        axis=1,
    )
    grad_expand_dev = (
        grad_expand_swapped.astype(F32).reshape(8, 32, 4, 128).transpose(1, 2, 0, 3).reshape(32, 4096)
    )
    tail = sums_all[37]
    rms = jnp.sqrt(tail[512:515] / (tail[515] * width))
    return (
        output, grad_inputs, grad_values_dev, grad_mix_dev, grad_out_dev, grad_expand_dev, grad_reduce_dev,
        grad_ema, mine[32:35], mine[35:37], tail[:256].reshape(2, 128), tail[256:384], tail[384:512], rms,
    )


def solution(mesh):
    in_specs = (
        P(("dp", "fsdp"), None),
        P(("dp", "fsdp"), None),
        P(("dp", "fsdp"), None),
        P(("dp", "fsdp"), None),
        P(("dp", "fsdp"), None),
        P(("dp", "fsdp"), None),
        P(("dp", "fsdp"), None),
        P(("dp", "fsdp"), None),
        P(None, ("dp", "fsdp")),
        P(None, ("dp", "fsdp")),
        P(),
        P(),
        P(),
        P(("dp", "fsdp"), None),
    )
    out_specs = (
        P(("dp", "fsdp"), None),
        P(("dp", "fsdp"), None),
        P(("dp", "fsdp"), None),
        P(("dp", "fsdp"), None),
        P(("dp", "fsdp"), None),
        P(("dp", "fsdp"), None),
        P(("dp", "fsdp"), None),
        P(("dp", "fsdp"), None),
        P(None, ("dp", "fsdp")),
        P(None, ("dp", "fsdp")),
        P(),
        P(),
        P(),
        P(),
    )
    planes = mesh.shape["dp"] == 8 and mesh.shape["fsdp"] == 4
    return jax.shard_map(
        on_plane if planes else on_device, mesh=mesh, in_specs=in_specs, out_specs=out_specs, check_vma=False
    )
```

```python
import functools

import jax
import jax.numpy as jnp
from jax import lax
from jax.experimental import pallas as pl
from jax.experimental.pallas import tpu as pltpu
from jax.sharding import PartitionSpec as P

EPS = 1e-05
NEG = -1e30
F32 = jnp.float32
LOW = jnp.bfloat16
MESH = pl.DeviceIdType.MESH
LINES = 112
STATES = 16


def silu(value):
    return value * jax.nn.sigmoid(value)


def silu_slope(value):
    sigma = jax.nn.sigmoid(value)
    return sigma * (1.0 + value * (1.0 - sigma))


def here():
    dp = lax.axis_index("dp")
    f = lax.axis_index("fsdp")
    return dp // 2, dp % 2, f // 2, f % 2


def device(z, y, x, c):
    return (z * 2 + y, x * 2 + c)


def slot_of(y, x, c):
    return y * 4 + x * 2 + c


def plane_peers(y, x, c):
    peers = []
    for mask in range(1, 8):
        peers.append(
            (
                1 - y if mask & 4 else y,
                1 - x if mask & 2 else x,
                1 - c if mask & 1 else c,
            )
        )
    return peers


def line_peers(z):
    return [z + 1 - 2 * (z % 2), 3 - z, (z + 2) % 4]


def greet(across=True):
    z, y, x, c = here()
    barrier = pltpu.get_barrier_semaphore()
    count = 7
    for peer in plane_peers(y, x, c):
        pl.semaphore_signal(barrier, inc=1, device_id=device(z, *peer), device_id_type=MESH)
    if across:
        count = 10
        for other in line_peers(z):
            pl.semaphore_signal(barrier, inc=1, device_id=device(other, y, x, c), device_id_type=MESH)
    pl.semaphore_wait(barrier, count)


class Net:
    def __init__(self, send, recv):
        self.send = send
        self.recv = recv
        self.used = 0

    def take(self, count):
        self.used += count
        return self.used - count

    def make(self, line, src, dst, target):
        return pltpu.make_async_remote_copy(
            src_ref=src,
            dst_ref=dst,
            send_sem=self.send.at[line],
            recv_sem=self.recv.at[line],
            device_id=target,
            device_id_type=MESH,
        )

    def copy(self, src, dst, target):
        made = self.make(self.take(1), src, dst, target)
        made.start()
        return made


def neighbours(y, x):
    return [(y, 1 - x), (1 - y, x), (1 - y, 1 - x)]


def gather_plane(net, src, dst):
    z, y, x, c = here()
    me = slot_of(y, x, c)
    near = [net.copy(src, dst.at[me], device(z, yy, xx, c)) for yy, xx in neighbours(y, x)]
    twin = [net.copy(src, dst.at[me], device(z, y, x, 1 - c))]
    dst[me] = src[...]
    yield
    for copy, (yy, xx) in zip(near, neighbours(y, x)):
        copy.wait_recv()
        block = dst.at[slot_of(yy, xx, c)]
        twin.append(net.copy(block, block, device(z, y, x, 1 - c)))
    yield
    for copy in twin:
        copy.wait()
    for copy in near:
        copy.wait_send()


def spread_plane(net, src, dst):
    z, y, x, c = here()
    me = slot_of(y, x, c)
    copies = [net.copy(src, dst.at[me], device(z, *peer)) for peer in plane_peers(y, x, c)]
    dst[me] = src[...]
    yield
    for copy in copies:
        copy.wait()


def swap_plane(net, src, dst):
    z, y, x, c = here()
    me = slot_of(y, x, c)
    copies = []
    for peer in plane_peers(y, x, c):
        copies.append(net.copy(src.at[slot_of(*peer)], dst.at[me], device(z, *peer)))
    dst[me] = src[me]
    yield
    for copy in copies:
        copy.wait()


def sum_plane(net, src, got, sent, far, out):
    z, y, x, c = here()
    chips = [(y, x)] + neighbours(y, x)
    first = []
    for k in (3, 1, 2, 0):
        yy, xx = chips[k]
        first.append((k, net.copy(src.at[slot_of(yy, xx, 1 - c)], got.at[k], device(z, y, x, 1 - c))))
    yield
    second = []
    for k, copy in first:
        copy.wait_recv()
        yy, xx = chips[k]
        pair = src[slot_of(yy, xx, c)].astype(F32) + got[k].astype(F32)
        if k == 0:
            out[...] = pair
        else:
            sent[k - 1] = pair.astype(LOW)
            second.append(net.copy(sent.at[k - 1], far.at[k - 1], device(z, yy, xx, c)))
    yield
    for k, copy in first:
        copy.wait_send()
    for copy in second:
        copy.wait()
    out[...] = out[...] + far[0].astype(F32) + far[1].astype(F32) + far[2].astype(F32)


def gather_line(net, bufs):
    z, y, x, c = here()
    near, mirror, _ = line_peers(z)
    waits = []
    for buf in bufs:
        waits.append(net.copy(buf.at[z], buf.at[z], device(near, y, x, c)))
        waits.append(net.copy(buf.at[z], buf.at[z], device(mirror, y, x, c)))
    yield
    relayed = (2 * z) % 3 + 3 * (z // 3)
    target = (3 * z + 2) % 5
    more = []
    for k, buf in enumerate(bufs):
        waits[2 * k].wait_recv()
        waits[2 * k + 1].wait_recv()
        more.append(net.copy(buf.at[relayed], buf.at[relayed], device(target, y, x, c)))
    yield
    for copy in waits:
        copy.wait_send()
    for copy in more:
        copy.wait()


def spread_line(net, buf):
    z, y, x, c = here()
    copies = [net.copy(buf.at[z], buf.at[z], device(other, y, x, c)) for other in line_peers(z)]
    yield
    for copy in copies:
        copy.wait()


def sum_line(net, bufs, gots, outs):
    z, y, x, c = here()
    near, mirror, across = line_peers(z)
    target = (2 * z + 1) % 5
    relayed = (2 * z) % 3 + 3 * (z // 3)
    first = []
    for buf, got in zip(bufs, gots):
        first.append(net.copy(buf.at[across], got.at[0], device(target, y, x, c)))
    yield
    second = []
    for copy, buf, got in zip(first, bufs, gots):
        copy.wait_recv()
        buf[relayed] = (buf[relayed].astype(F32) + got[0].astype(F32)).astype(LOW)
        second.append(net.copy(buf.at[near], got.at[1], device(near, y, x, c)))
        second.append(net.copy(buf.at[mirror], got.at[2], device(mirror, y, x, c)))
    yield
    for copy in first:
        copy.wait_send()
    for copy in second:
        copy.wait()
    for buf, got, out in zip(bufs, gots, outs):
        total = buf[z].astype(F32) + got[1].astype(F32) + got[2].astype(F32)
        out[...] = total.reshape(out.shape).astype(out.dtype)


def drive(*stages):
    live = list(stages)
    while live:
        live = [stage for stage in live if advance(stage)]


def advance(stage):
    for _ in stage:
        return True
    return False


VMEM = pl.BlockSpec(memory_space=pltpu.VMEM)


def exchange(kernel, name, outs, scratch, number, *operands, smem=()):
    specs = [
        pl.BlockSpec(memory_space=pltpu.SMEM) if index in smem else VMEM
        for index in range(len(operands))
    ]
    return pl.pallas_call(
        kernel,
        name=name,
        out_shape=[jax.ShapeDtypeStruct(shape, dtype) for shape, dtype in outs],
        in_specs=specs,
        out_specs=[VMEM] * len(outs),
        scratch_shapes=[pltpu.VMEM(shape, dtype) for shape, dtype in scratch]
        + [pltpu.SemaphoreType.DMA((LINES,)), pltpu.SemaphoreType.DMA((LINES,))],
        compiler_params=pltpu.CompilerParams(
            collective_id=number, has_side_effects=True, vmem_limit_bytes=58 << 20
        ),
    )(*operands)


def lanes_to_rows(wide, tall):
    for s in range(8):
        tall[:, s, :] = wide[:, s * 128 : (s + 1) * 128]


def pick_halves(arr, base, slot, pair):
    one = base + ((2 * pair * 8 + slot) // 2) * 128
    two = base + (((2 * pair + 1) * 8 + slot) // 2) * 128
    left = arr[:, one : one + 128].astype(F32)
    right = arr[:, two : two + 128].astype(F32)
    lane = lax.broadcasted_iota(jnp.int32, left.shape, 1)
    if slot % 2 == 0:
        return jnp.where(lane < 64, left, pltpu.roll(right, 64, 1)).astype(LOW)
    return jnp.where(lane < 64, pltpu.roll(left, 64, 1), right).astype(LOW)


def ema_forward(factor, gain, source, out):
    steps = source.shape[0]

    def step(t, states):
        column = source[t]
        new = []
        terms = []
        for j in range(STATES):
            state = factor[j] * states[j] + column
            new.append(state)
            terms.append(gain[j] * state)
        while len(terms) > 1:
            terms = [terms[i] + terms[i + 1] for i in range(0, len(terms), 2)]
        out[t] = terms[0]
        return tuple(new)

    zero = jnp.zeros(source.shape[1:], F32)
    lax.fori_loop(0, steps, step, (zero,) * STATES)


def front_kernel(
    x_ref, small_ref, wv_ref, wm_ref, wo_ref, cot_ref, lens_ref,
    wa_ref, wo_all, normed_all, mixed_all, cot_all, prm_ref, fac_ref, gain_ref, nrm_ref, pre_ref,
    blocks, small_all, turned, smooth, own_normed, own_mixed, own_cot, send, recv,
):
    net = Net(send, recv)
    z, y, x, c = here()
    greet()
    small_plane = spread_plane(net, small_ref, small_all.at[z])
    advance(small_plane)
    for s in range(8):
        for pair in range(2):
            blocks[s, :, pair * 128 : (pair + 1) * 128] = pick_halves(wv_ref, 0, s, pair)
            blocks[s, :, 512 + pair * 128 : 640 + pair * 128] = pick_halves(wm_ref, 1152, s, pair)
        blocks[s, :, 256:384] = wm_ref[:, s * 128 : (s + 1) * 128]
        blocks[s, :, 384:512] = wm_ref[:, 1024:1152]
        blocks[s, :, 768:896] = wm_ref[:, 3200 + s * 128 : 3328 + s * 128]
    weights_plane = swap_plane(net, blocks, wa_ref.at[z])
    advance(weights_plane)
    advance(small_plane)
    small_line = spread_line(net, small_all)
    advance(small_line)
    wo_all[z] = wo_ref[...]
    out_line = gather_line(net, [wo_all])
    advance(out_line)
    stream = x_ref[...].astype(F32)
    centered = stream - jnp.mean(stream, axis=-1, keepdims=True)
    spread = jnp.mean(centered * centered, axis=-1, keepdims=True)
    xhat = centered * lax.rsqrt(spread + EPS)
    pre_ref[...] = xhat
    row = lax.broadcasted_iota(jnp.int32, cot_ref.shape, 0)
    own_cot[...] = jnp.where(row < lens_ref[0, 0], cot_ref[...].astype(F32), 0.0).astype(LOW)
    advance(weights_plane)
    weights_line = gather_line(net, [wa_ref])
    advance(weights_line)
    advance(small_line)
    turned[...] = small_all[...].reshape(1024, 128).astype(F32).T
    damping = jax.nn.sigmoid(turned[0:16])
    mixing = jax.nn.sigmoid(turned[16:32])
    factor = 1.0 - mixing * damping
    gain = 0.25 * turned[48:64] * (mixing * turned[32:48])
    lanes_to_rows(factor, fac_ref)
    lanes_to_rows(gain, gain_ref)
    prm_ref[...] = turned[64:72]
    normed = pre_ref[...] * turned[64:65] + turned[67:68]
    own_normed[...] = normed.astype(LOW)
    normed_plane = gather_plane(net, own_normed, normed_all)
    advance(normed_plane)
    lanes_to_rows(normed, nrm_ref)
    pre_ref[...] = turned[65:66] * normed
    ema_forward(fac_ref, gain_ref, nrm_ref, smooth)
    for s in range(8):
        cols = slice(s * 128, (s + 1) * 128)
        pre_ref[:, cols] = pre_ref[:, cols] + smooth[:, s, :]
    own_mixed[...] = silu(pre_ref[...]).astype(LOW)
    mixed_plane = gather_plane(net, own_mixed, mixed_all)
    advance(mixed_plane)
    cot_plane = gather_plane(net, own_cot, cot_all)
    drive(normed_plane, mixed_plane, weights_line, out_line, cot_plane)


def front(inputs, small, w_values, w_mix, w_out, cotangent, lengths):
    rows, width = inputs.shape
    return exchange(
        front_kernel, "front",
        [
            ((4, 8, 32, 896), LOW), ((4, 64, 1024), LOW),
            ((8, rows, width), LOW), ((8, rows, width), LOW), ((8, rows, width), LOW),
            ((8, width), F32), ((16, 8, 128), F32), ((16, 8, 128), F32),
            ((rows, 8, 128), F32), ((rows, width), F32),
        ],
        [
            ((8, 32, 896), LOW), ((4, 8, 32, 128), LOW), ((128, 1024), F32), ((rows, 8, 128), F32),
            ((rows, width), LOW), ((rows, width), LOW), ((rows, width), LOW),
        ],
        1,
        inputs, small, w_values, w_mix, w_out, cotangent, lengths, smem=(6,),
    )


def swap_line(net, src, dst):
    z, y, x, c = here()
    copies = [net.copy(src.at[other], dst.at[z], device(other, y, x, c)) for other in line_peers(z)]
    dst[z] = src[z]
    yield
    for copy in copies:
        copy.wait()


def rows_dot(left, right):
    return lax.dot_general(left, right, (((0,), (0,)), ((), ())), preferred_element_type=F32)


def cols_dot(left, right):
    return lax.dot_general(left, right, (((1,), (1,)), ((), ())), preferred_element_type=F32)


class PlaneSum:
    def __init__(self, net, make, part, got, sent, far, total):
        self.net, self.make = net, make
        self.part, self.got, self.sent, self.far, self.total = part, got, sent, far, total
        self.base = net.take(7)

    def chip(self, k):
        z, y, x, c = here()
        return (y + k // 2) % 2, (x + k % 2) % 2

    def inner(self, k):
        z, y, x, c = here()
        return self.net.make(self.base + k, self.part.at[k], self.got.at[k], device(z, y, x, 1 - c))

    def outer(self, k):
        z, y, x, c = here()
        yy, xx = self.chip(k)
        return self.net.make(self.base + 3 + k, self.sent.at[k - 1], self.far.at[k - 1], device(z, yy, xx, c))

    def for_twin(self):
        z, y, x, c = here()

        @pl.loop(0, 4)
        def _(i):
            k = 3 - i
            yy, xx = self.chip(k)
            self.part[k] = self.make(slot_of(yy, xx, 1 - c)).astype(LOW)
            self.inner(k).start()

    def for_self(self):
        z, y, x, c = here()

        @pl.loop(0, 4)
        def _(i):
            k = 3 - i
            yy, xx = self.chip(k)
            block = self.make(slot_of(yy, xx, c))
            self.inner(k).wait_recv()
            pair = block + self.got[k].astype(F32)
            self.total[...] = pair

            @pl.when(i < 3)
            def _():
                self.sent[k - 1] = pair.astype(LOW)
                self.outer(k).start()

    def finish(self):
        @pl.loop(0, 4)
        def _(k):
            self.inner(k).wait_send()

        @pl.loop(1, 4)
        def _(k):
            self.outer(k).wait()
            self.total[...] = self.total[...] + self.far[k - 1].astype(F32)


def twin_scratch(rows, width):
    return [((4, rows, width), LOW), ((4, rows, width), LOW), ((3, rows, width), LOW), ((3, rows, width), LOW)]


def row_mean(value):
    return jnp.mean(value, axis=-1, keepdims=True)


def block_scores_of(zeta, heads, shift, table):
    query_low = (zeta * heads[0:1] + shift[...]).astype(LOW)
    key_low = (zeta * heads[1:2]).astype(LOW)
    scores = cols_dot(query_low, key_low) * (zeta.shape[1] ** (-0.5)) + table[...]
    row = lax.broadcasted_iota(jnp.int32, scores.shape, 0)
    col = lax.broadcasted_iota(jnp.int32, scores.shape, 1)
    scores = jnp.where(row >= col, scores, NEG)
    top = jnp.max(scores, axis=-1, keepdims=True)
    log_total = top + jnp.log(jnp.sum(jnp.exp(scores - top), axis=-1, keepdims=True))
    return query_low, key_low, jnp.exp(scores - log_total)


def middle_kernel(
    wa, wo, normed_all, mixed_all, x_ref, prm, table, heads, shift, we_ref, wr_ref,
    two_all, we_all, wr_all, value_pre, value_low, zeta_pre, weights_low, attended, reset_pre, gated,
    hidden_pre, update_pre, first,
    blocks, part, got, sent, far, update_part, update_all, own_two, send, recv,
):
    net = Net(send, recv)
    z, y, x, c = here()
    me = slot_of(y, x, c)
    greet()
    wr_all[z] = wr_ref[...]
    reduce_line = gather_line(net, [wr_all])
    advance(reduce_line)
    for s in range(8):
        for zz in range(4):
            blocks[s, :, zz * 128 : (zz + 1) * 128] = we_ref[:, (zz * 8 + s) * 128 : (zz * 8 + s + 1) * 128]
    expand_plane = swap_plane(net, blocks, we_all.at[z])
    advance(expand_plane)
    cand_cols = pl.ds(pl.multiple_of(me * 128, 128), 128)

    def attend(b):
        pre = jnp.dot(normed_all[b], wa[:, 0:256], preferred_element_type=F32)
        value_pre[b] = pre
        low_values = silu(pre).astype(LOW)
        value_low[b] = low_values
        mixture = jnp.dot(mixed_all[b], wa[:, 256:896], preferred_element_type=F32)
        update_part[b] = mixture[:, 0:128].astype(LOW)
        zeta_pre[b] = mixture[:, 128:256]
        _, _, probs = block_scores_of(silu(mixture[:, 128:256]), heads, shift, table)
        weights_low[b] = probs.astype(LOW)
        mixed_values = jnp.dot(probs.astype(LOW), low_values, preferred_element_type=F32)
        attended[b] = mixed_values
        reset_pre[b] = mixture[:, 256:512]
        gate = (mixed_values * silu(mixture[:, 256:512])).astype(LOW)
        gated[b] = gate
        hidden_pre[...] = jnp.dot(gate, wo[...], preferred_element_type=F32)
        hidden_pre[:, cand_cols] = hidden_pre[:, cand_cols] + mixture[:, 512:640]
        return hidden_pre[...]

    total = PlaneSum(net, attend, part, got, sent, far, hidden_pre)
    total.for_twin()
    advance(expand_plane)
    expand_line = gather_line(net, [we_all])
    advance(expand_line)
    total.for_self()
    update_plane = swap_plane(net, update_part, update_all)
    advance(update_plane)
    total.finish()
    advance(update_plane)
    for s in range(8):
        update_pre[:, s * 128 : (s + 1) * 128] = update_all[s].astype(F32)
    stream = x_ref[...].astype(F32)
    update = jax.nn.sigmoid(update_pre[...])
    first[...] = stream + update * (silu(hidden_pre[...]) - stream)
    centred = first[...] - row_mean(first[...])
    xhat = centred * lax.rsqrt(row_mean(centred * centred) + EPS)
    own_two[...] = (xhat * prm[2:3] + prm[4:5]).astype(LOW)
    two_plane = gather_plane(net, own_two, two_all)
    advance(two_plane)
    advance(reduce_line)
    advance(two_plane)
    drive(expand_line, two_plane, reduce_line)


def middle(wa, wo, normed_all, mixed_all, inputs, prm, table, heads, shift, w_expand, w_reduce):
    rows, width = inputs.shape
    wide = ((8, rows, 256), F32)
    own = ((rows, width), F32)
    return exchange(
        middle_kernel, "middle",
        [
            ((8, rows, width), LOW), ((4, 8, 32, 512), LOW), ((4, 128, width), LOW),
            wide, ((8, rows, 256), LOW), ((8, rows, 128), F32), ((8, rows, 128), LOW), wide, wide,
            ((8, rows, 256), LOW), own, own, own,
        ],
        [((8, 32, 512), LOW)] + twin_scratch(rows, width)
        + [((8, rows, 128), LOW), ((8, rows, 128), LOW), ((rows, width), LOW)],
        2,
        wa, wo, normed_all, mixed_all, inputs, prm, table, heads, shift, w_expand, w_reduce,
    )


def ema_backward(fac, gain, nrm, pull_ref, factor_sum, gain_sum, out):
    steps = nrm.shape[0]
    zero = jnp.zeros(nrm.shape[1:], F32)
    group = 4
    for base in range(0, STATES, group):

        def step(t, carry):
            column = nrm[t]
            pull = pull_ref[t]
            new = []
            for k in range(group):
                state, slope, by_factor, by_gain = carry[4 * k : 4 * k + 4]
                f = fac[base + k]
                slope = f * slope + state
                state = f * state + column
                new += [state, slope, by_factor + pull * slope, by_gain + pull * state]
            return tuple(new)

        done = lax.fori_loop(0, steps, step, (zero,) * (4 * group))
        for k in range(group):
            factor_sum[base + k] = done[4 * k + 2]
            gain_sum[base + k] = done[4 * k + 3]

    def turn(t, states):
        at = steps - 1 - t
        pull = pull_ref[at]
        new = []
        terms = []
        for j in range(STATES):
            state = fac[j] * states[j] + pull
            new.append(state)
            terms.append(gain[j] * state)
        while len(terms) > 1:
            terms = [terms[i] + terms[i + 1] for i in range(0, len(terms), 2)]
        out[at] = terms[0]
        return tuple(new)

    lax.fori_loop(0, steps, turn, (zero,) * STATES)


def back_kernel(
    wa, wo, we, wr, normed_all, mixed_all, two_all, cot_all,
    value_pre, value_low, zeta_pre, weights_low, attended, reset_pre, gated, hidden_pre, update_pre, first,
    x_ref, cot_ref, prm, fac, gain, nrm, pre_ref, table, heads, shift, lens,
    output, grad_inputs, grad_values, grad_mix, grad_out, grad_expand, grad_reduce, sums_out,
    expand_low, grad_pre, part, got, sent, far, got_b, sent_b, far_b, normed_two, branch, own_hid, hid_all,
    upd, upd_all, value_back, mixture_back, scores_part, scores_all, zeta_own, zeta_all,
    gr, gr_got, ge, ge_got, ge_sum, ge_all, go, go_got, ga, ga_got, ga_sum, ga_all, gz, gz_own, gz_line,
    pull, ema_out, fac_sum, gain_sum, sums, sum_blocks, sum_parts, sum_rows, sum_cols,
    send, recv,
):
    net = Net(send, recv)
    z, y, x, c = here()
    me = slot_of(y, x, c)
    near, mirror, across = line_peers(z)
    rows, width = x_ref.shape
    tokens = 8 * rows
    greet()
    valid_row = lax.broadcasted_iota(jnp.int32, (rows, 1), 0)
    valid = jnp.where(valid_row < lens[0, 0], 1.0, 0.0)

    def expand(b):
        pre = jnp.dot(two_all[b], we[...], preferred_element_type=F32)
        expand_low[b] = silu(pre).astype(LOW)
        grad = (cols_dot(cot_all[b], wr[...]) * silu_slope(pre)).astype(LOW)
        grad_pre[b] = grad
        return cols_dot(grad, we[...])

    normed_sum = PlaneSum(net, expand, part, got, sent, far, normed_two)
    normed_sum.for_twin()
    normed_sum.for_self()

    def reduce_grad(zz):
        cols = pl.ds(pl.multiple_of(zz * 128, 128), 128)
        gr[zz] = rows_dot(
            expand_low[:, :, cols].reshape(tokens, 128), cot_all[...].reshape(tokens, width)
        ).astype(LOW)

    def expand_grad(zz):
        cols = pl.ds(pl.multiple_of(zz * 256, 256), 256)
        ge[zz] = rows_dot(
            two_all[:, :, cols].reshape(tokens, 256), grad_pre[...].reshape(tokens, 512)
        ).astype(LOW)

    @pl.loop(0, 4)
    def _(zz):
        reduce_grad(zz)

    @pl.loop(0, 4)
    def _(zz):
        expand_grad(zz)

    ffn_line = sum_line(net, [gr, ge], [gr_got, ge_got], [grad_reduce, ge_sum])
    advance(ffn_line)
    normed_sum.finish()

    stream = x_ref[...].astype(F32)
    update = jax.nn.sigmoid(update_pre[...])
    hidden = silu(hidden_pre[...])
    centred = first[...] - row_mean(first[...])
    inverse = lax.rsqrt(row_mean(centred * centred) + EPS)
    xhat = centred * inverse
    grad_two = normed_two[...]
    sums[34:35] = jnp.sum(grad_two * xhat, axis=0, keepdims=True)
    sums[36:37] = jnp.sum(grad_two, axis=0, keepdims=True)
    gh = grad_two * prm[2:3]
    grad_first = cot_ref[...].astype(F32) * valid + inverse * (gh - row_mean(gh) - xhat * row_mean(gh * xhat))
    grad_inputs[...] = grad_first * (1.0 - update)
    grad_update = (grad_first * (hidden - stream) * update * (1.0 - update)).astype(LOW)
    own_hid[...] = (grad_first * update * silu_slope(hidden_pre[...])).astype(LOW)
    hid_plane = gather_plane(net, own_hid, hid_all)
    advance(hid_plane)
    for s in range(8):
        upd[s] = grad_update[:, s * 128 : (s + 1) * 128]
    upd_plane = swap_plane(net, upd, upd_all)
    advance(upd_plane)

    def branch_block(b):
        return jnp.dot(expand_low[b], wr[...], preferred_element_type=F32)

    branch_sum = PlaneSum(net, branch_block, part, got_b, sent_b, far_b, branch)
    branch_sum.for_twin()
    advance(hid_plane)
    branch_sum.for_self()
    drive(hid_plane)
    advance(upd_plane)
    advance(ffn_line)

    cand_cols = pl.ds(pl.multiple_of(me * 128, 128), 128)

    @pl.loop(0, 8)
    def _(b):
        gate_grad = cols_dot(hid_all[b], wo[...])
        pre = reset_pre[b]
        reset = silu(pre)
        low_grad = (gate_grad * reset).astype(LOW)
        scores_part[b] = cols_dot(low_grad, value_low[b])
        value_back[b] = (rows_dot(weights_low[b], low_grad) * silu_slope(value_pre[b])).astype(LOW)
        mixture_back[b, :, 0:128] = upd_all[b]
        mixture_back[b, :, 128:384] = (gate_grad * attended[b] * silu_slope(pre)).astype(LOW)
        mixture_back[b, :, 384:512] = hid_all[b, :, cand_cols]

    scores_plane = swap_plane(net, scores_part, scores_all)
    advance(scores_plane)

    def mixed_block(b):
        return cols_dot(mixture_back[b, :, 0:128], wa[:, 256:384]) + cols_dot(
            mixture_back[b, :, 128:512], wa[:, 512:896]
        )

    branch_sum.finish()
    mixed_sum = PlaneSum(net, mixed_block, part, got, sent, far, normed_two)
    mixed_sum.for_twin()
    mixed_sum.for_self()

    stream = x_ref[...].astype(F32)
    attn_branch = first[...] - stream
    branch_own = branch[...]
    output[...] = ((first[...] + branch_own) * valid).astype(LOW)
    square = [
        jnp.sum(jnp.sum(valid * item * item, axis=0, keepdims=True), axis=1, keepdims=True)
        for item in (stream, attn_branch, branch_own)
    ]
    square.append(jnp.sum(valid, axis=0, keepdims=True))

    @pl.loop(0, 4)
    def _(t):
        cols = pl.ds(pl.multiple_of(t * 256, 256), 256)
        grad = rows_dot(gated[...].reshape(tokens, 256), hid_all[:, :, cols].reshape(tokens, 256)).astype(LOW)
        for zz in range(4):
            go[zz, :, cols] = grad[zz * 64 : (zz + 1) * 64]

    @pl.loop(0, 4)
    def _(zz):
        cols = pl.ds(pl.multiple_of(zz * 256, 256), 256)
        ga[zz, :, 0:256] = rows_dot(
            normed_all[:, :, cols].reshape(tokens, 256), value_back[...].reshape(tokens, 256)
        ).astype(LOW)
        ga[zz, :, 256:768] = rows_dot(
            mixed_all[:, :, cols].reshape(tokens, 256), mixture_back[...].reshape(tokens, 512)
        ).astype(LOW)

    drive(ffn_line)
    attn_line = sum_line(net, [go, ga], [go_got, ga_got], [grad_out, ga_sum])
    advance(attn_line)

    advance(scores_plane)
    grad_weights = scores_all[0]
    for s in range(1, 8):
        grad_weights = grad_weights + scores_all[s]
    zeta_own_pre = zeta_pre[me]
    zeta = silu(zeta_own_pre)
    query_low, key_low, probs = block_scores_of(zeta, heads, shift, table)
    inner = jnp.sum(probs * grad_weights, axis=-1, keepdims=True)
    grad_scores = (probs * (grad_weights - inner)).astype(LOW)
    scale = zeta.shape[1] ** (-0.5)
    grad_query = jnp.dot(grad_scores, key_low, preferred_element_type=F32) * scale
    grad_key = rows_dot(grad_scores, query_low) * scale
    row = lax.broadcasted_iota(jnp.int32, grad_scores.shape, 0)
    col = lax.broadcasted_iota(jnp.int32, grad_scores.shape, 1)
    flip = jnp.where(row + col == rows - 1, 1.0, 0.0).astype(LOW)
    skewed = pltpu.roll(jnp.dot(grad_scores, flip, preferred_element_type=F32), 1, 1, stride=1, stride_axis=0)
    sums[37:38] = jnp.zeros((1, width), F32)
    sums[37:38, 0:128] = jnp.sum(grad_query * zeta, axis=0, keepdims=True)
    sums[37:38, 128:256] = jnp.sum(grad_key * zeta, axis=0, keepdims=True)
    sums[37:38, 256:384] = jnp.sum(grad_query, axis=0, keepdims=True)
    sums[37:38, 384:512] = jnp.sum(skewed, axis=0, keepdims=True)
    for k in range(4):
        sums[37:38, 512 + 128 * k : 640 + 128 * k] = jnp.broadcast_to(square[k], (1, 128))
    sums[38:40] = jnp.zeros((2, width), F32)
    grad_zeta = grad_query * heads[0:1] + grad_key * heads[1:2]
    zeta_own[...] = (grad_zeta * silu_slope(zeta_own_pre)).astype(LOW)
    zeta_plane = spread_plane(net, zeta_own, zeta_all)
    advance(zeta_plane)

    mixed_sum.finish()
    grad_mixed = normed_two[...] + cols_dot(zeta_own[...], wa[:, 384:512])
    grad_pull = grad_mixed * silu_slope(pre_ref[...])
    lanes_to_rows(grad_pull, pull)
    branch[...] = grad_pull

    def normed_block(b):
        return cols_dot(value_back[b], wa[:, 0:256])

    normed_sum_one = PlaneSum(net, normed_block, part, got_b, sent_b, far_b, normed_two)
    normed_sum_one.for_twin()
    normed_sum_one.for_self()
    advance(attn_line)
    ge_plane = swap_plane(net, ge_sum, ge_all)
    advance(ge_plane)
    ema_backward(fac, gain, nrm, pull, fac_sum, gain_sum, ema_out)
    for s in range(8):
        cols = slice(s * 128, (s + 1) * 128)
        sums[0:16, cols] = fac_sum[:, s, :]
        sums[16:32, cols] = gain_sum[:, s, :]
    normed_sum_one.finish()
    for s in range(8):
        cols = slice(s * 128, (s + 1) * 128)
        sums[33:34, cols] = jnp.sum(branch[:, cols] * nrm[:, s, :], axis=0, keepdims=True)
        normed_two[:, cols] = normed_two[:, cols] + branch[:, cols] * prm[1:2, cols] + ema_out[:, s, :]
    stream = x_ref[...].astype(F32)
    centred_one = stream - row_mean(stream)
    inverse_one = lax.rsqrt(row_mean(centred_one * centred_one) + EPS)
    xhat_one = centred_one * inverse_one
    grad_one = normed_two[...]
    sums[32:33] = jnp.sum(grad_one * xhat_one, axis=0, keepdims=True)
    sums[35:36] = jnp.sum(grad_one, axis=0, keepdims=True)
    gh_one = grad_one * prm[0:1]
    grad_inputs[...] = grad_inputs[...] + inverse_one * (
        gh_one - row_mean(gh_one) - xhat_one * row_mean(gh_one * xhat_one)
    )

    for s in range(8):
        sum_blocks[s] = sums[:, s * 128 : (s + 1) * 128]
    small = swap_plane(net, sum_blocks, sum_parts)
    advance(small)
    advance(zeta_plane)
    grad_zeta_all = rows_dot(mixed_all[...].reshape(tokens, width), zeta_all[...].reshape(tokens, 128))
    gz[...] = grad_zeta_all.reshape(4, 8, 32, 128)
    for zz in range(4):
        gz_own[zz] = gz[zz, me]
    zeta_line = swap_line(net, gz_own, gz_line)
    advance(zeta_line)
    advance(small)
    whole = sum_parts[0]
    for s in range(1, 8):
        whole = whole + sum_parts[s]
    sum_rows[z] = whole
    small_line = spread_line(net, sum_rows)
    advance(small_line)
    drive(attn_line)
    ga_plane = swap_plane(net, ga_sum, ga_all)
    advance(ga_plane)
    advance(small_line)
    sum_cols[...] = (sum_rows[0] + sum_rows[1]) + (sum_rows[2] + sum_rows[3])
    small_plane = spread_plane(net, sum_cols, sums_out)
    advance(small_plane)

    advance(ge_plane)
    for s in range(8):
        for zz in range(4):
            at = (zz * 8 + s) * 128
            grad_expand[:, at : at + 128] = ge_all[s, :, zz * 128 : (zz + 1) * 128].astype(F32)
    advance(zeta_line)
    grad_mix[:, 1024:1152] = (gz_line[0] + gz_line[1]) + (gz_line[2] + gz_line[3])
    advance(ga_plane)
    for s in range(8):
        grad_mix[:, s * 128 : (s + 1) * 128] = ga_all[s, :, 256:384].astype(F32)
        grad_mix[:, 3200 + s * 128 : 3328 + s * 128] = ga_all[s, :, 640:768].astype(F32)
    for q in range(4):
        place_halves(ga_all, 0, q, grad_values, 0)
        place_halves(ga_all, 384, q, grad_mix, 1152)
    advance(small_plane)


def place_halves(blocks, base, q, out, start):
    lane = lax.broadcasted_iota(jnp.int32, (blocks.shape[1], 128), 1)
    for zz in range(4):
        at = base + (zz // 2) * 128
        left = blocks[2 * q, :, at : at + 128].astype(F32)
        right = blocks[2 * q + 1, :, at : at + 128].astype(F32)
        if zz % 2:
            left = pltpu.roll(left, 64, 1)
        else:
            right = pltpu.roll(right, 64, 1)
        to = start + (zz * 4 + q) * 128
        out[:, to : to + 128] = jnp.where(lane < 64, left, right)


def back(operands):
    rows, width = operands[18].shape
    own = ((rows, width), F32)
    low_own = ((rows, width), LOW)
    all_low = ((8, rows, width), LOW)
    thin = ((8, rows, 128), LOW)
    state = ((16, 8, 128), F32)
    tall = ((rows, 8, 128), F32)
    return exchange(
        back_kernel, "back",
        [
            low_own, own, ((32, 2048), F32), ((32, 4224), F32), ((64, 1024), F32), ((32, 4096), F32),
            ((128, 1024), F32), ((8, 40, 128), F32),
        ],
        [((8, rows, 512), LOW), ((8, rows, 512), LOW)]
        + twin_scratch(rows, width)
        + [((4, rows, width), LOW), ((3, rows, width), LOW), ((3, rows, width), LOW), own, own, low_own, all_low]
        + [thin, thin, ((8, rows, 256), LOW), ((8, rows, 512), LOW), ((8, rows, 128), F32), ((8, rows, 128), F32)]
        + [((rows, 128), LOW), thin]
        + [((4, 128, 1024), LOW), ((3, 128, 1024), LOW), ((4, 256, 512), LOW), ((3, 256, 512), LOW)]
        + [((8, 32, 512), LOW), ((8, 32, 512), LOW), ((4, 64, 1024), LOW), ((3, 64, 1024), LOW)]
        + [((4, 256, 768), LOW), ((3, 256, 768), LOW), ((8, 32, 768), LOW), ((8, 32, 768), LOW)]
        + [((4, 8, 32, 128), F32), ((4, 32, 128), F32), ((4, 32, 128), F32)]
        + [tall, tall, state, state, ((40, 1024), F32)]
        + [((8, 40, 128), F32), ((8, 40, 128), F32), ((4, 40, 128), F32), ((40, 128), F32)],
        3,
        *operands, smem=(28,),
    )


def table_kernel(pos_ref, out_ref):
    wide = jnp.broadcast_to(pos_ref[...], out_ref.shape)
    out_ref[...] = pltpu.roll(wide, 1, 1, stride=1, stride_axis=0)


def distance_table(position):
    span = position.shape[0]
    return pl.pallas_call(
        table_kernel, name="distance_table", out_shape=jax.ShapeDtypeStruct((span, span), F32)
    )(position[::-1][None])


def on_plane(
    inputs, lengths, w_values, w_mix, w_out, w_expand, w_reduce, ema_params,
    norm_gains, norm_biases, head_gains, query_bias, position_bias, cotangent,
):
    rows, width = inputs.shape
    owner = lax.axis_index("dp") * 4 + lax.axis_index("fsdp")
    heads = head_gains.astype(F32)
    shift = query_bias.astype(F32)[None]
    table = distance_table(position_bias.astype(F32))
    small = jnp.concatenate(
        [ema_params, norm_gains.T, norm_biases.T, jnp.zeros((32, 59), LOW)], axis=1
    )
    wa, wo, normed_all, mixed_all, cot_all, prm, factor, gain, nrm, pre = front(
        inputs, small, w_values, w_mix, w_out, cotangent, lengths
    )
    wa = wa.reshape(1024, 896)
    wo = wo.reshape(256, 1024)
    (
        two_all, we, wr, value_pre, value_low, zeta_pre, weights_low, attended, reset_pre, gated,
        hidden_pre, update_pre, first,
    ) = middle(wa, wo, normed_all, mixed_all, inputs, prm, table, heads, shift, w_expand, w_reduce)
    we = we.reshape(1024, 512)
    wr = wr.reshape(512, 1024)
    (
        output, grad_inputs, grad_values, grad_mix, grad_out, grad_expand, grad_reduce, sums,
    ) = back(
        (
            wa, wo, we, wr, normed_all, mixed_all, two_all, cot_all,
            value_pre, value_low, zeta_pre, weights_low, attended, reset_pre, gated,
            hidden_pre, update_pre, first,
            inputs, cotangent, prm, factor, gain, nrm, pre, table, heads, shift, lengths,
        )
    )
    sums = sums.transpose(1, 0, 2).reshape(40, width)
    mine = lax.dynamic_slice_in_dim(sums, owner * 32, 32, 1)
    raw = ema_params.astype(F32)
    damping = jax.nn.sigmoid(raw[:, :16])
    mixing = jax.nn.sigmoid(raw[:, 16:32])
    expand = raw[:, 32:48]
    project = raw[:, 48:64]
    by_factor = mine[:16].T * (0.25 * project * mixing * expand)
    by_gain = mine[16:32].T
    by_inflow = 0.25 * project * by_gain
    grad_ema = jnp.concatenate(
        [
            -by_factor * mixing * damping * (1.0 - damping),
            (by_inflow * expand - by_factor * damping) * mixing * (1.0 - mixing),
            by_inflow * mixing,
            0.25 * mixing * expand * by_gain,
        ],
        axis=1,
    )
    tail = sums[37]
    rms = jnp.sqrt(tail[512:896:128] / (tail[896] * width))
    return (
        output, grad_inputs, grad_values, grad_mix, grad_out, grad_expand, grad_reduce,
        grad_ema, mine[32:35], mine[35:37], tail[:256].reshape(2, 128), tail[256:384], tail[384:512], rms,
    )


def layer_norm(value, gain, shift):
    centre = jnp.mean(value, axis=-1, keepdims=True)
    centered = value - centre
    spread = jnp.mean(centered * centered, axis=-1, keepdims=True)
    return centered * lax.rsqrt(spread + EPS) * gain + shift


def ema_mix(normed, keep, ema_params):
    count = ema_params.shape[1] // 4
    damping = jax.nn.sigmoid(ema_params[:, :count]).T
    mixing = jax.nn.sigmoid(ema_params[:, count : 2 * count]).T
    expand = ema_params[:, 2 * count : 3 * count].T
    project = ema_params[:, 3 * count :].T
    factor = 1.0 - mixing * damping
    inflow = mixing * expand

    def advance(state, item):
        column, flag = item
        state = factor * state * flag[:, None, None] + inflow * column[:, None, :]
        return (state, 0.25 * jnp.sum(project * state, axis=1))

    start = jnp.zeros((normed.shape[0], count, normed.shape[2]), jnp.float32)
    _, smooth = lax.scan(advance, start, (jnp.swapaxes(normed, 0, 1), jnp.swapaxes(keep, 0, 1)))
    return jnp.swapaxes(smooth, 0, 1)


def layout(lengths, rows):
    ends = jnp.cumsum(lengths, axis=1)
    starts = ends - lengths
    place = lax.broadcasted_iota(jnp.int32, (lengths.shape[0], rows), 1)
    begin = jnp.any(place[:, :, None] == starts[:, None, :], axis=2) | (place == ends)
    keep = jnp.where(begin, 0.0, 1.0).astype(jnp.float32)
    valid = jnp.where(place < ends, 1.0, 0.0).astype(jnp.float32)
    return (keep, valid)


def dot_rows(left, right):
    return lax.dot_general(
        left, right, (((0,), (0,)), ((), ())), preferred_element_type=jnp.float32
    )


def dot_cols(left, right):
    return lax.dot_general(
        left, right, (((1,), (1,)), ((), ())), preferred_element_type=jnp.float32
    )


def block_scores(query_low, key_low, position, scale):
    span = query_low.shape[1]
    row = lax.broadcasted_iota(jnp.int32, (span, span), 0)
    col = lax.broadcasted_iota(jnp.int32, (span, span), 1)
    table = position[jnp.clip(row - col, 0, span - 1)]
    scores = (
        jnp.einsum("kiz,kjz->kij", query_low, key_low, preferred_element_type=jnp.float32) * scale
        + table
    )
    return jnp.where(row >= col, scores, NEG)


def diagonal_sums(grid):
    size = grid.shape[0]
    flipped = grid[:, ::-1]
    padded = jnp.pad(flipped, ((0, 0), (0, size)))
    skewed = padded.reshape(-1)[: size * (2 * size - 1)].reshape(size, 2 * size - 1)
    return jnp.sum(skewed, axis=0)[size - 1 :]


def group_rows(value):
    return lax.all_gather(value, "fsdp", axis=0, tiled=True)


def group_total(value):
    return lax.psum_scatter(value, "fsdp", scatter_dimension=0, tiled=True)


def owner_layout(grad, owners):
    return grad.reshape(owners * 8, -1)


def owner_shard(piece, columns):
    return piece.reshape(-1, columns)


def on_device(
    inputs,
    lengths,
    w_values,
    w_mix,
    w_out,
    w_expand,
    w_reduce,
    ema_params,
    norm_gains,
    norm_biases,
    head_gains,
    query_bias,
    position_bias,
    cotangent,
):
    rows, width = inputs.shape
    span = position_bias.shape[0]
    blocks = rows // span
    key_width = head_gains.shape[1]
    scale = key_width ** (-0.5)
    keep, valid = layout(lengths, rows)
    mask = valid[0][:, None]
    gathered = (
        lax.all_gather(w_values, ("dp", "fsdp"), axis=0, tiled=True),
        lax.all_gather(w_mix, ("dp", "fsdp"), axis=0, tiled=True),
        lax.all_gather(w_out, ("dp", "fsdp"), axis=0, tiled=True),
        lax.all_gather(ema_params, ("dp", "fsdp"), axis=0, tiled=True),
        lax.all_gather(norm_gains, ("dp", "fsdp"), axis=1, tiled=True),
        lax.all_gather(norm_biases, ("dp", "fsdp"), axis=1, tiled=True),
    )
    values_full, mix_full, out_full, ema_full, gains_full, biases_full = gathered
    value_width = values_full.shape[1]
    group_size = lax.axis_size("fsdp")
    data_size = lax.axis_size("dp")
    owners = group_size * data_size
    shard_rows = w_expand.shape[0]
    hidden_units = w_expand.shape[1]
    unit_block = hidden_units // (group_size * data_size)
    pieces = w_expand.reshape(shard_rows, data_size, group_size, unit_block)
    swapped = lax.all_to_all(pieces, "fsdp", split_axis=2, concat_axis=0, tiled=True)
    expand_quarter, reduce_use = (
        lax.all_gather(swapped, "dp", axis=0, tiled=True),
        lax.all_gather(w_reduce, "dp", axis=0, tiled=True),
    )
    expand_use = expand_quarter.reshape(expand_quarter.shape[0], data_size * unit_block)
    gains_f = gains_full.astype(jnp.float32)
    biases_f = biases_full.astype(jnp.float32)
    heads_f = head_gains.astype(jnp.float32)
    query_shift = query_bias.astype(jnp.float32)
    position_f = position_bias.astype(jnp.float32)
    stream = inputs.astype(jnp.float32)

    def front(source, gain, shift, omega, params):
        normed_part = layer_norm(source, gain, shift)
        smooth = ema_mix(normed_part[None], keep, params)[0]
        return (normed_part, silu(smooth + omega * normed_part))

    (normed, mixed), front_back = jax.vjp(
        front, stream, gains_f[0], biases_f[0], gains_f[1], ema_full.astype(jnp.float32)
    )
    normed_low = normed.astype(jnp.bfloat16)
    mixed_low = mixed.astype(jnp.bfloat16)
    value_pre = jnp.dot(normed_low, values_full, preferred_element_type=jnp.float32)
    value_low = silu(value_pre).astype(jnp.bfloat16)
    mixture = jnp.dot(mixed_low, mix_full, preferred_element_type=jnp.float32)
    middle = width + key_width
    upper = middle + value_width
    update = jax.nn.sigmoid(mixture[:, :width])
    zeta_pre = mixture[:, width:middle]
    zeta = silu(zeta_pre)
    reset_pre = mixture[:, middle:upper]
    reset = silu(reset_pre)
    candidate = mixture[:, upper:]
    query_low = (
        (zeta * heads_f[0] + query_shift).astype(jnp.bfloat16).reshape(blocks, span, key_width)
    )
    key_low = (zeta * heads_f[1]).astype(jnp.bfloat16).reshape(blocks, span, key_width)
    value_blocks = value_low.reshape(blocks, span, value_width)
    scores = block_scores(query_low, key_low, position_f, scale)
    log_total = jax.nn.logsumexp(scores, axis=-1, keepdims=True)
    weights_low = jnp.exp(scores - log_total).astype(jnp.bfloat16)
    attended = jnp.einsum(
        "kij,kjv->kiv", weights_low, value_blocks, preferred_element_type=jnp.float32
    ).reshape(rows, value_width)
    gated_low = (attended * reset).astype(jnp.bfloat16)
    hidden_pre = candidate + jnp.dot(gated_low, out_full, preferred_element_type=jnp.float32)
    hidden = silu(hidden_pre)
    attn_branch = update * (hidden - stream)
    first = stream + attn_branch
    normed_two, norm_back = jax.vjp(layer_norm, first, gains_f[2], biases_f[1])
    normed_two_low = normed_two.astype(jnp.bfloat16)
    ffn_rows = group_rows(normed_two_low)
    expand_pre = jnp.dot(ffn_rows, expand_use, preferred_element_type=jnp.float32)
    expand_low = silu(expand_pre).astype(jnp.bfloat16)
    branch_part = jnp.dot(expand_low, reduce_use, preferred_element_type=jnp.float32)
    branch = group_total(branch_part)
    output = ((first + branch) * mask).astype(jnp.bfloat16)
    values_back, mix_back, out_back = (
        lax.all_gather(w_values, ("dp", "fsdp"), axis=0, tiled=True),
        lax.all_gather(w_mix, ("dp", "fsdp"), axis=0, tiled=True),
        lax.all_gather(w_out, ("dp", "fsdp"), axis=0, tiled=True),
    )
    grad_out = cotangent.astype(jnp.float32) * mask
    grad_branch = grad_out.astype(jnp.bfloat16)
    grad_rows = group_rows(grad_branch)
    grad_reduce = dot_rows(expand_low, grad_rows)
    grad_expand_out = dot_cols(grad_rows, reduce_use)
    grad_expand_pre = (grad_expand_out * silu_slope(expand_pre)).astype(jnp.bfloat16)
    grad_expand = dot_rows(ffn_rows, grad_expand_pre)
    normed_two_part = dot_cols(grad_expand_pre, expand_use)
    grad_normed_two = group_total(normed_two_part)
    grad_first_norm, grad_gain_two, grad_shift_two = norm_back(grad_normed_two)
    grad_first = grad_out + grad_first_norm
    grad_direct = grad_first * (1.0 - update)
    grad_update = grad_first * (hidden - stream)
    grad_hidden_pre = grad_first * update * silu_slope(hidden_pre)
    grad_hidden_low = grad_hidden_pre.astype(jnp.bfloat16)
    grad_out_proj = dot_rows(gated_low, grad_hidden_low)
    grad_gated = dot_cols(grad_hidden_low, out_back)
    grad_attended = (grad_gated * reset).astype(jnp.bfloat16).reshape(blocks, span, value_width)
    grad_reset = grad_gated * attended
    scores_again = block_scores(query_low, key_low, position_f, scale)
    probs = jnp.exp(scores_again - log_total)
    probs_low = probs.astype(jnp.bfloat16)
    grad_weights = jnp.einsum(
        "kiv,kjv->kij", grad_attended, value_blocks, preferred_element_type=jnp.float32
    )
    grad_value = jnp.einsum(
        "kij,kiv->kjv", probs_low, grad_attended, preferred_element_type=jnp.float32
    ).reshape(rows, value_width)
    inner = jnp.sum(probs * grad_weights, axis=-1, keepdims=True)
    grad_scores = (probs * (grad_weights - inner)).astype(jnp.bfloat16)
    grad_position = diagonal_sums(jnp.sum(grad_scores.astype(jnp.float32), axis=0))
    grad_query = (
        jnp.einsum(
            "kij,kjz->kiz", grad_scores, key_low, preferred_element_type=jnp.float32
        ).reshape(rows, key_width)
        * scale
    )
    grad_key = (
        jnp.einsum(
            "kij,kiz->kjz", grad_scores, query_low, preferred_element_type=jnp.float32
        ).reshape(rows, key_width)
        * scale
    )
    grad_value_pre = (grad_value * silu_slope(value_pre)).astype(jnp.bfloat16)
    grad_values = dot_rows(normed_low, grad_value_pre)
    grad_normed = dot_cols(grad_value_pre, values_back)
    grad_zeta = grad_query * heads_f[0] + grad_key * heads_f[1]
    grad_heads = jnp.stack([jnp.sum(grad_query * zeta, axis=0), jnp.sum(grad_key * zeta, axis=0)])
    grad_query_shift = jnp.sum(grad_query, axis=0)
    grad_mixture = jnp.concatenate(
        [
            grad_update * update * (1.0 - update),
            grad_zeta * silu_slope(zeta_pre),
            grad_reset * silu_slope(reset_pre),
            grad_hidden_pre,
        ],
        axis=1,
    ).astype(jnp.bfloat16)
    grad_mix = dot_rows(mixed_low, grad_mixture)
    grad_mixed = dot_cols(grad_mixture, mix_back)
    grad_source, grad_gain_one, grad_shift_one, grad_omega, grad_ema = front_back(
        (grad_normed, grad_mixed)
    )
    grad_inputs = grad_direct + grad_source
    grad_gains = jnp.stack([grad_gain_one, grad_omega, grad_gain_two])
    grad_shifts = jnp.stack([grad_shift_one, grad_shift_two])
    summed_expand, grad_reduce_dev = (
        lax.psum_scatter(grad_expand, "dp", scatter_dimension=0, tiled=True),
        lax.psum_scatter(grad_reduce, "dp", scatter_dimension=0, tiled=True),
    )
    summed_pieces = summed_expand.reshape(group_size * shard_rows, data_size, 1, unit_block)
    owned = lax.all_to_all(summed_pieces, "fsdp", split_axis=0, concat_axis=2, tiled=True)
    grad_expand_dev = owned.reshape(shard_rows, hidden_units)
    summed_block = (
        lax.psum_scatter(
            owner_layout(grad_values, owners), ("dp", "fsdp"), scatter_dimension=0, tiled=True
        ),
        lax.psum_scatter(
            owner_layout(grad_mix, owners), ("dp", "fsdp"), scatter_dimension=0, tiled=True
        ),
        lax.psum_scatter(grad_out_proj, ("dp", "fsdp"), scatter_dimension=0, tiled=True),
        lax.psum_scatter(
            owner_layout(grad_ema, owners), ("dp", "fsdp"), scatter_dimension=0, tiled=True
        ),
        lax.psum_scatter(grad_gains, ("dp", "fsdp"), scatter_dimension=1, tiled=True),
        lax.psum_scatter(grad_shifts, ("dp", "fsdp"), scatter_dimension=1, tiled=True),
    )
    values_flat, mix_flat, grad_out_dev, ema_flat, grad_gains_dev, grad_shifts_dev = summed_block
    grad_values_dev = owner_shard(values_flat, grad_values.shape[1])
    grad_mix_dev = owner_shard(mix_flat, grad_mix.shape[1])
    grad_ema_dev = owner_shard(ema_flat, grad_ema.shape[1])
    squares = jnp.stack(
        [
            jnp.sum(mask * stream * stream),
            jnp.sum(mask * attn_branch * attn_branch),
            jnp.sum(mask * branch * branch),
        ]
    )
    square_sums, tokens_seen, heads_total, shift_total, position_total = lax.psum(
        (squares, jnp.sum(valid), grad_heads, grad_query_shift, grad_position), ("dp", "fsdp")
    )
    rms = jnp.sqrt(square_sums / (tokens_seen * width))
    return (
        output,
        grad_inputs,
        grad_values_dev,
        grad_mix_dev,
        grad_out_dev,
        grad_expand_dev,
        grad_reduce_dev,
        grad_ema_dev,
        grad_gains_dev,
        grad_shifts_dev,
        heads_total,
        shift_total,
        position_total,
        rms,
    )


def solution(mesh):
    in_specs = (
        P(("dp", "fsdp"), None),
        P(("dp", "fsdp"), None),
        P(("dp", "fsdp"), None),
        P(("dp", "fsdp"), None),
        P(("dp", "fsdp"), None),
        P(("dp", "fsdp"), None),
        P(("dp", "fsdp"), None),
        P(("dp", "fsdp"), None),
        P(None, ("dp", "fsdp")),
        P(None, ("dp", "fsdp")),
        P(),
        P(),
        P(),
        P(("dp", "fsdp"), None),
    )
    out_specs = (
        P(("dp", "fsdp"), None),
        P(("dp", "fsdp"), None),
        P(("dp", "fsdp"), None),
        P(("dp", "fsdp"), None),
        P(("dp", "fsdp"), None),
        P(("dp", "fsdp"), None),
        P(("dp", "fsdp"), None),
        P(("dp", "fsdp"), None),
        P(None, ("dp", "fsdp")),
        P(None, ("dp", "fsdp")),
        P(),
        P(),
        P(),
        P(),
    )
    planes = mesh.shape["dp"] == 8 and mesh.shape["fsdp"] == 4
    return jax.shard_map(
        on_plane if planes else on_device, mesh=mesh, in_specs=in_specs, out_specs=out_specs, check_vma=False
    )
```

```python
import jax
import jax.numpy as jnp
from jax import lax
from jax.experimental import pallas as pl
from jax.experimental.pallas import tpu as pltpu
from jax.sharding import PartitionSpec as P

EPS = 1e-05
NEG = -1e30
F32 = jnp.float32
LOW = jnp.bfloat16
MESH = pl.DeviceIdType.MESH
LINES = 200
STATES = 16


def silu(value):
    return value * jax.nn.sigmoid(value)


def silu_slope(value):
    sigma = jax.nn.sigmoid(value)
    return sigma * (1.0 + value * (1.0 - sigma))


def here():
    dp = lax.axis_index("dp")
    f = lax.axis_index("fsdp")
    return dp // 2, dp % 2, f // 2, f % 2


def device(z, y, x, c):
    return (z * 2 + y, x * 2 + c)


def slot_of(y, x, c):
    return y * 4 + x * 2 + c


def plane_peers(y, x, c):
    peers = []
    for mask in range(1, 8):
        peers.append(
            (
                1 - y if mask & 4 else y,
                1 - x if mask & 2 else x,
                1 - c if mask & 1 else c,
            )
        )
    return peers


def line_peers(z):
    return [z + 1 - 2 * (z % 2), 3 - z, (z + 2) % 4]


def greet(across=True):
    z, y, x, c = here()
    barrier = pltpu.get_barrier_semaphore()
    count = 7
    for peer in plane_peers(y, x, c):
        pl.semaphore_signal(barrier, inc=1, device_id=device(z, *peer), device_id_type=MESH)
    if across:
        count = 10
        for other in line_peers(z):
            pl.semaphore_signal(barrier, inc=1, device_id=device(other, y, x, c), device_id_type=MESH)
    pl.semaphore_wait(barrier, count)


class Net:
    def __init__(self, send, recv):
        self.send = send
        self.recv = recv
        self.used = 0

    def take(self, count):
        self.used += count
        assert self.used <= LINES
        return self.used - count

    def make(self, line, src, dst, target):
        return pltpu.make_async_remote_copy(
            src_ref=src,
            dst_ref=dst,
            send_sem=self.send.at[line],
            recv_sem=self.recv.at[line],
            device_id=target,
            device_id_type=MESH,
        )

    def copy(self, src, dst, target):
        made = self.make(self.take(1), src, dst, target)
        made.start()
        return made


VMEM = pl.BlockSpec(memory_space=pltpu.VMEM)


def rows_dot(left, right):
    return lax.dot_general(left, right, (((0,), (0,)), ((), ())), preferred_element_type=F32)


def cols_dot(left, right):
    return lax.dot_general(left, right, (((1,), (1,)), ((), ())), preferred_element_type=F32)


def lanes_to_rows(wide, tall):
    for s in range(8):
        tall[:, s, :] = wide[:, s * 128 : (s + 1) * 128]


def pick_halves(arr, base, slot, pair):
    one = base + ((2 * pair * 8 + slot) // 2) * 128
    two = base + (((2 * pair + 1) * 8 + slot) // 2) * 128
    left = arr[:, one : one + 128].astype(F32)
    right = arr[:, two : two + 128].astype(F32)
    lane = lax.broadcasted_iota(jnp.int32, left.shape, 1)
    if slot % 2 == 0:
        return jnp.where(lane < 64, left, pltpu.roll(right, 64, 1)).astype(LOW)
    return jnp.where(lane < 64, pltpu.roll(left, 64, 1), right).astype(LOW)


def ema_forward(factor, gain, source, out):
    steps = source.shape[0]

    def step(t, states):
        column = source[t]
        new = []
        terms = []
        for j in range(STATES):
            state = factor[j] * states[j] + column
            new.append(state)
            terms.append(gain[j] * state)
        while len(terms) > 1:
            terms = [terms[i] + terms[i + 1] for i in range(0, len(terms), 2)]
        out[t] = terms[0]
        return tuple(new)

    zero = jnp.zeros(source.shape[1:], F32)
    lax.fori_loop(0, steps, step, (zero,) * STATES)


def ema_backward(fac, gain, nrm, pull_ref, factor_sum, gain_sum, out):
    steps = nrm.shape[0]
    zero = jnp.zeros(nrm.shape[1:], F32)
    group = 4
    for base in range(0, STATES, group):

        def step(t, carry):
            column = nrm[t]
            pull = pull_ref[t]
            new = []
            for k in range(group):
                state, slope, by_factor, by_gain = carry[4 * k : 4 * k + 4]
                f = fac[base + k]
                slope = f * slope + state
                state = f * state + column
                new += [state, slope, by_factor + pull * slope, by_gain + pull * state]
            return tuple(new)

        done = lax.fori_loop(0, steps, step, (zero,) * (4 * group))
        for k in range(group):
            factor_sum[base + k] = done[4 * k + 2]
            gain_sum[base + k] = done[4 * k + 3]

    def turn(t, states):
        at = steps - 1 - t
        pull = pull_ref[at]
        new = []
        terms = []
        for j in range(STATES):
            state = fac[j] * states[j] + pull
            new.append(state)
            terms.append(gain[j] * state)
        while len(terms) > 1:
            terms = [terms[i] + terms[i + 1] for i in range(0, len(terms), 2)]
        out[at] = terms[0]
        return tuple(new)

    lax.fori_loop(0, steps, turn, (zero,) * STATES)


class PlaneGather:
    def __init__(self, net, src, dst):
        z, y, x, c = here()
        self.net, self.src, self.dst = net, src, dst
        self.base = net.take(7)
        self.me = slot_of(y, x, c)

    def near(self, k):
        z, y, x, c = here()
        yy, xx = chip_of(k)
        return self.net.make(self.base + k - 1, self.src, self.dst.at[self.me], device(z, yy, xx, c))

    def twin(self, k):
        z, y, x, c = here()
        yy, xx = chip_of(k)
        block = self.dst.at[slot_of(yy, xx, c)]
        return self.net.make(self.base + 3 + k, block, block, device(z, y, x, 1 - c))

    def start(self):
        self.dst[self.me] = self.src[...]
        for k in (1, 2, 3):
            self.near(k).start()
        self.twin(0).start()

    def take_near(self, k):
        self.near(k).wait_recv()
        self.twin(k).start()

    def take_twin(self, k):
        self.twin(k).wait_recv()

    def take_rest(self):
        for k in (1, 2, 3):
            self.take_near(k)
        for k in range(4):
            self.take_twin(k)

    def finish(self):
        for k in (1, 2, 3):
            self.near(k).wait_send()
        for k in range(4):
            self.twin(k).wait_send()


def chip_of(k):
    z, y, x, c = here()
    return (y + k // 2) % 2, (x + k % 2) % 2


class PlaneSum:
    def __init__(self, net, part, got, sent, far, total):
        self.net = net
        self.part, self.got, self.sent, self.far, self.total = part, got, sent, far, total
        self.base = net.take(7)

    def inner(self, k):
        z, y, x, c = here()
        return self.net.make(self.base + k, self.part.at[k], self.got.at[k], device(z, y, x, 1 - c))

    def outer(self, k):
        z, y, x, c = here()
        yy, xx = chip_of(k)
        return self.net.make(self.base + 3 + k, self.sent.at[k - 1], self.far.at[k - 1], device(z, yy, xx, c))

    def give(self, k, block):
        self.part[k] = block.astype(self.part.dtype)
        self.inner(k).start()

    def pair(self, k, block):
        self.inner(k).wait_recv()
        both = block + self.got[k].astype(F32)

        @pl.when(k == 0)
        def _():
            self.total[...] = both

        @pl.when(k > 0)
        def _():
            self.sent[k - 1] = both.astype(self.sent.dtype)
            self.outer(k).start()

    def run(self, make):
        z, y, x, c = here()

        @pl.loop(0, 4)
        def _(i):
            k = 3 - i
            yy, xx = chip_of(k)
            self.give(k, make(slot_of(yy, xx, 1 - c)))
            self.pair(k, make(slot_of(yy, xx, c)))

    def finish(self):
        @pl.loop(0, 4)
        def _(k):
            self.inner(k).wait_send()

        @pl.loop(1, 4)
        def _(k):
            self.outer(k).wait()
            self.total[...] = self.total[...] + self.far[k - 1].astype(F32)


class LineGather:
    def __init__(self, net, buf):
        z, y, x, c = here()
        near, mirror, _ = line_peers(z)
        self.inside = z % 3 > 0
        relayed = (2 * z) % 3 + 3 * (z // 3)
        self.first = net.make(net.take(1), buf.at[z], buf.at[z], device(near, y, x, c))
        self.second = net.make(net.take(1), buf.at[z], buf.at[z], device(mirror, y, x, c))
        self.third = net.make(net.take(1), buf.at[relayed], buf.at[relayed], device((3 * z + 2) % 5, y, x, c))

    def start(self):
        self.first.start()
        self.second.start()

        @pl.when(jnp.logical_not(self.inside))
        def _():
            self.third.start()

    def relay(self):
        @pl.when(self.inside)
        def _():
            self.second.wait_recv()
            self.third.start()

    def finish(self):
        self.first.wait()
        self.second.wait_send()

        @pl.when(jnp.logical_not(self.inside))
        def _():
            self.second.wait_recv()

        self.third.wait()


class LineSum:
    def __init__(self, net, buf, got, out):
        z, y, x, c = here()
        near, mirror, across = line_peers(z)
        self.buf, self.got, self.out = buf, got, out
        self.inside = z % 3 > 0
        self.relayed = (2 * z) % 3 + 3 * (z // 3)
        self.first = net.make(net.take(1), buf.at[across], got.at[0], device((2 * z + 1) % 5, y, x, c))
        self.second = net.make(net.take(1), buf.at[near], got.at[1], device(near, y, x, c))
        self.third = net.make(net.take(1), buf.at[mirror], got.at[2], device(mirror, y, x, c))

    def start(self):
        self.first.start()
        self.second.start()

        @pl.when(jnp.logical_not(self.inside))
        def _():
            self.third.start()

    def relay(self):
        @pl.when(self.inside)
        def _():
            self.first.wait_recv()
            self.buf[self.relayed] = (self.buf[self.relayed].astype(F32) + self.got[0].astype(F32)).astype(LOW)
            self.third.start()

    def finish(self):
        z, y, x, c = here()
        self.first.wait_send()
        self.second.wait()
        self.third.wait()
        total = self.buf[z].astype(F32) + self.got[1].astype(F32) + self.got[2].astype(F32)
        self.out[...] = total.reshape(self.out.shape).astype(self.out.dtype)

        @pl.when(jnp.logical_not(self.inside))
        def _():
            self.first.wait_recv()
            whole = total + self.got[0].astype(F32)
            self.out[...] = whole.reshape(self.out.shape).astype(self.out.dtype)


class Spread:
    def __init__(self, copies):
        self.copies = copies

    def finish(self):
        for copy in self.copies:
            copy.wait()


def spread_plane(net, src, dst):
    z, y, x, c = here()
    me = slot_of(y, x, c)
    spread = Spread([net.copy(src, dst.at[me], device(z, *peer)) for peer in plane_peers(y, x, c)])
    dst[me] = src[...]
    return spread


def swap_plane(net, src, dst):
    z, y, x, c = here()
    me = slot_of(y, x, c)
    spread = Spread(
        [net.copy(src.at[slot_of(*peer)], dst.at[me], device(z, *peer)) for peer in plane_peers(y, x, c)]
    )
    dst[me] = src[me]
    return spread


def spread_line(net, buf, part=None):
    z, y, x, c = here()
    block = buf.at[z] if part is None else buf.at[z, part]
    return Spread([net.copy(block, block, device(other, y, x, c)) for other in line_peers(z)])


def swap_line(net, src, dst):
    z, y, x, c = here()
    spread = Spread([net.copy(src.at[other], dst.at[z], device(other, y, x, c)) for other in line_peers(z)])
    dst[z] = src[z]
    return spread


def row_mean(value):
    return jnp.mean(value, axis=-1, keepdims=True)


def standardized(value):
    centred = value - row_mean(value)
    inverse = lax.rsqrt(row_mean(centred * centred) + EPS)
    return centred * inverse, inverse


def norm_back(grad, xhat, inverse, gain):
    scaled = grad * gain
    return inverse * (scaled - row_mean(scaled) - xhat * row_mean(scaled * xhat))


def block_scores_of(zeta, heads, shift, table):
    query_low = (zeta * heads[0:1] + shift).astype(LOW)
    key_low = (zeta * heads[1:2]).astype(LOW)
    scores = cols_dot(query_low, key_low) * (zeta.shape[1] ** (-0.5)) + table[...]
    row = lax.broadcasted_iota(jnp.int32, scores.shape, 0)
    col = lax.broadcasted_iota(jnp.int32, scores.shape, 1)
    scores = jnp.where(row >= col, scores, NEG)
    top = jnp.max(scores, axis=-1, keepdims=True)
    log_total = top + jnp.log(jnp.sum(jnp.exp(scores - top), axis=-1, keepdims=True))
    return query_low, key_low, jnp.exp(scores - log_total)


def mirror_matrix(size):
    row = lax.broadcasted_iota(jnp.int32, (size, size), 0)
    col = lax.broadcasted_iota(jnp.int32, (size, size), 1)
    return jnp.where(row + col == size - 1, 1.0, 0.0).astype(LOW)


def column_of(line):
    size = line.shape[1]
    row = lax.broadcasted_iota(jnp.int32, (size, size), 0)
    col = lax.broadcasted_iota(jnp.int32, (size, size), 1)
    return jnp.sum(jnp.where(row == col, line, 0.0), axis=1, keepdims=True)


def cols_at(index, size):
    return pl.ds(pl.multiple_of(index * size, size), size)


def put_rows(sums, at, wide):
    sums[at : at + 1] = jnp.sum(wide, axis=0, keepdims=True)


ROWS = 128
WIDE = 1024
INPUTS = (
    "x", "cot", "wv", "wm", "wo_own", "we_own", "wr_own", "ema", "norm_gains", "norm_biases", "consts", "lens",
)
RESULTS = (
    ("output", (ROWS, WIDE), LOW),
    ("grad_inputs", (ROWS, WIDE), F32),
    ("grad_out", (64, WIDE), F32),
    ("grad_reduce", (ROWS, WIDE), F32),
    ("ge_all", (8, 32, 512), LOW),
    ("ga_all", (8, 32, 768), LOW),
    ("gz_line", (4, 32, 128), F32),
    ("sums_all", (8, 40, 128), F32),
    ("square_line", (4, 8, 128), F32),
)
ALL = (8, ROWS, WIDE)
OWN = (ROWS, WIDE)
SCRATCH = (
    ("small_wide", (32, 128), F32),
    ("small", (32, 128), LOW),
    ("small_all", (4, 8, 32, 128), LOW),
    ("prm", (128, WIDE), F32),
    ("blocks_a", (8, 32, 896), LOW),
    ("blocks_e", (8, 32, 512), LOW),
    ("wa", (4, 8, 32, 896), LOW),
    ("wo", (4, 64, WIDE), LOW),
    ("we", (4, 8, 32, 512), LOW),
    ("wr", (4, ROWS, WIDE), LOW),
    ("table", (128, 128), F32),
    ("heads", (8, 128), F32),
    ("x_near", (3, ROWS, WIDE), LOW),
    ("own_low", OWN, LOW),
    ("normed_all", ALL, LOW),
    ("mixed_all", ALL, LOW),
    ("cot_all", ALL, LOW),
    ("two_all", ALL, LOW),
    ("hid_all", ALL, LOW),
    ("fac", (16, 8, 128), F32),
    ("gain", (16, 8, 128), F32),
    ("fac_sum", (16, 8, 128), F32),
    ("gain_sum", (16, 8, 128), F32),
    ("nrm", (ROWS, 8, 128), F32),
    ("tall", (ROWS, 8, 128), F32),
    ("tall_out", (ROWS, 8, 128), F32),
    ("pre", OWN, F32),
    ("value_pre", (8, ROWS, 256), F32),
    ("value_low", (8, ROWS, 256), LOW),
    ("zeta_pre", (8, ROWS, 128), F32),
    ("weights_low", (8, ROWS, 128), LOW),
    ("attended", (8, ROWS, 256), F32),
    ("reset_pre", (8, ROWS, 256), F32),
    ("gated", (8, ROWS, 256), LOW),
    ("work", OWN, F32),
    ("hidden_pre", OWN, F32),
    ("update_pre", OWN, F32),
    ("first", OWN, F32),
    ("update_part", (8, ROWS, 128), LOW),
    ("update_all", (8, ROWS, 128), LOW),
    ("part", (4, ROWS, WIDE), LOW),
    ("got", (4, ROWS, WIDE), LOW),
    ("sent", (3, ROWS, WIDE), LOW),
    ("far", (3, ROWS, WIDE), LOW),
    ("got_b", (4, ROWS, WIDE), LOW),
    ("sent_b", (3, ROWS, WIDE), LOW),
    ("far_b", (3, ROWS, WIDE), LOW),
    ("expand_low", (8, ROWS, 512), LOW),
    ("grad_pre", (8, ROWS, 512), LOW),
    ("branch", OWN, F32),
    ("value_back", (8, ROWS, 256), LOW),
    ("mixture_back", (8, ROWS, 512), LOW),
    ("scores_part", (4, ROWS, 128), F32),
    ("scores_got", (4, ROWS, 128), F32),
    ("scores_sent", (3, ROWS, 128), F32),
    ("scores_far", (3, ROWS, 128), F32),
    ("scores_sum", (ROWS, 128), F32),
    ("zeta_own", (ROWS, 128), LOW),
    ("zeta_all", (8, ROWS, 128), LOW),
    ("gr", (4, ROWS, WIDE), LOW),
    ("gr_got", (3, ROWS, WIDE), LOW),
    ("ge", (4, 256, 512), LOW),
    ("ge_got", (3, 256, 512), LOW),
    ("ge_sum", (8, 32, 512), LOW),
    ("go", (4, 64, WIDE), LOW),
    ("go_got", (3, 64, WIDE), LOW),
    ("ga", (4, 256, 768), LOW),
    ("ga_got", (3, 256, 768), LOW),
    ("ga_sum", (8, 32, 768), LOW),
    ("gz", (4, 8, 32, 128), F32),
    ("gz_own", (4, 32, 128), F32),
    ("sums", (40, WIDE), F32),
    ("sum_blocks", (8, 40, 128), F32),
    ("sum_parts", (8, 40, 128), F32),
    ("sum_rows", (4, 40, 128), F32),
    ("sum_cols", (40, 128), F32),
    ("square_own", (8, 128), F32),
    ("square_all", (8, 8, 128), F32),
)
NAMES = INPUTS + tuple(item[0] for item in RESULTS) + tuple(item[0] for item in SCRATCH) + ("send", "recv")


class Refs:
    def __init__(self, refs):
        for name, ref in zip(NAMES, refs):
            setattr(self, name, ref)


def layer_kernel(*refs):
    r = Refs(refs)
    net = Net(r.send, r.recv)
    z, y, x, c = here()
    me = slot_of(y, x, c)
    twin = device(z, y, x, 1 - c)
    tokens = 8 * ROWS
    greet()

    lane = lax.broadcasted_iota(jnp.int32, (32, 128), 1)
    r.small_wide[...] = jnp.zeros((32, 128), F32)
    r.small_wide[:, 0:64] = r.ema[...].astype(F32)
    small = r.small_wide[...]
    for k in range(5):
        line = r.norm_gains[k : k + 1, :] if k < 3 else r.norm_biases[k - 3 : k - 2, :]
        small = jnp.where(lane == 64 + k, column_of(line.astype(F32)), small)
    r.small[...] = small.astype(LOW)
    small_plane = spread_plane(net, r.small, r.small_all.at[z])
    r.wo[z] = r.wo_own[...]
    out_line = LineGather(net, r.wo)
    out_line.start()
    for s in range(8):
        for pair in range(2):
            r.blocks_a[s, :, pair * 128 : (pair + 1) * 128] = pick_halves(r.wv, 0, s, pair)
            r.blocks_a[s, :, 512 + pair * 128 : 640 + pair * 128] = pick_halves(r.wm, 1152, s, pair)
        r.blocks_a[s, :, 256:384] = r.wm[:, s * 128 : (s + 1) * 128]
        r.blocks_a[s, :, 384:512] = r.wm[:, 1024:1152]
        r.blocks_a[s, :, 768:896] = r.wm[:, 3200 + s * 128 : 3328 + s * 128]
    attn_plane = swap_plane(net, r.blocks_a, r.wa.at[z])
    near_base = net.take(3)

    def near(k):
        yy, xx = chip_of(k)
        return net.make(near_base + k - 1, r.x, r.x_near.at[k - 1], device(z, yy, xx, c))

    for k in (1, 2, 3):
        near(k).start()
    row = lax.broadcasted_iota(jnp.int32, OWN, 0)
    r.own_low[...] = jnp.where(row < r.lens[0, 0], r.cot[...].astype(F32), 0.0).astype(LOW)
    for s in range(8):
        for zz in range(4):
            r.blocks_e[s, :, zz * 128 : (zz + 1) * 128] = r.we_own[:, (zz * 8 + s) * 128 : (zz * 8 + s + 1) * 128]
    small_plane.finish()
    half = pl.ds(c * 4, 4)
    small_line = spread_line(net, r.small_all, half)
    expand_plane = swap_plane(net, r.blocks_e, r.we.at[z])
    cot_plane = PlaneGather(net, r.own_low, r.cot_all)
    cot_plane.start()
    r.heads[0:4] = r.consts[...].astype(F32)
    wide = jnp.broadcast_to(r.consts[3:4].astype(F32), (128, 128)).astype(LOW)
    turned = jnp.dot(wide, mirror_matrix(128), preferred_element_type=F32)
    r.table[...] = pltpu.roll(turned, 1, 1, stride=1, stride_axis=0)
    attn_plane.finish()
    attn_line = LineGather(net, r.wa)
    attn_line.start()
    small_line.finish()
    halves = []
    for other in line_peers(z):
        block = r.small_all.at[other, half]
        halves.append(net.copy(block, block, twin))
    for copy in halves:
        copy.wait()
    out_line.relay()

    r.prm[...] = r.small_all[...].reshape(WIDE, 128).astype(F32).T
    damping = jax.nn.sigmoid(r.prm[0:16])
    mixing = jax.nn.sigmoid(r.prm[16:32])
    lanes_to_rows(1.0 - mixing * damping, r.fac)
    lanes_to_rows(0.25 * r.prm[48:64] * (mixing * r.prm[32:48]), r.gain)
    pair_base = net.take(8)

    def pair_normed(k):
        yy, xx = chip_of(k)
        block = r.normed_all.at[slot_of(yy, xx, c)]
        return net.make(pair_base + k, block, block, twin)

    def pair_mixed(k):
        yy, xx = chip_of(k)
        block = r.mixed_all.at[slot_of(yy, xx, c)]
        return net.make(pair_base + 4 + k, block, block, twin)

    def mix(k, source, tall, pre):
        yy, xx = chip_of(k)
        slot = slot_of(yy, xx, c)
        xhat, _ = standardized(source.astype(F32))
        normed = xhat * r.prm[64:65] + r.prm[67:68]
        r.normed_all[slot] = normed.astype(LOW)
        pair_normed(k).start()
        lanes_to_rows(normed, tall)
        pre[...] = r.prm[65:66] * normed
        ema_forward(r.fac, r.gain, tall, r.tall_out)
        for s in range(8):
            cols = slice(s * 128, (s + 1) * 128)
            pre[:, cols] = pre[:, cols] + r.tall_out[:, s, :]
        r.mixed_all[slot] = silu(pre[...]).astype(LOW)
        pair_mixed(k).start()

    mix(0, r.x[...], r.nrm, r.pre)

    @pl.loop(1, 4)
    def _(k):
        near(k).wait_recv()
        mix(k, r.x_near[k - 1], r.tall, r.work)

    attn_line.relay()
    r.wr[z] = r.wr_own[...]
    reduce_line = LineGather(net, r.wr)
    reduce_line.start()
    expand_plane.finish()
    expand_line = LineGather(net, r.we)
    expand_line.start()
    cot_plane.take_rest()
    cot_plane.finish()
    for k in (1, 2, 3):
        near(k).wait_send()
    for k in range(4):
        pair_normed(k).wait()
        pair_mixed(k).wait()
    out_line.finish()
    attn_line.finish()

    cand_cols = cols_at(me, 128)
    shift = r.heads[2:3]

    def weights_a(first, last):
        return r.wa[:, :, :, first:last].reshape(WIDE, last - first)

    def attend(b):
        pre = jnp.dot(r.normed_all[b], weights_a(0, 256), preferred_element_type=F32)
        r.value_pre[b] = pre
        low_values = silu(pre).astype(LOW)
        r.value_low[b] = low_values
        mixture = jnp.dot(r.mixed_all[b], weights_a(256, 896), preferred_element_type=F32)
        r.update_part[b] = mixture[:, 0:128].astype(LOW)
        r.zeta_pre[b] = mixture[:, 128:256]
        _, _, probs = block_scores_of(silu(mixture[:, 128:256]), r.heads, shift, r.table)
        r.weights_low[b] = probs.astype(LOW)
        mixed_values = jnp.dot(probs.astype(LOW), low_values, preferred_element_type=F32)
        r.attended[b] = mixed_values
        r.reset_pre[b] = mixture[:, 256:512]
        gate = (mixed_values * silu(mixture[:, 256:512])).astype(LOW)
        r.gated[b] = gate
        r.work[...] = jnp.dot(gate, r.wo[...].reshape(256, WIDE), preferred_element_type=F32)
        r.work[:, cand_cols] = r.work[:, cand_cols] + mixture[:, 512:640]
        return r.work[...]

    hidden_sum = PlaneSum(net, r.part, r.got, r.sent, r.far, r.hidden_pre)
    hidden_sum.run(attend)
    update_plane = swap_plane(net, r.update_part, r.update_all)
    hidden_sum.finish()
    update_plane.finish()
    for s in range(8):
        r.update_pre[:, s * 128 : (s + 1) * 128] = r.update_all[s].astype(F32)
    stream = r.x[...].astype(F32)
    r.first[...] = stream + jax.nn.sigmoid(r.update_pre[...]) * (silu(r.hidden_pre[...]) - stream)
    xhat, _ = standardized(r.first[...])
    r.own_low[...] = (xhat * r.prm[66:67] + r.prm[68:69]).astype(LOW)
    two_plane = PlaneGather(net, r.own_low, r.two_all)
    two_plane.start()
    reduce_line.relay()
    expand_line.relay()
    reduce_line.finish()
    expand_line.finish()

    def reduce_rows():
        return r.wr[...].reshape(512, WIDE)

    def expand_rows():
        return r.we[...].reshape(WIDE, 512)

    def expand(b):
        pre = jnp.dot(r.two_all[b], expand_rows(), preferred_element_type=F32)
        r.expand_low[b] = silu(pre).astype(LOW)
        grad = (cols_dot(r.cot_all[b], reduce_rows()) * silu_slope(pre)).astype(LOW)
        r.grad_pre[b] = grad
        return cols_dot(grad, expand_rows())

    two_sum = PlaneSum(net, r.part, r.got, r.sent, r.far, r.work)

    @pl.loop(0, 4)
    def _(k):
        yy, xx = chip_of(k)

        @pl.when(k > 0)
        def _():
            two_plane.take_near(k)

        two_plane.take_twin(k)
        two_sum.give(k, expand(slot_of(yy, xx, 1 - c)))
        two_sum.pair(k, expand(slot_of(yy, xx, c)))

    two_plane.finish()
    reduce_sum = LineSum(net, r.gr, r.gr_got, r.grad_reduce)
    expand_sum = LineSum(net, r.ge, r.ge_got, r.ge_sum)

    @pl.loop(0, 4)
    def _(zz):
        r.gr[zz] = rows_dot(
            r.expand_low[:, :, cols_at(zz, 128)].reshape(tokens, 128), r.cot_all[...].reshape(tokens, WIDE)
        ).astype(LOW)

    reduce_sum.start()

    @pl.loop(0, 4)
    def _(zz):
        r.ge[zz] = rows_dot(
            r.two_all[:, :, cols_at(zz, 256)].reshape(tokens, 256), r.grad_pre[...].reshape(tokens, 512)
        ).astype(LOW)

    expand_sum.start()
    two_sum.finish()

    valid = jnp.where(lax.broadcasted_iota(jnp.int32, (ROWS, 1), 0) < r.lens[0, 0], 1.0, 0.0)
    stream = r.x[...].astype(F32)
    update = jax.nn.sigmoid(r.update_pre[...])
    xhat, inverse = standardized(r.first[...])
    grad_two = r.work[...]
    put_rows(r.sums, 34, grad_two * xhat)
    put_rows(r.sums, 36, grad_two)
    grad_first = r.cot[...].astype(F32) * valid + norm_back(grad_two, xhat, inverse, r.prm[66:67])
    r.grad_inputs[...] = grad_first * (1.0 - update)
    grad_update = (
        grad_first * (silu(r.hidden_pre[...]) - stream) * update * (1.0 - update)
    ).astype(LOW)
    r.own_low[...] = (grad_first * update * silu_slope(r.hidden_pre[...])).astype(LOW)
    hid_plane = PlaneGather(net, r.own_low, r.hid_all)
    for s in range(8):
        r.update_part[s] = grad_update[:, s * 128 : (s + 1) * 128]
    upd_plane = swap_plane(net, r.update_part, r.update_all)
    hid_plane.start()
    reduce_sum.relay()

    upd_plane.finish()
    scores_plane = PlaneSum(net, r.scores_part, r.scores_got, r.scores_sent, r.scores_far, r.scores_sum)
    mixed_sum = PlaneSum(net, r.part, r.got, r.sent, r.far, r.work)

    def attend_back(b):
        gate_grad = cols_dot(r.hid_all[b], r.wo[...].reshape(256, WIDE))
        pre = r.reset_pre[b]
        low_grad = (gate_grad * silu(pre)).astype(LOW)
        r.value_back[b] = (rows_dot(r.weights_low[b], low_grad) * silu_slope(r.value_pre[b])).astype(LOW)
        r.mixture_back[b, :, 0:128] = r.update_all[b]
        r.mixture_back[b, :, 128:384] = (gate_grad * r.attended[b] * silu_slope(pre)).astype(LOW)
        r.mixture_back[b, :, 384:512] = r.hid_all[b, :, cand_cols]
        return cols_dot(low_grad, r.value_low[b])

    def mixed_block(b):
        return cols_dot(r.mixture_back[b, :, 0:128], weights_a(256, 384)) + cols_dot(
            r.mixture_back[b, :, 128:512], weights_a(512, 896)
        )

    @pl.loop(0, 4)
    def _(k):
        yy, xx = chip_of(k)

        @pl.when(k > 0)
        def _():
            hid_plane.take_near(k)

        hid_plane.take_twin(k)
        other = slot_of(yy, xx, 1 - c)
        mine = slot_of(yy, xx, c)
        scores_plane.give(k, attend_back(other))
        mixed_sum.give(k, mixed_block(other))
        scores_plane.pair(k, attend_back(mine))
        mixed_sum.pair(k, mixed_block(mine))

    hid_plane.finish()
    expand_sum.relay()
    out_sum = LineSum(net, r.go, r.go_got, r.grad_out)
    attn_sum = LineSum(net, r.ga, r.ga_got, r.ga_sum)

    @pl.loop(0, 4)
    def _(t):
        cols = cols_at(t, 256)
        grad = rows_dot(
            r.gated[...].reshape(tokens, 256), r.hid_all[:, :, cols].reshape(tokens, 256)
        ).astype(LOW)
        for zz in range(4):
            r.go[zz, :, cols] = grad[zz * 64 : (zz + 1) * 64]

    out_sum.start()

    @pl.loop(0, 4)
    def _(zz):
        cols = cols_at(zz, 256)
        r.ga[zz, :, 0:256] = rows_dot(
            r.normed_all[:, :, cols].reshape(tokens, 256), r.value_back[...].reshape(tokens, 256)
        ).astype(LOW)
        r.ga[zz, :, 256:768] = rows_dot(
            r.mixed_all[:, :, cols].reshape(tokens, 256), r.mixture_back[...].reshape(tokens, 512)
        ).astype(LOW)

    attn_sum.start()

    scores_plane.finish()
    grad_weights = r.scores_sum[...]
    zeta_own_pre = r.zeta_pre[me]
    zeta = silu(zeta_own_pre)
    query_low, key_low, probs = block_scores_of(zeta, r.heads, shift, r.table)
    grad_scores = (probs * (grad_weights - jnp.sum(probs * grad_weights, axis=-1, keepdims=True))).astype(LOW)
    scale = zeta.shape[1] ** (-0.5)
    grad_query = jnp.dot(grad_scores, key_low, preferred_element_type=F32) * scale
    grad_key = rows_dot(grad_scores, query_low) * scale
    skewed = pltpu.roll(
        jnp.dot(grad_scores, mirror_matrix(ROWS), preferred_element_type=F32), 1, 1, stride=1, stride_axis=0
    )
    r.sums[37:40] = jnp.zeros((3, WIDE), F32)
    r.sums[37:38, 0:128] = jnp.sum(grad_query * zeta, axis=0, keepdims=True)
    r.sums[37:38, 128:256] = jnp.sum(grad_key * zeta, axis=0, keepdims=True)
    r.sums[37:38, 256:384] = jnp.sum(grad_query, axis=0, keepdims=True)
    r.sums[37:38, 384:512] = jnp.sum(skewed, axis=0, keepdims=True)
    grad_zeta = grad_query * r.heads[0:1] + grad_key * r.heads[1:2]
    r.zeta_own[...] = (grad_zeta * silu_slope(zeta_own_pre)).astype(LOW)
    zeta_plane = spread_plane(net, r.zeta_own, r.zeta_all)

    mixed_sum.finish()
    normed_sum = PlaneSum(net, r.part, r.got_b, r.sent_b, r.far_b, r.branch)
    normed_sum.run(lambda b: cols_dot(r.value_back[b], weights_a(0, 256)))
    grad_mixed = r.work[...] + cols_dot(r.zeta_own[...], weights_a(384, 512))
    pull = grad_mixed * silu_slope(r.pre[...])
    lanes_to_rows(pull, r.tall)
    r.pre[...] = pull
    out_sum.relay()
    attn_sum.relay()
    ema_backward(r.fac, r.gain, r.nrm, r.tall, r.fac_sum, r.gain_sum, r.tall_out)
    for s in range(8):
        cols = slice(s * 128, (s + 1) * 128)
        r.sums[0:16, cols] = r.fac_sum[:, s, :]
        r.sums[16:32, cols] = r.gain_sum[:, s, :]
        r.sums[33:34, cols] = jnp.sum(r.pre[:, cols] * r.nrm[:, s, :], axis=0, keepdims=True)
    normed_sum.finish()
    for s in range(8):
        cols = slice(s * 128, (s + 1) * 128)
        r.branch[:, cols] = r.branch[:, cols] + r.pre[:, cols] * r.prm[65:66, cols] + r.tall_out[:, s, :]
    xhat_one, inverse_one = standardized(r.x[...].astype(F32))
    grad_one = r.branch[...]
    put_rows(r.sums, 32, grad_one * xhat_one)
    put_rows(r.sums, 35, grad_one)
    r.grad_inputs[...] = r.grad_inputs[...] + norm_back(grad_one, xhat_one, inverse_one, r.prm[64:65])

    for s in range(8):
        r.sum_blocks[s] = r.sums[:, s * 128 : (s + 1) * 128]
    small_sum = swap_plane(net, r.sum_blocks, r.sum_parts)
    reduce_sum.finish()
    expand_sum.finish()
    ge_plane = swap_plane(net, r.ge_sum, r.ge_all)
    branch_sum = PlaneSum(net, r.part, r.got, r.sent, r.far, r.branch)
    branch_sum.run(lambda b: jnp.dot(r.expand_low[b], reduce_rows(), preferred_element_type=F32))
    small_sum.finish()
    whole = r.sum_parts[0]
    for s in range(1, 8):
        whole = whole + r.sum_parts[s]
    r.sum_rows[z] = whole
    small_rows = spread_line(net, r.sum_rows)
    zeta_plane.finish()
    r.gz[...] = rows_dot(
        r.mixed_all[...].reshape(tokens, WIDE), r.zeta_all[...].reshape(tokens, 128)
    ).reshape(4, 8, 32, 128)
    for zz in range(4):
        r.gz_own[zz] = r.gz[zz, me]
    zeta_line = swap_line(net, r.gz_own, r.gz_line)
    out_sum.finish()
    attn_sum.finish()
    ga_plane = swap_plane(net, r.ga_sum, r.ga_all)
    branch_sum.finish()
    stream = r.x[...].astype(F32)
    first = r.first[...]
    branch = r.branch[...]
    attn_branch = first - stream
    r.output[...] = ((first + branch) * valid).astype(LOW)
    r.square_own[...] = jnp.zeros((8, 128), F32)
    for k, item in enumerate((stream, attn_branch, branch)):
        squares = jnp.sum(valid * item * item, axis=0, keepdims=True)
        r.square_own[k : k + 1] = jnp.broadcast_to(jnp.sum(squares, axis=1, keepdims=True), (1, 128))
    r.square_own[3:4] = jnp.broadcast_to(jnp.sum(valid, axis=0, keepdims=True), (1, 128))
    square_plane = spread_plane(net, r.square_own, r.square_all)
    small_rows.finish()
    r.sum_cols[...] = (r.sum_rows[0] + r.sum_rows[1]) + (r.sum_rows[2] + r.sum_rows[3])
    small_cols = spread_plane(net, r.sum_cols, r.sums_all)
    square_plane.finish()
    squares = r.square_all[0]
    for s in range(1, 8):
        squares = squares + r.square_all[s]
    r.square_line[z] = squares
    square_rows = spread_line(net, r.square_line)
    ge_plane.finish()
    zeta_line.finish()
    ga_plane.finish()
    small_cols.finish()
    square_rows.finish()


def layer(*operands):
    return pl.pallas_call(
        layer_kernel,
        name="layer",
        out_shape=[jax.ShapeDtypeStruct(shape, dtype) for _, shape, dtype in RESULTS],
        in_specs=[
            pl.BlockSpec(memory_space=pltpu.SMEM) if name == "lens" else VMEM for name in INPUTS
        ],
        out_specs=[VMEM] * len(RESULTS),
        scratch_shapes=[pltpu.VMEM(shape, dtype) for _, shape, dtype in SCRATCH]
        + [pltpu.SemaphoreType.DMA((LINES,)), pltpu.SemaphoreType.DMA((LINES,))],
        compiler_params=pltpu.CompilerParams(
            collective_id=1, has_side_effects=True, vmem_limit_bytes=60 << 20
        ),
    )(*operands)


def place_halves(blocks, base, q, out, start):
    lane = lax.broadcasted_iota(jnp.int32, (blocks.shape[1], 128), 1)
    for zz in range(4):
        at = base + (zz // 2) * 128
        left = blocks[2 * q, :, at : at + 128].astype(F32)
        right = blocks[2 * q + 1, :, at : at + 128].astype(F32)
        if zz % 2:
            left = pltpu.roll(left, 64, 1)
        else:
            right = pltpu.roll(right, 64, 1)
        to = start + (zz * 4 + q) * 128
        out[:, to : to + 128] = jnp.where(lane < 64, left, right)


def outputs_kernel(
    output, grad_inputs, grad_out, grad_reduce, ge_all, ga_all, gz_line, sums_all, square_line, ema,
    output_o, grad_inputs_o, values_o, mix_o, out_o, expand_o, reduce_o, ema_o, gains_o, biases_o, heads_o,
    shift_o, position_o, rms_o, turned,
):
    output_o[...] = output[...]
    grad_inputs_o[...] = grad_inputs[...]
    out_o[...] = grad_out[...]
    reduce_o[...] = grad_reduce[...]
    for s in range(8):
        for zz in range(4):
            at = (zz * 8 + s) * 128
            expand_o[:, at : at + 128] = ge_all[s, :, zz * 128 : (zz + 1) * 128].astype(F32)
        mix_o[:, s * 128 : (s + 1) * 128] = ga_all[s, :, 256:384].astype(F32)
        mix_o[:, 3200 + s * 128 : 3328 + s * 128] = ga_all[s, :, 640:768].astype(F32)
    mix_o[:, 1024:1152] = (gz_line[0] + gz_line[1]) + (gz_line[2] + gz_line[3])
    for q in range(4):
        place_halves(ga_all, 0, q, values_o, 0)
        place_halves(ga_all, 384, q, mix_o, 1152)
    mine = sums_all[lax.axis_index("dp")]
    mine = pltpu.roll(mine, (128 - 32 * lax.axis_index("fsdp")) % 128, 1)
    turned[0:40] = mine
    turned[40:128] = jnp.zeros((88, 128), F32)
    gains_o[...] = turned[32:35, 0:32]
    biases_o[...] = turned[35:37, 0:32]
    flipped = turned[...].T
    raw = ema[...].astype(F32)
    damping = jax.nn.sigmoid(raw[:, 0:16])
    mixing = jax.nn.sigmoid(raw[:, 16:32])
    expand = raw[:, 32:48]
    project = raw[:, 48:64]
    by_factor = flipped[0:32, 0:16] * (0.25 * project * mixing * expand)
    by_gain = flipped[0:32, 16:32]
    by_inflow = 0.25 * project * by_gain
    ema_o[:, 0:16] = -by_factor * mixing * damping * (1.0 - damping)
    ema_o[:, 16:32] = (by_inflow * expand - by_factor * damping) * mixing * (1.0 - mixing)
    ema_o[:, 32:48] = by_inflow * mixing
    ema_o[:, 48:64] = 0.25 * mixing * expand * by_gain
    heads_o[0:1] = sums_all[0, 37:38]
    heads_o[1:2] = sums_all[1, 37:38]
    shift_o[...] = sums_all[2, 37]
    position_o[...] = sums_all[3, 37]
    squares = (square_line[0] + square_line[1]) + (square_line[2] + square_line[3])
    roots = jnp.sqrt(squares / (squares[3:4] * WIDE))
    col = lax.broadcasted_iota(jnp.int32, (1, 128), 1)
    line = jnp.where(col == 0, roots[0:1], jnp.where(col == 1, roots[1:2], roots[2:3]))
    rms_o[...] = line


def outputs(parts, ema_params):
    shapes = (
        ((ROWS, WIDE), LOW), ((ROWS, WIDE), F32), ((32, 2048), F32), ((32, 4224), F32), ((64, WIDE), F32),
        ((32, 4096), F32), ((ROWS, WIDE), F32), ((32, 64), F32), ((3, 32), F32), ((2, 32), F32), ((2, 128), F32),
        ((128,), F32), ((128,), F32), ((1, 128), F32),
    )
    return pl.pallas_call(
        outputs_kernel,
        name="outputs",
        out_shape=[jax.ShapeDtypeStruct(shape, dtype) for shape, dtype in shapes],
        in_specs=[VMEM] * 10,
        out_specs=[VMEM] * len(shapes),
        scratch_shapes=[pltpu.VMEM((128, 128), F32)],
    )(*parts, ema_params)


def on_plane(
    inputs, lengths, w_values, w_mix, w_out, w_expand, w_reduce, ema_params,
    norm_gains, norm_biases, head_gains, query_bias, position_bias, cotangent,
):
    consts = jnp.concatenate([head_gains, query_bias[None], position_bias[None]])
    parts = layer(
        inputs, cotangent, w_values, w_mix, w_out, w_expand, w_reduce, ema_params, norm_gains, norm_biases,
        consts, lengths,
    )
    done = outputs(parts, ema_params)
    return (*done[:13], done[13][0, :3])


def layer_norm(value, gain, shift):
    centre = jnp.mean(value, axis=-1, keepdims=True)
    centered = value - centre
    spread = jnp.mean(centered * centered, axis=-1, keepdims=True)
    return centered * lax.rsqrt(spread + EPS) * gain + shift


def ema_mix(normed, keep, ema_params):
    count = ema_params.shape[1] // 4
    damping = jax.nn.sigmoid(ema_params[:, :count]).T
    mixing = jax.nn.sigmoid(ema_params[:, count : 2 * count]).T
    expand = ema_params[:, 2 * count : 3 * count].T
    project = ema_params[:, 3 * count :].T
    factor = 1.0 - mixing * damping
    inflow = mixing * expand

    def advance(state, item):
        column, flag = item
        state = factor * state * flag[:, None, None] + inflow * column[:, None, :]
        return (state, 0.25 * jnp.sum(project * state, axis=1))

    start = jnp.zeros((normed.shape[0], count, normed.shape[2]), jnp.float32)
    _, smooth = lax.scan(advance, start, (jnp.swapaxes(normed, 0, 1), jnp.swapaxes(keep, 0, 1)))
    return jnp.swapaxes(smooth, 0, 1)


def layout(lengths, rows):
    ends = jnp.cumsum(lengths, axis=1)
    starts = ends - lengths
    place = lax.broadcasted_iota(jnp.int32, (lengths.shape[0], rows), 1)
    begin = jnp.any(place[:, :, None] == starts[:, None, :], axis=2) | (place == ends)
    keep = jnp.where(begin, 0.0, 1.0).astype(jnp.float32)
    valid = jnp.where(place < ends, 1.0, 0.0).astype(jnp.float32)
    return (keep, valid)


def dot_rows(left, right):
    return lax.dot_general(
        left, right, (((0,), (0,)), ((), ())), preferred_element_type=jnp.float32
    )


def dot_cols(left, right):
    return lax.dot_general(
        left, right, (((1,), (1,)), ((), ())), preferred_element_type=jnp.float32
    )


def block_scores(query_low, key_low, position, scale):
    span = query_low.shape[1]
    row = lax.broadcasted_iota(jnp.int32, (span, span), 0)
    col = lax.broadcasted_iota(jnp.int32, (span, span), 1)
    table = position[jnp.clip(row - col, 0, span - 1)]
    scores = (
        jnp.einsum("kiz,kjz->kij", query_low, key_low, preferred_element_type=jnp.float32) * scale
        + table
    )
    return jnp.where(row >= col, scores, NEG)


def diagonal_sums(grid):
    size = grid.shape[0]
    flipped = grid[:, ::-1]
    padded = jnp.pad(flipped, ((0, 0), (0, size)))
    skewed = padded.reshape(-1)[: size * (2 * size - 1)].reshape(size, 2 * size - 1)
    return jnp.sum(skewed, axis=0)[size - 1 :]


def group_rows(value):
    return lax.all_gather(value, "fsdp", axis=0, tiled=True)


def group_total(value):
    return lax.psum_scatter(value, "fsdp", scatter_dimension=0, tiled=True)


def owner_layout(grad, owners):
    return grad.reshape(owners * 8, -1)


def owner_shard(piece, columns):
    return piece.reshape(-1, columns)


def on_device(
    inputs,
    lengths,
    w_values,
    w_mix,
    w_out,
    w_expand,
    w_reduce,
    ema_params,
    norm_gains,
    norm_biases,
    head_gains,
    query_bias,
    position_bias,
    cotangent,
):
    rows, width = inputs.shape
    span = position_bias.shape[0]
    blocks = rows // span
    key_width = head_gains.shape[1]
    scale = key_width ** (-0.5)
    keep, valid = layout(lengths, rows)
    mask = valid[0][:, None]
    gathered = (
        lax.all_gather(w_values, ("dp", "fsdp"), axis=0, tiled=True),
        lax.all_gather(w_mix, ("dp", "fsdp"), axis=0, tiled=True),
        lax.all_gather(w_out, ("dp", "fsdp"), axis=0, tiled=True),
        lax.all_gather(ema_params, ("dp", "fsdp"), axis=0, tiled=True),
        lax.all_gather(norm_gains, ("dp", "fsdp"), axis=1, tiled=True),
        lax.all_gather(norm_biases, ("dp", "fsdp"), axis=1, tiled=True),
    )
    values_full, mix_full, out_full, ema_full, gains_full, biases_full = gathered
    value_width = values_full.shape[1]
    group_size = lax.axis_size("fsdp")
    data_size = lax.axis_size("dp")
    owners = group_size * data_size
    shard_rows = w_expand.shape[0]
    hidden_units = w_expand.shape[1]
    unit_block = hidden_units // (group_size * data_size)
    pieces = w_expand.reshape(shard_rows, data_size, group_size, unit_block)
    swapped = lax.all_to_all(pieces, "fsdp", split_axis=2, concat_axis=0, tiled=True)
    expand_quarter, reduce_use = (
        lax.all_gather(swapped, "dp", axis=0, tiled=True),
        lax.all_gather(w_reduce, "dp", axis=0, tiled=True),
    )
    expand_use = expand_quarter.reshape(expand_quarter.shape[0], data_size * unit_block)
    gains_f = gains_full.astype(jnp.float32)
    biases_f = biases_full.astype(jnp.float32)
    heads_f = head_gains.astype(jnp.float32)
    query_shift = query_bias.astype(jnp.float32)
    position_f = position_bias.astype(jnp.float32)
    stream = inputs.astype(jnp.float32)

    def front(source, gain, shift, omega, params):
        normed_part = layer_norm(source, gain, shift)
        smooth = ema_mix(normed_part[None], keep, params)[0]
        return (normed_part, silu(smooth + omega * normed_part))

    (normed, mixed), front_back = jax.vjp(
        front, stream, gains_f[0], biases_f[0], gains_f[1], ema_full.astype(jnp.float32)
    )
    normed_low = normed.astype(jnp.bfloat16)
    mixed_low = mixed.astype(jnp.bfloat16)
    value_pre = jnp.dot(normed_low, values_full, preferred_element_type=jnp.float32)
    value_low = silu(value_pre).astype(jnp.bfloat16)
    mixture = jnp.dot(mixed_low, mix_full, preferred_element_type=jnp.float32)
    middle = width + key_width
    upper = middle + value_width
    update = jax.nn.sigmoid(mixture[:, :width])
    zeta_pre = mixture[:, width:middle]
    zeta = silu(zeta_pre)
    reset_pre = mixture[:, middle:upper]
    reset = silu(reset_pre)
    candidate = mixture[:, upper:]
    query_low = (
        (zeta * heads_f[0] + query_shift).astype(jnp.bfloat16).reshape(blocks, span, key_width)
    )
    key_low = (zeta * heads_f[1]).astype(jnp.bfloat16).reshape(blocks, span, key_width)
    value_blocks = value_low.reshape(blocks, span, value_width)
    scores = block_scores(query_low, key_low, position_f, scale)
    log_total = jax.nn.logsumexp(scores, axis=-1, keepdims=True)
    weights_low = jnp.exp(scores - log_total).astype(jnp.bfloat16)
    attended = jnp.einsum(
        "kij,kjv->kiv", weights_low, value_blocks, preferred_element_type=jnp.float32
    ).reshape(rows, value_width)
    gated_low = (attended * reset).astype(jnp.bfloat16)
    hidden_pre = candidate + jnp.dot(gated_low, out_full, preferred_element_type=jnp.float32)
    hidden = silu(hidden_pre)
    attn_branch = update * (hidden - stream)
    first = stream + attn_branch
    normed_two, norm_back = jax.vjp(layer_norm, first, gains_f[2], biases_f[1])
    normed_two_low = normed_two.astype(jnp.bfloat16)
    ffn_rows = group_rows(normed_two_low)
    expand_pre = jnp.dot(ffn_rows, expand_use, preferred_element_type=jnp.float32)
    expand_low = silu(expand_pre).astype(jnp.bfloat16)
    branch_part = jnp.dot(expand_low, reduce_use, preferred_element_type=jnp.float32)
    branch = group_total(branch_part)
    output = ((first + branch) * mask).astype(jnp.bfloat16)
    values_back, mix_back, out_back = (
        lax.all_gather(w_values, ("dp", "fsdp"), axis=0, tiled=True),
        lax.all_gather(w_mix, ("dp", "fsdp"), axis=0, tiled=True),
        lax.all_gather(w_out, ("dp", "fsdp"), axis=0, tiled=True),
    )
    grad_out = cotangent.astype(jnp.float32) * mask
    grad_branch = grad_out.astype(jnp.bfloat16)
    grad_rows = group_rows(grad_branch)
    grad_reduce = dot_rows(expand_low, grad_rows)
    grad_expand_out = dot_cols(grad_rows, reduce_use)
    grad_expand_pre = (grad_expand_out * silu_slope(expand_pre)).astype(jnp.bfloat16)
    grad_expand = dot_rows(ffn_rows, grad_expand_pre)
    normed_two_part = dot_cols(grad_expand_pre, expand_use)
    grad_normed_two = group_total(normed_two_part)
    grad_first_norm, grad_gain_two, grad_shift_two = norm_back(grad_normed_two)
    grad_first = grad_out + grad_first_norm
    grad_direct = grad_first * (1.0 - update)
    grad_update = grad_first * (hidden - stream)
    grad_hidden_pre = grad_first * update * silu_slope(hidden_pre)
    grad_hidden_low = grad_hidden_pre.astype(jnp.bfloat16)
    grad_out_proj = dot_rows(gated_low, grad_hidden_low)
    grad_gated = dot_cols(grad_hidden_low, out_back)
    grad_attended = (grad_gated * reset).astype(jnp.bfloat16).reshape(blocks, span, value_width)
    grad_reset = grad_gated * attended
    scores_again = block_scores(query_low, key_low, position_f, scale)
    probs = jnp.exp(scores_again - log_total)
    probs_low = probs.astype(jnp.bfloat16)
    grad_weights = jnp.einsum(
        "kiv,kjv->kij", grad_attended, value_blocks, preferred_element_type=jnp.float32
    )
    grad_value = jnp.einsum(
        "kij,kiv->kjv", probs_low, grad_attended, preferred_element_type=jnp.float32
    ).reshape(rows, value_width)
    inner = jnp.sum(probs * grad_weights, axis=-1, keepdims=True)
    grad_scores = (probs * (grad_weights - inner)).astype(jnp.bfloat16)
    grad_position = diagonal_sums(jnp.sum(grad_scores.astype(jnp.float32), axis=0))
    grad_query = (
        jnp.einsum(
            "kij,kjz->kiz", grad_scores, key_low, preferred_element_type=jnp.float32
        ).reshape(rows, key_width)
        * scale
    )
    grad_key = (
        jnp.einsum(
            "kij,kiz->kjz", grad_scores, query_low, preferred_element_type=jnp.float32
        ).reshape(rows, key_width)
        * scale
    )
    grad_value_pre = (grad_value * silu_slope(value_pre)).astype(jnp.bfloat16)
    grad_values = dot_rows(normed_low, grad_value_pre)
    grad_normed = dot_cols(grad_value_pre, values_back)
    grad_zeta = grad_query * heads_f[0] + grad_key * heads_f[1]
    grad_heads = jnp.stack([jnp.sum(grad_query * zeta, axis=0), jnp.sum(grad_key * zeta, axis=0)])
    grad_query_shift = jnp.sum(grad_query, axis=0)
    grad_mixture = jnp.concatenate(
        [
            grad_update * update * (1.0 - update),
            grad_zeta * silu_slope(zeta_pre),
            grad_reset * silu_slope(reset_pre),
            grad_hidden_pre,
        ],
        axis=1,
    ).astype(jnp.bfloat16)
    grad_mix = dot_rows(mixed_low, grad_mixture)
    grad_mixed = dot_cols(grad_mixture, mix_back)
    grad_source, grad_gain_one, grad_shift_one, grad_omega, grad_ema = front_back(
        (grad_normed, grad_mixed)
    )
    grad_inputs = grad_direct + grad_source
    grad_gains = jnp.stack([grad_gain_one, grad_omega, grad_gain_two])
    grad_shifts = jnp.stack([grad_shift_one, grad_shift_two])
    summed_expand, grad_reduce_dev = (
        lax.psum_scatter(grad_expand, "dp", scatter_dimension=0, tiled=True),
        lax.psum_scatter(grad_reduce, "dp", scatter_dimension=0, tiled=True),
    )
    summed_pieces = summed_expand.reshape(group_size * shard_rows, data_size, 1, unit_block)
    owned = lax.all_to_all(summed_pieces, "fsdp", split_axis=0, concat_axis=2, tiled=True)
    grad_expand_dev = owned.reshape(shard_rows, hidden_units)
    summed_block = (
        lax.psum_scatter(
            owner_layout(grad_values, owners), ("dp", "fsdp"), scatter_dimension=0, tiled=True
        ),
        lax.psum_scatter(
            owner_layout(grad_mix, owners), ("dp", "fsdp"), scatter_dimension=0, tiled=True
        ),
        lax.psum_scatter(grad_out_proj, ("dp", "fsdp"), scatter_dimension=0, tiled=True),
        lax.psum_scatter(
            owner_layout(grad_ema, owners), ("dp", "fsdp"), scatter_dimension=0, tiled=True
        ),
        lax.psum_scatter(grad_gains, ("dp", "fsdp"), scatter_dimension=1, tiled=True),
        lax.psum_scatter(grad_shifts, ("dp", "fsdp"), scatter_dimension=1, tiled=True),
    )
    values_flat, mix_flat, grad_out_dev, ema_flat, grad_gains_dev, grad_shifts_dev = summed_block
    grad_values_dev = owner_shard(values_flat, grad_values.shape[1])
    grad_mix_dev = owner_shard(mix_flat, grad_mix.shape[1])
    grad_ema_dev = owner_shard(ema_flat, grad_ema.shape[1])
    squares = jnp.stack(
        [
            jnp.sum(mask * stream * stream),
            jnp.sum(mask * attn_branch * attn_branch),
            jnp.sum(mask * branch * branch),
        ]
    )
    square_sums, tokens_seen, heads_total, shift_total, position_total = lax.psum(
        (squares, jnp.sum(valid), grad_heads, grad_query_shift, grad_position), ("dp", "fsdp")
    )
    rms = jnp.sqrt(square_sums / (tokens_seen * width))
    return (
        output,
        grad_inputs,
        grad_values_dev,
        grad_mix_dev,
        grad_out_dev,
        grad_expand_dev,
        grad_reduce_dev,
        grad_ema_dev,
        grad_gains_dev,
        grad_shifts_dev,
        heads_total,
        shift_total,
        position_total,
        rms,
    )


def solution(mesh):
    in_specs = (
        P(("dp", "fsdp"), None),
        P(("dp", "fsdp"), None),
        P(("dp", "fsdp"), None),
        P(("dp", "fsdp"), None),
        P(("dp", "fsdp"), None),
        P(("dp", "fsdp"), None),
        P(("dp", "fsdp"), None),
        P(("dp", "fsdp"), None),
        P(None, ("dp", "fsdp")),
        P(None, ("dp", "fsdp")),
        P(),
        P(),
        P(),
        P(("dp", "fsdp"), None),
    )
    out_specs = (
        P(("dp", "fsdp"), None),
        P(("dp", "fsdp"), None),
        P(("dp", "fsdp"), None),
        P(("dp", "fsdp"), None),
        P(("dp", "fsdp"), None),
        P(("dp", "fsdp"), None),
        P(("dp", "fsdp"), None),
        P(("dp", "fsdp"), None),
        P(None, ("dp", "fsdp")),
        P(None, ("dp", "fsdp")),
        P(),
        P(),
        P(),
        P(),
    )
    planes = mesh.shape["dp"] == 8 and mesh.shape["fsdp"] == 4
    return jax.shard_map(
        on_plane if planes else on_device, mesh=mesh, in_specs=in_specs, out_specs=out_specs, check_vma=False
    )
```

```python
import jax
import jax.numpy as jnp
from jax import lax
from jax.experimental import pallas as pl
from jax.experimental.pallas import tpu as pltpu
from jax.sharding import PartitionSpec as P

EPS = 1e-05
NEG = -1e30
F32 = jnp.float32
LOW = jnp.bfloat16
MESH = pl.DeviceIdType.MESH
LINES = 200
STATES = 16


def silu(value):
    return value * jax.nn.sigmoid(value)


def silu_slope(value):
    sigma = jax.nn.sigmoid(value)
    return sigma * (1.0 + value * (1.0 - sigma))


def here():
    dp = lax.axis_index("dp")
    f = lax.axis_index("fsdp")
    return dp // 2, dp % 2, f // 2, f % 2


def device(z, y, x, c):
    return (z * 2 + y, x * 2 + c)


def slot_of(y, x, c):
    return y * 4 + x * 2 + c


def plane_peers(y, x, c):
    peers = []
    for mask in range(1, 8):
        peers.append(
            (
                1 - y if mask & 4 else y,
                1 - x if mask & 2 else x,
                1 - c if mask & 1 else c,
            )
        )
    return peers


def line_peers(z):
    return [z + 1 - 2 * (z % 2), 3 - z, (z + 2) % 4]


def greet(across=True):
    z, y, x, c = here()
    barrier = pltpu.get_barrier_semaphore()
    count = 7
    for peer in plane_peers(y, x, c):
        pl.semaphore_signal(barrier, inc=1, device_id=device(z, *peer), device_id_type=MESH)
    if across:
        count = 10
        for other in line_peers(z):
            pl.semaphore_signal(barrier, inc=1, device_id=device(other, y, x, c), device_id_type=MESH)
    pl.semaphore_wait(barrier, count)


class Net:
    def __init__(self, send, recv):
        self.send = send
        self.recv = recv
        self.used = 0

    def take(self, count):
        self.used += count
        assert self.used <= LINES
        return self.used - count

    def make(self, line, src, dst, target):
        return pltpu.make_async_remote_copy(
            src_ref=src,
            dst_ref=dst,
            send_sem=self.send.at[line],
            recv_sem=self.recv.at[line],
            device_id=target,
            device_id_type=MESH,
        )

    def copy(self, src, dst, target):
        made = self.make(self.take(1), src, dst, target)
        made.start()
        return made


VMEM = pl.BlockSpec(memory_space=pltpu.VMEM)


def rows_dot(left, right):
    return lax.dot_general(left, right, (((0,), (0,)), ((), ())), preferred_element_type=F32)


def cols_dot(left, right):
    return lax.dot_general(left, right, (((1,), (1,)), ((), ())), preferred_element_type=F32)


def lanes_to_rows(wide, tall):
    for s in range(8):
        tall[:, s, :] = wide[:, s * 128 : (s + 1) * 128]


def pick_halves(arr, base, slot, pair):
    one = base + ((2 * pair * 8 + slot) // 2) * 128
    two = base + (((2 * pair + 1) * 8 + slot) // 2) * 128
    left = arr[:, one : one + 128].astype(F32)
    right = arr[:, two : two + 128].astype(F32)
    lane = lax.broadcasted_iota(jnp.int32, left.shape, 1)
    if slot % 2 == 0:
        return jnp.where(lane < 64, left, pltpu.roll(right, 64, 1)).astype(LOW)
    return jnp.where(lane < 64, pltpu.roll(left, 64, 1), right).astype(LOW)


def ema_forward(factor, gain, source, out):
    steps = source.shape[0]

    def step(t, states):
        column = source[t]
        new = []
        terms = []
        for j in range(STATES):
            state = factor[j] * states[j] + column
            new.append(state)
            terms.append(gain[j] * state)
        while len(terms) > 1:
            terms = [terms[i] + terms[i + 1] for i in range(0, len(terms), 2)]
        out[t] = terms[0]
        return tuple(new)

    zero = jnp.zeros(source.shape[1:], F32)
    lax.fori_loop(0, steps, step, (zero,) * STATES)


def ema_backward(fac, gain, nrm, pull_ref, factor_sum, gain_sum, out):
    steps = nrm.shape[0]
    zero = jnp.zeros(nrm.shape[1:], F32)
    group = 4
    for base in range(0, STATES, group):

        def step(t, carry):
            column = nrm[t]
            pull = pull_ref[t]
            new = []
            for k in range(group):
                state, slope, by_factor, by_gain = carry[4 * k : 4 * k + 4]
                f = fac[base + k]
                slope = f * slope + state
                state = f * state + column
                new += [state, slope, by_factor + pull * slope, by_gain + pull * state]
            return tuple(new)

        done = lax.fori_loop(0, steps, step, (zero,) * (4 * group))
        for k in range(group):
            factor_sum[base + k] = done[4 * k + 2]
            gain_sum[base + k] = done[4 * k + 3]

    def turn(t, states):
        at = steps - 1 - t
        pull = pull_ref[at]
        new = []
        terms = []
        for j in range(STATES):
            state = fac[j] * states[j] + pull
            new.append(state)
            terms.append(gain[j] * state)
        while len(terms) > 1:
            terms = [terms[i] + terms[i + 1] for i in range(0, len(terms), 2)]
        out[at] = terms[0]
        return tuple(new)

    lax.fori_loop(0, steps, turn, (zero,) * STATES)


class PlaneGather:
    def __init__(self, net, src, dst):
        z, y, x, c = here()
        self.net, self.src, self.dst = net, src, dst
        self.base = net.take(7)
        self.me = slot_of(y, x, c)

    def near(self, k):
        z, y, x, c = here()
        yy, xx = chip_of(k)
        return self.net.make(self.base + k - 1, self.src, self.dst.at[self.me], device(z, yy, xx, c))

    def twin(self, k):
        z, y, x, c = here()
        yy, xx = chip_of(k)
        block = self.dst.at[slot_of(yy, xx, c)]
        return self.net.make(self.base + 3 + k, block, block, device(z, y, x, 1 - c))

    def start(self):
        self.dst[self.me] = self.src[...]
        for k in (1, 2, 3):
            self.near(k).start()
        self.twin(0).start()

    def take_near(self, k):
        self.near(k).wait_recv()
        self.twin(k).start()

    def take_twin(self, k):
        self.twin(k).wait_recv()

    def take_rest(self):
        for k in (1, 2, 3):
            self.take_near(k)
        for k in range(4):
            self.take_twin(k)

    def finish(self):
        for k in (1, 2, 3):
            self.near(k).wait_send()
        for k in range(4):
            self.twin(k).wait_send()


def chip_of(k):
    z, y, x, c = here()
    return (y + k // 2) % 2, (x + k % 2) % 2


class PlaneSum:
    def __init__(self, net, part, got, sent, far, total, pairs, keep):
        self.net = net
        self.part, self.got, self.sent, self.far, self.total = part, got, sent, far, total
        self.pairs, self.keep = pairs, keep
        self.base = net.take(7)

    def inner(self, k):
        z, y, x, c = here()
        return self.net.make(self.base + k, self.part.at[k], self.got.at[k], device(z, y, x, 1 - c))

    def outer(self, k):
        z, y, x, c = here()
        yy, xx = chip_of(k)
        return self.net.make(self.base + 3 + k, self.sent.at[k - 1], self.far.at[k - 1], device(z, yy, xx, c))

    def give(self, k):
        z, y, x, c = here()
        self.part[k] = self.pairs[1 - c].astype(self.part.dtype)
        self.inner(k).start()

    def hold(self):
        z, y, x, c = here()
        self.keep[...] = self.pairs[c]

    def pair(self, k, send=True):
        self.inner(k).wait_recv()
        both = self.keep[...] + self.got[k].astype(F32)

        @pl.when(k == 0)
        def _():
            self.total[...] = both

        @pl.when(k > 0)
        def _():
            self.sent[k - 1] = both.astype(self.sent.dtype)
            if send:
                self.outer(k).start()

    def run(self, make, send=True):
        @pl.loop(0, 4)
        def _(i):
            make(3 - i)
            self.give(3 - i)

            @pl.when(i > 0)
            def _():
                self.pair(4 - i, send)

            self.hold()

        self.pair(0, send)

    def send(self):
        for k in (1, 2, 3):
            self.outer(k).start()

    def settle(self):
        @pl.loop(0, 4)
        def _(k):
            self.inner(k).wait_send()

    def finish(self):
        @pl.loop(1, 4)
        def _(k):
            self.outer(k).wait()
            self.total[...] = self.total[...] + self.far[k - 1].astype(F32)


class LineGather:
    def __init__(self, net, buf):
        z, y, x, c = here()
        near, mirror, _ = line_peers(z)
        self.inside = z % 3 > 0
        relayed = (2 * z) % 3 + 3 * (z // 3)
        self.first = net.make(net.take(1), buf.at[z], buf.at[z], device(near, y, x, c))
        self.second = net.make(net.take(1), buf.at[z], buf.at[z], device(mirror, y, x, c))
        self.third = net.make(net.take(1), buf.at[relayed], buf.at[relayed], device((3 * z + 2) % 5, y, x, c))

    def start(self):
        self.first.start()
        self.second.start()

        @pl.when(jnp.logical_not(self.inside))
        def _():
            self.third.start()

    def relay(self):
        @pl.when(self.inside)
        def _():
            self.second.wait_recv()
            self.third.start()

    def finish(self):
        self.first.wait()
        self.second.wait_send()

        @pl.when(jnp.logical_not(self.inside))
        def _():
            self.second.wait_recv()

        self.third.wait()


class LineSum:
    def __init__(self, net, buf, got, out):
        z, y, x, c = here()
        near, mirror, across = line_peers(z)
        self.buf, self.got, self.out = buf, got, out
        self.inside = z % 3 > 0
        self.relayed = (2 * z) % 3 + 3 * (z // 3)
        self.first = net.make(net.take(1), buf.at[across], got.at[0], device((2 * z + 1) % 5, y, x, c))
        self.second = net.make(net.take(1), buf.at[near], got.at[1], device(near, y, x, c))
        self.third = net.make(net.take(1), buf.at[mirror], got.at[2], device(mirror, y, x, c))

    def start(self):
        self.first.start()
        self.second.start()

        @pl.when(jnp.logical_not(self.inside))
        def _():
            self.third.start()

    def relay(self):
        @pl.when(self.inside)
        def _():
            self.first.wait_recv()
            self.buf[self.relayed] = (self.buf[self.relayed].astype(F32) + self.got[0].astype(F32)).astype(LOW)
            self.third.start()

    def finish(self):
        z, y, x, c = here()
        self.first.wait_send()
        self.second.wait()
        self.third.wait()
        total = self.buf[z].astype(F32) + self.got[1].astype(F32) + self.got[2].astype(F32)
        self.out[...] = total.reshape(self.out.shape).astype(self.out.dtype)

        @pl.when(jnp.logical_not(self.inside))
        def _():
            self.first.wait_recv()
            whole = total + self.got[0].astype(F32)
            self.out[...] = whole.reshape(self.out.shape).astype(self.out.dtype)


class Spread:
    def __init__(self, copies):
        self.copies = copies

    def finish(self):
        for copy in self.copies:
            copy.wait()


def spread_plane(net, src, dst):
    z, y, x, c = here()
    me = slot_of(y, x, c)
    spread = Spread([net.copy(src, dst.at[me], device(z, *peer)) for peer in plane_peers(y, x, c)])
    dst[me] = src[...]
    return spread


def swap_plane(net, src, dst):
    z, y, x, c = here()
    me = slot_of(y, x, c)
    spread = Spread(
        [net.copy(src.at[slot_of(*peer)], dst.at[me], device(z, *peer)) for peer in plane_peers(y, x, c)]
    )
    dst[me] = src[me]
    return spread


def spread_line(net, buf, part=None):
    z, y, x, c = here()
    block = buf.at[z] if part is None else buf.at[z, part]
    return Spread([net.copy(block, block, device(other, y, x, c)) for other in line_peers(z)])


def swap_line(net, src, dst):
    z, y, x, c = here()
    spread = Spread([net.copy(src.at[other], dst.at[z], device(other, y, x, c)) for other in line_peers(z)])
    dst[z] = src[z]
    return spread


def row_mean(value):
    return jnp.mean(value, axis=-1, keepdims=True)


def standardized(value):
    centred = value - row_mean(value)
    inverse = lax.rsqrt(row_mean(centred * centred) + EPS)
    return centred * inverse, inverse


def norm_back(grad, xhat, inverse, gain):
    scaled = grad * gain
    return inverse * (scaled - row_mean(scaled) - xhat * row_mean(scaled * xhat))


def block_scores_of(zeta, heads, shift, table):
    query_low = (zeta * heads[0:1] + shift).astype(LOW)
    key_low = (zeta * heads[1:2]).astype(LOW)
    scores = cols_dot(query_low, key_low) * (zeta.shape[1] ** (-0.5)) + table[...]
    row = lax.broadcasted_iota(jnp.int32, scores.shape, 0)
    col = lax.broadcasted_iota(jnp.int32, scores.shape, 1)
    scores = jnp.where(row >= col, scores, NEG)
    top = jnp.max(scores, axis=-1, keepdims=True)
    log_total = top + jnp.log(jnp.sum(jnp.exp(scores - top), axis=-1, keepdims=True))
    return query_low, key_low, jnp.exp(scores - log_total)


def mirror_matrix(size):
    row = lax.broadcasted_iota(jnp.int32, (size, size), 0)
    col = lax.broadcasted_iota(jnp.int32, (size, size), 1)
    return jnp.where(row + col == size - 1, 1.0, 0.0).astype(LOW)


def column_of(line):
    size = line.shape[1]
    row = lax.broadcasted_iota(jnp.int32, (size, size), 0)
    col = lax.broadcasted_iota(jnp.int32, (size, size), 1)
    return jnp.sum(jnp.where(row == col, line, 0.0), axis=1, keepdims=True)


def cols_at(index, size):
    return pl.ds(pl.multiple_of(index * size, size), size)


def put_rows(sums, at, wide):
    sums[at : at + 1] = jnp.sum(wide, axis=0, keepdims=True)


ROWS = 128
WIDE = 1024
INPUTS = (
    "x", "cot", "wv", "wm", "wo_own", "we_own", "wr_own", "ema", "norm_gains", "norm_biases", "consts", "lens",
)
RESULTS = (
    ("output", (ROWS, WIDE), LOW),
    ("grad_inputs", (ROWS, WIDE), F32),
    ("grad_out", (64, WIDE), F32),
    ("grad_reduce", (ROWS, WIDE), F32),
    ("ge_all", (8, 32, 512), LOW),
    ("ga_all", (8, 32, 768), LOW),
    ("gz_line", (4, 32, 128), F32),
    ("sums_all", (8, 40, 128), F32),
    ("square_line", (4, 8, 128), F32),
)
ALL = (8, ROWS, WIDE)
OWN = (ROWS, WIDE)
SCRATCH = (
    ("small_wide", (32, 128), F32),
    ("small_all", (4, 8, 32, 128), LOW),
    ("prm", (72, WIDE), F32),
    ("blocks_a", (8, 32, 896), LOW),
    ("blocks_e", (8, 32, 512), LOW),
    ("wa", (4, 8, 32, 896), LOW),
    ("wo", (4, 64, WIDE), LOW),
    ("we", (4, 8, 32, 512), LOW),
    ("wr", (4, ROWS, WIDE), LOW),
    ("table", (128, 128), F32),
    ("heads", (8, 128), F32),
    ("own_low", OWN, LOW),
    ("normed_all", ALL, LOW),
    ("mixed_all", ALL, LOW),
    ("cot_all", ALL, LOW),
    ("two_all", ALL, LOW),
    ("hid_all", ALL, LOW),
    ("fac", (16, 8, 128), F32),
    ("gain", (16, 8, 128), F32),
    ("fac_sum", (16, 8, 128), F32),
    ("gain_sum", (16, 8, 128), F32),
    ("nrm", (ROWS, 8, 128), F32),
    ("tall", (ROWS, 8, 128), F32),
    ("tall_out", (ROWS, 8, 128), F32),
    ("pre", OWN, F32),
    ("value_pre", (8, ROWS, 256), F32),
    ("value_low", (8, ROWS, 256), LOW),
    ("zeta_pre", (8, ROWS, 128), F32),
    ("weights_low", (8, ROWS, 128), LOW),
    ("attended", (8, ROWS, 256), F32),
    ("reset_pre", (8, ROWS, 256), F32),
    ("gated", (8, ROWS, 256), LOW),
    ("work", OWN, F32),
    ("hidden_pre", OWN, F32),
    ("update_pre", OWN, F32),
    ("first", OWN, F32),
    ("update_part", (8, ROWS, 128), LOW),
    ("update_all", (8, ROWS, 128), LOW),
    ("part", (4, ROWS, WIDE), LOW),
    ("got", (4, ROWS, WIDE), LOW),
    ("sent", (3, ROWS, WIDE), LOW),
    ("far", (3, ROWS, WIDE), LOW),
    ("got_b", (4, ROWS, WIDE), LOW),
    ("sent_b", (3, ROWS, WIDE), LOW),
    ("far_b", (3, ROWS, WIDE), LOW),
    ("got_c", (4, ROWS, WIDE), LOW),
    ("sent_c", (3, ROWS, WIDE), LOW),
    ("far_c", (3, ROWS, WIDE), LOW),
    ("pairs", (2, ROWS, WIDE), F32),
    ("grad_two", OWN, F32),
    ("scores_pairs", (2, ROWS, 128), F32),
    ("scores_keep", (ROWS, 128), F32),
    ("expand_pre", (8, ROWS, 512), F32),
    ("expand_low", (8, ROWS, 512), LOW),
    ("grad_pre", (8, ROWS, 512), LOW),
    ("branch", OWN, F32),
    ("value_back", (8, ROWS, 256), LOW),
    ("mixture_back", (8, ROWS, 512), LOW),
    ("scores_part", (4, ROWS, 128), F32),
    ("scores_got", (4, ROWS, 128), F32),
    ("scores_sent", (3, ROWS, 128), F32),
    ("scores_far", (3, ROWS, 128), F32),
    ("scores_sum", (ROWS, 128), F32),
    ("zeta_own", (ROWS, 128), LOW),
    ("zeta_all", (8, ROWS, 128), LOW),
    ("gr", (4, ROWS, WIDE), LOW),
    ("gr_got", (3, ROWS, WIDE), LOW),
    ("ge", (4, 256, 512), LOW),
    ("ge_got", (3, 256, 512), LOW),
    ("ge_sum", (8, 32, 512), LOW),
    ("go", (4, 64, WIDE), LOW),
    ("go_got", (3, 64, WIDE), LOW),
    ("ga", (4, 256, 768), LOW),
    ("ga_got", (3, 256, 768), LOW),
    ("ga_sum", (8, 32, 768), LOW),
    ("gz", (4, 8, 32, 128), F32),
    ("gz_own", (4, 32, 128), F32),
    ("sums", (40, WIDE), F32),
    ("sum_blocks", (8, 40, 128), F32),
    ("sum_parts", (8, 40, 128), F32),
    ("sum_rows", (4, 40, 128), F32),
    ("sum_cols", (40, 128), F32),
    ("square_own", (8, 128), F32),
    ("square_all", (8, 8, 128), F32),
)
NAMES = INPUTS + tuple(item[0] for item in RESULTS) + tuple(item[0] for item in SCRATCH) + ("send", "recv")


class Refs:
    def __init__(self, refs):
        for name, ref in zip(NAMES, refs):
            setattr(self, name, ref)


def layer_kernel(*refs):
    r = Refs(refs)
    net = Net(r.send, r.recv)
    z, y, x, c = here()
    me = slot_of(y, x, c)
    twin = device(z, y, x, 1 - c)
    tokens = 8 * ROWS
    greet()

    lane = lax.broadcasted_iota(jnp.int32, (32, 128), 1)
    r.small_wide[...] = jnp.zeros((32, 128), F32)
    r.small_wide[:, 0:64] = r.ema[...].astype(F32)
    small = r.small_wide[...]
    for k in range(5):
        line = r.norm_gains[k : k + 1, :] if k < 3 else r.norm_biases[k - 3 : k - 2, :]
        small = jnp.where(lane == 64 + k, column_of(line.astype(F32)), small)
    r.small_all[z, me] = small.astype(LOW)
    small_line = spread_line(net, r.small_all, me)
    for s in range(8):
        for pair in range(2):
            r.blocks_a[s, :, pair * 128 : (pair + 1) * 128] = pick_halves(r.wv, 0, s, pair)
            r.blocks_a[s, :, 512 + pair * 128 : 640 + pair * 128] = pick_halves(r.wm, 1152, s, pair)
        r.blocks_a[s, :, 256:384] = r.wm[:, s * 128 : (s + 1) * 128]
        r.blocks_a[s, :, 384:512] = r.wm[:, 1024:1152]
        r.blocks_a[s, :, 768:896] = r.wm[:, 3200 + s * 128 : 3328 + s * 128]
    attn_plane = swap_plane(net, r.blocks_a, r.wa.at[z])
    r.wo[z] = r.wo_own[...]
    out_line = LineGather(net, r.wo)
    out_line.start()
    r.wr[z] = r.wr_own[...]
    for s in range(8):
        for zz in range(4):
            r.blocks_e[s, :, zz * 128 : (zz + 1) * 128] = r.we_own[:, (zz * 8 + s) * 128 : (zz * 8 + s + 1) * 128]
    small_line.finish()
    column = r.small_all.at[:, me]
    small_plane = Spread([net.copy(column, column, device(z, *peer)) for peer in plane_peers(y, x, c)])
    near_base = net.take(3)

    def near(k):
        yy, xx = chip_of(k)
        return net.make(near_base + k - 1, r.x, r.mixed_all.at[me], device(z, yy, xx, c))

    for k in (1, 2, 3):
        near(k).start()
    expand_plane = swap_plane(net, r.blocks_e, r.we.at[z])
    row = lax.broadcasted_iota(jnp.int32, OWN, 0)
    r.own_low[...] = jnp.where(row < r.lens[0, 0], r.cot[...].astype(F32), 0.0).astype(LOW)
    cot_plane = PlaneGather(net, r.own_low, r.cot_all)
    cot_plane.start()
    r.heads[0:4] = r.consts[...].astype(F32)
    wide = jnp.broadcast_to(r.consts[3:4].astype(F32), (128, 128)).astype(LOW)
    turned = jnp.dot(wide, mirror_matrix(128), preferred_element_type=F32)
    r.table[...] = pltpu.roll(turned, 1, 1, stride=1, stride_axis=0)
    out_line.relay()
    attn_plane.finish()
    attn_line = LineGather(net, r.wa)
    attn_line.start()
    small_plane.finish()

    r.prm[...] = r.small_all[...].reshape(WIDE, 128).astype(F32).T[0:72]
    damping = jax.nn.sigmoid(r.prm[0:16])
    mixing = jax.nn.sigmoid(r.prm[16:32])
    lanes_to_rows(1.0 - mixing * damping, r.fac)
    lanes_to_rows(0.25 * r.prm[48:64] * (mixing * r.prm[32:48]), r.gain)
    pair_base = net.take(8)

    def pair_normed(k):
        yy, xx = chip_of(k)
        block = r.normed_all.at[slot_of(yy, xx, c)]
        return net.make(pair_base + k, block, block, twin)

    def pair_mixed(k):
        yy, xx = chip_of(k)
        block = r.mixed_all.at[slot_of(yy, xx, c)]
        return net.make(pair_base + 4 + k, block, block, twin)

    def mix(k, tall, pre):
        yy, xx = chip_of(k)
        slot = slot_of(yy, xx, c)
        source = r.mixed_all[slot]
        xhat, _ = standardized(source.astype(F32))
        normed = xhat * r.prm[64:65] + r.prm[67:68]
        r.normed_all[slot] = normed.astype(LOW)
        pair_normed(k).start()
        lanes_to_rows(normed, tall)
        pre[...] = r.prm[65:66] * normed
        ema_forward(r.fac, r.gain, tall, r.tall_out)
        for s in range(8):
            cols = slice(s * 128, (s + 1) * 128)
            pre[:, cols] = pre[:, cols] + r.tall_out[:, s, :]
        r.mixed_all[slot] = silu(pre[...]).astype(LOW)
        pair_mixed(k).start()

    r.mixed_all[me] = r.x[...]
    mix(0, r.nrm, r.pre)

    @pl.loop(1, 4)
    def _(k):
        near(k).wait_recv()

        @pl.when(k == 3)
        def _():
            attn_line.relay()

        mix(k, r.tall, r.work)

    expand_plane.finish()
    expand_line = LineGather(net, r.we)
    expand_line.start()
    reduce_line = LineGather(net, r.wr)
    reduce_line.start()
    cot_plane.take_rest()
    cot_plane.finish()
    for k in (1, 2, 3):
        near(k).wait_send()
    for k in range(4):
        pair_normed(k).wait()
        pair_mixed(k).wait()
    out_line.finish()
    attn_line.finish()

    cand_cols = cols_at(me, 128)
    shift = r.heads[2:3]

    def weights_a(first, last):
        return r.wa[:, :, :, first:last].reshape(WIDE, last - first)

    def pair_of(k):
        yy, xx = chip_of(k)
        return pl.ds((yy * 2 + xx) * 2, 2)

    def rows_of(ref, k):
        return ref[pair_of(k)].reshape(2 * ROWS, ref.shape[2])

    def put(ref, k, value):
        ref[pair_of(k)] = value.reshape(2, ROWS, ref.shape[2]).astype(ref.dtype)

    def attend(k):
        pre = jnp.dot(rows_of(r.normed_all, k), weights_a(0, 256), preferred_element_type=F32)
        put(r.value_pre, k, pre)
        low_values = silu(pre).astype(LOW)
        put(r.value_low, k, low_values)
        mixture = jnp.dot(rows_of(r.mixed_all, k), weights_a(256, 896), preferred_element_type=F32)
        put(r.update_part, k, mixture[:, 0:128])
        put(r.zeta_pre, k, mixture[:, 128:256])
        put(r.reset_pre, k, mixture[:, 256:512])
        zeta = silu(mixture[:, 128:256])
        values = []
        weights = []
        for h in range(2):
            rows = slice(h * ROWS, (h + 1) * ROWS)
            _, _, probs = block_scores_of(zeta[rows], r.heads, shift, r.table)
            weights.append(probs.astype(LOW))
            values.append(jnp.dot(weights[h], low_values[rows], preferred_element_type=F32))
        put(r.weights_low, k, jnp.concatenate(weights, axis=0))
        mixed_values = jnp.concatenate(values, axis=0)
        put(r.attended, k, mixed_values)
        gate = (mixed_values * silu(mixture[:, 256:512])).astype(LOW)
        put(r.gated, k, gate)
        hidden = jnp.dot(gate, r.wo[...].reshape(256, WIDE), preferred_element_type=F32)
        r.pairs[...] = hidden.reshape(2, ROWS, WIDE)
        r.pairs[:, :, cand_cols] = r.pairs[:, :, cand_cols] + mixture[:, 512:640].reshape(2, ROWS, 128)

    hidden_sum = PlaneSum(net, r.part, r.got, r.sent, r.far, r.hidden_pre, r.pairs, r.work)
    hidden_sum.run(attend)
    update_plane = swap_plane(net, r.update_part, r.update_all)
    expand_line.relay()
    hidden_sum.settle()
    hidden_sum.finish()
    update_plane.finish()
    for s in range(8):
        r.update_pre[:, s * 128 : (s + 1) * 128] = r.update_all[s].astype(F32)
    stream = r.x[...].astype(F32)
    r.first[...] = stream + jax.nn.sigmoid(r.update_pre[...]) * (silu(r.hidden_pre[...]) - stream)
    xhat, _ = standardized(r.first[...])
    r.own_low[...] = (xhat * r.prm[66:67] + r.prm[68:69]).astype(LOW)
    two_plane = PlaneGather(net, r.own_low, r.two_all)
    two_plane.start()
    reduce_line.relay()
    expand_line.finish()

    def reduce_rows():
        return r.wr[...].reshape(512, WIDE)

    def expand_rows():
        return r.we[...].reshape(WIDE, 512)

    @pl.loop(0, 4)
    def _(k):
        @pl.when(k > 0)
        def _():
            two_plane.take_near(k)

        two_plane.take_twin(k)
        pre = jnp.dot(rows_of(r.two_all, k), expand_rows(), preferred_element_type=F32)
        put(r.expand_pre, k, pre)
        put(r.expand_low, k, silu(pre))

    two_plane.finish()
    reduce_sum = LineSum(net, r.gr, r.gr_got, r.grad_reduce)
    expand_sum = LineSum(net, r.ge, r.ge_got, r.ge_sum)

    @pl.loop(0, 4)
    def _(zz):
        r.gr[zz] = rows_dot(
            r.expand_low[:, :, cols_at(zz, 128)].reshape(tokens, 128), r.cot_all[...].reshape(tokens, WIDE)
        ).astype(LOW)

    reduce_sum.start()
    reduce_line.finish()

    def expand_back(k):
        grad = (cols_dot(rows_of(r.cot_all, k), reduce_rows()) * silu_slope(rows_of(r.expand_pre, k))).astype(LOW)
        put(r.grad_pre, k, grad)
        r.pairs[...] = cols_dot(grad, expand_rows()).reshape(2, ROWS, WIDE)

    two_sum = PlaneSum(net, r.part, r.got, r.sent, r.far, r.grad_two, r.pairs, r.work)
    two_sum.run(expand_back)

    @pl.loop(0, 4)
    def _(zz):
        r.ge[zz] = rows_dot(
            r.two_all[:, :, cols_at(zz, 256)].reshape(tokens, 256), r.grad_pre[...].reshape(tokens, 512)
        ).astype(LOW)

    expand_sum.start()

    def branch_blocks(k):
        branch = jnp.dot(rows_of(r.expand_low, k), reduce_rows(), preferred_element_type=F32)
        r.pairs[...] = branch.reshape(2, ROWS, WIDE)

    two_sum.settle()
    branch_sum = PlaneSum(net, r.part, r.got_b, r.sent_b, r.far_b, r.branch, r.pairs, r.work)
    branch_sum.run(branch_blocks, send=False)
    reduce_sum.relay()
    two_sum.finish()

    valid = jnp.where(lax.broadcasted_iota(jnp.int32, (ROWS, 1), 0) < r.lens[0, 0], 1.0, 0.0)
    stream = r.x[...].astype(F32)
    update = jax.nn.sigmoid(r.update_pre[...])
    xhat, inverse = standardized(r.first[...])
    grad_two = r.grad_two[...]
    put_rows(r.sums, 34, grad_two * xhat)
    put_rows(r.sums, 36, grad_two)
    grad_first = r.cot[...].astype(F32) * valid + norm_back(grad_two, xhat, inverse, r.prm[66:67])
    r.grad_inputs[...] = grad_first * (1.0 - update)
    grad_update = (
        grad_first * (silu(r.hidden_pre[...]) - stream) * update * (1.0 - update)
    ).astype(LOW)
    r.own_low[...] = (grad_first * update * silu_slope(r.hidden_pre[...])).astype(LOW)
    hid_plane = PlaneGather(net, r.own_low, r.hid_all)
    for s in range(8):
        r.update_part[s] = grad_update[:, s * 128 : (s + 1) * 128]
    upd_plane = swap_plane(net, r.update_part, r.update_all)
    hid_plane.start()

    upd_plane.finish()
    branch_sum.settle()
    expand_sum.relay()
    scores_plane = PlaneSum(
        net, r.scores_part, r.scores_got, r.scores_sent, r.scores_far, r.scores_sum, r.scores_pairs, r.scores_keep
    )
    mixed_sum = PlaneSum(net, r.part, r.got, r.sent, r.far, r.grad_two, r.pairs, r.work)

    def attend_back(k):
        gate_grad = cols_dot(rows_of(r.hid_all, k), r.wo[...].reshape(256, WIDE))
        pre = rows_of(r.reset_pre, k)
        low_grad = (gate_grad * silu(pre)).astype(LOW)
        low_values = rows_of(r.value_low, k)
        weights = rows_of(r.weights_low, k)
        backs = []
        for h in range(2):
            rows = slice(h * ROWS, (h + 1) * ROWS)
            r.scores_pairs[h] = cols_dot(low_grad[rows], low_values[rows])
            backs.append(rows_dot(weights[rows], low_grad[rows]))
        put(r.value_back, k, jnp.concatenate(backs, axis=0) * silu_slope(rows_of(r.value_pre, k)))
        pair = pair_of(k)
        r.mixture_back[pair, :, 0:128] = r.update_all[pair]
        r.mixture_back[pair, :, 128:384] = (
            (gate_grad * rows_of(r.attended, k) * silu_slope(pre)).astype(LOW).reshape(2, ROWS, 256)
        )
        r.mixture_back[pair, :, 384:512] = r.hid_all[pair, :, cand_cols]
        mixture = rows_of(r.mixture_back, k)
        mixed = cols_dot(mixture[:, 0:128], weights_a(256, 384)) + cols_dot(mixture[:, 128:512], weights_a(512, 896))
        r.pairs[...] = mixed.reshape(2, ROWS, WIDE)

    @pl.loop(0, 4)
    def _(k):
        @pl.when(k > 0)
        def _():
            hid_plane.take_near(k)

        hid_plane.take_twin(k)
        attend_back(k)
        scores_plane.give(k)
        mixed_sum.give(k)

        @pl.when(k > 0)
        def _():
            scores_plane.pair(k - 1)
            mixed_sum.pair(k - 1)

        scores_plane.hold()
        mixed_sum.hold()

    scores_plane.pair(3)
    mixed_sum.pair(3)
    hid_plane.finish()
    out_sum = LineSum(net, r.go, r.go_got, r.grad_out)
    attn_sum = LineSum(net, r.ga, r.ga_got, r.ga_sum)

    @pl.loop(0, 4)
    def _(t):
        cols = cols_at(t, 256)
        grad = rows_dot(
            r.gated[...].reshape(tokens, 256), r.hid_all[:, :, cols].reshape(tokens, 256)
        ).astype(LOW)
        for zz in range(4):
            r.go[zz, :, cols] = grad[zz * 64 : (zz + 1) * 64]

    out_sum.start()

    @pl.loop(0, 4)
    def _(zz):
        cols = cols_at(zz, 256)
        r.ga[zz, :, 0:256] = rows_dot(
            r.normed_all[:, :, cols].reshape(tokens, 256), r.value_back[...].reshape(tokens, 256)
        ).astype(LOW)
        r.ga[zz, :, 256:768] = rows_dot(
            r.mixed_all[:, :, cols].reshape(tokens, 256), r.mixture_back[...].reshape(tokens, 512)
        ).astype(LOW)

    attn_sum.start()

    mixed_sum.settle()
    normed_sum = PlaneSum(net, r.part, r.got_c, r.sent_c, r.far_c, r.hidden_pre, r.pairs, r.work)

    def normed_blocks(k):
        normed = cols_dot(rows_of(r.value_back, k), weights_a(0, 256))
        r.pairs[...] = normed.reshape(2, ROWS, WIDE)

    normed_sum.run(normed_blocks)

    scores_plane.settle()
    scores_plane.finish()
    grad_weights = r.scores_sum[...]
    zeta_own_pre = r.zeta_pre[me]
    zeta = silu(zeta_own_pre)
    query_low, key_low, probs = block_scores_of(zeta, r.heads, shift, r.table)
    grad_scores = (probs * (grad_weights - jnp.sum(probs * grad_weights, axis=-1, keepdims=True))).astype(LOW)
    scale = zeta.shape[1] ** (-0.5)
    grad_query = jnp.dot(grad_scores, key_low, preferred_element_type=F32) * scale
    grad_key = rows_dot(grad_scores, query_low) * scale
    skewed = pltpu.roll(
        jnp.dot(grad_scores, mirror_matrix(ROWS), preferred_element_type=F32), 1, 1, stride=1, stride_axis=0
    )
    r.sums[37:40] = jnp.zeros((3, WIDE), F32)
    r.sums[37:38, 0:128] = jnp.sum(grad_query * zeta, axis=0, keepdims=True)
    r.sums[37:38, 128:256] = jnp.sum(grad_key * zeta, axis=0, keepdims=True)
    r.sums[37:38, 256:384] = jnp.sum(grad_query, axis=0, keepdims=True)
    r.sums[37:38, 384:512] = jnp.sum(skewed, axis=0, keepdims=True)
    grad_zeta = grad_query * r.heads[0:1] + grad_key * r.heads[1:2]
    r.zeta_own[...] = (grad_zeta * silu_slope(zeta_own_pre)).astype(LOW)
    zeta_plane = spread_plane(net, r.zeta_own, r.zeta_all)

    mixed_sum.finish()
    branch_sum.send()
    grad_mixed = r.grad_two[...] + cols_dot(r.zeta_own[...], weights_a(384, 512))
    pull = grad_mixed * silu_slope(r.pre[...])
    lanes_to_rows(pull, r.tall)
    r.pre[...] = pull
    out_sum.relay()
    attn_sum.relay()
    ema_backward(r.fac, r.gain, r.nrm, r.tall, r.fac_sum, r.gain_sum, r.tall_out)
    for s in range(8):
        cols = slice(s * 128, (s + 1) * 128)
        r.sums[0:16, cols] = r.fac_sum[:, s, :]
        r.sums[16:32, cols] = r.gain_sum[:, s, :]
        r.sums[33:34, cols] = jnp.sum(r.pre[:, cols] * r.nrm[:, s, :], axis=0, keepdims=True)
    normed_sum.settle()
    normed_sum.finish()
    for s in range(8):
        cols = slice(s * 128, (s + 1) * 128)
        r.hidden_pre[:, cols] = r.hidden_pre[:, cols] + r.pre[:, cols] * r.prm[65:66, cols] + r.tall_out[:, s, :]
    xhat_one, inverse_one = standardized(r.x[...].astype(F32))
    grad_one = r.hidden_pre[...]
    put_rows(r.sums, 32, grad_one * xhat_one)
    put_rows(r.sums, 35, grad_one)
    r.grad_inputs[...] = r.grad_inputs[...] + norm_back(grad_one, xhat_one, inverse_one, r.prm[64:65])

    for s in range(8):
        r.sum_blocks[s] = r.sums[:, s * 128 : (s + 1) * 128]
    small_sum = swap_plane(net, r.sum_blocks, r.sum_parts)
    reduce_sum.finish()
    expand_sum.finish()
    ge_plane = swap_plane(net, r.ge_sum, r.ge_all)
    small_sum.finish()
    whole = r.sum_parts[0]
    for s in range(1, 8):
        whole = whole + r.sum_parts[s]
    r.sum_rows[z] = whole
    small_rows = spread_line(net, r.sum_rows)
    zeta_plane.finish()
    r.gz[...] = rows_dot(
        r.mixed_all[...].reshape(tokens, WIDE), r.zeta_all[...].reshape(tokens, 128)
    ).reshape(4, 8, 32, 128)
    for zz in range(4):
        r.gz_own[zz] = r.gz[zz, me]
    zeta_line = swap_line(net, r.gz_own, r.gz_line)
    out_sum.finish()
    attn_sum.finish()
    ga_plane = swap_plane(net, r.ga_sum, r.ga_all)
    branch_sum.finish()
    stream = r.x[...].astype(F32)
    first = r.first[...]
    branch = r.branch[...]
    attn_branch = first - stream
    r.output[...] = ((first + branch) * valid).astype(LOW)
    r.square_own[...] = jnp.zeros((8, 128), F32)
    for k, item in enumerate((stream, attn_branch, branch)):
        squares = jnp.sum(valid * item * item, axis=0, keepdims=True)
        r.square_own[k : k + 1] = jnp.broadcast_to(jnp.sum(squares, axis=1, keepdims=True), (1, 128))
    r.square_own[3:4] = jnp.broadcast_to(jnp.sum(valid, axis=0, keepdims=True), (1, 128))
    square_plane = spread_plane(net, r.square_own, r.square_all)
    small_rows.finish()
    r.sum_cols[...] = (r.sum_rows[0] + r.sum_rows[1]) + (r.sum_rows[2] + r.sum_rows[3])
    small_cols = spread_plane(net, r.sum_cols, r.sums_all)
    square_plane.finish()
    squares = r.square_all[0]
    for s in range(1, 8):
        squares = squares + r.square_all[s]
    r.square_line[z] = squares
    square_rows = spread_line(net, r.square_line)
    ge_plane.finish()
    zeta_line.finish()
    ga_plane.finish()
    small_cols.finish()
    square_rows.finish()


def layer(*operands):
    return pl.pallas_call(
        layer_kernel,
        name="layer",
        out_shape=[jax.ShapeDtypeStruct(shape, dtype) for _, shape, dtype in RESULTS],
        in_specs=[
            pl.BlockSpec(memory_space=pltpu.SMEM) if name == "lens" else VMEM for name in INPUTS
        ],
        out_specs=[VMEM] * len(RESULTS),
        scratch_shapes=[pltpu.VMEM(shape, dtype) for _, shape, dtype in SCRATCH]
        + [pltpu.SemaphoreType.DMA((LINES,)), pltpu.SemaphoreType.DMA((LINES,))],
        compiler_params=pltpu.CompilerParams(
            collective_id=1, has_side_effects=True, vmem_limit_bytes=60 << 20
        ),
    )(*operands)


def place_halves(blocks, base, q, out, start):
    lane = lax.broadcasted_iota(jnp.int32, (blocks.shape[1], 128), 1)
    for zz in range(4):
        at = base + (zz // 2) * 128
        left = blocks[2 * q, :, at : at + 128].astype(F32)
        right = blocks[2 * q + 1, :, at : at + 128].astype(F32)
        if zz % 2:
            left = pltpu.roll(left, 64, 1)
        else:
            right = pltpu.roll(right, 64, 1)
        to = start + (zz * 4 + q) * 128
        out[:, to : to + 128] = jnp.where(lane < 64, left, right)


def outputs_kernel(
    output, grad_inputs, grad_out, grad_reduce, ge_all, ga_all, gz_line, sums_all, square_line, ema,
    output_o, grad_inputs_o, values_o, mix_o, out_o, expand_o, reduce_o, ema_o, gains_o, biases_o, heads_o,
    shift_o, position_o, rms_o, turned,
):
    output_o[...] = output[...]
    grad_inputs_o[...] = grad_inputs[...]
    out_o[...] = grad_out[...]
    reduce_o[...] = grad_reduce[...]
    for s in range(8):
        for zz in range(4):
            at = (zz * 8 + s) * 128
            expand_o[:, at : at + 128] = ge_all[s, :, zz * 128 : (zz + 1) * 128].astype(F32)
        mix_o[:, s * 128 : (s + 1) * 128] = ga_all[s, :, 256:384].astype(F32)
        mix_o[:, 3200 + s * 128 : 3328 + s * 128] = ga_all[s, :, 640:768].astype(F32)
    mix_o[:, 1024:1152] = (gz_line[0] + gz_line[1]) + (gz_line[2] + gz_line[3])
    for q in range(4):
        place_halves(ga_all, 0, q, values_o, 0)
        place_halves(ga_all, 384, q, mix_o, 1152)
    mine = sums_all[lax.axis_index("dp")]
    mine = pltpu.roll(mine, (128 - 32 * lax.axis_index("fsdp")) % 128, 1)
    turned[0:40] = mine
    turned[40:128] = jnp.zeros((88, 128), F32)
    gains_o[...] = turned[32:35, 0:32]
    biases_o[...] = turned[35:37, 0:32]
    flipped = turned[...].T
    raw = ema[...].astype(F32)
    damping = jax.nn.sigmoid(raw[:, 0:16])
    mixing = jax.nn.sigmoid(raw[:, 16:32])
    expand = raw[:, 32:48]
    project = raw[:, 48:64]
    by_factor = flipped[0:32, 0:16] * (0.25 * project * mixing * expand)
    by_gain = flipped[0:32, 16:32]
    by_inflow = 0.25 * project * by_gain
    ema_o[:, 0:16] = -by_factor * mixing * damping * (1.0 - damping)
    ema_o[:, 16:32] = (by_inflow * expand - by_factor * damping) * mixing * (1.0 - mixing)
    ema_o[:, 32:48] = by_inflow * mixing
    ema_o[:, 48:64] = 0.25 * mixing * expand * by_gain
    heads_o[0:1] = sums_all[0, 37:38]
    heads_o[1:2] = sums_all[1, 37:38]
    shift_o[...] = sums_all[2, 37]
    position_o[...] = sums_all[3, 37]
    squares = (square_line[0] + square_line[1]) + (square_line[2] + square_line[3])
    roots = jnp.sqrt(squares / (squares[3:4] * WIDE))
    col = lax.broadcasted_iota(jnp.int32, (1, 128), 1)
    line = jnp.where(col == 0, roots[0:1], jnp.where(col == 1, roots[1:2], roots[2:3]))
    rms_o[...] = line


def outputs(parts, ema_params):
    shapes = (
        ((ROWS, WIDE), LOW), ((ROWS, WIDE), F32), ((32, 2048), F32), ((32, 4224), F32), ((64, WIDE), F32),
        ((32, 4096), F32), ((ROWS, WIDE), F32), ((32, 64), F32), ((3, 32), F32), ((2, 32), F32), ((2, 128), F32),
        ((128,), F32), ((128,), F32), ((1, 128), F32),
    )
    return pl.pallas_call(
        outputs_kernel,
        name="outputs",
        out_shape=[jax.ShapeDtypeStruct(shape, dtype) for shape, dtype in shapes],
        in_specs=[VMEM] * 10,
        out_specs=[VMEM] * len(shapes),
        scratch_shapes=[pltpu.VMEM((128, 128), F32)],
    )(*parts, ema_params)


def on_plane(
    inputs, lengths, w_values, w_mix, w_out, w_expand, w_reduce, ema_params,
    norm_gains, norm_biases, head_gains, query_bias, position_bias, cotangent,
):
    consts = jnp.concatenate([head_gains, query_bias[None], position_bias[None]])
    parts = layer(
        inputs, cotangent, w_values, w_mix, w_out, w_expand, w_reduce, ema_params, norm_gains, norm_biases,
        consts, lengths,
    )
    done = outputs(parts, ema_params)
    return (*done[:13], done[13][0, :3])


def layer_norm(value, gain, shift):
    centre = jnp.mean(value, axis=-1, keepdims=True)
    centered = value - centre
    spread = jnp.mean(centered * centered, axis=-1, keepdims=True)
    return centered * lax.rsqrt(spread + EPS) * gain + shift


def ema_mix(normed, keep, ema_params):
    count = ema_params.shape[1] // 4
    damping = jax.nn.sigmoid(ema_params[:, :count]).T
    mixing = jax.nn.sigmoid(ema_params[:, count : 2 * count]).T
    expand = ema_params[:, 2 * count : 3 * count].T
    project = ema_params[:, 3 * count :].T
    factor = 1.0 - mixing * damping
    inflow = mixing * expand

    def advance(state, item):
        column, flag = item
        state = factor * state * flag[:, None, None] + inflow * column[:, None, :]
        return (state, 0.25 * jnp.sum(project * state, axis=1))

    start = jnp.zeros((normed.shape[0], count, normed.shape[2]), jnp.float32)
    _, smooth = lax.scan(advance, start, (jnp.swapaxes(normed, 0, 1), jnp.swapaxes(keep, 0, 1)))
    return jnp.swapaxes(smooth, 0, 1)


def layout(lengths, rows):
    ends = jnp.cumsum(lengths, axis=1)
    starts = ends - lengths
    place = lax.broadcasted_iota(jnp.int32, (lengths.shape[0], rows), 1)
    begin = jnp.any(place[:, :, None] == starts[:, None, :], axis=2) | (place == ends)
    keep = jnp.where(begin, 0.0, 1.0).astype(jnp.float32)
    valid = jnp.where(place < ends, 1.0, 0.0).astype(jnp.float32)
    return (keep, valid)


def dot_rows(left, right):
    return lax.dot_general(
        left, right, (((0,), (0,)), ((), ())), preferred_element_type=jnp.float32
    )


def dot_cols(left, right):
    return lax.dot_general(
        left, right, (((1,), (1,)), ((), ())), preferred_element_type=jnp.float32
    )


def block_scores(query_low, key_low, position, scale):
    span = query_low.shape[1]
    row = lax.broadcasted_iota(jnp.int32, (span, span), 0)
    col = lax.broadcasted_iota(jnp.int32, (span, span), 1)
    table = position[jnp.clip(row - col, 0, span - 1)]
    scores = (
        jnp.einsum("kiz,kjz->kij", query_low, key_low, preferred_element_type=jnp.float32) * scale
        + table
    )
    return jnp.where(row >= col, scores, NEG)


def diagonal_sums(grid):
    size = grid.shape[0]
    flipped = grid[:, ::-1]
    padded = jnp.pad(flipped, ((0, 0), (0, size)))
    skewed = padded.reshape(-1)[: size * (2 * size - 1)].reshape(size, 2 * size - 1)
    return jnp.sum(skewed, axis=0)[size - 1 :]


def group_rows(value):
    return lax.all_gather(value, "fsdp", axis=0, tiled=True)


def group_total(value):
    return lax.psum_scatter(value, "fsdp", scatter_dimension=0, tiled=True)


def owner_layout(grad, owners):
    return grad.reshape(owners * 8, -1)


def owner_shard(piece, columns):
    return piece.reshape(-1, columns)


def on_device(
    inputs,
    lengths,
    w_values,
    w_mix,
    w_out,
    w_expand,
    w_reduce,
    ema_params,
    norm_gains,
    norm_biases,
    head_gains,
    query_bias,
    position_bias,
    cotangent,
):
    rows, width = inputs.shape
    span = position_bias.shape[0]
    blocks = rows // span
    key_width = head_gains.shape[1]
    scale = key_width ** (-0.5)
    keep, valid = layout(lengths, rows)
    mask = valid[0][:, None]
    gathered = (
        lax.all_gather(w_values, ("dp", "fsdp"), axis=0, tiled=True),
        lax.all_gather(w_mix, ("dp", "fsdp"), axis=0, tiled=True),
        lax.all_gather(w_out, ("dp", "fsdp"), axis=0, tiled=True),
        lax.all_gather(ema_params, ("dp", "fsdp"), axis=0, tiled=True),
        lax.all_gather(norm_gains, ("dp", "fsdp"), axis=1, tiled=True),
        lax.all_gather(norm_biases, ("dp", "fsdp"), axis=1, tiled=True),
    )
    values_full, mix_full, out_full, ema_full, gains_full, biases_full = gathered
    value_width = values_full.shape[1]
    group_size = lax.axis_size("fsdp")
    data_size = lax.axis_size("dp")
    owners = group_size * data_size
    shard_rows = w_expand.shape[0]
    hidden_units = w_expand.shape[1]
    unit_block = hidden_units // (group_size * data_size)
    pieces = w_expand.reshape(shard_rows, data_size, group_size, unit_block)
    swapped = lax.all_to_all(pieces, "fsdp", split_axis=2, concat_axis=0, tiled=True)
    expand_quarter, reduce_use = (
        lax.all_gather(swapped, "dp", axis=0, tiled=True),
        lax.all_gather(w_reduce, "dp", axis=0, tiled=True),
    )
    expand_use = expand_quarter.reshape(expand_quarter.shape[0], data_size * unit_block)
    gains_f = gains_full.astype(jnp.float32)
    biases_f = biases_full.astype(jnp.float32)
    heads_f = head_gains.astype(jnp.float32)
    query_shift = query_bias.astype(jnp.float32)
    position_f = position_bias.astype(jnp.float32)
    stream = inputs.astype(jnp.float32)

    def front(source, gain, shift, omega, params):
        normed_part = layer_norm(source, gain, shift)
        smooth = ema_mix(normed_part[None], keep, params)[0]
        return (normed_part, silu(smooth + omega * normed_part))

    (normed, mixed), front_back = jax.vjp(
        front, stream, gains_f[0], biases_f[0], gains_f[1], ema_full.astype(jnp.float32)
    )
    normed_low = normed.astype(jnp.bfloat16)
    mixed_low = mixed.astype(jnp.bfloat16)
    value_pre = jnp.dot(normed_low, values_full, preferred_element_type=jnp.float32)
    value_low = silu(value_pre).astype(jnp.bfloat16)
    mixture = jnp.dot(mixed_low, mix_full, preferred_element_type=jnp.float32)
    middle = width + key_width
    upper = middle + value_width
    update = jax.nn.sigmoid(mixture[:, :width])
    zeta_pre = mixture[:, width:middle]
    zeta = silu(zeta_pre)
    reset_pre = mixture[:, middle:upper]
    reset = silu(reset_pre)
    candidate = mixture[:, upper:]
    query_low = (
        (zeta * heads_f[0] + query_shift).astype(jnp.bfloat16).reshape(blocks, span, key_width)
    )
    key_low = (zeta * heads_f[1]).astype(jnp.bfloat16).reshape(blocks, span, key_width)
    value_blocks = value_low.reshape(blocks, span, value_width)
    scores = block_scores(query_low, key_low, position_f, scale)
    log_total = jax.nn.logsumexp(scores, axis=-1, keepdims=True)
    weights_low = jnp.exp(scores - log_total).astype(jnp.bfloat16)
    attended = jnp.einsum(
        "kij,kjv->kiv", weights_low, value_blocks, preferred_element_type=jnp.float32
    ).reshape(rows, value_width)
    gated_low = (attended * reset).astype(jnp.bfloat16)
    hidden_pre = candidate + jnp.dot(gated_low, out_full, preferred_element_type=jnp.float32)
    hidden = silu(hidden_pre)
    attn_branch = update * (hidden - stream)
    first = stream + attn_branch
    normed_two, norm_back = jax.vjp(layer_norm, first, gains_f[2], biases_f[1])
    normed_two_low = normed_two.astype(jnp.bfloat16)
    ffn_rows = group_rows(normed_two_low)
    expand_pre = jnp.dot(ffn_rows, expand_use, preferred_element_type=jnp.float32)
    expand_low = silu(expand_pre).astype(jnp.bfloat16)
    branch_part = jnp.dot(expand_low, reduce_use, preferred_element_type=jnp.float32)
    branch = group_total(branch_part)
    output = ((first + branch) * mask).astype(jnp.bfloat16)
    values_back, mix_back, out_back = (
        lax.all_gather(w_values, ("dp", "fsdp"), axis=0, tiled=True),
        lax.all_gather(w_mix, ("dp", "fsdp"), axis=0, tiled=True),
        lax.all_gather(w_out, ("dp", "fsdp"), axis=0, tiled=True),
    )
    grad_out = cotangent.astype(jnp.float32) * mask
    grad_branch = grad_out.astype(jnp.bfloat16)
    grad_rows = group_rows(grad_branch)
    grad_reduce = dot_rows(expand_low, grad_rows)
    grad_expand_out = dot_cols(grad_rows, reduce_use)
    grad_expand_pre = (grad_expand_out * silu_slope(expand_pre)).astype(jnp.bfloat16)
    grad_expand = dot_rows(ffn_rows, grad_expand_pre)
    normed_two_part = dot_cols(grad_expand_pre, expand_use)
    grad_normed_two = group_total(normed_two_part)
    grad_first_norm, grad_gain_two, grad_shift_two = norm_back(grad_normed_two)
    grad_first = grad_out + grad_first_norm
    grad_direct = grad_first * (1.0 - update)
    grad_update = grad_first * (hidden - stream)
    grad_hidden_pre = grad_first * update * silu_slope(hidden_pre)
    grad_hidden_low = grad_hidden_pre.astype(jnp.bfloat16)
    grad_out_proj = dot_rows(gated_low, grad_hidden_low)
    grad_gated = dot_cols(grad_hidden_low, out_back)
    grad_attended = (grad_gated * reset).astype(jnp.bfloat16).reshape(blocks, span, value_width)
    grad_reset = grad_gated * attended
    scores_again = block_scores(query_low, key_low, position_f, scale)
    probs = jnp.exp(scores_again - log_total)
    probs_low = probs.astype(jnp.bfloat16)
    grad_weights = jnp.einsum(
        "kiv,kjv->kij", grad_attended, value_blocks, preferred_element_type=jnp.float32
    )
    grad_value = jnp.einsum(
        "kij,kiv->kjv", probs_low, grad_attended, preferred_element_type=jnp.float32
    ).reshape(rows, value_width)
    inner = jnp.sum(probs * grad_weights, axis=-1, keepdims=True)
    grad_scores = (probs * (grad_weights - inner)).astype(jnp.bfloat16)
    grad_position = diagonal_sums(jnp.sum(grad_scores.astype(jnp.float32), axis=0))
    grad_query = (
        jnp.einsum(
            "kij,kjz->kiz", grad_scores, key_low, preferred_element_type=jnp.float32
        ).reshape(rows, key_width)
        * scale
    )
    grad_key = (
        jnp.einsum(
            "kij,kiz->kjz", grad_scores, query_low, preferred_element_type=jnp.float32
        ).reshape(rows, key_width)
        * scale
    )
    grad_value_pre = (grad_value * silu_slope(value_pre)).astype(jnp.bfloat16)
    grad_values = dot_rows(normed_low, grad_value_pre)
    grad_normed = dot_cols(grad_value_pre, values_back)
    grad_zeta = grad_query * heads_f[0] + grad_key * heads_f[1]
    grad_heads = jnp.stack([jnp.sum(grad_query * zeta, axis=0), jnp.sum(grad_key * zeta, axis=0)])
    grad_query_shift = jnp.sum(grad_query, axis=0)
    grad_mixture = jnp.concatenate(
        [
            grad_update * update * (1.0 - update),
            grad_zeta * silu_slope(zeta_pre),
            grad_reset * silu_slope(reset_pre),
            grad_hidden_pre,
        ],
        axis=1,
    ).astype(jnp.bfloat16)
    grad_mix = dot_rows(mixed_low, grad_mixture)
    grad_mixed = dot_cols(grad_mixture, mix_back)
    grad_source, grad_gain_one, grad_shift_one, grad_omega, grad_ema = front_back(
        (grad_normed, grad_mixed)
    )
    grad_inputs = grad_direct + grad_source
    grad_gains = jnp.stack([grad_gain_one, grad_omega, grad_gain_two])
    grad_shifts = jnp.stack([grad_shift_one, grad_shift_two])
    summed_expand, grad_reduce_dev = (
        lax.psum_scatter(grad_expand, "dp", scatter_dimension=0, tiled=True),
        lax.psum_scatter(grad_reduce, "dp", scatter_dimension=0, tiled=True),
    )
    summed_pieces = summed_expand.reshape(group_size * shard_rows, data_size, 1, unit_block)
    owned = lax.all_to_all(summed_pieces, "fsdp", split_axis=0, concat_axis=2, tiled=True)
    grad_expand_dev = owned.reshape(shard_rows, hidden_units)
    summed_block = (
        lax.psum_scatter(
            owner_layout(grad_values, owners), ("dp", "fsdp"), scatter_dimension=0, tiled=True
        ),
        lax.psum_scatter(
            owner_layout(grad_mix, owners), ("dp", "fsdp"), scatter_dimension=0, tiled=True
        ),
        lax.psum_scatter(grad_out_proj, ("dp", "fsdp"), scatter_dimension=0, tiled=True),
        lax.psum_scatter(
            owner_layout(grad_ema, owners), ("dp", "fsdp"), scatter_dimension=0, tiled=True
        ),
        lax.psum_scatter(grad_gains, ("dp", "fsdp"), scatter_dimension=1, tiled=True),
        lax.psum_scatter(grad_shifts, ("dp", "fsdp"), scatter_dimension=1, tiled=True),
    )
    values_flat, mix_flat, grad_out_dev, ema_flat, grad_gains_dev, grad_shifts_dev = summed_block
    grad_values_dev = owner_shard(values_flat, grad_values.shape[1])
    grad_mix_dev = owner_shard(mix_flat, grad_mix.shape[1])
    grad_ema_dev = owner_shard(ema_flat, grad_ema.shape[1])
    squares = jnp.stack(
        [
            jnp.sum(mask * stream * stream),
            jnp.sum(mask * attn_branch * attn_branch),
            jnp.sum(mask * branch * branch),
        ]
    )
    square_sums, tokens_seen, heads_total, shift_total, position_total = lax.psum(
        (squares, jnp.sum(valid), grad_heads, grad_query_shift, grad_position), ("dp", "fsdp")
    )
    rms = jnp.sqrt(square_sums / (tokens_seen * width))
    return (
        output,
        grad_inputs,
        grad_values_dev,
        grad_mix_dev,
        grad_out_dev,
        grad_expand_dev,
        grad_reduce_dev,
        grad_ema_dev,
        grad_gains_dev,
        grad_shifts_dev,
        heads_total,
        shift_total,
        position_total,
        rms,
    )


def solution(mesh):
    in_specs = (
        P(("dp", "fsdp"), None),
        P(("dp", "fsdp"), None),
        P(("dp", "fsdp"), None),
        P(("dp", "fsdp"), None),
        P(("dp", "fsdp"), None),
        P(("dp", "fsdp"), None),
        P(("dp", "fsdp"), None),
        P(("dp", "fsdp"), None),
        P(None, ("dp", "fsdp")),
        P(None, ("dp", "fsdp")),
        P(),
        P(),
        P(),
        P(("dp", "fsdp"), None),
    )
    out_specs = (
        P(("dp", "fsdp"), None),
        P(("dp", "fsdp"), None),
        P(("dp", "fsdp"), None),
        P(("dp", "fsdp"), None),
        P(("dp", "fsdp"), None),
        P(("dp", "fsdp"), None),
        P(("dp", "fsdp"), None),
        P(("dp", "fsdp"), None),
        P(None, ("dp", "fsdp")),
        P(None, ("dp", "fsdp")),
        P(),
        P(),
        P(),
        P(),
    )
    planes = mesh.shape["dp"] == 8 and mesh.shape["fsdp"] == 4
    return jax.shard_map(
        on_plane if planes else on_device, mesh=mesh, in_specs=in_specs, out_specs=out_specs, check_vma=False
    )
```

```python
import jax
import jax.numpy as jnp
from jax import lax
from jax.experimental import pallas as pl
from jax.experimental.pallas import tpu as pltpu
from jax.sharding import PartitionSpec as P

EPS = 1e-05
NEG = -1e30
F32 = jnp.float32
LOW = jnp.bfloat16
MESH = pl.DeviceIdType.MESH
LINES = 128
STATES = 16


def silu(value):
    return value * jax.nn.sigmoid(value)


def silu_slope(value):
    sigma = jax.nn.sigmoid(value)
    return sigma * (1.0 + value * (1.0 - sigma))


def here():
    dp = lax.axis_index("dp")
    f = lax.axis_index("fsdp")
    return dp // 2, dp % 2, f // 2, f % 2


def device(z, y, x, c):
    return (z * 2 + y, x * 2 + c)


def slot_of(y, x, c):
    return y * 4 + x * 2 + c


def plane_peers(y, x, c):
    peers = []
    for mask in range(1, 8):
        peers.append(
            (
                1 - y if mask & 4 else y,
                1 - x if mask & 2 else x,
                1 - c if mask & 1 else c,
            )
        )
    return peers


def line_peers(z):
    return [z + 1 - 2 * (z % 2), 3 - z, (z + 2) % 4]


def greet(across=True):
    z, y, x, c = here()
    barrier = pltpu.get_barrier_semaphore()
    count = 7
    for peer in plane_peers(y, x, c):
        pl.semaphore_signal(barrier, inc=1, device_id=device(z, *peer), device_id_type=MESH)
    if across:
        count = 10
        for other in line_peers(z):
            pl.semaphore_signal(barrier, inc=1, device_id=device(other, y, x, c), device_id_type=MESH)
    pl.semaphore_wait(barrier, count)


class Net:
    def __init__(self, send, recv):
        self.send = send
        self.recv = recv
        self.used = 0

    def take(self, count):
        self.used += count
        assert self.used <= LINES
        return self.used - count

    def make(self, line, src, dst, target):
        return pltpu.make_async_remote_copy(
            src_ref=src,
            dst_ref=dst,
            send_sem=self.send.at[line],
            recv_sem=self.recv.at[line],
            device_id=target,
            device_id_type=MESH,
        )

    def copy(self, src, dst, target):
        made = self.make(self.take(1), src, dst, target)
        made.start()
        return made


VMEM = pl.BlockSpec(memory_space=pltpu.VMEM)


def rows_dot(left, right):
    return lax.dot_general(left, right, (((0,), (0,)), ((), ())), preferred_element_type=F32)


def cols_dot(left, right):
    return lax.dot_general(left, right, (((1,), (1,)), ((), ())), preferred_element_type=F32)


def lanes_to_rows(wide, tall):
    for s in range(8):
        tall[:, s, :] = wide[:, s * 128 : (s + 1) * 128]


def pick_halves(arr, base, slot, pair):
    one = base + ((2 * pair * 8 + slot) // 2) * 128
    two = base + (((2 * pair + 1) * 8 + slot) // 2) * 128
    left = arr[:, one : one + 128].astype(F32)
    right = arr[:, two : two + 128].astype(F32)
    lane = lax.broadcasted_iota(jnp.int32, left.shape, 1)
    if slot % 2 == 0:
        return jnp.where(lane < 64, left, pltpu.roll(right, 64, 1)).astype(LOW)
    return jnp.where(lane < 64, pltpu.roll(left, 64, 1), right).astype(LOW)


def ema_forward(factor, gain, source, out):
    steps = source.shape[0]

    def step(t, states):
        column = source[t]
        new = []
        terms = []
        for j in range(STATES):
            state = factor[j] * states[j] + column
            new.append(state)
            terms.append(gain[j] * state)
        while len(terms) > 1:
            terms = [terms[i] + terms[i + 1] for i in range(0, len(terms), 2)]
        out[t] = terms[0]
        return tuple(new)

    zero = jnp.zeros(source.shape[1:], F32)
    lax.fori_loop(0, steps, step, (zero,) * STATES)


def ema_backward(fac, gain, nrm, pull_ref, factor_sum, gain_sum, out):
    steps = nrm.shape[0]
    zero = jnp.zeros(nrm.shape[1:], F32)
    group = 4
    for base in range(0, STATES, group):

        def step(t, carry):
            at = steps - 1 - t
            column = nrm[at]
            pull = pull_ref[at]
            new = []
            terms = []
            for k in range(group):
                state, slope, by_factor, by_gain = carry[4 * k : 4 * k + 4]
                f = fac[base + k]
                slope = f * slope + state
                state = f * state + pull
                new += [state, slope, by_factor + column * slope, by_gain + column * state]
                terms.append(gain[base + k] * state)
            total = (terms[0] + terms[1]) + (terms[2] + terms[3])
            out[at] = total if base == 0 else out[at] + total
            return tuple(new)

        done = lax.fori_loop(0, steps, step, (zero,) * (4 * group))
        for k in range(group):
            factor_sum[base + k] = done[4 * k + 2]
            gain_sum[base + k] = done[4 * k + 3]


class PlaneGather:
    def __init__(self, net, src, dst):
        z, y, x, c = here()
        self.net, self.src, self.dst = net, src, dst
        self.base = net.take(7)
        self.me = slot_of(y, x, c)

    def near(self, k):
        z, y, x, c = here()
        yy, xx = chip_of(k)
        return self.net.make(self.base + k - 1, self.src, self.dst.at[self.me], device(z, yy, xx, c))

    def twin(self, k):
        z, y, x, c = here()
        yy, xx = chip_of(k)
        block = self.dst.at[slot_of(yy, xx, c)]
        return self.net.make(self.base + 3 + k, block, block, device(z, y, x, 1 - c))

    def start(self, last=True):
        self.dst[self.me] = self.src[...]
        self.twin(0).start()
        for k in (1, 2, 3) if last else (1, 2):
            self.near(k).start()

    def start_last(self):
        self.near(3).start()

    def take_near(self, k):
        self.near(k).wait_recv()
        self.twin(k).start()

    def take_twin(self, k):
        self.twin(k).wait_recv()

    def take_rest(self):
        for k in (1, 2, 3):
            self.take_near(k)
        for k in range(4):
            self.take_twin(k)

    def finish(self):
        for k in (1, 2, 3):
            self.near(k).wait_send()
        for k in range(4):
            self.twin(k).wait_send()


def chip_of(k):
    z, y, x, c = here()
    return (y + k // 2) % 2, (x + k % 2) % 2


class PlaneSum:
    def __init__(self, net, part, got, sent, far, total, pairs, keep):
        self.net = net
        self.part, self.got, self.sent, self.far, self.total = part, got, sent, far, total
        self.pairs, self.keep = pairs, keep
        self.base = net.take(7)

    def inner(self, k):
        z, y, x, c = here()
        return self.net.make(self.base + k, self.part.at[k], self.got.at[k], device(z, y, x, 1 - c))

    def outer(self, k):
        z, y, x, c = here()
        yy, xx = chip_of(k)
        return self.net.make(self.base + 3 + k, self.sent.at[k - 1], self.far.at[k - 1], device(z, yy, xx, c))

    def give(self, k):
        z, y, x, c = here()
        self.part[k] = self.pairs[1 - c].astype(self.part.dtype)
        self.inner(k).start()

    def hold(self):
        z, y, x, c = here()
        self.keep[...] = self.pairs[c]

    def pair(self, k, send=True):
        self.inner(k).wait_recv()
        both = self.keep[...] + self.got[k].astype(F32)

        @pl.when(k == 0)
        def _():
            self.total[...] = both

        @pl.when(k > 0)
        def _():
            self.sent[k - 1] = both.astype(self.sent.dtype)
            if send:
                self.outer(k).start()

    def run(self, make, send=True):
        @pl.loop(0, 4)
        def _(i):
            make(3 - i)
            self.give(3 - i)

            @pl.when(i > 0)
            def _():
                self.pair(4 - i, send)

            self.hold()

        self.pair(0, send)

    def send(self):
        for k in (1, 2, 3):
            self.outer(k).start()

    def settle(self):
        @pl.loop(0, 4)
        def _(k):
            self.inner(k).wait_send()

    def finish(self):
        @pl.loop(1, 4)
        def _(k):
            self.outer(k).wait()
            self.total[...] = self.total[...] + self.far[k - 1].astype(F32)


class LineGather:
    def __init__(self, net, buf):
        z, y, x, c = here()
        near, mirror, _ = line_peers(z)
        self.inside = z % 3 > 0
        relayed = (2 * z) % 3 + 3 * (z // 3)
        self.first = net.make(net.take(1), buf.at[z], buf.at[z], device(near, y, x, c))
        self.second = net.make(net.take(1), buf.at[z], buf.at[z], device(mirror, y, x, c))
        self.third = net.make(net.take(1), buf.at[relayed], buf.at[relayed], device((3 * z + 2) % 5, y, x, c))

    def start(self):
        self.first.start()
        self.second.start()

        @pl.when(jnp.logical_not(self.inside))
        def _():
            self.third.start()

    def relay(self):
        @pl.when(self.inside)
        def _():
            self.second.wait_recv()
            self.third.start()

    def finish(self):
        self.first.wait()
        self.second.wait_send()

        @pl.when(jnp.logical_not(self.inside))
        def _():
            self.second.wait_recv()

        self.third.wait()


class LineSum:
    def __init__(self, net, buf, got, out):
        z, y, x, c = here()
        near, mirror, across = line_peers(z)
        self.buf, self.got, self.out = buf, got, out
        self.inside = z % 3 > 0
        self.relayed = (2 * z) % 3 + 3 * (z // 3)
        self.first = net.make(net.take(1), buf.at[across], got.at[0], device((2 * z + 1) % 5, y, x, c))
        self.second = net.make(net.take(1), buf.at[near], got.at[1], device(near, y, x, c))
        self.third = net.make(net.take(1), buf.at[mirror], got.at[2], device(mirror, y, x, c))

    def run(self, make):
        z, y, x, c = here()

        @pl.loop(0, 4)
        def _(i):
            bits = (2 + 3 * i) % 4
            make((z // 2 + bits // 2) % 2 * 2 + (z + bits) % 2)

            @pl.when(i == 0)
            def _():
                self.first.start()

            @pl.when(i == 1)
            def _():
                self.second.start()

        @pl.when(jnp.logical_not(self.inside))
        def _():
            self.third.start()

    def start(self):
        self.first.start()
        self.second.start()

        @pl.when(jnp.logical_not(self.inside))
        def _():
            self.third.start()

    def relay(self):
        @pl.when(self.inside)
        def _():
            self.first.wait_recv()
            self.buf[self.relayed] = (self.buf[self.relayed].astype(F32) + self.got[0].astype(F32)).astype(LOW)
            self.third.start()

    def finish(self):
        z, y, x, c = here()
        self.first.wait_send()
        self.second.wait()
        self.third.wait()
        total = self.buf[z].astype(F32) + self.got[1].astype(F32) + self.got[2].astype(F32)
        self.out[...] = total.reshape(self.out.shape).astype(self.out.dtype)

        @pl.when(jnp.logical_not(self.inside))
        def _():
            self.first.wait_recv()
            whole = total + self.got[0].astype(F32)
            self.out[...] = whole.reshape(self.out.shape).astype(self.out.dtype)


class Spread:
    def __init__(self, net, sends, whole):
        self.net, self.whole = net, whole
        self.line = net.take(1)
        for src, dst, target in sends:
            net.make(self.line, src, dst, target).start()

    def finish(self):
        pltpu.make_async_copy(self.whole, self.whole, self.net.recv.at[self.line]).wait()
        pltpu.make_async_copy(self.whole, self.whole, self.net.send.at[self.line]).wait()


def spread_plane(net, src, dst):
    z, y, x, c = here()
    me = slot_of(y, x, c)
    dst[me] = src[...]
    sends = [(src, dst.at[me], device(z, *peer)) for peer in plane_peers(y, x, c)]
    return Spread(net, sends, dst.at[pl.ds(0, 7)])


def spread_column(net, buf):
    z, y, x, c = here()
    block = buf.at[:, slot_of(y, x, c)]
    sends = [(block, block, device(z, *peer)) for peer in plane_peers(y, x, c)]
    return Spread(net, sends, buf.at[:, pl.ds(0, 7)])


def swap_plane(net, src, dst):
    z, y, x, c = here()
    me = slot_of(y, x, c)
    dst[me] = src[me]
    sends = [(src.at[slot_of(*peer)], dst.at[me], device(z, *peer)) for peer in plane_peers(y, x, c)]
    return Spread(net, sends, dst.at[pl.ds(0, 7)])


def spread_line(net, buf, part=None):
    z, y, x, c = here()
    block = buf.at[z] if part is None else buf.at[z, part]
    whole = buf.at[pl.ds(0, 3)] if part is None else buf.at[pl.ds(0, 3), part]
    return Spread(net, [(block, block, device(other, y, x, c)) for other in line_peers(z)], whole)


def swap_line(net, src, dst):
    z, y, x, c = here()
    dst[z] = src[z]
    sends = [(src.at[other], dst.at[z], device(other, y, x, c)) for other in line_peers(z)]
    return Spread(net, sends, dst.at[pl.ds(0, 3)])


class ChipSwap:
    def __init__(self, net, src, dst):
        z, y, x, c = here()
        self.net, self.src, self.dst = net, src, dst
        self.me = slot_of(y, x, c)
        self.base = net.take(8)

    def copy(self, k, twin):
        z, y, x, c = here()
        yy, xx = chip_of(k)
        cc = (c + twin) % 2
        return self.net.make(
            self.base + 2 * k + twin, self.src.at[slot_of(yy, xx, cc)], self.dst.at[self.me], device(z, yy, xx, cc)
        )

    def start(self):
        self.dst[self.me] = self.src[self.me]
        self.copy(0, 1).start()
        for k in (1, 2, 3):
            for twin in range(2):
                self.copy(k, twin).start()

    def take(self, k):
        self.copy(k, 1).wait_recv()

        @pl.when(k > 0)
        def _():
            self.copy(k, 0).wait_recv()

    def finish(self):
        self.copy(0, 1).wait_send()
        for k in (1, 2, 3):
            for twin in range(2):
                self.copy(k, twin).wait_send()


def row_mean(value):
    return jnp.mean(value, axis=-1, keepdims=True)


def standardized(value):
    centred = value - row_mean(value)
    inverse = lax.rsqrt(row_mean(centred * centred) + EPS)
    return centred * inverse, inverse


def norm_back(grad, xhat, inverse, gain):
    scaled = grad * gain
    return inverse * (scaled - row_mean(scaled) - xhat * row_mean(scaled * xhat))


def block_scores_of(zeta, heads, shift, table):
    query_low = (zeta * heads[0:1] + shift).astype(LOW)
    key_low = (zeta * heads[1:2]).astype(LOW)
    scores = cols_dot(query_low, key_low) * (zeta.shape[1] ** (-0.5)) + table[...]
    row = lax.broadcasted_iota(jnp.int32, scores.shape, 0)
    col = lax.broadcasted_iota(jnp.int32, scores.shape, 1)
    scores = jnp.where(row >= col, scores, NEG)
    top = jnp.max(scores, axis=-1, keepdims=True)
    log_total = top + jnp.log(jnp.sum(jnp.exp(scores - top), axis=-1, keepdims=True))
    return query_low, key_low, jnp.exp(scores - log_total)


def mirror_matrix(size):
    row = lax.broadcasted_iota(jnp.int32, (size, size), 0)
    col = lax.broadcasted_iota(jnp.int32, (size, size), 1)
    return jnp.where(row + col == size - 1, 1.0, 0.0).astype(LOW)


def column_of(line):
    size = line.shape[1]
    row = lax.broadcasted_iota(jnp.int32, (size, size), 0)
    col = lax.broadcasted_iota(jnp.int32, (size, size), 1)
    return jnp.sum(jnp.where(row == col, line, 0.0), axis=1, keepdims=True)


def cols_at(index, size):
    return pl.ds(pl.multiple_of(index * size, size), size)


def put_rows(sums, at, wide):
    sums[at : at + 1] = jnp.sum(wide, axis=0, keepdims=True)


ROWS = 128
WIDE = 1024
ALL = (8, ROWS, WIDE)
OWN = (ROWS, WIDE)


ANY = pl.BlockSpec(memory_space=pl.ANY)


class Inputs:
    x_in = ANY
    cot_in = ANY
    wv_in = ANY
    wm_in = ANY
    wo_in = ANY
    we_in = ANY
    wr_in = ANY
    ema = VMEM
    norm_gains = VMEM
    norm_biases = VMEM
    consts = VMEM
    lens = pl.BlockSpec(memory_space=pltpu.SMEM)


class Results:
    output = (ROWS, WIDE), LOW
    grad_inputs = (ROWS, WIDE), F32
    grad_out = (64, WIDE), F32
    grad_reduce = (ROWS, WIDE), F32
    ge_all = (8, 32, 512), LOW
    ga_all = (8, 32, 768), LOW
    gz_line = (4, 32, 128), F32
    sums_all = (8, 40, 128), F32
    square_line = (4, 8, 128), F32


class Scratch:
    x = OWN, LOW
    cot = OWN, LOW
    wv = (32, 2048), LOW
    wm = (32, 4224), LOW
    we_own = (32, 4096), LOW
    small_wide = (32, 128), F32
    wz = (4, 8, 32, 128), LOW
    inverse = (ROWS, 128), F32
    small_all = (4, 8, 32, 128), LOW
    prm = (72, WIDE), F32
    blocks_a = (8, 32, 768), LOW
    blocks_e = (8, 32, 512), LOW
    wa = (4, 8, 32, 768), LOW
    wo = (4, 64, WIDE), LOW
    we = (4, 8, 32, 512), LOW
    wr = (4, ROWS, WIDE), LOW
    table = (128, 128), F32
    heads = (8, 128), F32
    own_low = OWN, LOW
    normed_all = ALL, LOW
    mixed_all = ALL, LOW
    cot_all = ALL, LOW
    two_all = ALL, LOW
    hid_all = ALL, LOW
    fac = (16, 8, 128), F32
    gain = (16, 8, 128), F32
    fac_sum = (16, 8, 128), F32
    gain_sum = (16, 8, 128), F32
    nrm = (ROWS, 8, 128), F32
    tall = (ROWS, 8, 128), F32
    tall_out = (ROWS, 8, 128), F32
    pre = OWN, F32
    value_pre = (8, ROWS, 256), F32
    value_low = (8, ROWS, 256), LOW
    zeta_pre = (8, ROWS, 128), F32
    weights_low = (8, ROWS, 128), LOW
    attended = (8, ROWS, 256), F32
    reset_pre = (8, ROWS, 256), F32
    gated = (8, ROWS, 256), LOW
    work = OWN, F32
    hidden_pre = OWN, F32
    update_pre = OWN, F32
    first = OWN, F32
    update_part = (8, ROWS, 128), LOW
    update_all = (8, ROWS, 128), LOW
    part = (4, ROWS, WIDE), LOW
    got = (4, ROWS, WIDE), LOW
    sent = (3, ROWS, WIDE), LOW
    far = (3, ROWS, WIDE), LOW
    got_b = (4, ROWS, WIDE), LOW
    sent_b = (3, ROWS, WIDE), LOW
    far_b = (3, ROWS, WIDE), LOW
    got_c = (4, ROWS, WIDE), LOW
    sent_c = (3, ROWS, WIDE), LOW
    far_c = (3, ROWS, WIDE), LOW
    pairs = (2, ROWS, WIDE), F32
    grad_two = OWN, F32
    scores_pairs = (2, ROWS, 128), F32
    scores_keep = (ROWS, 128), F32
    expand_pre = (8, ROWS, 512), F32
    expand_low = (8, ROWS, 512), LOW
    grad_pre = (8, ROWS, 512), LOW
    branch = OWN, F32
    value_back = (8, ROWS, 256), LOW
    mixture_back = (8, ROWS, 512), LOW
    scores_part = (4, ROWS, 128), F32
    scores_got = (4, ROWS, 128), F32
    scores_sent = (3, ROWS, 128), F32
    scores_far = (3, ROWS, 128), F32
    scores_sum = (ROWS, 128), F32
    zeta_own = (ROWS, 128), LOW
    zeta_all = (8, ROWS, 128), LOW
    gr = (4, ROWS, WIDE), LOW
    gr_got = (3, ROWS, WIDE), LOW
    ge = (4, 256, 512), LOW
    ge_got = (3, 256, 512), LOW
    ge_sum = (8, 32, 512), LOW
    go = (4, 64, WIDE), LOW
    go_got = (3, 64, WIDE), LOW
    ga = (4, 256, 768), LOW
    ga_got = (3, 256, 768), LOW
    ga_sum = (8, 32, 768), LOW
    gz = (4, 8, 32, 128), F32
    gz_own = (4, 32, 128), F32
    sums = (40, WIDE), F32
    sum_blocks = (8, 40, 128), F32
    sum_parts = (8, 40, 128), F32
    sum_rows = (4, 40, 128), F32
    sum_cols = (40, 128), F32
    square_own = (8, 128), F32
    square_all = (8, 8, 128), F32


class Lines:
    send = (LINES,)
    recv = (LINES,)
    load = (7,)


def fields(group):
    return {name: item for name, item in vars(group).items() if not name.startswith("_")}


class Refs:
    def __init__(self, refs):
        names = [name for group in (Inputs, Results, Scratch, Lines) for name in fields(group)]
        for name, ref in zip(names, refs, strict=True):
            setattr(self, name, ref)


def layer_kernel(*refs):
    r = Refs(refs)
    net = Net(r.send, r.recv)
    z, y, x, c = here()
    me = slot_of(y, x, c)
    twin = device(z, y, x, 1 - c)
    tokens = 8 * ROWS
    loads = [
        pltpu.make_async_copy(src, dst, r.load.at[line])
        for line, (src, dst) in enumerate(
            (
                (r.wm_in, r.wm), (r.wv_in, r.wv), (r.wo_in, r.wo.at[z]), (r.x_in, r.x), (r.we_in, r.we_own),
                (r.wr_in, r.wr.at[z]), (r.cot_in, r.cot),
            )
        )
    ]
    for load in loads:
        load.start()
    greet()
    for load in loads:
        load.wait()

    lane = lax.broadcasted_iota(jnp.int32, (32, 128), 1)
    r.small_wide[...] = jnp.zeros((32, 128), F32)
    r.small_wide[:, 0:64] = r.ema[...].astype(F32)
    small = r.small_wide[...]
    for k in range(5):
        line = r.norm_gains[k : k + 1, :] if k < 3 else r.norm_biases[k - 3 : k - 2, :]
        small = jnp.where(lane == 64 + k, column_of(line.astype(F32)), small)
    r.small_all[z, me] = small.astype(LOW)
    small_line = spread_line(net, r.small_all, me)
    r.wz[z, me] = r.wm[:, 1024:1152]
    zeta_line = spread_line(net, r.wz, me)
    for s in range(8):
        for pair in range(2):
            r.blocks_a[s, :, pair * 128 : (pair + 1) * 128] = pick_halves(r.wv, 0, s, pair)
            r.blocks_a[s, :, 384 + pair * 128 : 512 + pair * 128] = pick_halves(r.wm, 1152, s, pair)
        r.blocks_a[s, :, 256:384] = r.wm[:, s * 128 : (s + 1) * 128]
        r.blocks_a[s, :, 640:768] = r.wm[:, 3200 + s * 128 : 3328 + s * 128]
    attn_plane = swap_plane(net, r.blocks_a, r.wa.at[z])
    out_line = LineGather(net, r.wo)
    out_line.start()
    for s in range(8):
        for zz in range(4):
            r.blocks_e[s, :, zz * 128 : (zz + 1) * 128] = r.we_own[:, (zz * 8 + s) * 128 : (zz * 8 + s + 1) * 128]
    small_line.finish()
    small_plane = spread_column(net, r.small_all)
    near_base = net.take(3)

    def near(k):
        yy, xx = chip_of(k)
        return net.make(near_base + k - 1, r.x, r.mixed_all.at[me], device(z, yy, xx, c))

    for k in (1, 2, 3):
        near(k).start()
    zeta_line.finish()
    zeta_plane = spread_column(net, r.wz)
    expand_plane = swap_plane(net, r.blocks_e, r.we.at[z])
    row = lax.broadcasted_iota(jnp.int32, OWN, 0)
    r.own_low[...] = jnp.where(row < r.lens[0, 0], r.cot[...].astype(F32), 0.0).astype(LOW)
    cot_plane = PlaneGather(net, r.own_low, r.cot_all)
    cot_plane.start()
    r.heads[0:4] = r.consts[...].astype(F32)
    wide = jnp.broadcast_to(r.consts[3:4].astype(F32), (128, 128)).astype(LOW)
    turned = jnp.dot(wide, mirror_matrix(128), preferred_element_type=F32)
    r.table[...] = pltpu.roll(turned, 1, 1, stride=1, stride_axis=0)
    out_line.relay()
    attn_plane.finish()
    attn_line = LineGather(net, r.wa)
    attn_line.start()
    small_plane.finish()

    r.prm[...] = r.small_all[...].reshape(WIDE, 128).astype(F32).T[0:72]
    damping = jax.nn.sigmoid(r.prm[0:16])
    mixing = jax.nn.sigmoid(r.prm[16:32])
    lanes_to_rows(1.0 - mixing * damping, r.fac)
    lanes_to_rows(0.25 * r.prm[48:64] * (mixing * r.prm[32:48]), r.gain)
    pair_base = net.take(8)

    def pair_normed(k):
        yy, xx = chip_of(k)
        block = r.normed_all.at[slot_of(yy, xx, c)]
        return net.make(pair_base + k, block, block, twin)

    def pair_mixed(k):
        yy, xx = chip_of(k)
        block = r.mixed_all.at[slot_of(yy, xx, c)]
        return net.make(pair_base + 4 + k, block, block, twin)

    def mix(k, tall, pre):
        yy, xx = chip_of(k)
        slot = slot_of(yy, xx, c)
        source = r.mixed_all[slot]
        xhat, _ = standardized(source.astype(F32))
        normed = xhat * r.prm[64:65] + r.prm[67:68]
        r.normed_all[slot] = normed.astype(LOW)
        pair_normed(k).start()
        lanes_to_rows(normed, tall)
        pre[...] = r.prm[65:66] * normed
        ema_forward(r.fac, r.gain, tall, r.tall_out)
        for s in range(8):
            cols = slice(s * 128, (s + 1) * 128)
            pre[:, cols] = pre[:, cols] + r.tall_out[:, s, :]
        r.mixed_all[slot] = silu(pre[...]).astype(LOW)
        pair_mixed(k).start()

    r.mixed_all[me] = r.x[...]
    mix(0, r.nrm, r.pre)

    @pl.loop(1, 4)
    def _(k):
        near(k).wait_recv()

        @pl.when(k == 3)
        def _():
            attn_line.relay()

        mix(k, r.tall, r.work)

    expand_plane.finish()
    expand_line = LineGather(net, r.we)
    expand_line.start()
    reduce_line = LineGather(net, r.wr)
    reduce_line.start()
    cot_plane.take_rest()
    cot_plane.finish()
    for k in (1, 2, 3):
        near(k).wait_send()
    for k in range(4):
        pair_normed(k).wait()
        pair_mixed(k).wait()
    zeta_plane.finish()
    out_line.finish()
    attn_line.finish()

    cand_cols = cols_at(me, 128)
    shift = r.heads[2:3]

    def weights_a(first, last):
        return r.wa[:, :, :, first:last].reshape(WIDE, last - first)

    def zeta_weights():
        return r.wz[...].reshape(WIDE, 128)

    def pair_of(k):
        yy, xx = chip_of(k)
        return pl.ds((yy * 2 + xx) * 2, 2)

    def rows_of(ref, k):
        return ref[pair_of(k)].reshape(2 * ROWS, ref.shape[2])

    def put(ref, k, value):
        ref[pair_of(k)] = value.reshape(2, ROWS, ref.shape[2]).astype(ref.dtype)

    def attend(k):
        pre = jnp.dot(rows_of(r.normed_all, k), weights_a(0, 256), preferred_element_type=F32)
        put(r.value_pre, k, pre)
        low_values = silu(pre).astype(LOW)
        put(r.value_low, k, low_values)
        mixed = rows_of(r.mixed_all, k)
        mixture = jnp.dot(mixed, weights_a(256, 768), preferred_element_type=F32)
        put(r.update_part, k, mixture[:, 0:128])
        put(r.reset_pre, k, mixture[:, 128:384])
        zeta = jnp.dot(mixed, zeta_weights(), preferred_element_type=F32)
        put(r.zeta_pre, k, zeta)
        zeta = silu(zeta)
        values = []
        weights = []
        for h in range(2):
            rows = slice(h * ROWS, (h + 1) * ROWS)
            _, _, probs = block_scores_of(zeta[rows], r.heads, shift, r.table)
            weights.append(probs.astype(LOW))
            values.append(jnp.dot(weights[h], low_values[rows], preferred_element_type=F32))
        put(r.weights_low, k, jnp.concatenate(weights, axis=0))
        mixed_values = jnp.concatenate(values, axis=0)
        put(r.attended, k, mixed_values)
        gate = (mixed_values * silu(mixture[:, 128:384])).astype(LOW)
        put(r.gated, k, gate)
        hidden = jnp.dot(gate, r.wo[...].reshape(256, WIDE), preferred_element_type=F32)
        r.pairs[...] = hidden.reshape(2, ROWS, WIDE)
        r.pairs[:, :, cand_cols] = r.pairs[:, :, cand_cols] + mixture[:, 384:512].reshape(2, ROWS, 128)

    hidden_sum = PlaneSum(net, r.part, r.got, r.sent, r.far, r.hidden_pre, r.pairs, r.work)
    hidden_sum.run(attend)
    update_plane = swap_plane(net, r.update_part, r.update_all)
    expand_line.relay()
    hidden_sum.settle()
    hidden_sum.finish()
    update_plane.finish()
    for s in range(8):
        r.update_pre[:, s * 128 : (s + 1) * 128] = r.update_all[s].astype(F32)
    stream = r.x[...].astype(F32)
    r.first[...] = stream + jax.nn.sigmoid(r.update_pre[...]) * (silu(r.hidden_pre[...]) - stream)
    xhat, _ = standardized(r.first[...])
    r.own_low[...] = (xhat * r.prm[66:67] + r.prm[68:69]).astype(LOW)
    two_plane = PlaneGather(net, r.own_low, r.two_all)
    two_plane.start()
    reduce_line.relay()
    expand_line.finish()

    def reduce_rows():
        return r.wr[...].reshape(512, WIDE)

    def expand_rows():
        return r.we[...].reshape(WIDE, 512)

    @pl.loop(0, 4)
    def _(k):
        @pl.when(k > 0)
        def _():
            two_plane.take_near(k)

        two_plane.take_twin(k)
        pre = jnp.dot(rows_of(r.two_all, k), expand_rows(), preferred_element_type=F32)
        put(r.expand_pre, k, pre)
        put(r.expand_low, k, silu(pre))

    two_plane.finish()
    reduce_sum = LineSum(net, r.gr, r.gr_got, r.grad_reduce)
    expand_sum = LineSum(net, r.ge, r.ge_got, r.ge_sum)

    def reduce_grad(zz):
        r.gr[zz] = rows_dot(
            r.expand_low[:, :, cols_at(zz, 128)].reshape(tokens, 128), r.cot_all[...].reshape(tokens, WIDE)
        ).astype(LOW)

    reduce_sum.run(reduce_grad)
    reduce_line.finish()

    def expand_back(k):
        grad = (cols_dot(rows_of(r.cot_all, k), reduce_rows()) * silu_slope(rows_of(r.expand_pre, k))).astype(LOW)
        put(r.grad_pre, k, grad)
        r.pairs[...] = cols_dot(grad, expand_rows()).reshape(2, ROWS, WIDE)

    two_sum = PlaneSum(net, r.part, r.got, r.sent, r.far, r.grad_two, r.pairs, r.work)
    two_sum.run(expand_back)

    @pl.loop(0, 4)
    def _(zz):
        r.ge[zz] = rows_dot(
            r.two_all[:, :, cols_at(zz, 256)].reshape(tokens, 256), r.grad_pre[...].reshape(tokens, 512)
        ).astype(LOW)

    expand_sum.start()

    def branch_blocks(k):
        branch = jnp.dot(rows_of(r.expand_low, k), reduce_rows(), preferred_element_type=F32)
        r.pairs[...] = branch.reshape(2, ROWS, WIDE)

    two_sum.settle()
    branch_sum = PlaneSum(net, r.part, r.got_b, r.sent_b, r.far_b, r.branch, r.pairs, r.work)
    branch_sum.run(branch_blocks, send=False)
    reduce_sum.relay()
    valid = jnp.where(lax.broadcasted_iota(jnp.int32, (ROWS, 1), 0) < r.lens[0, 0], 1.0, 0.0)
    update = jax.nn.sigmoid(r.update_pre[...])
    hidden = r.hidden_pre[...]
    r.work[...] = update * silu_slope(hidden)
    r.pairs[1] = (silu(hidden) - r.x[...].astype(F32)) * update * (1.0 - update)
    xhat, inverse = standardized(r.first[...])
    r.pairs[0] = xhat
    r.inverse[...] = jnp.broadcast_to(inverse, (ROWS, 128))
    two_sum.finish()

    grad_first = r.cot[...].astype(F32) * valid + norm_back(
        r.grad_two[...], r.pairs[0], r.inverse[:, 0:1], r.prm[66:67]
    )
    r.own_low[...] = (grad_first * r.work[...]).astype(LOW)
    hid_plane = PlaneGather(net, r.own_low, r.hid_all)
    hid_plane.start(last=False)
    grad_update = (grad_first * r.pairs[1]).astype(LOW)
    for s in range(8):
        r.update_part[s] = grad_update[:, s * 128 : (s + 1) * 128]
    upd_plane = ChipSwap(net, r.update_part, r.update_all)
    upd_plane.start()
    hid_plane.start_last()
    r.grad_inputs[...] = grad_first * (1.0 - jax.nn.sigmoid(r.update_pre[...]))
    put_rows(r.sums, 34, r.grad_two[...] * r.pairs[0])
    put_rows(r.sums, 36, r.grad_two[...])

    branch_sum.settle()
    expand_sum.relay()
    scores_plane = PlaneSum(
        net, r.scores_part, r.scores_got, r.scores_sent, r.scores_far, r.scores_sum, r.scores_pairs, r.scores_keep
    )
    mixed_sum = PlaneSum(net, r.part, r.got, r.sent, r.far, r.grad_two, r.pairs, r.work)

    def attend_back(k):
        gate_grad = cols_dot(rows_of(r.hid_all, k), r.wo[...].reshape(256, WIDE))
        pre = rows_of(r.reset_pre, k)
        low_grad = (gate_grad * silu(pre)).astype(LOW)
        low_values = rows_of(r.value_low, k)
        weights = rows_of(r.weights_low, k)
        backs = []
        for h in range(2):
            rows = slice(h * ROWS, (h + 1) * ROWS)
            r.scores_pairs[h] = cols_dot(low_grad[rows], low_values[rows])
            backs.append(rows_dot(weights[rows], low_grad[rows]))
        put(r.value_back, k, jnp.concatenate(backs, axis=0) * silu_slope(rows_of(r.value_pre, k)))
        pair = pair_of(k)
        r.mixture_back[pair, :, 0:128] = r.update_all[pair]
        r.mixture_back[pair, :, 128:384] = (
            (gate_grad * rows_of(r.attended, k) * silu_slope(pre)).astype(LOW).reshape(2, ROWS, 256)
        )
        r.mixture_back[pair, :, 384:512] = r.hid_all[pair, :, cand_cols]
        mixture = rows_of(r.mixture_back, k)
        mixed = cols_dot(mixture, weights_a(256, 768))
        r.pairs[...] = mixed.reshape(2, ROWS, WIDE)

    @pl.loop(0, 4)
    def _(k):
        @pl.when(k > 0)
        def _():
            hid_plane.take_near(k)

        hid_plane.take_twin(k)
        upd_plane.take(k)
        attend_back(k)
        scores_plane.give(k)
        mixed_sum.give(k)

        @pl.when(k > 0)
        def _():
            scores_plane.pair(k - 1)
            mixed_sum.pair(k - 1)

        scores_plane.hold()
        mixed_sum.hold()

    scores_plane.pair(3)
    mixed_sum.pair(3)
    hid_plane.finish()
    upd_plane.finish()
    out_sum = LineSum(net, r.go, r.go_got, r.grad_out)
    attn_sum = LineSum(net, r.ga, r.ga_got, r.ga_sum)

    @pl.loop(0, 4)
    def _(t):
        cols = cols_at(t, 256)
        grad = rows_dot(
            r.gated[...].reshape(tokens, 256), r.hid_all[:, :, cols].reshape(tokens, 256)
        ).astype(LOW)
        for zz in range(4):
            r.go[zz, :, cols] = grad[zz * 64 : (zz + 1) * 64]

    out_sum.start()

    def attn_grad(zz):
        cols = cols_at(zz, 256)
        r.ga[zz, :, 0:256] = rows_dot(
            r.normed_all[:, :, cols].reshape(tokens, 256), r.value_back[...].reshape(tokens, 256)
        ).astype(LOW)
        r.ga[zz, :, 256:768] = rows_dot(
            r.mixed_all[:, :, cols].reshape(tokens, 256), r.mixture_back[...].reshape(tokens, 512)
        ).astype(LOW)

    attn_sum.run(attn_grad)

    mixed_sum.settle()
    normed_sum = PlaneSum(net, r.part, r.got_c, r.sent_c, r.far_c, r.hidden_pre, r.pairs, r.work)

    def normed_blocks(k):
        normed = cols_dot(rows_of(r.value_back, k), weights_a(0, 256))
        r.pairs[...] = normed.reshape(2, ROWS, WIDE)

    normed_sum.run(normed_blocks)

    scores_plane.settle()
    scores_plane.finish()
    grad_weights = r.scores_sum[...]
    zeta_own_pre = r.zeta_pre[me]
    zeta = silu(zeta_own_pre)
    query_low, key_low, probs = block_scores_of(zeta, r.heads, shift, r.table)
    grad_scores = (probs * (grad_weights - jnp.sum(probs * grad_weights, axis=-1, keepdims=True))).astype(LOW)
    scale = zeta.shape[1] ** (-0.5)
    grad_query = jnp.dot(grad_scores, key_low, preferred_element_type=F32) * scale
    grad_key = rows_dot(grad_scores, query_low) * scale
    skewed = pltpu.roll(
        jnp.dot(grad_scores, mirror_matrix(ROWS), preferred_element_type=F32), 1, 1, stride=1, stride_axis=0
    )
    r.sums[37:40] = jnp.zeros((3, WIDE), F32)
    r.sums[37:38, 0:128] = jnp.sum(grad_query * zeta, axis=0, keepdims=True)
    r.sums[37:38, 128:256] = jnp.sum(grad_key * zeta, axis=0, keepdims=True)
    r.sums[37:38, 256:384] = jnp.sum(grad_query, axis=0, keepdims=True)
    r.sums[37:38, 384:512] = jnp.sum(skewed, axis=0, keepdims=True)
    grad_zeta = grad_query * r.heads[0:1] + grad_key * r.heads[1:2]
    r.zeta_own[...] = (grad_zeta * silu_slope(zeta_own_pre)).astype(LOW)
    zeta_tokens = spread_plane(net, r.zeta_own, r.zeta_all)

    mixed_sum.finish()
    grad_mixed = r.grad_two[...] + cols_dot(r.zeta_own[...], zeta_weights())
    pull = grad_mixed * silu_slope(r.pre[...])
    lanes_to_rows(pull, r.tall)
    r.pre[...] = pull
    out_sum.relay()
    attn_sum.relay()
    ema_backward(r.fac, r.gain, r.nrm, r.tall, r.fac_sum, r.gain_sum, r.tall_out)
    for s in range(8):
        cols = slice(s * 128, (s + 1) * 128)
        r.sums[0:16, cols] = r.fac_sum[:, s, :]
        r.sums[16:32, cols] = r.gain_sum[:, s, :]
        r.sums[33:34, cols] = jnp.sum(r.pre[:, cols] * r.nrm[:, s, :], axis=0, keepdims=True)
    normed_sum.settle()
    normed_sum.finish()
    for s in range(8):
        cols = slice(s * 128, (s + 1) * 128)
        r.hidden_pre[:, cols] = r.hidden_pre[:, cols] + r.pre[:, cols] * r.prm[65:66, cols] + r.tall_out[:, s, :]
    xhat_one, inverse_one = standardized(r.x[...].astype(F32))
    grad_one = r.hidden_pre[...]
    put_rows(r.sums, 32, grad_one * xhat_one)
    put_rows(r.sums, 35, grad_one)
    r.grad_inputs[...] = r.grad_inputs[...] + norm_back(grad_one, xhat_one, inverse_one, r.prm[64:65])

    for s in range(8):
        r.sum_blocks[s] = r.sums[:, s * 128 : (s + 1) * 128]
    small_sum = swap_plane(net, r.sum_blocks, r.sum_parts)
    branch_sum.send()
    reduce_sum.finish()
    expand_sum.finish()
    ge_plane = swap_plane(net, r.ge_sum, r.ge_all)
    small_sum.finish()
    whole = r.sum_parts[0]
    for s in range(1, 8):
        whole = whole + r.sum_parts[s]
    r.sum_rows[z] = whole
    small_rows = spread_line(net, r.sum_rows)
    zeta_tokens.finish()
    r.gz[...] = rows_dot(
        r.mixed_all[...].reshape(tokens, WIDE), r.zeta_all[...].reshape(tokens, 128)
    ).reshape(4, 8, 32, 128)
    for zz in range(4):
        r.gz_own[zz] = r.gz[zz, me]
    zeta_grad = swap_line(net, r.gz_own, r.gz_line)
    out_sum.finish()
    attn_sum.finish()
    ga_plane = swap_plane(net, r.ga_sum, r.ga_all)
    branch_sum.finish()
    stream = r.x[...].astype(F32)
    first = r.first[...]
    branch = r.branch[...]
    attn_branch = first - stream
    r.output[...] = ((first + branch) * valid).astype(LOW)
    r.square_own[...] = jnp.zeros((8, 128), F32)
    for k, item in enumerate((stream, attn_branch, branch)):
        squares = jnp.sum(valid * item * item, axis=0, keepdims=True)
        r.square_own[k : k + 1] = jnp.broadcast_to(jnp.sum(squares, axis=1, keepdims=True), (1, 128))
    r.square_own[3:4] = jnp.broadcast_to(jnp.sum(valid, axis=0, keepdims=True), (1, 128))
    square_plane = spread_plane(net, r.square_own, r.square_all)
    small_rows.finish()
    r.sum_cols[...] = (r.sum_rows[0] + r.sum_rows[1]) + (r.sum_rows[2] + r.sum_rows[3])
    small_cols = spread_plane(net, r.sum_cols, r.sums_all)
    square_plane.finish()
    squares = r.square_all[0]
    for s in range(1, 8):
        squares = squares + r.square_all[s]
    r.square_line[z] = squares
    square_rows = spread_line(net, r.square_line)
    ge_plane.finish()
    zeta_grad.finish()
    ga_plane.finish()
    small_cols.finish()
    square_rows.finish()


def layer(*operands):
    return pl.pallas_call(
        layer_kernel,
        name="layer",
        out_shape=[jax.ShapeDtypeStruct(*item) for item in fields(Results).values()],
        in_specs=list(fields(Inputs).values()),
        out_specs=[VMEM] * len(fields(Results)),
        scratch_shapes=[pltpu.VMEM(*item) for item in fields(Scratch).values()]
        + [pltpu.SemaphoreType.DMA(item) for item in fields(Lines).values()],
        compiler_params=pltpu.CompilerParams(
            collective_id=1, has_side_effects=True, vmem_limit_bytes=60 << 20
        ),
    )(*operands)


def place_halves(blocks, base, q, out, start):
    lane = lax.broadcasted_iota(jnp.int32, (blocks.shape[1], 128), 1)
    for zz in range(4):
        at = base + (zz // 2) * 128
        left = blocks[2 * q, :, at : at + 128].astype(F32)
        right = blocks[2 * q + 1, :, at : at + 128].astype(F32)
        if zz % 2:
            left = pltpu.roll(left, 64, 1)
        else:
            right = pltpu.roll(right, 64, 1)
        to = start + (zz * 4 + q) * 128
        out[:, to : to + 128] = jnp.where(lane < 64, left, right)


def outputs_kernel(
    output, grad_inputs, grad_out, grad_reduce, ge_all, ga_all, gz_line, sums_all, square_line, ema,
    output_o, grad_inputs_o, values_o, mix_o, out_o, expand_o, reduce_o, ema_o, gains_o, biases_o, heads_o,
    shift_o, position_o, rms_o, turned,
):
    output_o[...] = output[...]
    grad_inputs_o[...] = grad_inputs[...]
    out_o[...] = grad_out[...]
    reduce_o[...] = grad_reduce[...]
    for s in range(8):
        for zz in range(4):
            at = (zz * 8 + s) * 128
            expand_o[:, at : at + 128] = ge_all[s, :, zz * 128 : (zz + 1) * 128].astype(F32)
        mix_o[:, s * 128 : (s + 1) * 128] = ga_all[s, :, 256:384].astype(F32)
        mix_o[:, 3200 + s * 128 : 3328 + s * 128] = ga_all[s, :, 640:768].astype(F32)
    mix_o[:, 1024:1152] = (gz_line[0] + gz_line[1]) + (gz_line[2] + gz_line[3])
    for q in range(4):
        place_halves(ga_all, 0, q, values_o, 0)
        place_halves(ga_all, 384, q, mix_o, 1152)
    mine = sums_all[lax.axis_index("dp")]
    mine = pltpu.roll(mine, (128 - 32 * lax.axis_index("fsdp")) % 128, 1)
    turned[0:40] = mine
    turned[40:128] = jnp.zeros((88, 128), F32)
    gains_o[...] = turned[32:35, 0:32]
    biases_o[...] = turned[35:37, 0:32]
    flipped = turned[...].T
    raw = ema[...].astype(F32)
    damping = jax.nn.sigmoid(raw[:, 0:16])
    mixing = jax.nn.sigmoid(raw[:, 16:32])
    expand = raw[:, 32:48]
    project = raw[:, 48:64]
    by_factor = flipped[0:32, 0:16] * (0.25 * project * mixing * expand)
    by_gain = flipped[0:32, 16:32]
    by_inflow = 0.25 * project * by_gain
    ema_o[:, 0:16] = -by_factor * mixing * damping * (1.0 - damping)
    ema_o[:, 16:32] = (by_inflow * expand - by_factor * damping) * mixing * (1.0 - mixing)
    ema_o[:, 32:48] = by_inflow * mixing
    ema_o[:, 48:64] = 0.25 * mixing * expand * by_gain
    heads_o[0:1] = sums_all[0, 37:38]
    heads_o[1:2] = sums_all[1, 37:38]
    shift_o[...] = sums_all[2, 37]
    position_o[...] = sums_all[3, 37]
    squares = (square_line[0] + square_line[1]) + (square_line[2] + square_line[3])
    roots = jnp.sqrt(squares / (squares[3:4] * WIDE))
    col = lax.broadcasted_iota(jnp.int32, (1, 128), 1)
    line = jnp.where(col == 0, roots[0:1], jnp.where(col == 1, roots[1:2], roots[2:3]))
    rms_o[...] = line


def outputs(parts, ema_params):
    shapes = (
        ((ROWS, WIDE), LOW), ((ROWS, WIDE), F32), ((32, 2048), F32), ((32, 4224), F32), ((64, WIDE), F32),
        ((32, 4096), F32), ((ROWS, WIDE), F32), ((32, 64), F32), ((3, 32), F32), ((2, 32), F32), ((2, 128), F32),
        ((128,), F32), ((128,), F32), ((1, 128), F32),
    )
    return pl.pallas_call(
        outputs_kernel,
        name="outputs",
        out_shape=[jax.ShapeDtypeStruct(shape, dtype) for shape, dtype in shapes],
        in_specs=[VMEM] * 10,
        out_specs=[VMEM] * len(shapes),
        scratch_shapes=[pltpu.VMEM((128, 128), F32)],
    )(*parts, ema_params)


def on_plane(
    inputs, lengths, w_values, w_mix, w_out, w_expand, w_reduce, ema_params,
    norm_gains, norm_biases, head_gains, query_bias, position_bias, cotangent,
):
    consts = jnp.concatenate([head_gains, query_bias[None], position_bias[None]])
    parts = layer(
        inputs, cotangent, w_values, w_mix, w_out, w_expand, w_reduce, ema_params, norm_gains, norm_biases,
        consts, lengths,
    )
    done = outputs(parts, ema_params)
    return (*done[:13], done[13][0, :3])


def layer_norm(value, gain, shift):
    centre = jnp.mean(value, axis=-1, keepdims=True)
    centered = value - centre
    spread = jnp.mean(centered * centered, axis=-1, keepdims=True)
    return centered * lax.rsqrt(spread + EPS) * gain + shift


def ema_mix(normed, keep, ema_params):
    count = ema_params.shape[1] // 4
    damping = jax.nn.sigmoid(ema_params[:, :count]).T
    mixing = jax.nn.sigmoid(ema_params[:, count : 2 * count]).T
    expand = ema_params[:, 2 * count : 3 * count].T
    project = ema_params[:, 3 * count :].T
    factor = 1.0 - mixing * damping
    inflow = mixing * expand

    def advance(state, item):
        column, flag = item
        state = factor * state * flag[:, None, None] + inflow * column[:, None, :]
        return (state, 0.25 * jnp.sum(project * state, axis=1))

    start = jnp.zeros((normed.shape[0], count, normed.shape[2]), jnp.float32)
    _, smooth = lax.scan(advance, start, (jnp.swapaxes(normed, 0, 1), jnp.swapaxes(keep, 0, 1)))
    return jnp.swapaxes(smooth, 0, 1)


def layout(lengths, rows):
    ends = jnp.cumsum(lengths, axis=1)
    starts = ends - lengths
    place = lax.broadcasted_iota(jnp.int32, (lengths.shape[0], rows), 1)
    begin = jnp.any(place[:, :, None] == starts[:, None, :], axis=2) | (place == ends)
    keep = jnp.where(begin, 0.0, 1.0).astype(jnp.float32)
    valid = jnp.where(place < ends, 1.0, 0.0).astype(jnp.float32)
    return (keep, valid)


def dot_rows(left, right):
    return lax.dot_general(
        left, right, (((0,), (0,)), ((), ())), preferred_element_type=jnp.float32
    )


def dot_cols(left, right):
    return lax.dot_general(
        left, right, (((1,), (1,)), ((), ())), preferred_element_type=jnp.float32
    )


def block_scores(query_low, key_low, position, scale):
    span = query_low.shape[1]
    row = lax.broadcasted_iota(jnp.int32, (span, span), 0)
    col = lax.broadcasted_iota(jnp.int32, (span, span), 1)
    table = position[jnp.clip(row - col, 0, span - 1)]
    scores = (
        jnp.einsum("kiz,kjz->kij", query_low, key_low, preferred_element_type=jnp.float32) * scale
        + table
    )
    return jnp.where(row >= col, scores, NEG)


def diagonal_sums(grid):
    size = grid.shape[0]
    flipped = grid[:, ::-1]
    padded = jnp.pad(flipped, ((0, 0), (0, size)))
    skewed = padded.reshape(-1)[: size * (2 * size - 1)].reshape(size, 2 * size - 1)
    return jnp.sum(skewed, axis=0)[size - 1 :]


def group_rows(value):
    return lax.all_gather(value, "fsdp", axis=0, tiled=True)


def group_total(value):
    return lax.psum_scatter(value, "fsdp", scatter_dimension=0, tiled=True)


def owner_layout(grad, owners):
    return grad.reshape(owners * 8, -1)


def owner_shard(piece, columns):
    return piece.reshape(-1, columns)


def on_device(
    inputs,
    lengths,
    w_values,
    w_mix,
    w_out,
    w_expand,
    w_reduce,
    ema_params,
    norm_gains,
    norm_biases,
    head_gains,
    query_bias,
    position_bias,
    cotangent,
):
    rows, width = inputs.shape
    span = position_bias.shape[0]
    blocks = rows // span
    key_width = head_gains.shape[1]
    scale = key_width ** (-0.5)
    keep, valid = layout(lengths, rows)
    mask = valid[0][:, None]
    gathered = (
        lax.all_gather(w_values, ("dp", "fsdp"), axis=0, tiled=True),
        lax.all_gather(w_mix, ("dp", "fsdp"), axis=0, tiled=True),
        lax.all_gather(w_out, ("dp", "fsdp"), axis=0, tiled=True),
        lax.all_gather(ema_params, ("dp", "fsdp"), axis=0, tiled=True),
        lax.all_gather(norm_gains, ("dp", "fsdp"), axis=1, tiled=True),
        lax.all_gather(norm_biases, ("dp", "fsdp"), axis=1, tiled=True),
    )
    values_full, mix_full, out_full, ema_full, gains_full, biases_full = gathered
    value_width = values_full.shape[1]
    group_size = lax.axis_size("fsdp")
    data_size = lax.axis_size("dp")
    owners = group_size * data_size
    shard_rows = w_expand.shape[0]
    hidden_units = w_expand.shape[1]
    unit_block = hidden_units // (group_size * data_size)
    pieces = w_expand.reshape(shard_rows, data_size, group_size, unit_block)
    swapped = lax.all_to_all(pieces, "fsdp", split_axis=2, concat_axis=0, tiled=True)
    expand_quarter, reduce_use = (
        lax.all_gather(swapped, "dp", axis=0, tiled=True),
        lax.all_gather(w_reduce, "dp", axis=0, tiled=True),
    )
    expand_use = expand_quarter.reshape(expand_quarter.shape[0], data_size * unit_block)
    gains_f = gains_full.astype(jnp.float32)
    biases_f = biases_full.astype(jnp.float32)
    heads_f = head_gains.astype(jnp.float32)
    query_shift = query_bias.astype(jnp.float32)
    position_f = position_bias.astype(jnp.float32)
    stream = inputs.astype(jnp.float32)

    def front(source, gain, shift, omega, params):
        normed_part = layer_norm(source, gain, shift)
        smooth = ema_mix(normed_part[None], keep, params)[0]
        return (normed_part, silu(smooth + omega * normed_part))

    (normed, mixed), front_back = jax.vjp(
        front, stream, gains_f[0], biases_f[0], gains_f[1], ema_full.astype(jnp.float32)
    )
    normed_low = normed.astype(jnp.bfloat16)
    mixed_low = mixed.astype(jnp.bfloat16)
    value_pre = jnp.dot(normed_low, values_full, preferred_element_type=jnp.float32)
    value_low = silu(value_pre).astype(jnp.bfloat16)
    mixture = jnp.dot(mixed_low, mix_full, preferred_element_type=jnp.float32)
    middle = width + key_width
    upper = middle + value_width
    update = jax.nn.sigmoid(mixture[:, :width])
    zeta_pre = mixture[:, width:middle]
    zeta = silu(zeta_pre)
    reset_pre = mixture[:, middle:upper]
    reset = silu(reset_pre)
    candidate = mixture[:, upper:]
    query_low = (
        (zeta * heads_f[0] + query_shift).astype(jnp.bfloat16).reshape(blocks, span, key_width)
    )
    key_low = (zeta * heads_f[1]).astype(jnp.bfloat16).reshape(blocks, span, key_width)
    value_blocks = value_low.reshape(blocks, span, value_width)
    scores = block_scores(query_low, key_low, position_f, scale)
    log_total = jax.nn.logsumexp(scores, axis=-1, keepdims=True)
    weights_low = jnp.exp(scores - log_total).astype(jnp.bfloat16)
    attended = jnp.einsum(
        "kij,kjv->kiv", weights_low, value_blocks, preferred_element_type=jnp.float32
    ).reshape(rows, value_width)
    gated_low = (attended * reset).astype(jnp.bfloat16)
    hidden_pre = candidate + jnp.dot(gated_low, out_full, preferred_element_type=jnp.float32)
    hidden = silu(hidden_pre)
    attn_branch = update * (hidden - stream)
    first = stream + attn_branch
    normed_two, norm_back = jax.vjp(layer_norm, first, gains_f[2], biases_f[1])
    normed_two_low = normed_two.astype(jnp.bfloat16)
    ffn_rows = group_rows(normed_two_low)
    expand_pre = jnp.dot(ffn_rows, expand_use, preferred_element_type=jnp.float32)
    expand_low = silu(expand_pre).astype(jnp.bfloat16)
    branch_part = jnp.dot(expand_low, reduce_use, preferred_element_type=jnp.float32)
    branch = group_total(branch_part)
    output = ((first + branch) * mask).astype(jnp.bfloat16)
    values_back, mix_back, out_back = (
        lax.all_gather(w_values, ("dp", "fsdp"), axis=0, tiled=True),
        lax.all_gather(w_mix, ("dp", "fsdp"), axis=0, tiled=True),
        lax.all_gather(w_out, ("dp", "fsdp"), axis=0, tiled=True),
    )
    grad_out = cotangent.astype(jnp.float32) * mask
    grad_branch = grad_out.astype(jnp.bfloat16)
    grad_rows = group_rows(grad_branch)
    grad_reduce = dot_rows(expand_low, grad_rows)
    grad_expand_out = dot_cols(grad_rows, reduce_use)
    grad_expand_pre = (grad_expand_out * silu_slope(expand_pre)).astype(jnp.bfloat16)
    grad_expand = dot_rows(ffn_rows, grad_expand_pre)
    normed_two_part = dot_cols(grad_expand_pre, expand_use)
    grad_normed_two = group_total(normed_two_part)
    grad_first_norm, grad_gain_two, grad_shift_two = norm_back(grad_normed_two)
    grad_first = grad_out + grad_first_norm
    grad_direct = grad_first * (1.0 - update)
    grad_update = grad_first * (hidden - stream)
    grad_hidden_pre = grad_first * update * silu_slope(hidden_pre)
    grad_hidden_low = grad_hidden_pre.astype(jnp.bfloat16)
    grad_out_proj = dot_rows(gated_low, grad_hidden_low)
    grad_gated = dot_cols(grad_hidden_low, out_back)
    grad_attended = (grad_gated * reset).astype(jnp.bfloat16).reshape(blocks, span, value_width)
    grad_reset = grad_gated * attended
    scores_again = block_scores(query_low, key_low, position_f, scale)
    probs = jnp.exp(scores_again - log_total)
    probs_low = probs.astype(jnp.bfloat16)
    grad_weights = jnp.einsum(
        "kiv,kjv->kij", grad_attended, value_blocks, preferred_element_type=jnp.float32
    )
    grad_value = jnp.einsum(
        "kij,kiv->kjv", probs_low, grad_attended, preferred_element_type=jnp.float32
    ).reshape(rows, value_width)
    inner = jnp.sum(probs * grad_weights, axis=-1, keepdims=True)
    grad_scores = (probs * (grad_weights - inner)).astype(jnp.bfloat16)
    grad_position = diagonal_sums(jnp.sum(grad_scores.astype(jnp.float32), axis=0))
    grad_query = (
        jnp.einsum(
            "kij,kjz->kiz", grad_scores, key_low, preferred_element_type=jnp.float32
        ).reshape(rows, key_width)
        * scale
    )
    grad_key = (
        jnp.einsum(
            "kij,kiz->kjz", grad_scores, query_low, preferred_element_type=jnp.float32
        ).reshape(rows, key_width)
        * scale
    )
    grad_value_pre = (grad_value * silu_slope(value_pre)).astype(jnp.bfloat16)
    grad_values = dot_rows(normed_low, grad_value_pre)
    grad_normed = dot_cols(grad_value_pre, values_back)
    grad_zeta = grad_query * heads_f[0] + grad_key * heads_f[1]
    grad_heads = jnp.stack([jnp.sum(grad_query * zeta, axis=0), jnp.sum(grad_key * zeta, axis=0)])
    grad_query_shift = jnp.sum(grad_query, axis=0)
    grad_mixture = jnp.concatenate(
        [
            grad_update * update * (1.0 - update),
            grad_zeta * silu_slope(zeta_pre),
            grad_reset * silu_slope(reset_pre),
            grad_hidden_pre,
        ],
        axis=1,
    ).astype(jnp.bfloat16)
    grad_mix = dot_rows(mixed_low, grad_mixture)
    grad_mixed = dot_cols(grad_mixture, mix_back)
    grad_source, grad_gain_one, grad_shift_one, grad_omega, grad_ema = front_back(
        (grad_normed, grad_mixed)
    )
    grad_inputs = grad_direct + grad_source
    grad_gains = jnp.stack([grad_gain_one, grad_omega, grad_gain_two])
    grad_shifts = jnp.stack([grad_shift_one, grad_shift_two])
    summed_expand, grad_reduce_dev = (
        lax.psum_scatter(grad_expand, "dp", scatter_dimension=0, tiled=True),
        lax.psum_scatter(grad_reduce, "dp", scatter_dimension=0, tiled=True),
    )
    summed_pieces = summed_expand.reshape(group_size * shard_rows, data_size, 1, unit_block)
    owned = lax.all_to_all(summed_pieces, "fsdp", split_axis=0, concat_axis=2, tiled=True)
    grad_expand_dev = owned.reshape(shard_rows, hidden_units)
    summed_block = (
        lax.psum_scatter(
            owner_layout(grad_values, owners), ("dp", "fsdp"), scatter_dimension=0, tiled=True
        ),
        lax.psum_scatter(
            owner_layout(grad_mix, owners), ("dp", "fsdp"), scatter_dimension=0, tiled=True
        ),
        lax.psum_scatter(grad_out_proj, ("dp", "fsdp"), scatter_dimension=0, tiled=True),
        lax.psum_scatter(
            owner_layout(grad_ema, owners), ("dp", "fsdp"), scatter_dimension=0, tiled=True
        ),
        lax.psum_scatter(grad_gains, ("dp", "fsdp"), scatter_dimension=1, tiled=True),
        lax.psum_scatter(grad_shifts, ("dp", "fsdp"), scatter_dimension=1, tiled=True),
    )
    values_flat, mix_flat, grad_out_dev, ema_flat, grad_gains_dev, grad_shifts_dev = summed_block
    grad_values_dev = owner_shard(values_flat, grad_values.shape[1])
    grad_mix_dev = owner_shard(mix_flat, grad_mix.shape[1])
    grad_ema_dev = owner_shard(ema_flat, grad_ema.shape[1])
    squares = jnp.stack(
        [
            jnp.sum(mask * stream * stream),
            jnp.sum(mask * attn_branch * attn_branch),
            jnp.sum(mask * branch * branch),
        ]
    )
    square_sums, tokens_seen, heads_total, shift_total, position_total = lax.psum(
        (squares, jnp.sum(valid), grad_heads, grad_query_shift, grad_position), ("dp", "fsdp")
    )
    rms = jnp.sqrt(square_sums / (tokens_seen * width))
    return (
        output,
        grad_inputs,
        grad_values_dev,
        grad_mix_dev,
        grad_out_dev,
        grad_expand_dev,
        grad_reduce_dev,
        grad_ema_dev,
        grad_gains_dev,
        grad_shifts_dev,
        heads_total,
        shift_total,
        position_total,
        rms,
    )


def solution(mesh):
    in_specs = (
        P(("dp", "fsdp"), None),
        P(("dp", "fsdp"), None),
        P(("dp", "fsdp"), None),
        P(("dp", "fsdp"), None),
        P(("dp", "fsdp"), None),
        P(("dp", "fsdp"), None),
        P(("dp", "fsdp"), None),
        P(("dp", "fsdp"), None),
        P(None, ("dp", "fsdp")),
        P(None, ("dp", "fsdp")),
        P(),
        P(),
        P(),
        P(("dp", "fsdp"), None),
    )
    out_specs = (
        P(("dp", "fsdp"), None),
        P(("dp", "fsdp"), None),
        P(("dp", "fsdp"), None),
        P(("dp", "fsdp"), None),
        P(("dp", "fsdp"), None),
        P(("dp", "fsdp"), None),
        P(("dp", "fsdp"), None),
        P(("dp", "fsdp"), None),
        P(None, ("dp", "fsdp")),
        P(None, ("dp", "fsdp")),
        P(),
        P(),
        P(),
        P(),
    )
    planes = mesh.shape["dp"] == 8 and mesh.shape["fsdp"] == 4
    return jax.shard_map(
        on_plane if planes else on_device, mesh=mesh, in_specs=in_specs, out_specs=out_specs, check_vma=False
    )
```

```python
import jax
import jax.numpy as jnp
from jax import lax
from jax.experimental import pallas as pl
from jax.experimental.pallas import tpu as pltpu
from jax.sharding import PartitionSpec as P

EPS = 1e-05
NEG = -1e30
F32 = jnp.float32
LOW = jnp.bfloat16
MESH = pl.DeviceIdType.MESH
LINES = 128
STATES = 16


def silu(value):
    return value * jax.nn.sigmoid(value)


def silu_slope(value):
    sigma = jax.nn.sigmoid(value)
    return sigma * (1.0 + value * (1.0 - sigma))


def here():
    dp = lax.axis_index("dp")
    f = lax.axis_index("fsdp")
    return dp // 2, dp % 2, f // 2, f % 2


def device(z, y, x, c):
    return (z * 2 + y, x * 2 + c)


def slot_of(y, x, c):
    return y * 4 + x * 2 + c


def plane_peers(y, x, c):
    peers = []
    for mask in range(1, 8):
        peers.append(
            (
                1 - y if mask & 4 else y,
                1 - x if mask & 2 else x,
                1 - c if mask & 1 else c,
            )
        )
    return peers


def line_peers(z):
    return [z + 1 - 2 * (z % 2), 3 - z, (z + 2) % 4]


def greet(across=True):
    z, y, x, c = here()
    barrier = pltpu.get_barrier_semaphore()
    count = 7
    for peer in plane_peers(y, x, c):
        pl.semaphore_signal(barrier, inc=1, device_id=device(z, *peer), device_id_type=MESH)
    if across:
        count = 10
        for other in line_peers(z):
            pl.semaphore_signal(barrier, inc=1, device_id=device(other, y, x, c), device_id_type=MESH)
    pl.semaphore_wait(barrier, count)


class Net:
    def __init__(self, send, recv):
        self.send = send
        self.recv = recv
        self.used = 0

    def take(self, count):
        self.used += count
        assert self.used <= LINES
        return self.used - count

    def make(self, line, src, dst, target):
        return pltpu.make_async_remote_copy(
            src_ref=src,
            dst_ref=dst,
            send_sem=self.send.at[line],
            recv_sem=self.recv.at[line],
            device_id=target,
            device_id_type=MESH,
        )

    def copy(self, src, dst, target):
        made = self.make(self.take(1), src, dst, target)
        made.start()
        return made


VMEM = pl.BlockSpec(memory_space=pltpu.VMEM)


def rows_dot(left, right):
    return lax.dot_general(left, right, (((0,), (0,)), ((), ())), preferred_element_type=F32)


def cols_dot(left, right):
    return lax.dot_general(left, right, (((1,), (1,)), ((), ())), preferred_element_type=F32)


def lanes_to_rows(wide, tall):
    for s in range(8):
        tall[:, s, :] = wide[:, s * 128 : (s + 1) * 128]


def pick_halves(arr, base, slot, pair):
    one = base + ((2 * pair * 8 + slot) // 2) * 128
    two = base + (((2 * pair + 1) * 8 + slot) // 2) * 128
    left = arr[:, one : one + 128].astype(F32)
    right = arr[:, two : two + 128].astype(F32)
    lane = lax.broadcasted_iota(jnp.int32, left.shape, 1)
    if slot % 2 == 0:
        return jnp.where(lane < 64, left, pltpu.roll(right, 64, 1)).astype(LOW)
    return jnp.where(lane < 64, pltpu.roll(left, 64, 1), right).astype(LOW)


def ema_forward(factor, gain, source, out):
    steps = source.shape[0]

    def step(t, states):
        column = source[t]
        new = []
        terms = []
        for j in range(STATES):
            state = factor[j] * states[j] + column
            new.append(state)
            terms.append(gain[j] * state)
        while len(terms) > 1:
            terms = [terms[i] + terms[i + 1] for i in range(0, len(terms), 2)]
        out[t] = terms[0]
        return tuple(new)

    zero = jnp.zeros(source.shape[1:], F32)
    lax.fori_loop(0, steps, step, (zero,) * STATES)


def ema_backward(fac, gain, nrm, pull_ref, factor_sum, gain_sum, out):
    steps = nrm.shape[0]
    zero = jnp.zeros(nrm.shape[1:], F32)
    group = 4
    for base in range(0, STATES, group):

        def step(t, carry):
            at = steps - 1 - t
            column = nrm[at]
            pull = pull_ref[at]
            new = []
            terms = []
            for k in range(group):
                state, slope, by_factor, by_gain = carry[4 * k : 4 * k + 4]
                f = fac[base + k]
                slope = f * slope + state
                state = f * state + pull
                new += [state, slope, by_factor + column * slope, by_gain + column * state]
                terms.append(gain[base + k] * state)
            total = (terms[0] + terms[1]) + (terms[2] + terms[3])
            out[at] = total if base == 0 else out[at] + total
            return tuple(new)

        done = lax.fori_loop(0, steps, step, (zero,) * (4 * group))
        for k in range(group):
            factor_sum[base + k] = done[4 * k + 2]
            gain_sum[base + k] = done[4 * k + 3]


class PlaneGather:
    def __init__(self, net, src, dst):
        z, y, x, c = here()
        self.net, self.src, self.dst = net, src, dst
        self.base = net.take(7)
        self.me = slot_of(y, x, c)

    def near(self, k):
        z, y, x, c = here()
        yy, xx = chip_of(k)
        return self.net.make(self.base + k - 1, self.src, self.dst.at[self.me], device(z, yy, xx, c))

    def twin(self, k):
        z, y, x, c = here()
        yy, xx = chip_of(k)
        block = self.dst.at[slot_of(yy, xx, c)]
        return self.net.make(self.base + 3 + k, block, block, device(z, y, x, 1 - c))

    def start(self, last=True):
        self.dst[self.me] = self.src[...]
        self.twin(0).start()
        for k in (1, 2, 3) if last else (1, 2):
            self.near(k).start()

    def start_last(self):
        self.near(3).start()

    def take_near(self, k):
        self.near(k).wait_recv()
        self.twin(k).start()

    def take_twin(self, k):
        self.twin(k).wait_recv()

    def take_rest(self):
        for k in (1, 2, 3):
            self.take_near(k)
        for k in range(4):
            self.take_twin(k)

    def finish(self):
        for k in (1, 2, 3):
            self.near(k).wait_send()
        for k in range(4):
            self.twin(k).wait_send()


def chip_of(k):
    z, y, x, c = here()
    return (y + k // 2) % 2, (x + k % 2) % 2


class PlaneSum:
    def __init__(self, net, part, got, sent, far, total, pairs, keep):
        self.net = net
        self.part, self.got, self.sent, self.far, self.total = part, got, sent, far, total
        self.pairs, self.keep = pairs, keep
        self.base = net.take(8)

    def inner(self, k):
        z, y, x, c = here()
        return self.net.make(self.base + k, self.part.at[k], self.got.at[k], device(z, y, x, 1 - c))

    def outer(self, k):
        z, y, x, c = here()
        yy, xx = chip_of(k)
        return self.net.make(self.base + 3 + k, self.sent.at[k - 1], self.far.at[k - 1], device(z, yy, xx, c))

    def give(self, k):
        z, y, x, c = here()
        self.part[k] = self.pairs[1 - c].astype(self.part.dtype)
        self.inner(k).start()

    def hold(self):
        z, y, x, c = here()
        self.keep[...] = self.pairs[c]

    def pair(self, k):
        self.inner(k).wait_recv()
        both = self.keep[...] + self.got[k].astype(F32)

        @pl.when(k == 0)
        def _():
            self.total[...] = both

        @pl.when(k > 0)
        def _():
            self.sent[k - 1] = both.astype(self.sent.dtype)

        self.leave(k)

    def leave(self, k):
        @pl.when(k > 0)
        def _():
            self.outer(k).start()

    def run(self, make):
        @pl.loop(0, 4)
        def _(i):
            make(3 - i)
            self.give(3 - i)

            @pl.when(i > 0)
            def _():
                self.pair(4 - i)

            self.hold()

        self.pair(0)

    def settle(self):
        @pl.loop(0, 4)
        def _(k):
            self.inner(k).wait_send()

    def finish(self):
        @pl.loop(1, 4)
        def _(k):
            self.outer(k).wait()
            self.total[...] = self.total[...] + self.far[k - 1].astype(F32)


class RelayedSum(PlaneSum):
    def half(self, h):
        z, y, x, c = here()
        yy, xx = chip_of(1 + h)
        rows = pl.ds(h * 64, 64)
        return self.net.make(
            self.base + 6 + h, self.sent.at[2, rows], self.far.at[2, rows], device(z, yy, xx, c)
        )

    def leave(self, k):
        @pl.when(k == 3)
        def _():
            self.half(0).start()
            self.half(1).start()

    def relay(self):
        for h in range(2):
            self.half(h).wait_recv()
            at = 1 - h
            rows = slice(h * 64, (h + 1) * 64)
            self.sent[at, rows] = (self.sent[at, rows].astype(F32) + self.far[2, rows].astype(F32)).astype(LOW)
            self.outer(at + 1).start()

    def finish(self):
        for k in (1, 2):
            self.half(k - 1).wait_send()
            self.outer(k).wait()
        self.total[...] = self.total[...] + self.far[0].astype(F32) + self.far[1].astype(F32)


class LineGather:
    def __init__(self, net, buf):
        z, y, x, c = here()
        near, mirror, _ = line_peers(z)
        self.inside = z % 3 > 0
        relayed = (2 * z) % 3 + 3 * (z // 3)
        self.first = net.make(net.take(1), buf.at[z], buf.at[z], device(near, y, x, c))
        self.second = net.make(net.take(1), buf.at[z], buf.at[z], device(mirror, y, x, c))
        self.third = net.make(net.take(1), buf.at[relayed], buf.at[relayed], device((3 * z + 2) % 5, y, x, c))

    def start(self):
        self.first.start()
        self.second.start()

        @pl.when(jnp.logical_not(self.inside))
        def _():
            self.third.start()

    def relay(self):
        @pl.when(self.inside)
        def _():
            self.second.wait_recv()
            self.third.start()

    def finish(self):
        self.first.wait()
        self.second.wait_send()

        @pl.when(jnp.logical_not(self.inside))
        def _():
            self.second.wait_recv()

        self.third.wait()


class LineSum:
    def __init__(self, net, buf, got, out):
        z, y, x, c = here()
        near, mirror, across = line_peers(z)
        self.buf, self.got, self.out = buf, got, out
        self.inside = z % 3 > 0
        self.relayed = (2 * z) % 3 + 3 * (z // 3)
        self.first = net.make(net.take(1), buf.at[across], got.at[0], device((2 * z + 1) % 5, y, x, c))
        self.second = net.make(net.take(1), buf.at[near], got.at[1], device(near, y, x, c))
        self.third = net.make(net.take(1), buf.at[mirror], got.at[2], device(mirror, y, x, c))

    def run(self, make):
        z, y, x, c = here()

        @pl.loop(0, 4)
        def _(i):
            bits = (2 + 3 * i) % 4
            make((z // 2 + bits // 2) % 2 * 2 + (z + bits) % 2)

            @pl.when(i == 0)
            def _():
                self.first.start()

            @pl.when(i == 1)
            def _():
                self.second.start()

        @pl.when(jnp.logical_not(self.inside))
        def _():
            self.third.start()

    def start(self):
        self.first.start()
        self.second.start()

        @pl.when(jnp.logical_not(self.inside))
        def _():
            self.third.start()

    def relay(self):
        @pl.when(self.inside)
        def _():
            self.first.wait_recv()
            self.buf[self.relayed] = (self.buf[self.relayed].astype(F32) + self.got[0].astype(F32)).astype(LOW)
            self.third.start()

    def finish(self):
        z, y, x, c = here()
        self.first.wait_send()
        self.second.wait()
        self.third.wait()
        total = self.buf[z].astype(F32) + self.got[1].astype(F32) + self.got[2].astype(F32)
        self.out[...] = total.reshape(self.out.shape).astype(self.out.dtype)

        @pl.when(jnp.logical_not(self.inside))
        def _():
            self.first.wait_recv()
            whole = total + self.got[0].astype(F32)
            self.out[...] = whole.reshape(self.out.shape).astype(self.out.dtype)


class Spread:
    def __init__(self, net, sends, whole):
        self.net, self.whole = net, whole
        self.line = net.take(1)
        for src, dst, target in sends:
            net.make(self.line, src, dst, target).start()

    def finish(self):
        pltpu.make_async_copy(self.whole, self.whole, self.net.recv.at[self.line]).wait()
        pltpu.make_async_copy(self.whole, self.whole, self.net.send.at[self.line]).wait()


def spread_plane(net, src, dst):
    z, y, x, c = here()
    me = slot_of(y, x, c)
    dst[me] = src[...]
    sends = [(src, dst.at[me], device(z, *peer)) for peer in plane_peers(y, x, c)]
    return Spread(net, sends, dst.at[pl.ds(0, 7)])


def spread_column(net, buf):
    z, y, x, c = here()
    block = buf.at[:, slot_of(y, x, c)]
    sends = [(block, block, device(z, *peer)) for peer in plane_peers(y, x, c)]
    return Spread(net, sends, buf.at[:, pl.ds(0, 7)])


def swap_plane(net, src, dst):
    z, y, x, c = here()
    me = slot_of(y, x, c)
    dst[me] = src[me]
    sends = [(src.at[slot_of(*peer)], dst.at[me], device(z, *peer)) for peer in plane_peers(y, x, c)]
    return Spread(net, sends, dst.at[pl.ds(0, 7)])


def spread_line(net, buf, part=None):
    z, y, x, c = here()
    block = buf.at[z] if part is None else buf.at[z, part]
    whole = buf.at[pl.ds(0, 3)] if part is None else buf.at[pl.ds(0, 3), part]
    return Spread(net, [(block, block, device(other, y, x, c)) for other in line_peers(z)], whole)


def swap_line(net, src, dst):
    z, y, x, c = here()
    dst[z] = src[z]
    sends = [(src.at[other], dst.at[z], device(other, y, x, c)) for other in line_peers(z)]
    return Spread(net, sends, dst.at[pl.ds(0, 3)])


class ChipSwap:
    def __init__(self, net, src, dst):
        z, y, x, c = here()
        self.net, self.src, self.dst = net, src, dst
        self.me = slot_of(y, x, c)
        self.base = net.take(8)

    def copy(self, k, twin):
        z, y, x, c = here()
        yy, xx = chip_of(k)
        cc = (c + twin) % 2
        return self.net.make(
            self.base + 2 * k + twin, self.src.at[slot_of(yy, xx, cc)], self.dst.at[self.me], device(z, yy, xx, cc)
        )

    def start(self):
        self.dst[self.me] = self.src[self.me]
        self.copy(0, 1).start()
        for k in (1, 2, 3):
            for twin in range(2):
                self.copy(k, twin).start()

    def take(self, k):
        self.copy(k, 1).wait_recv()

        @pl.when(k > 0)
        def _():
            self.copy(k, 0).wait_recv()

    def finish(self):
        self.copy(0, 1).wait_send()
        for k in (1, 2, 3):
            for twin in range(2):
                self.copy(k, twin).wait_send()


def row_mean(value):
    return jnp.mean(value, axis=-1, keepdims=True)


def standardized(value):
    centred = value - row_mean(value)
    inverse = lax.rsqrt(row_mean(centred * centred) + EPS)
    return centred * inverse, inverse


def norm_back(grad, xhat, inverse, gain):
    scaled = grad * gain
    return inverse * (scaled - row_mean(scaled) - xhat * row_mean(scaled * xhat))


def block_scores_of(zeta, heads, shift, table):
    query_low = (zeta * heads[0:1] + shift).astype(LOW)
    key_low = (zeta * heads[1:2]).astype(LOW)
    scores = cols_dot(query_low, key_low) * (zeta.shape[1] ** (-0.5)) + table[...]
    row = lax.broadcasted_iota(jnp.int32, scores.shape, 0)
    col = lax.broadcasted_iota(jnp.int32, scores.shape, 1)
    scores = jnp.where(row >= col, scores, NEG)
    top = jnp.max(scores, axis=-1, keepdims=True)
    log_total = top + jnp.log(jnp.sum(jnp.exp(scores - top), axis=-1, keepdims=True))
    return query_low, key_low, jnp.exp(scores - log_total)


def mirror_matrix(size):
    row = lax.broadcasted_iota(jnp.int32, (size, size), 0)
    col = lax.broadcasted_iota(jnp.int32, (size, size), 1)
    return jnp.where(row + col == size - 1, 1.0, 0.0).astype(LOW)


def column_of(line):
    size = line.shape[1]
    row = lax.broadcasted_iota(jnp.int32, (size, size), 0)
    col = lax.broadcasted_iota(jnp.int32, (size, size), 1)
    return jnp.sum(jnp.where(row == col, line, 0.0), axis=1, keepdims=True)


def cols_at(index, size):
    return pl.ds(pl.multiple_of(index * size, size), size)


def put_rows(sums, at, wide):
    sums[at : at + 1] = jnp.sum(wide, axis=0, keepdims=True)


ROWS = 128
WIDE = 1024
ALL = (8, ROWS, WIDE)
OWN = (ROWS, WIDE)


ANY = pl.BlockSpec(memory_space=pl.ANY)


class Inputs:
    x_in = ANY
    cot_in = ANY
    wv_in = ANY
    wm_in = ANY
    wo_in = ANY
    we_in = ANY
    wr_in = ANY
    ema = VMEM
    norm_gains = VMEM
    norm_biases = VMEM
    consts = VMEM
    lens = pl.BlockSpec(memory_space=pltpu.SMEM)


class Results:
    output = (ROWS, WIDE), LOW
    grad_inputs = (ROWS, WIDE), F32
    grad_out = (64, WIDE), F32
    grad_reduce = (ROWS, WIDE), F32
    ge_all = (8, 32, 512), LOW
    ga_all = (8, 32, 768), LOW
    gz_line = (4, 32, 128), F32
    sums_all = (8, 40, 128), F32
    square_line = (4, 8, 128), F32


class Scratch:
    x = OWN, LOW
    cot = OWN, LOW
    wv = (32, 2048), LOW
    wm = (32, 4224), LOW
    we_own = (32, 4096), LOW
    small_wide = (32, 128), F32
    wz = (4, 8, 32, 128), LOW
    inverse = (ROWS, 128), F32
    small_all = (4, 8, 32, 128), LOW
    prm = (72, WIDE), F32
    blocks_a = (8, 32, 768), LOW
    blocks_e = (8, 32, 512), LOW
    wa = (4, 8, 32, 768), LOW
    wo = (4, 64, WIDE), LOW
    we = (4, 8, 32, 512), LOW
    wr = (4, ROWS, WIDE), LOW
    table = (128, 128), F32
    heads = (8, 128), F32
    own_low = OWN, LOW
    normed_all = ALL, LOW
    mixed_all = ALL, LOW
    cot_all = ALL, LOW
    two_all = ALL, LOW
    hid_all = ALL, LOW
    fac = (16, 8, 128), F32
    gain = (16, 8, 128), F32
    fac_sum = (16, 8, 128), F32
    gain_sum = (16, 8, 128), F32
    nrm = (ROWS, 8, 128), F32
    tall = (ROWS, 8, 128), F32
    tall_out = (ROWS, 8, 128), F32
    pre = OWN, F32
    value_pre = (8, ROWS, 256), F32
    value_low = (8, ROWS, 256), LOW
    zeta_pre = (8, ROWS, 128), F32
    weights_low = (8, ROWS, 128), LOW
    attended = (8, ROWS, 256), F32
    reset_pre = (8, ROWS, 256), F32
    gated = (8, ROWS, 256), LOW
    work = OWN, F32
    hidden_pre = OWN, F32
    update_pre = OWN, F32
    first = OWN, F32
    update_part = (8, ROWS, 128), LOW
    update_all = (8, ROWS, 128), LOW
    part = (4, ROWS, WIDE), LOW
    got = (4, ROWS, WIDE), LOW
    sent = (3, ROWS, WIDE), LOW
    far = (3, ROWS, WIDE), LOW
    got_b = (4, ROWS, WIDE), LOW
    sent_b = (3, ROWS, WIDE), LOW
    far_b = (3, ROWS, WIDE), LOW
    got_c = (4, ROWS, WIDE), LOW
    sent_c = (3, ROWS, WIDE), LOW
    far_c = (3, ROWS, WIDE), LOW
    pairs = (2, ROWS, WIDE), F32
    grad_two = OWN, F32
    scores_pairs = (2, ROWS, 128), F32
    scores_keep = (ROWS, 128), F32
    expand_pre = (8, ROWS, 512), F32
    expand_low = (8, ROWS, 512), LOW
    grad_pre = (8, ROWS, 512), LOW
    branch = OWN, F32
    value_back = (8, ROWS, 256), LOW
    mixture_back = (8, ROWS, 512), LOW
    scores_part = (4, ROWS, 128), F32
    scores_got = (4, ROWS, 128), F32
    scores_sent = (3, ROWS, 128), LOW
    scores_far = (3, ROWS, 128), LOW
    scores_sum = (ROWS, 128), F32
    zeta_own = (ROWS, 128), LOW
    zeta_all = (8, ROWS, 128), LOW
    gr = (4, ROWS, WIDE), LOW
    gr_got = (3, ROWS, WIDE), LOW
    ge = (4, 256, 512), LOW
    ge_got = (3, 256, 512), LOW
    ge_sum = (8, 32, 512), LOW
    go = (4, 64, WIDE), LOW
    go_got = (3, 64, WIDE), LOW
    ga = (4, 256, 768), LOW
    ga_got = (3, 256, 768), LOW
    ga_sum = (8, 32, 768), LOW
    gz = (4, 8, 32, 128), F32
    gz_own = (4, 32, 128), F32
    sums = (40, WIDE), F32
    sum_blocks = (8, 40, 128), F32
    sum_parts = (8, 40, 128), F32
    sum_rows = (4, 40, 128), F32
    sum_cols = (40, 128), F32
    square_own = (8, 128), F32
    square_all = (8, 8, 128), F32


class Lines:
    send = (LINES,)
    recv = (LINES,)
    load = (7,)


def fields(group):
    return {name: item for name, item in vars(group).items() if not name.startswith("_")}


class Refs:
    def __init__(self, refs):
        names = [name for group in (Inputs, Results, Scratch, Lines) for name in fields(group)]
        for name, ref in zip(names, refs, strict=True):
            setattr(self, name, ref)


def layer_kernel(*refs):
    r = Refs(refs)
    net = Net(r.send, r.recv)
    z, y, x, c = here()
    me = slot_of(y, x, c)
    twin = device(z, y, x, 1 - c)
    tokens = 8 * ROWS
    loads = [
        pltpu.make_async_copy(src, dst, r.load.at[line])
        for line, (src, dst) in enumerate(
            (
                (r.wm_in, r.wm), (r.wv_in, r.wv), (r.wo_in, r.wo.at[z]), (r.x_in, r.x), (r.we_in, r.we_own),
                (r.wr_in, r.wr.at[z]), (r.cot_in, r.cot),
            )
        )
    ]
    for load in loads:
        load.start()
    greet()
    for load in loads:
        load.wait()

    lane = lax.broadcasted_iota(jnp.int32, (32, 128), 1)
    r.small_wide[...] = jnp.zeros((32, 128), F32)
    r.small_wide[:, 0:64] = r.ema[...].astype(F32)
    small = r.small_wide[...]
    for k in range(5):
        line = r.norm_gains[k : k + 1, :] if k < 3 else r.norm_biases[k - 3 : k - 2, :]
        small = jnp.where(lane == 64 + k, column_of(line.astype(F32)), small)
    r.small_all[z, me] = small.astype(LOW)
    small_line = spread_line(net, r.small_all, me)
    r.wz[z, me] = r.wm[:, 1024:1152]
    zeta_line = spread_line(net, r.wz, me)
    for s in range(8):
        for pair in range(2):
            r.blocks_a[s, :, pair * 128 : (pair + 1) * 128] = pick_halves(r.wv, 0, s, pair)
            r.blocks_a[s, :, 384 + pair * 128 : 512 + pair * 128] = pick_halves(r.wm, 1152, s, pair)
        r.blocks_a[s, :, 256:384] = r.wm[:, s * 128 : (s + 1) * 128]
        r.blocks_a[s, :, 640:768] = r.wm[:, 3200 + s * 128 : 3328 + s * 128]
    attn_plane = swap_plane(net, r.blocks_a, r.wa.at[z])
    out_line = LineGather(net, r.wo)
    out_line.start()
    for s in range(8):
        for zz in range(4):
            r.blocks_e[s, :, zz * 128 : (zz + 1) * 128] = r.we_own[:, (zz * 8 + s) * 128 : (zz * 8 + s + 1) * 128]
    small_line.finish()
    small_plane = spread_column(net, r.small_all)
    near_base = net.take(3)

    def near(k):
        yy, xx = chip_of(k)
        return net.make(near_base + k - 1, r.x, r.mixed_all.at[me], device(z, yy, xx, c))

    for k in (1, 2, 3):
        near(k).start()
    zeta_line.finish()
    zeta_plane = spread_column(net, r.wz)
    expand_plane = swap_plane(net, r.blocks_e, r.we.at[z])
    row = lax.broadcasted_iota(jnp.int32, OWN, 0)
    r.own_low[...] = jnp.where(row < r.lens[0, 0], r.cot[...].astype(F32), 0.0).astype(LOW)
    cot_plane = PlaneGather(net, r.own_low, r.cot_all)
    cot_plane.start()
    r.heads[0:4] = r.consts[...].astype(F32)
    wide = jnp.broadcast_to(r.consts[3:4].astype(F32), (128, 128)).astype(LOW)
    turned = jnp.dot(wide, mirror_matrix(128), preferred_element_type=F32)
    r.table[...] = pltpu.roll(turned, 1, 1, stride=1, stride_axis=0)
    out_line.relay()
    attn_plane.finish()
    attn_line = LineGather(net, r.wa)
    attn_line.start()
    small_plane.finish()

    r.prm[...] = r.small_all[...].reshape(WIDE, 128).astype(F32).T[0:72]
    damping = jax.nn.sigmoid(r.prm[0:16])
    mixing = jax.nn.sigmoid(r.prm[16:32])
    lanes_to_rows(1.0 - mixing * damping, r.fac)
    lanes_to_rows(0.25 * r.prm[48:64] * (mixing * r.prm[32:48]), r.gain)
    pair_base = net.take(8)

    def pair_normed(k):
        yy, xx = chip_of(k)
        block = r.normed_all.at[slot_of(yy, xx, c)]
        return net.make(pair_base + k, block, block, twin)

    def pair_mixed(k):
        yy, xx = chip_of(k)
        block = r.mixed_all.at[slot_of(yy, xx, c)]
        return net.make(pair_base + 4 + k, block, block, twin)

    def mix(k, tall, pre):
        yy, xx = chip_of(k)
        slot = slot_of(yy, xx, c)
        source = r.mixed_all[slot]
        xhat, _ = standardized(source.astype(F32))
        normed = xhat * r.prm[64:65] + r.prm[67:68]
        r.normed_all[slot] = normed.astype(LOW)
        pair_normed(k).start()
        lanes_to_rows(normed, tall)
        pre[...] = r.prm[65:66] * normed
        ema_forward(r.fac, r.gain, tall, r.tall_out)
        for s in range(8):
            cols = slice(s * 128, (s + 1) * 128)
            pre[:, cols] = pre[:, cols] + r.tall_out[:, s, :]
        r.mixed_all[slot] = silu(pre[...]).astype(LOW)
        pair_mixed(k).start()

    r.mixed_all[me] = r.x[...]
    mix(0, r.nrm, r.pre)

    @pl.loop(1, 4)
    def _(k):
        near(k).wait_recv()

        @pl.when(k == 3)
        def _():
            attn_line.relay()

        mix(k, r.tall, r.work)

    expand_plane.finish()
    expand_line = LineGather(net, r.we)
    expand_line.start()
    reduce_line = LineGather(net, r.wr)
    reduce_line.start()
    cot_plane.take_rest()
    cot_plane.finish()
    for k in (1, 2, 3):
        near(k).wait_send()
    for k in range(4):
        pair_normed(k).wait()
        pair_mixed(k).wait()
    zeta_plane.finish()
    out_line.finish()
    attn_line.finish()

    cand_cols = cols_at(me, 128)
    shift = r.heads[2:3]

    def weights_a(first, last):
        return r.wa[:, :, :, first:last].reshape(WIDE, last - first)

    def zeta_weights():
        return r.wz[...].reshape(WIDE, 128)

    def pair_of(k):
        yy, xx = chip_of(k)
        return pl.ds((yy * 2 + xx) * 2, 2)

    def rows_of(ref, k):
        return ref[pair_of(k)].reshape(2 * ROWS, ref.shape[2])

    def put(ref, k, value):
        ref[pair_of(k)] = value.reshape(2, ROWS, ref.shape[2]).astype(ref.dtype)

    def attend(k):
        pre = jnp.dot(rows_of(r.normed_all, k), weights_a(0, 256), preferred_element_type=F32)
        put(r.value_pre, k, pre)
        low_values = silu(pre).astype(LOW)
        put(r.value_low, k, low_values)
        mixed = rows_of(r.mixed_all, k)
        mixture = jnp.dot(mixed, weights_a(256, 768), preferred_element_type=F32)
        put(r.update_part, k, mixture[:, 0:128])
        put(r.reset_pre, k, mixture[:, 128:384])
        zeta = jnp.dot(mixed, zeta_weights(), preferred_element_type=F32)
        put(r.zeta_pre, k, zeta)
        zeta = silu(zeta)
        values = []
        weights = []
        for h in range(2):
            rows = slice(h * ROWS, (h + 1) * ROWS)
            _, _, probs = block_scores_of(zeta[rows], r.heads, shift, r.table)
            weights.append(probs.astype(LOW))
            values.append(jnp.dot(weights[h], low_values[rows], preferred_element_type=F32))
        put(r.weights_low, k, jnp.concatenate(weights, axis=0))
        mixed_values = jnp.concatenate(values, axis=0)
        put(r.attended, k, mixed_values)
        gate = (mixed_values * silu(mixture[:, 128:384])).astype(LOW)
        put(r.gated, k, gate)
        hidden = jnp.dot(gate, r.wo[...].reshape(256, WIDE), preferred_element_type=F32)
        r.pairs[...] = hidden.reshape(2, ROWS, WIDE)
        r.pairs[:, :, cand_cols] = r.pairs[:, :, cand_cols] + mixture[:, 384:512].reshape(2, ROWS, 128)

    hidden_sum = PlaneSum(net, r.part, r.got, r.sent, r.far, r.hidden_pre, r.pairs, r.work)
    hidden_sum.run(attend)
    update_plane = swap_plane(net, r.update_part, r.update_all)
    expand_line.relay()
    hidden_sum.settle()
    hidden_sum.finish()
    update_plane.finish()
    for s in range(8):
        r.update_pre[:, s * 128 : (s + 1) * 128] = r.update_all[s].astype(F32)
    stream = r.x[...].astype(F32)
    r.first[...] = stream + jax.nn.sigmoid(r.update_pre[...]) * (silu(r.hidden_pre[...]) - stream)
    xhat, _ = standardized(r.first[...])
    r.own_low[...] = (xhat * r.prm[66:67] + r.prm[68:69]).astype(LOW)
    two_plane = PlaneGather(net, r.own_low, r.two_all)
    two_plane.start()
    reduce_line.relay()
    expand_line.finish()

    def reduce_rows():
        return r.wr[...].reshape(512, WIDE)

    def expand_rows():
        return r.we[...].reshape(WIDE, 512)

    @pl.loop(0, 4)
    def _(k):
        @pl.when(k > 0)
        def _():
            two_plane.take_near(k)

        two_plane.take_twin(k)
        pre = jnp.dot(rows_of(r.two_all, k), expand_rows(), preferred_element_type=F32)
        put(r.expand_pre, k, pre)
        put(r.expand_low, k, silu(pre))

    two_plane.finish()
    reduce_sum = LineSum(net, r.gr, r.gr_got, r.grad_reduce)
    expand_sum = LineSum(net, r.ge, r.ge_got, r.ge_sum)

    def reduce_grad(zz):
        r.gr[zz] = rows_dot(
            r.expand_low[:, :, cols_at(zz, 128)].reshape(tokens, 128), r.cot_all[...].reshape(tokens, WIDE)
        ).astype(LOW)

    reduce_sum.run(reduce_grad)
    reduce_line.finish()

    def expand_back(k):
        grad = (cols_dot(rows_of(r.cot_all, k), reduce_rows()) * silu_slope(rows_of(r.expand_pre, k))).astype(LOW)
        put(r.grad_pre, k, grad)
        r.pairs[...] = cols_dot(grad, expand_rows()).reshape(2, ROWS, WIDE)

    two_sum = PlaneSum(net, r.part, r.got, r.sent, r.far, r.grad_two, r.pairs, r.work)
    two_sum.run(expand_back)

    @pl.loop(0, 4)
    def _(zz):
        r.ge[zz] = rows_dot(
            r.two_all[:, :, cols_at(zz, 256)].reshape(tokens, 256), r.grad_pre[...].reshape(tokens, 512)
        ).astype(LOW)

    expand_sum.start()

    def branch_blocks(k):
        branch = jnp.dot(rows_of(r.expand_low, k), reduce_rows(), preferred_element_type=F32)
        r.pairs[...] = branch.reshape(2, ROWS, WIDE)

    two_sum.settle()
    branch_sum = RelayedSum(net, r.part, r.got_b, r.sent_b, r.far_b, r.branch, r.pairs, r.work)
    branch_sum.run(branch_blocks)
    reduce_sum.relay()
    valid = jnp.where(lax.broadcasted_iota(jnp.int32, (ROWS, 1), 0) < r.lens[0, 0], 1.0, 0.0)
    update = jax.nn.sigmoid(r.update_pre[...])
    hidden = r.hidden_pre[...]
    r.work[...] = update * silu_slope(hidden)
    r.pairs[1] = (silu(hidden) - r.x[...].astype(F32)) * update * (1.0 - update)
    xhat, inverse = standardized(r.first[...])
    r.pairs[0] = xhat
    r.inverse[...] = jnp.broadcast_to(inverse, (ROWS, 128))
    two_sum.finish()

    grad_first = r.cot[...].astype(F32) * valid + norm_back(
        r.grad_two[...], r.pairs[0], r.inverse[:, 0:1], r.prm[66:67]
    )
    r.own_low[...] = (grad_first * r.work[...]).astype(LOW)
    hid_plane = PlaneGather(net, r.own_low, r.hid_all)
    hid_plane.start(last=False)
    grad_update = (grad_first * r.pairs[1]).astype(LOW)
    for s in range(8):
        r.update_part[s] = grad_update[:, s * 128 : (s + 1) * 128]
    upd_plane = ChipSwap(net, r.update_part, r.update_all)
    upd_plane.start()
    hid_plane.start_last()
    r.grad_inputs[...] = grad_first * (1.0 - jax.nn.sigmoid(r.update_pre[...]))
    put_rows(r.sums, 34, r.grad_two[...] * r.pairs[0])
    put_rows(r.sums, 36, r.grad_two[...])

    branch_sum.settle()
    expand_sum.relay()
    scores_plane = PlaneSum(
        net, r.scores_part, r.scores_got, r.scores_sent, r.scores_far, r.scores_sum, r.scores_pairs, r.scores_keep
    )
    mixed_sum = PlaneSum(net, r.part, r.got, r.sent, r.far, r.grad_two, r.pairs, r.work)

    def attend_back(k):
        gate_grad = cols_dot(rows_of(r.hid_all, k), r.wo[...].reshape(256, WIDE))
        pre = rows_of(r.reset_pre, k)
        low_grad = (gate_grad * silu(pre)).astype(LOW)
        low_values = rows_of(r.value_low, k)
        weights = rows_of(r.weights_low, k)
        backs = []
        for h in range(2):
            rows = slice(h * ROWS, (h + 1) * ROWS)
            r.scores_pairs[h] = cols_dot(low_grad[rows], low_values[rows])
            backs.append(rows_dot(weights[rows], low_grad[rows]))
        put(r.value_back, k, jnp.concatenate(backs, axis=0) * silu_slope(rows_of(r.value_pre, k)))
        pair = pair_of(k)
        r.mixture_back[pair, :, 0:128] = r.update_all[pair]
        r.mixture_back[pair, :, 128:384] = (
            (gate_grad * rows_of(r.attended, k) * silu_slope(pre)).astype(LOW).reshape(2, ROWS, 256)
        )
        r.mixture_back[pair, :, 384:512] = r.hid_all[pair, :, cand_cols]
        mixture = rows_of(r.mixture_back, k)
        mixed = cols_dot(mixture, weights_a(256, 768))
        r.pairs[...] = mixed.reshape(2, ROWS, WIDE)

    @pl.loop(0, 4)
    def _(k):
        @pl.when(k > 0)
        def _():
            hid_plane.take_near(k)

        hid_plane.take_twin(k)
        upd_plane.take(k)
        attend_back(k)
        scores_plane.give(k)
        mixed_sum.give(k)

        @pl.when(k > 0)
        def _():
            scores_plane.pair(k - 1)
            mixed_sum.pair(k - 1)

        scores_plane.hold()
        mixed_sum.hold()

    scores_plane.pair(3)
    mixed_sum.pair(3)
    hid_plane.finish()
    upd_plane.finish()
    out_sum = LineSum(net, r.go, r.go_got, r.grad_out)
    attn_sum = LineSum(net, r.ga, r.ga_got, r.ga_sum)

    def attn_grad(zz):
        cols = cols_at(zz, 256)
        r.ga[zz, :, 0:256] = rows_dot(
            r.normed_all[:, :, cols].reshape(tokens, 256), r.value_back[...].reshape(tokens, 256)
        ).astype(LOW)
        r.ga[zz, :, 256:768] = rows_dot(
            r.mixed_all[:, :, cols].reshape(tokens, 256), r.mixture_back[...].reshape(tokens, 512)
        ).astype(LOW)

    attn_sum.run(attn_grad)

    @pl.loop(0, 4)
    def _(t):
        cols = cols_at(t, 256)
        grad = rows_dot(
            r.gated[...].reshape(tokens, 256), r.hid_all[:, :, cols].reshape(tokens, 256)
        ).astype(LOW)
        for zz in range(4):
            r.go[zz, :, cols] = grad[zz * 64 : (zz + 1) * 64]


    reduce_sum.finish()
    expand_sum.finish()
    ge_plane = swap_plane(net, r.ge_sum, r.ge_all)
    mixed_sum.settle()
    normed_sum = RelayedSum(net, r.part, r.got_c, r.sent_c, r.far_c, r.hidden_pre, r.pairs, r.work)

    def normed_blocks(k):
        normed = cols_dot(rows_of(r.value_back, k), weights_a(0, 256))
        r.pairs[...] = normed.reshape(2, ROWS, WIDE)

    normed_sum.run(normed_blocks)

    scores_plane.settle()
    scores_plane.finish()
    grad_weights = r.scores_sum[...]
    zeta_own_pre = r.zeta_pre[me]
    zeta = silu(zeta_own_pre)
    query_low, key_low, probs = block_scores_of(zeta, r.heads, shift, r.table)
    grad_scores = (probs * (grad_weights - jnp.sum(probs * grad_weights, axis=-1, keepdims=True))).astype(LOW)
    scale = zeta.shape[1] ** (-0.5)
    grad_query = jnp.dot(grad_scores, key_low, preferred_element_type=F32) * scale
    grad_key = rows_dot(grad_scores, query_low) * scale
    skewed = pltpu.roll(
        jnp.dot(grad_scores, mirror_matrix(ROWS), preferred_element_type=F32), 1, 1, stride=1, stride_axis=0
    )
    r.sums[37:40] = jnp.zeros((3, WIDE), F32)
    r.sums[37:38, 0:128] = jnp.sum(grad_query * zeta, axis=0, keepdims=True)
    r.sums[37:38, 128:256] = jnp.sum(grad_key * zeta, axis=0, keepdims=True)
    r.sums[37:38, 256:384] = jnp.sum(grad_query, axis=0, keepdims=True)
    r.sums[37:38, 384:512] = jnp.sum(skewed, axis=0, keepdims=True)
    grad_zeta = grad_query * r.heads[0:1] + grad_key * r.heads[1:2]
    r.zeta_own[...] = (grad_zeta * silu_slope(zeta_own_pre)).astype(LOW)
    zeta_tokens = spread_plane(net, r.zeta_own, r.zeta_all)

    normed_sum.relay()
    branch_sum.relay()
    mixed_sum.finish()
    grad_mixed = r.grad_two[...] + cols_dot(r.zeta_own[...], zeta_weights())
    pull = grad_mixed * silu_slope(r.pre[...])
    lanes_to_rows(pull, r.tall)
    r.pre[...] = pull
    attn_sum.relay()
    ema_backward(r.fac, r.gain, r.nrm, r.tall, r.fac_sum, r.gain_sum, r.tall_out)
    for s in range(8):
        cols = slice(s * 128, (s + 1) * 128)
        r.sums[0:16, cols] = r.fac_sum[:, s, :]
        r.sums[16:32, cols] = r.gain_sum[:, s, :]
        r.sums[33:34, cols] = jnp.sum(r.pre[:, cols] * r.nrm[:, s, :], axis=0, keepdims=True)
    normed_sum.settle()
    normed_sum.finish()
    for s in range(8):
        cols = slice(s * 128, (s + 1) * 128)
        r.hidden_pre[:, cols] = r.hidden_pre[:, cols] + r.pre[:, cols] * r.prm[65:66, cols] + r.tall_out[:, s, :]
    xhat_one, inverse_one = standardized(r.x[...].astype(F32))
    grad_one = r.hidden_pre[...]
    put_rows(r.sums, 32, grad_one * xhat_one)
    put_rows(r.sums, 35, grad_one)
    r.grad_inputs[...] = r.grad_inputs[...] + norm_back(grad_one, xhat_one, inverse_one, r.prm[64:65])

    for s in range(8):
        r.sum_blocks[s] = r.sums[:, s * 128 : (s + 1) * 128]
    small_sum = swap_plane(net, r.sum_blocks, r.sum_parts)
    small_sum.finish()
    whole = r.sum_parts[0]
    for s in range(1, 8):
        whole = whole + r.sum_parts[s]
    r.sum_rows[z] = whole
    small_rows = spread_line(net, r.sum_rows)
    out_sum.start()
    attn_sum.finish()
    ga_plane = swap_plane(net, r.ga_sum, r.ga_all)
    zeta_tokens.finish()
    r.gz[...] = rows_dot(
        r.mixed_all[...].reshape(tokens, WIDE), r.zeta_all[...].reshape(tokens, 128)
    ).reshape(4, 8, 32, 128)
    for zz in range(4):
        r.gz_own[zz] = r.gz[zz, me]
    zeta_grad = swap_line(net, r.gz_own, r.gz_line)
    out_sum.relay()
    branch_sum.finish()
    stream = r.x[...].astype(F32)
    first = r.first[...]
    branch = r.branch[...]
    attn_branch = first - stream
    r.output[...] = ((first + branch) * valid).astype(LOW)
    r.square_own[...] = jnp.zeros((8, 128), F32)
    for k, item in enumerate((stream, attn_branch, branch)):
        squares = jnp.sum(valid * item * item, axis=0, keepdims=True)
        r.square_own[k : k + 1] = jnp.broadcast_to(jnp.sum(squares, axis=1, keepdims=True), (1, 128))
    r.square_own[3:4] = jnp.broadcast_to(jnp.sum(valid, axis=0, keepdims=True), (1, 128))
    square_plane = spread_plane(net, r.square_own, r.square_all)
    small_rows.finish()
    r.sum_cols[...] = (r.sum_rows[0] + r.sum_rows[1]) + (r.sum_rows[2] + r.sum_rows[3])
    small_cols = spread_plane(net, r.sum_cols, r.sums_all)
    square_plane.finish()
    squares = r.square_all[0]
    for s in range(1, 8):
        squares = squares + r.square_all[s]
    r.square_line[z] = squares
    square_rows = spread_line(net, r.square_line)
    out_sum.finish()
    ge_plane.finish()
    zeta_grad.finish()
    ga_plane.finish()
    small_cols.finish()
    square_rows.finish()


def layer(*operands):
    return pl.pallas_call(
        layer_kernel,
        name="layer",
        out_shape=[jax.ShapeDtypeStruct(*item) for item in fields(Results).values()],
        in_specs=list(fields(Inputs).values()),
        out_specs=[VMEM] * len(fields(Results)),
        scratch_shapes=[pltpu.VMEM(*item) for item in fields(Scratch).values()]
        + [pltpu.SemaphoreType.DMA(item) for item in fields(Lines).values()],
        compiler_params=pltpu.CompilerParams(
            collective_id=1, has_side_effects=True, vmem_limit_bytes=60 << 20
        ),
    )(*operands)


def place_halves(blocks, base, q, out, start):
    lane = lax.broadcasted_iota(jnp.int32, (blocks.shape[1], 128), 1)
    for zz in range(4):
        at = base + (zz // 2) * 128
        left = blocks[2 * q, :, at : at + 128].astype(F32)
        right = blocks[2 * q + 1, :, at : at + 128].astype(F32)
        if zz % 2:
            left = pltpu.roll(left, 64, 1)
        else:
            right = pltpu.roll(right, 64, 1)
        to = start + (zz * 4 + q) * 128
        out[:, to : to + 128] = jnp.where(lane < 64, left, right)


def outputs_kernel(
    output, grad_inputs, grad_out, grad_reduce, ge_all, ga_all, gz_line, sums_all, square_line, ema,
    output_o, grad_inputs_o, values_o, mix_o, out_o, expand_o, reduce_o, ema_o, gains_o, biases_o, heads_o,
    shift_o, position_o, rms_o, turned,
):
    output_o[...] = output[...]
    grad_inputs_o[...] = grad_inputs[...]
    out_o[...] = grad_out[...]
    reduce_o[...] = grad_reduce[...]
    for s in range(8):
        for zz in range(4):
            at = (zz * 8 + s) * 128
            expand_o[:, at : at + 128] = ge_all[s, :, zz * 128 : (zz + 1) * 128].astype(F32)
        mix_o[:, s * 128 : (s + 1) * 128] = ga_all[s, :, 256:384].astype(F32)
        mix_o[:, 3200 + s * 128 : 3328 + s * 128] = ga_all[s, :, 640:768].astype(F32)
    mix_o[:, 1024:1152] = (gz_line[0] + gz_line[1]) + (gz_line[2] + gz_line[3])
    for q in range(4):
        place_halves(ga_all, 0, q, values_o, 0)
        place_halves(ga_all, 384, q, mix_o, 1152)
    mine = sums_all[lax.axis_index("dp")]
    mine = pltpu.roll(mine, (128 - 32 * lax.axis_index("fsdp")) % 128, 1)
    turned[0:40] = mine
    turned[40:128] = jnp.zeros((88, 128), F32)
    gains_o[...] = turned[32:35, 0:32]
    biases_o[...] = turned[35:37, 0:32]
    flipped = turned[...].T
    raw = ema[...].astype(F32)
    damping = jax.nn.sigmoid(raw[:, 0:16])
    mixing = jax.nn.sigmoid(raw[:, 16:32])
    expand = raw[:, 32:48]
    project = raw[:, 48:64]
    by_factor = flipped[0:32, 0:16] * (0.25 * project * mixing * expand)
    by_gain = flipped[0:32, 16:32]
    by_inflow = 0.25 * project * by_gain
    ema_o[:, 0:16] = -by_factor * mixing * damping * (1.0 - damping)
    ema_o[:, 16:32] = (by_inflow * expand - by_factor * damping) * mixing * (1.0 - mixing)
    ema_o[:, 32:48] = by_inflow * mixing
    ema_o[:, 48:64] = 0.25 * mixing * expand * by_gain
    heads_o[0:1] = sums_all[0, 37:38]
    heads_o[1:2] = sums_all[1, 37:38]
    shift_o[...] = sums_all[2, 37]
    position_o[...] = sums_all[3, 37]
    squares = (square_line[0] + square_line[1]) + (square_line[2] + square_line[3])
    roots = jnp.sqrt(squares / (squares[3:4] * WIDE))
    col = lax.broadcasted_iota(jnp.int32, (1, 128), 1)
    line = jnp.where(col == 0, roots[0:1], jnp.where(col == 1, roots[1:2], roots[2:3]))
    rms_o[...] = line[0, 0:3]


def outputs(parts, ema_params):
    shapes = (
        ((ROWS, WIDE), LOW), ((ROWS, WIDE), F32), ((32, 2048), F32), ((32, 4224), F32), ((64, WIDE), F32),
        ((32, 4096), F32), ((ROWS, WIDE), F32), ((32, 64), F32), ((3, 32), F32), ((2, 32), F32), ((2, 128), F32),
        ((128,), F32), ((128,), F32), ((3,), F32),
    )
    return pl.pallas_call(
        outputs_kernel,
        name="outputs",
        out_shape=[jax.ShapeDtypeStruct(shape, dtype) for shape, dtype in shapes],
        in_specs=[VMEM] * 10,
        out_specs=[VMEM] * len(shapes),
        scratch_shapes=[pltpu.VMEM((128, 128), F32)],
    )(*parts, ema_params)


def on_plane(
    inputs, lengths, w_values, w_mix, w_out, w_expand, w_reduce, ema_params,
    norm_gains, norm_biases, head_gains, query_bias, position_bias, cotangent,
):
    consts = jnp.concatenate([head_gains, query_bias[None], position_bias[None]])
    parts = layer(
        inputs, cotangent, w_values, w_mix, w_out, w_expand, w_reduce, ema_params, norm_gains, norm_biases,
        consts, lengths,
    )
    done = outputs(parts, ema_params)
    return tuple(done)


def layer_norm(value, gain, shift):
    centre = jnp.mean(value, axis=-1, keepdims=True)
    centered = value - centre
    spread = jnp.mean(centered * centered, axis=-1, keepdims=True)
    return centered * lax.rsqrt(spread + EPS) * gain + shift


def ema_mix(normed, keep, ema_params):
    count = ema_params.shape[1] // 4
    damping = jax.nn.sigmoid(ema_params[:, :count]).T
    mixing = jax.nn.sigmoid(ema_params[:, count : 2 * count]).T
    expand = ema_params[:, 2 * count : 3 * count].T
    project = ema_params[:, 3 * count :].T
    factor = 1.0 - mixing * damping
    inflow = mixing * expand

    def advance(state, item):
        column, flag = item
        state = factor * state * flag[:, None, None] + inflow * column[:, None, :]
        return (state, 0.25 * jnp.sum(project * state, axis=1))

    start = jnp.zeros((normed.shape[0], count, normed.shape[2]), jnp.float32)
    _, smooth = lax.scan(advance, start, (jnp.swapaxes(normed, 0, 1), jnp.swapaxes(keep, 0, 1)))
    return jnp.swapaxes(smooth, 0, 1)


def layout(lengths, rows):
    ends = jnp.cumsum(lengths, axis=1)
    starts = ends - lengths
    place = lax.broadcasted_iota(jnp.int32, (lengths.shape[0], rows), 1)
    begin = jnp.any(place[:, :, None] == starts[:, None, :], axis=2) | (place == ends)
    keep = jnp.where(begin, 0.0, 1.0).astype(jnp.float32)
    valid = jnp.where(place < ends, 1.0, 0.0).astype(jnp.float32)
    return (keep, valid)


def dot_rows(left, right):
    return lax.dot_general(
        left, right, (((0,), (0,)), ((), ())), preferred_element_type=jnp.float32
    )


def dot_cols(left, right):
    return lax.dot_general(
        left, right, (((1,), (1,)), ((), ())), preferred_element_type=jnp.float32
    )


def block_scores(query_low, key_low, position, scale):
    span = query_low.shape[1]
    row = lax.broadcasted_iota(jnp.int32, (span, span), 0)
    col = lax.broadcasted_iota(jnp.int32, (span, span), 1)
    table = position[jnp.clip(row - col, 0, span - 1)]
    scores = (
        jnp.einsum("kiz,kjz->kij", query_low, key_low, preferred_element_type=jnp.float32) * scale
        + table
    )
    return jnp.where(row >= col, scores, NEG)


def diagonal_sums(grid):
    size = grid.shape[0]
    flipped = grid[:, ::-1]
    padded = jnp.pad(flipped, ((0, 0), (0, size)))
    skewed = padded.reshape(-1)[: size * (2 * size - 1)].reshape(size, 2 * size - 1)
    return jnp.sum(skewed, axis=0)[size - 1 :]


def group_rows(value):
    return lax.all_gather(value, "fsdp", axis=0, tiled=True)


def group_total(value):
    return lax.psum_scatter(value, "fsdp", scatter_dimension=0, tiled=True)


def owner_layout(grad, owners):
    return grad.reshape(owners * 8, -1)


def owner_shard(piece, columns):
    return piece.reshape(-1, columns)


def on_device(
    inputs,
    lengths,
    w_values,
    w_mix,
    w_out,
    w_expand,
    w_reduce,
    ema_params,
    norm_gains,
    norm_biases,
    head_gains,
    query_bias,
    position_bias,
    cotangent,
):
    rows, width = inputs.shape
    span = position_bias.shape[0]
    blocks = rows // span
    key_width = head_gains.shape[1]
    scale = key_width ** (-0.5)
    keep, valid = layout(lengths, rows)
    mask = valid[0][:, None]
    gathered = (
        lax.all_gather(w_values, ("dp", "fsdp"), axis=0, tiled=True),
        lax.all_gather(w_mix, ("dp", "fsdp"), axis=0, tiled=True),
        lax.all_gather(w_out, ("dp", "fsdp"), axis=0, tiled=True),
        lax.all_gather(ema_params, ("dp", "fsdp"), axis=0, tiled=True),
        lax.all_gather(norm_gains, ("dp", "fsdp"), axis=1, tiled=True),
        lax.all_gather(norm_biases, ("dp", "fsdp"), axis=1, tiled=True),
    )
    values_full, mix_full, out_full, ema_full, gains_full, biases_full = gathered
    value_width = values_full.shape[1]
    group_size = lax.axis_size("fsdp")
    data_size = lax.axis_size("dp")
    owners = group_size * data_size
    shard_rows = w_expand.shape[0]
    hidden_units = w_expand.shape[1]
    unit_block = hidden_units // (group_size * data_size)
    pieces = w_expand.reshape(shard_rows, data_size, group_size, unit_block)
    swapped = lax.all_to_all(pieces, "fsdp", split_axis=2, concat_axis=0, tiled=True)
    expand_quarter, reduce_use = (
        lax.all_gather(swapped, "dp", axis=0, tiled=True),
        lax.all_gather(w_reduce, "dp", axis=0, tiled=True),
    )
    expand_use = expand_quarter.reshape(expand_quarter.shape[0], data_size * unit_block)
    gains_f = gains_full.astype(jnp.float32)
    biases_f = biases_full.astype(jnp.float32)
    heads_f = head_gains.astype(jnp.float32)
    query_shift = query_bias.astype(jnp.float32)
    position_f = position_bias.astype(jnp.float32)
    stream = inputs.astype(jnp.float32)

    def front(source, gain, shift, omega, params):
        normed_part = layer_norm(source, gain, shift)
        smooth = ema_mix(normed_part[None], keep, params)[0]
        return (normed_part, silu(smooth + omega * normed_part))

    (normed, mixed), front_back = jax.vjp(
        front, stream, gains_f[0], biases_f[0], gains_f[1], ema_full.astype(jnp.float32)
    )
    normed_low = normed.astype(jnp.bfloat16)
    mixed_low = mixed.astype(jnp.bfloat16)
    value_pre = jnp.dot(normed_low, values_full, preferred_element_type=jnp.float32)
    value_low = silu(value_pre).astype(jnp.bfloat16)
    mixture = jnp.dot(mixed_low, mix_full, preferred_element_type=jnp.float32)
    middle = width + key_width
    upper = middle + value_width
    update = jax.nn.sigmoid(mixture[:, :width])
    zeta_pre = mixture[:, width:middle]
    zeta = silu(zeta_pre)
    reset_pre = mixture[:, middle:upper]
    reset = silu(reset_pre)
    candidate = mixture[:, upper:]
    query_low = (
        (zeta * heads_f[0] + query_shift).astype(jnp.bfloat16).reshape(blocks, span, key_width)
    )
    key_low = (zeta * heads_f[1]).astype(jnp.bfloat16).reshape(blocks, span, key_width)
    value_blocks = value_low.reshape(blocks, span, value_width)
    scores = block_scores(query_low, key_low, position_f, scale)
    log_total = jax.nn.logsumexp(scores, axis=-1, keepdims=True)
    weights_low = jnp.exp(scores - log_total).astype(jnp.bfloat16)
    attended = jnp.einsum(
        "kij,kjv->kiv", weights_low, value_blocks, preferred_element_type=jnp.float32
    ).reshape(rows, value_width)
    gated_low = (attended * reset).astype(jnp.bfloat16)
    hidden_pre = candidate + jnp.dot(gated_low, out_full, preferred_element_type=jnp.float32)
    hidden = silu(hidden_pre)
    attn_branch = update * (hidden - stream)
    first = stream + attn_branch
    normed_two, norm_back = jax.vjp(layer_norm, first, gains_f[2], biases_f[1])
    normed_two_low = normed_two.astype(jnp.bfloat16)
    ffn_rows = group_rows(normed_two_low)
    expand_pre = jnp.dot(ffn_rows, expand_use, preferred_element_type=jnp.float32)
    expand_low = silu(expand_pre).astype(jnp.bfloat16)
    branch_part = jnp.dot(expand_low, reduce_use, preferred_element_type=jnp.float32)
    branch = group_total(branch_part)
    output = ((first + branch) * mask).astype(jnp.bfloat16)
    values_back, mix_back, out_back = (
        lax.all_gather(w_values, ("dp", "fsdp"), axis=0, tiled=True),
        lax.all_gather(w_mix, ("dp", "fsdp"), axis=0, tiled=True),
        lax.all_gather(w_out, ("dp", "fsdp"), axis=0, tiled=True),
    )
    grad_out = cotangent.astype(jnp.float32) * mask
    grad_branch = grad_out.astype(jnp.bfloat16)
    grad_rows = group_rows(grad_branch)
    grad_reduce = dot_rows(expand_low, grad_rows)
    grad_expand_out = dot_cols(grad_rows, reduce_use)
    grad_expand_pre = (grad_expand_out * silu_slope(expand_pre)).astype(jnp.bfloat16)
    grad_expand = dot_rows(ffn_rows, grad_expand_pre)
    normed_two_part = dot_cols(grad_expand_pre, expand_use)
    grad_normed_two = group_total(normed_two_part)
    grad_first_norm, grad_gain_two, grad_shift_two = norm_back(grad_normed_two)
    grad_first = grad_out + grad_first_norm
    grad_direct = grad_first * (1.0 - update)
    grad_update = grad_first * (hidden - stream)
    grad_hidden_pre = grad_first * update * silu_slope(hidden_pre)
    grad_hidden_low = grad_hidden_pre.astype(jnp.bfloat16)
    grad_out_proj = dot_rows(gated_low, grad_hidden_low)
    grad_gated = dot_cols(grad_hidden_low, out_back)
    grad_attended = (grad_gated * reset).astype(jnp.bfloat16).reshape(blocks, span, value_width)
    grad_reset = grad_gated * attended
    scores_again = block_scores(query_low, key_low, position_f, scale)
    probs = jnp.exp(scores_again - log_total)
    probs_low = probs.astype(jnp.bfloat16)
    grad_weights = jnp.einsum(
        "kiv,kjv->kij", grad_attended, value_blocks, preferred_element_type=jnp.float32
    )
    grad_value = jnp.einsum(
        "kij,kiv->kjv", probs_low, grad_attended, preferred_element_type=jnp.float32
    ).reshape(rows, value_width)
    inner = jnp.sum(probs * grad_weights, axis=-1, keepdims=True)
    grad_scores = (probs * (grad_weights - inner)).astype(jnp.bfloat16)
    grad_position = diagonal_sums(jnp.sum(grad_scores.astype(jnp.float32), axis=0))
    grad_query = (
        jnp.einsum(
            "kij,kjz->kiz", grad_scores, key_low, preferred_element_type=jnp.float32
        ).reshape(rows, key_width)
        * scale
    )
    grad_key = (
        jnp.einsum(
            "kij,kiz->kjz", grad_scores, query_low, preferred_element_type=jnp.float32
        ).reshape(rows, key_width)
        * scale
    )
    grad_value_pre = (grad_value * silu_slope(value_pre)).astype(jnp.bfloat16)
    grad_values = dot_rows(normed_low, grad_value_pre)
    grad_normed = dot_cols(grad_value_pre, values_back)
    grad_zeta = grad_query * heads_f[0] + grad_key * heads_f[1]
    grad_heads = jnp.stack([jnp.sum(grad_query * zeta, axis=0), jnp.sum(grad_key * zeta, axis=0)])
    grad_query_shift = jnp.sum(grad_query, axis=0)
    grad_mixture = jnp.concatenate(
        [
            grad_update * update * (1.0 - update),
            grad_zeta * silu_slope(zeta_pre),
            grad_reset * silu_slope(reset_pre),
            grad_hidden_pre,
        ],
        axis=1,
    ).astype(jnp.bfloat16)
    grad_mix = dot_rows(mixed_low, grad_mixture)
    grad_mixed = dot_cols(grad_mixture, mix_back)
    grad_source, grad_gain_one, grad_shift_one, grad_omega, grad_ema = front_back(
        (grad_normed, grad_mixed)
    )
    grad_inputs = grad_direct + grad_source
    grad_gains = jnp.stack([grad_gain_one, grad_omega, grad_gain_two])
    grad_shifts = jnp.stack([grad_shift_one, grad_shift_two])
    summed_expand, grad_reduce_dev = (
        lax.psum_scatter(grad_expand, "dp", scatter_dimension=0, tiled=True),
        lax.psum_scatter(grad_reduce, "dp", scatter_dimension=0, tiled=True),
    )
    summed_pieces = summed_expand.reshape(group_size * shard_rows, data_size, 1, unit_block)
    owned = lax.all_to_all(summed_pieces, "fsdp", split_axis=0, concat_axis=2, tiled=True)
    grad_expand_dev = owned.reshape(shard_rows, hidden_units)
    summed_block = (
        lax.psum_scatter(
            owner_layout(grad_values, owners), ("dp", "fsdp"), scatter_dimension=0, tiled=True
        ),
        lax.psum_scatter(
            owner_layout(grad_mix, owners), ("dp", "fsdp"), scatter_dimension=0, tiled=True
        ),
        lax.psum_scatter(grad_out_proj, ("dp", "fsdp"), scatter_dimension=0, tiled=True),
        lax.psum_scatter(
            owner_layout(grad_ema, owners), ("dp", "fsdp"), scatter_dimension=0, tiled=True
        ),
        lax.psum_scatter(grad_gains, ("dp", "fsdp"), scatter_dimension=1, tiled=True),
        lax.psum_scatter(grad_shifts, ("dp", "fsdp"), scatter_dimension=1, tiled=True),
    )
    values_flat, mix_flat, grad_out_dev, ema_flat, grad_gains_dev, grad_shifts_dev = summed_block
    grad_values_dev = owner_shard(values_flat, grad_values.shape[1])
    grad_mix_dev = owner_shard(mix_flat, grad_mix.shape[1])
    grad_ema_dev = owner_shard(ema_flat, grad_ema.shape[1])
    squares = jnp.stack(
        [
            jnp.sum(mask * stream * stream),
            jnp.sum(mask * attn_branch * attn_branch),
            jnp.sum(mask * branch * branch),
        ]
    )
    square_sums, tokens_seen, heads_total, shift_total, position_total = lax.psum(
        (squares, jnp.sum(valid), grad_heads, grad_query_shift, grad_position), ("dp", "fsdp")
    )
    rms = jnp.sqrt(square_sums / (tokens_seen * width))
    return (
        output,
        grad_inputs,
        grad_values_dev,
        grad_mix_dev,
        grad_out_dev,
        grad_expand_dev,
        grad_reduce_dev,
        grad_ema_dev,
        grad_gains_dev,
        grad_shifts_dev,
        heads_total,
        shift_total,
        position_total,
        rms,
    )


def solution(mesh):
    in_specs = (
        P(("dp", "fsdp"), None),
        P(("dp", "fsdp"), None),
        P(("dp", "fsdp"), None),
        P(("dp", "fsdp"), None),
        P(("dp", "fsdp"), None),
        P(("dp", "fsdp"), None),
        P(("dp", "fsdp"), None),
        P(("dp", "fsdp"), None),
        P(None, ("dp", "fsdp")),
        P(None, ("dp", "fsdp")),
        P(),
        P(),
        P(),
        P(("dp", "fsdp"), None),
    )
    out_specs = (
        P(("dp", "fsdp"), None),
        P(("dp", "fsdp"), None),
        P(("dp", "fsdp"), None),
        P(("dp", "fsdp"), None),
        P(("dp", "fsdp"), None),
        P(("dp", "fsdp"), None),
        P(("dp", "fsdp"), None),
        P(("dp", "fsdp"), None),
        P(None, ("dp", "fsdp")),
        P(None, ("dp", "fsdp")),
        P(),
        P(),
        P(),
        P(),
    )
    planes = mesh.shape["dp"] == 8 and mesh.shape["fsdp"] == 4
    return jax.shard_map(
        on_plane if planes else on_device, mesh=mesh, in_specs=in_specs, out_specs=out_specs, check_vma=False
    )
```

```python
import jax
import jax.numpy as jnp
from jax import lax
from jax.experimental import pallas as pl
from jax.experimental.pallas import tpu as pltpu
from jax.sharding import PartitionSpec as P

EPS = 1e-05
NEG = -1e30
F32 = jnp.float32
LOW = jnp.bfloat16
MESH = pl.DeviceIdType.MESH
LINES = 128
STATES = 16


def silu(value):
    return value * jax.nn.sigmoid(value)


def silu_slope(value):
    sigma = jax.nn.sigmoid(value)
    return sigma * (1.0 + value * (1.0 - sigma))


def here():
    dp = lax.axis_index("dp")
    f = lax.axis_index("fsdp")
    return dp // 2, dp % 2, f // 2, f % 2


def device(z, y, x, c):
    return (z * 2 + y, x * 2 + c)


def slot_of(y, x, c):
    return y * 4 + x * 2 + c


def plane_peers(y, x, c):
    peers = []
    for mask in range(1, 8):
        peers.append(
            (
                1 - y if mask & 4 else y,
                1 - x if mask & 2 else x,
                1 - c if mask & 1 else c,
            )
        )
    return peers


def line_peers(z):
    return [z + 1 - 2 * (z % 2), 3 - z, (z + 2) % 4]


def greet(across=True):
    z, y, x, c = here()
    barrier = pltpu.get_barrier_semaphore()
    count = 7
    for peer in plane_peers(y, x, c):
        pl.semaphore_signal(barrier, inc=1, device_id=device(z, *peer), device_id_type=MESH)
    if across:
        count = 10
        for other in line_peers(z):
            pl.semaphore_signal(barrier, inc=1, device_id=device(other, y, x, c), device_id_type=MESH)
    pl.semaphore_wait(barrier, count)


class Net:
    def __init__(self, send, recv):
        self.send = send
        self.recv = recv
        self.used = 0

    def take(self, count):
        self.used += count
        assert self.used <= LINES
        return self.used - count

    def make(self, line, src, dst, target):
        return pltpu.make_async_remote_copy(
            src_ref=src,
            dst_ref=dst,
            send_sem=self.send.at[line],
            recv_sem=self.recv.at[line],
            device_id=target,
            device_id_type=MESH,
        )

    def copy(self, src, dst, target):
        made = self.make(self.take(1), src, dst, target)
        made.start()
        return made


VMEM = pl.BlockSpec(memory_space=pltpu.VMEM)


def rows_dot(left, right):
    return lax.dot_general(left, right, (((0,), (0,)), ((), ())), preferred_element_type=F32)


def cols_dot(left, right):
    return lax.dot_general(left, right, (((1,), (1,)), ((), ())), preferred_element_type=F32)


def lanes_to_rows(wide, tall):
    for s in range(8):
        tall[:, s, :] = wide[:, s * 128 : (s + 1) * 128]


def pick_halves(arr, base, slot, pair):
    one = base + ((2 * pair * 8 + slot) // 2) * 128
    two = base + (((2 * pair + 1) * 8 + slot) // 2) * 128
    left = arr[:, one : one + 128].astype(F32)
    right = arr[:, two : two + 128].astype(F32)
    lane = lax.broadcasted_iota(jnp.int32, left.shape, 1)
    if slot % 2 == 0:
        return jnp.where(lane < 64, left, pltpu.roll(right, 64, 1)).astype(LOW)
    return jnp.where(lane < 64, pltpu.roll(left, 64, 1), right).astype(LOW)


def ema_forward(factor, gain, source, out):
    steps = source.shape[0]

    def step(t, states):
        column = source[t]
        new = []
        terms = []
        for j in range(STATES):
            state = factor[j] * states[j] + column
            new.append(state)
            terms.append(gain[j] * state)
        while len(terms) > 1:
            terms = [terms[i] + terms[i + 1] for i in range(0, len(terms), 2)]
        out[t] = terms[0]
        return tuple(new)

    zero = jnp.zeros(source.shape[1:], F32)
    lax.fori_loop(0, steps, step, (zero,) * STATES)


def ema_backward(fac, gain, nrm, pull_ref, factor_sum, gain_sum, out):
    steps = nrm.shape[0]
    zero = jnp.zeros(nrm.shape[1:], F32)
    group = 4
    for base in range(0, STATES, group):

        def step(t, carry):
            at = steps - 1 - t
            column = nrm[at]
            pull = pull_ref[at]
            new = []
            terms = []
            for k in range(group):
                state, slope, by_factor, by_gain = carry[4 * k : 4 * k + 4]
                f = fac[base + k]
                slope = f * slope + state
                state = f * state + pull
                new += [state, slope, by_factor + column * slope, by_gain + column * state]
                terms.append(gain[base + k] * state)
            total = (terms[0] + terms[1]) + (terms[2] + terms[3])
            out[at] = total if base == 0 else out[at] + total
            return tuple(new)

        done = lax.fori_loop(0, steps, step, (zero,) * (4 * group))
        for k in range(group):
            factor_sum[base + k] = done[4 * k + 2]
            gain_sum[base + k] = done[4 * k + 3]


class PlaneGather:
    def __init__(self, net, src, dst):
        z, y, x, c = here()
        self.net, self.src, self.dst = net, src, dst
        self.base = net.take(7)
        self.me = slot_of(y, x, c)

    def near(self, k):
        z, y, x, c = here()
        yy, xx = chip_of(k)
        return self.net.make(self.base + k - 1, self.src, self.dst.at[self.me], device(z, yy, xx, c))

    def twin(self, k):
        z, y, x, c = here()
        yy, xx = chip_of(k)
        block = self.dst.at[slot_of(yy, xx, c)]
        return self.net.make(self.base + 3 + k, block, block, device(z, y, x, 1 - c))

    def start(self, last=True):
        self.dst[self.me] = self.src[...]
        self.twin(0).start()
        for k in (1, 2, 3) if last else (1, 2):
            self.near(k).start()

    def start_last(self):
        self.near(3).start()

    def take_near(self, k):
        self.near(k).wait_recv()
        self.twin(k).start()

    def take_twin(self, k):
        self.twin(k).wait_recv()

    def take_rest(self):
        for k in (1, 2, 3):
            self.take_near(k)
        for k in range(4):
            self.take_twin(k)

    def finish(self):
        for k in (1, 2, 3):
            self.near(k).wait_send()
        for k in range(4):
            self.twin(k).wait_send()


def chip_of(k):
    z, y, x, c = here()
    return (y + k // 2) % 2, (x + k % 2) % 2


class PlaneSum:
    def __init__(self, net, part, got, sent, far, total, pairs, keep):
        self.net = net
        self.part, self.got, self.sent, self.far, self.total = part, got, sent, far, total
        self.pairs, self.keep = pairs, keep
        self.base = net.take(8)

    def inner(self, k):
        z, y, x, c = here()
        return self.net.make(self.base + k, self.part.at[k], self.got.at[k], device(z, y, x, 1 - c))

    def outer(self, k):
        z, y, x, c = here()
        yy, xx = chip_of(k)
        return self.net.make(self.base + 3 + k, self.sent.at[k - 1], self.far.at[k - 1], device(z, yy, xx, c))

    def give(self, k):
        z, y, x, c = here()
        self.part[k] = self.pairs[1 - c].astype(self.part.dtype)
        self.inner(k).start()

    def hold(self):
        z, y, x, c = here()
        self.keep[...] = self.pairs[c]

    def pair(self, k):
        self.inner(k).wait_recv()
        both = self.keep[...] + self.got[k].astype(F32)

        @pl.when(k == 0)
        def _():
            self.total[...] = both

        @pl.when(k > 0)
        def _():
            self.sent[k - 1] = both.astype(self.sent.dtype)

        self.leave(k)

    def leave(self, k):
        @pl.when(k > 0)
        def _():
            self.outer(k).start()

    def run(self, make):
        @pl.loop(0, 4)
        def _(i):
            make(3 - i)
            self.give(3 - i)

            @pl.when(i > 0)
            def _():
                self.pair(4 - i)

            self.hold()

        self.pair(0)

    def settle(self):
        @pl.loop(0, 4)
        def _(k):
            self.inner(k).wait_send()

    def finish(self):
        @pl.loop(1, 4)
        def _(k):
            self.outer(k).wait()
            self.total[...] = self.total[...] + self.far[k - 1].astype(F32)


class RelayedSum(PlaneSum):
    def half(self, h):
        z, y, x, c = here()
        yy, xx = chip_of(1 + h)
        rows = pl.ds(h * 64, 64)
        return self.net.make(
            self.base + 6 + h, self.sent.at[2, rows], self.far.at[2, rows], device(z, yy, xx, c)
        )

    def leave(self, k):
        @pl.when(k == 3)
        def _():
            self.half(0).start()
            self.half(1).start()

    def relay(self):
        for h in range(2):
            self.half(h).wait_recv()
            at = 1 - h
            rows = slice(h * 64, (h + 1) * 64)
            self.sent[at, rows] = (self.sent[at, rows].astype(F32) + self.far[2, rows].astype(F32)).astype(LOW)
            self.outer(at + 1).start()

    def finish(self):
        for k in (1, 2):
            self.half(k - 1).wait_send()
            self.outer(k).wait()
        self.total[...] = self.total[...] + self.far[0].astype(F32) + self.far[1].astype(F32)


class LineGather:
    def __init__(self, net, buf):
        z, y, x, c = here()
        near, mirror, _ = line_peers(z)
        self.inside = z % 3 > 0
        relayed = (2 * z) % 3 + 3 * (z // 3)
        self.first = net.make(net.take(1), buf.at[z], buf.at[z], device(near, y, x, c))
        self.second = net.make(net.take(1), buf.at[z], buf.at[z], device(mirror, y, x, c))
        self.third = net.make(net.take(1), buf.at[relayed], buf.at[relayed], device((3 * z + 2) % 5, y, x, c))

    def start(self):
        self.first.start()
        self.second.start()

        @pl.when(jnp.logical_not(self.inside))
        def _():
            self.third.start()

    def relay(self):
        @pl.when(self.inside)
        def _():
            self.second.wait_recv()
            self.third.start()

    def finish(self):
        self.first.wait()
        self.second.wait_send()

        @pl.when(jnp.logical_not(self.inside))
        def _():
            self.second.wait_recv()

        self.third.wait()


class LineSum:
    def __init__(self, net, buf, got, out):
        z, y, x, c = here()
        near, mirror, across = line_peers(z)
        self.buf, self.got, self.out = buf, got, out
        self.inside = z % 3 > 0
        self.relayed = (2 * z) % 3 + 3 * (z // 3)
        self.first = net.make(net.take(1), buf.at[across], got.at[0], device((2 * z + 1) % 5, y, x, c))
        self.second = net.make(net.take(1), buf.at[near], got.at[1], device(near, y, x, c))
        self.third = net.make(net.take(1), buf.at[mirror], got.at[2], device(mirror, y, x, c))

    def run(self, make):
        z, y, x, c = here()

        @pl.loop(0, 4)
        def _(i):
            bits = (2 + 3 * i) % 4
            make((z // 2 + bits // 2) % 2 * 2 + (z + bits) % 2)

            @pl.when(i == 0)
            def _():
                self.first.start()

            @pl.when(i == 1)
            def _():
                self.second.start()

        self.start_last()

    def start(self, last=True):
        self.first.start()
        self.second.start()
        if last:
            self.start_last()

    def start_last(self):
        @pl.when(jnp.logical_not(self.inside))
        def _():
            self.third.start()

    def relay(self):
        @pl.when(self.inside)
        def _():
            self.first.wait_recv()
            self.buf[self.relayed] = (self.buf[self.relayed].astype(F32) + self.got[0].astype(F32)).astype(LOW)
            self.third.start()

    def finish(self):
        z, y, x, c = here()
        self.first.wait_send()
        self.second.wait()
        self.third.wait()
        total = self.buf[z].astype(F32) + self.got[1].astype(F32) + self.got[2].astype(F32)
        self.out[...] = total.reshape(self.out.shape).astype(self.out.dtype)

        @pl.when(jnp.logical_not(self.inside))
        def _():
            self.first.wait_recv()
            whole = total + self.got[0].astype(F32)
            self.out[...] = whole.reshape(self.out.shape).astype(self.out.dtype)


class Spread:
    def __init__(self, net, sends, whole):
        self.net, self.whole = net, whole
        self.line = net.take(1)
        for src, dst, target in sends:
            net.make(self.line, src, dst, target).start()

    def finish(self):
        pltpu.make_async_copy(self.whole, self.whole, self.net.recv.at[self.line]).wait()
        pltpu.make_async_copy(self.whole, self.whole, self.net.send.at[self.line]).wait()


def spread_plane(net, src, dst):
    z, y, x, c = here()
    me = slot_of(y, x, c)
    dst[me] = src[...]
    sends = [(src, dst.at[me], device(z, *peer)) for peer in plane_peers(y, x, c)]
    return Spread(net, sends, dst.at[pl.ds(0, 7)])


def spread_column(net, buf):
    z, y, x, c = here()
    block = buf.at[:, slot_of(y, x, c)]
    sends = [(block, block, device(z, *peer)) for peer in plane_peers(y, x, c)]
    return Spread(net, sends, buf.at[:, pl.ds(0, 7)])


def swap_plane(net, src, dst):
    z, y, x, c = here()
    me = slot_of(y, x, c)
    dst[me] = src[me]
    sends = [(src.at[slot_of(*peer)], dst.at[me], device(z, *peer)) for peer in plane_peers(y, x, c)]
    return Spread(net, sends, dst.at[pl.ds(0, 7)])


def spread_line(net, buf, part=None):
    z, y, x, c = here()
    block = buf.at[z] if part is None else buf.at[z, part]
    whole = buf.at[pl.ds(0, 3)] if part is None else buf.at[pl.ds(0, 3), part]
    return Spread(net, [(block, block, device(other, y, x, c)) for other in line_peers(z)], whole)


def swap_line(net, src, dst):
    z, y, x, c = here()
    dst[z] = src[z]
    sends = [(src.at[other], dst.at[z], device(other, y, x, c)) for other in line_peers(z)]
    return Spread(net, sends, dst.at[pl.ds(0, 3)])


class ChipSwap:
    def __init__(self, net, src, dst):
        z, y, x, c = here()
        self.net, self.src, self.dst = net, src, dst
        self.me = slot_of(y, x, c)
        self.base = net.take(8)

    def copy(self, k, twin):
        z, y, x, c = here()
        yy, xx = chip_of(k)
        cc = (c + twin) % 2
        return self.net.make(
            self.base + 2 * k + twin, self.src.at[slot_of(yy, xx, cc)], self.dst.at[self.me], device(z, yy, xx, cc)
        )

    def start(self):
        self.dst[self.me] = self.src[self.me]
        self.copy(0, 1).start()
        for k in (1, 2, 3):
            for twin in range(2):
                self.copy(k, twin).start()

    def take(self, k):
        self.copy(k, 1).wait_recv()

        @pl.when(k > 0)
        def _():
            self.copy(k, 0).wait_recv()

    def finish(self):
        self.copy(0, 1).wait_send()
        for k in (1, 2, 3):
            for twin in range(2):
                self.copy(k, twin).wait_send()


def row_mean(value):
    return jnp.mean(value, axis=-1, keepdims=True)


def standardized(value):
    centred = value - row_mean(value)
    inverse = lax.rsqrt(row_mean(centred * centred) + EPS)
    return centred * inverse, inverse


def norm_back(grad, xhat, inverse, gain):
    scaled = grad * gain
    return inverse * (scaled - row_mean(scaled) - xhat * row_mean(scaled * xhat))


def block_scores_of(zeta, heads, shift, table):
    query_low = (zeta * heads[0:1] + shift).astype(LOW)
    key_low = (zeta * heads[1:2]).astype(LOW)
    scores = cols_dot(query_low, key_low) * (zeta.shape[1] ** (-0.5)) + table[...]
    row = lax.broadcasted_iota(jnp.int32, scores.shape, 0)
    col = lax.broadcasted_iota(jnp.int32, scores.shape, 1)
    scores = jnp.where(row >= col, scores, NEG)
    top = jnp.max(scores, axis=-1, keepdims=True)
    log_total = top + jnp.log(jnp.sum(jnp.exp(scores - top), axis=-1, keepdims=True))
    return query_low, key_low, jnp.exp(scores - log_total)


def mirror_matrix(size):
    row = lax.broadcasted_iota(jnp.int32, (size, size), 0)
    col = lax.broadcasted_iota(jnp.int32, (size, size), 1)
    return jnp.where(row + col == size - 1, 1.0, 0.0).astype(LOW)


def column_of(line):
    size = line.shape[1]
    row = lax.broadcasted_iota(jnp.int32, (size, size), 0)
    col = lax.broadcasted_iota(jnp.int32, (size, size), 1)
    return jnp.sum(jnp.where(row == col, line, 0.0), axis=1, keepdims=True)


def cols_at(index, size):
    return pl.ds(pl.multiple_of(index * size, size), size)


def put_rows(sums, at, wide):
    sums[at : at + 1] = jnp.sum(wide, axis=0, keepdims=True)


ROWS = 128
WIDE = 1024
ALL = (8, ROWS, WIDE)
OWN = (ROWS, WIDE)


ANY = pl.BlockSpec(memory_space=pl.ANY)


class Inputs:
    x_in = ANY
    cot_in = ANY
    wv_in = ANY
    wm_in = ANY
    wo_in = ANY
    we_in = ANY
    wr_in = ANY
    ema = VMEM
    norm_gains = VMEM
    norm_biases = VMEM
    head_gains = VMEM
    query_bias = VMEM
    position_bias = VMEM
    lens = VMEM


class Results:
    output_hbm = (ROWS, WIDE), LOW
    grad_inputs_hbm = (ROWS, WIDE), F32
    grad_out_hbm = (64, WIDE), F32
    grad_reduce_hbm = (ROWS, WIDE), F32
    ge_hbm = (8, 32, 512), LOW
    ga_hbm = (8, 32, 768), LOW
    gz_hbm = (4, 32, 128), F32
    sums_hbm = (8, 40, 128), F32
    square_hbm = (4, 8, 128), F32


class Scratch:
    output = (ROWS, WIDE), LOW
    grad_inputs = (ROWS, WIDE), F32
    grad_out = (64, WIDE), F32
    grad_reduce = (ROWS, WIDE), F32
    ge_all = (8, 32, 512), LOW
    ga_all = (8, 32, 768), LOW
    gz_line = (4, 32, 128), F32
    sums_all = (8, 40, 128), F32
    square_line = (4, 8, 128), F32
    x = OWN, LOW
    cot = OWN, LOW
    wv = (32, 2048), LOW
    wm = (32, 4224), LOW
    we_own = (32, 4096), LOW
    small_wide = (32, 128), F32
    wz = (4, 8, 32, 128), LOW
    inverse = (ROWS, 128), F32
    small_all = (4, 8, 32, 128), LOW
    prm = (72, WIDE), F32
    blocks_a = (8, 32, 768), LOW
    blocks_e = (8, 32, 512), LOW
    wa = (4, 8, 32, 768), LOW
    wo = (4, 64, WIDE), LOW
    we = (4, 8, 32, 512), LOW
    wr = (4, ROWS, WIDE), LOW
    table = (128, 128), F32
    heads = (8, 128), F32
    own_low = OWN, LOW
    normed_all = ALL, LOW
    mixed_all = ALL, LOW
    cot_all = ALL, LOW
    two_all = ALL, LOW
    hid_all = ALL, LOW
    fac = (16, 8, 128), F32
    gain = (16, 8, 128), F32
    fac_sum = (16, 8, 128), F32
    gain_sum = (16, 8, 128), F32
    nrm = (ROWS, 8, 128), F32
    tall = (ROWS, 8, 128), F32
    tall_out = (ROWS, 8, 128), F32
    pre = OWN, F32
    value_pre = (8, ROWS, 256), F32
    value_low = (8, ROWS, 256), LOW
    zeta_pre = (8, ROWS, 128), F32
    weights_low = (8, ROWS, 128), LOW
    attended = (8, ROWS, 256), F32
    reset_pre = (8, ROWS, 256), F32
    gated = (8, ROWS, 256), LOW
    work = OWN, F32
    hidden_pre = OWN, F32
    update_pre = OWN, F32
    first = OWN, F32
    update_part = (8, ROWS, 128), LOW
    update_all = (8, ROWS, 128), LOW
    part = (4, ROWS, WIDE), LOW
    got = (4, ROWS, WIDE), LOW
    sent = (3, ROWS, WIDE), LOW
    far = (3, ROWS, WIDE), LOW
    got_b = (4, ROWS, WIDE), LOW
    sent_b = (3, ROWS, WIDE), LOW
    far_b = (3, ROWS, WIDE), LOW
    got_c = (4, ROWS, WIDE), LOW
    sent_c = (3, ROWS, WIDE), LOW
    far_c = (3, ROWS, WIDE), LOW
    pairs = (2, ROWS, WIDE), F32
    grad_two = OWN, F32
    scores_pairs = (2, ROWS, 128), F32
    scores_keep = (ROWS, 128), F32
    expand_pre = (8, ROWS, 512), F32
    expand_low = (8, ROWS, 512), LOW
    grad_pre = (8, ROWS, 512), LOW
    branch = OWN, F32
    value_back = (8, ROWS, 256), LOW
    mixture_back = (8, ROWS, 512), LOW
    scores_part = (4, ROWS, 128), F32
    scores_got = (4, ROWS, 128), F32
    scores_sent = (3, ROWS, 128), F32
    scores_far = (3, ROWS, 128), F32
    scores_sum = (ROWS, 128), F32
    zeta_own = (ROWS, 128), LOW
    zeta_all = (8, ROWS, 128), LOW
    gr = (4, ROWS, WIDE), LOW
    gr_got = (3, ROWS, WIDE), LOW
    ge = (4, 256, 512), LOW
    ge_got = (3, 256, 512), LOW
    ge_sum = (8, 32, 512), LOW
    go = (4, 64, WIDE), LOW
    go_got = (3, 64, WIDE), LOW
    ga = (4, 256, 768), LOW
    ga_got = (3, 256, 768), LOW
    ga_sum = (8, 32, 768), LOW
    gz = (4, 8, 32, 128), F32
    gz_own = (4, 32, 128), F32
    sums = (40, WIDE), F32
    sum_blocks = (8, 40, 128), F32
    sum_parts = (8, 40, 128), F32
    sum_rows = (4, 40, 128), F32
    sum_cols = (40, 128), F32
    square_own = (8, 128), F32
    square_all = (8, 8, 128), F32


class Lines:
    send = (LINES,)
    recv = (LINES,)
    load = (7,)
    store = (9,)


def fields(group):
    return {name: item for name, item in vars(group).items() if not name.startswith("_")}


class Refs:
    def __init__(self, refs):
        names = [name for group in (Inputs, Results, Scratch, Lines) for name in fields(group)]
        for name, ref in zip(names, refs, strict=True):
            setattr(self, name, ref)


class Stores:
    def __init__(self, sems):
        self.sems, self.made = sems, []

    def put(self, src, dst):
        copy = pltpu.make_async_copy(src, dst, self.sems.at[len(self.made)])
        copy.start()
        self.made.append(copy)

    def finish(self):
        for copy in self.made:
            copy.wait()


def layer_kernel(*refs):
    r = Refs(refs)
    net = Net(r.send, r.recv)
    z, y, x, c = here()
    me = slot_of(y, x, c)
    twin = device(z, y, x, 1 - c)
    tokens = 8 * ROWS
    stores = Stores(r.store)
    loads = [
        pltpu.make_async_copy(src, dst, r.load.at[line])
        for line, (src, dst) in enumerate(
            (
                (r.wm_in, r.wm), (r.wv_in, r.wv), (r.wo_in, r.wo.at[z]), (r.x_in, r.x), (r.we_in, r.we_own),
                (r.wr_in, r.wr.at[z]), (r.cot_in, r.cot),
            )
        )
    ]
    for load in loads:
        load.start()
    greet()
    for load in loads:
        load.wait()

    lane = lax.broadcasted_iota(jnp.int32, (32, 128), 1)
    r.small_wide[...] = jnp.zeros((32, 128), F32)
    r.small_wide[:, 0:64] = r.ema[...].astype(F32)
    small = r.small_wide[...]
    for k in range(5):
        line = r.norm_gains[k : k + 1, :] if k < 3 else r.norm_biases[k - 3 : k - 2, :]
        small = jnp.where(lane == 64 + k, column_of(line.astype(F32)), small)
    r.small_all[z, me] = small.astype(LOW)
    small_line = spread_line(net, r.small_all, me)
    r.wz[z, me] = r.wm[:, 1024:1152]
    zeta_line = spread_line(net, r.wz, me)
    for s in range(8):
        for pair in range(2):
            r.blocks_a[s, :, pair * 128 : (pair + 1) * 128] = pick_halves(r.wv, 0, s, pair)
            r.blocks_a[s, :, 384 + pair * 128 : 512 + pair * 128] = pick_halves(r.wm, 1152, s, pair)
        r.blocks_a[s, :, 256:384] = r.wm[:, s * 128 : (s + 1) * 128]
        r.blocks_a[s, :, 640:768] = r.wm[:, 3200 + s * 128 : 3328 + s * 128]
    attn_plane = swap_plane(net, r.blocks_a, r.wa.at[z])
    out_line = LineGather(net, r.wo)
    out_line.start()
    for s in range(8):
        for zz in range(4):
            r.blocks_e[s, :, zz * 128 : (zz + 1) * 128] = r.we_own[:, (zz * 8 + s) * 128 : (zz * 8 + s + 1) * 128]
    small_line.finish()
    small_plane = spread_column(net, r.small_all)
    near_base = net.take(3)

    def near(k):
        yy, xx = chip_of(k)
        return net.make(near_base + k - 1, r.x, r.mixed_all.at[me], device(z, yy, xx, c))

    for k in (1, 2, 3):
        near(k).start()
    zeta_line.finish()
    zeta_plane = spread_column(net, r.wz)
    expand_plane = swap_plane(net, r.blocks_e, r.we.at[z])
    row = lax.broadcasted_iota(jnp.int32, OWN, 0)
    r.own_low[...] = jnp.where(row < r.lens[...], r.cot[...].astype(F32), 0.0).astype(LOW)
    cot_plane = PlaneGather(net, r.own_low, r.cot_all)
    cot_plane.start()
    r.heads[0:2] = r.head_gains[...].astype(F32)
    r.heads[2:3] = r.query_bias[...].astype(F32).reshape(1, 128)
    wide = jnp.broadcast_to(r.position_bias[...].astype(F32).reshape(1, 128), (128, 128)).astype(LOW)
    turned = jnp.dot(wide, mirror_matrix(128), preferred_element_type=F32)
    r.table[...] = pltpu.roll(turned, 1, 1, stride=1, stride_axis=0)
    out_line.relay()
    attn_plane.finish()
    attn_line = LineGather(net, r.wa)
    attn_line.start()
    small_plane.finish()

    r.prm[...] = r.small_all[...].reshape(WIDE, 128).astype(F32).T[0:72]
    damping = jax.nn.sigmoid(r.prm[0:16])
    mixing = jax.nn.sigmoid(r.prm[16:32])
    lanes_to_rows(1.0 - mixing * damping, r.fac)
    lanes_to_rows(0.25 * r.prm[48:64] * (mixing * r.prm[32:48]), r.gain)
    pair_base = net.take(8)

    def pair_normed(k):
        yy, xx = chip_of(k)
        block = r.normed_all.at[slot_of(yy, xx, c)]
        return net.make(pair_base + k, block, block, twin)

    def pair_mixed(k):
        yy, xx = chip_of(k)
        block = r.mixed_all.at[slot_of(yy, xx, c)]
        return net.make(pair_base + 4 + k, block, block, twin)

    def mix(k, tall, pre):
        yy, xx = chip_of(k)
        slot = slot_of(yy, xx, c)
        source = r.mixed_all[slot]
        xhat, _ = standardized(source.astype(F32))
        normed = xhat * r.prm[64:65] + r.prm[67:68]
        r.normed_all[slot] = normed.astype(LOW)
        pair_normed(k).start()
        lanes_to_rows(normed, tall)
        pre[...] = r.prm[65:66] * normed
        ema_forward(r.fac, r.gain, tall, r.tall_out)
        for s in range(8):
            cols = slice(s * 128, (s + 1) * 128)
            pre[:, cols] = pre[:, cols] + r.tall_out[:, s, :]
        r.mixed_all[slot] = silu(pre[...]).astype(LOW)
        pair_mixed(k).start()

    r.mixed_all[me] = r.x[...]
    mix(0, r.nrm, r.pre)

    @pl.loop(1, 4)
    def _(k):
        near(k).wait_recv()

        @pl.when(k == 3)
        def _():
            attn_line.relay()

        mix(k, r.tall, r.work)

    expand_plane.finish()
    expand_line = LineGather(net, r.we)
    expand_line.start()
    reduce_line = LineGather(net, r.wr)
    reduce_line.start()
    cot_plane.take_rest()
    cot_plane.finish()
    for k in (1, 2, 3):
        near(k).wait_send()
    for k in range(4):
        pair_normed(k).wait()
        pair_mixed(k).wait()
    zeta_plane.finish()
    out_line.finish()
    attn_line.finish()

    cand_cols = cols_at(me, 128)
    shift = r.heads[2:3]

    def weights_a(first, last):
        return r.wa[:, :, :, first:last].reshape(WIDE, last - first)

    def zeta_weights():
        return r.wz[...].reshape(WIDE, 128)

    def pair_of(k):
        yy, xx = chip_of(k)
        return pl.ds((yy * 2 + xx) * 2, 2)

    def rows_of(ref, k):
        return ref[pair_of(k)].reshape(2 * ROWS, ref.shape[2])

    def put(ref, k, value):
        ref[pair_of(k)] = value.reshape(2, ROWS, ref.shape[2]).astype(ref.dtype)

    def attend(k):
        pre = jnp.dot(rows_of(r.normed_all, k), weights_a(0, 256), preferred_element_type=F32)
        put(r.value_pre, k, pre)
        low_values = silu(pre).astype(LOW)
        put(r.value_low, k, low_values)
        mixed = rows_of(r.mixed_all, k)
        mixture = jnp.dot(mixed, weights_a(256, 768), preferred_element_type=F32)
        put(r.update_part, k, mixture[:, 0:128])
        put(r.reset_pre, k, mixture[:, 128:384])
        zeta = jnp.dot(mixed, zeta_weights(), preferred_element_type=F32)
        put(r.zeta_pre, k, zeta)
        zeta = silu(zeta)
        values = []
        weights = []
        for h in range(2):
            rows = slice(h * ROWS, (h + 1) * ROWS)
            _, _, probs = block_scores_of(zeta[rows], r.heads, shift, r.table)
            weights.append(probs.astype(LOW))
            values.append(jnp.dot(weights[h], low_values[rows], preferred_element_type=F32))
        put(r.weights_low, k, jnp.concatenate(weights, axis=0))
        mixed_values = jnp.concatenate(values, axis=0)
        put(r.attended, k, mixed_values)
        gate = (mixed_values * silu(mixture[:, 128:384])).astype(LOW)
        put(r.gated, k, gate)
        hidden = jnp.dot(gate, r.wo[...].reshape(256, WIDE), preferred_element_type=F32)
        r.pairs[...] = hidden.reshape(2, ROWS, WIDE)
        r.pairs[:, :, cand_cols] = r.pairs[:, :, cand_cols] + mixture[:, 384:512].reshape(2, ROWS, 128)

    hidden_sum = PlaneSum(net, r.part, r.got, r.sent, r.far, r.hidden_pre, r.pairs, r.work)
    hidden_sum.run(attend)
    update_plane = swap_plane(net, r.update_part, r.update_all)
    expand_line.relay()
    hidden_sum.settle()
    hidden_sum.finish()
    update_plane.finish()
    for s in range(8):
        r.update_pre[:, s * 128 : (s + 1) * 128] = r.update_all[s].astype(F32)
    stream = r.x[...].astype(F32)
    r.first[...] = stream + jax.nn.sigmoid(r.update_pre[...]) * (silu(r.hidden_pre[...]) - stream)
    xhat, _ = standardized(r.first[...])
    r.own_low[...] = (xhat * r.prm[66:67] + r.prm[68:69]).astype(LOW)
    two_plane = PlaneGather(net, r.own_low, r.two_all)
    two_plane.start()
    reduce_line.relay()
    expand_line.finish()

    def reduce_rows():
        return r.wr[...].reshape(512, WIDE)

    def expand_rows():
        return r.we[...].reshape(WIDE, 512)

    @pl.loop(0, 4)
    def _(k):
        @pl.when(k > 0)
        def _():
            two_plane.take_near(k)

        two_plane.take_twin(k)
        pre = jnp.dot(rows_of(r.two_all, k), expand_rows(), preferred_element_type=F32)
        put(r.expand_pre, k, pre)
        put(r.expand_low, k, silu(pre))

    two_plane.finish()
    reduce_sum = LineSum(net, r.gr, r.gr_got, r.grad_reduce)
    expand_sum = LineSum(net, r.ge, r.ge_got, r.ge_sum)

    def reduce_grad(zz):
        r.gr[zz] = rows_dot(
            r.expand_low[:, :, cols_at(zz, 128)].reshape(tokens, 128), r.cot_all[...].reshape(tokens, WIDE)
        ).astype(LOW)

    reduce_sum.run(reduce_grad)
    reduce_line.finish()

    def expand_back(k):
        grad = (cols_dot(rows_of(r.cot_all, k), reduce_rows()) * silu_slope(rows_of(r.expand_pre, k))).astype(LOW)
        put(r.grad_pre, k, grad)
        r.pairs[...] = cols_dot(grad, expand_rows()).reshape(2, ROWS, WIDE)

    two_sum = PlaneSum(net, r.part, r.got, r.sent, r.far, r.grad_two, r.pairs, r.work)
    two_sum.run(expand_back)

    @pl.loop(0, 4)
    def _(zz):
        r.ge[zz] = rows_dot(
            r.two_all[:, :, cols_at(zz, 256)].reshape(tokens, 256), r.grad_pre[...].reshape(tokens, 512)
        ).astype(LOW)

    expand_sum.start()

    def branch_blocks(k):
        branch = jnp.dot(rows_of(r.expand_low, k), reduce_rows(), preferred_element_type=F32)
        r.pairs[...] = branch.reshape(2, ROWS, WIDE)

    two_sum.settle()
    branch_sum = RelayedSum(net, r.part, r.got_b, r.sent_b, r.far_b, r.branch, r.pairs, r.work)
    branch_sum.run(branch_blocks)
    reduce_sum.relay()
    valid = jnp.where(lax.broadcasted_iota(jnp.int32, (ROWS, 1), 0) < r.lens[...], 1.0, 0.0)
    update = jax.nn.sigmoid(r.update_pre[...])
    hidden = r.hidden_pre[...]
    r.work[...] = update * silu_slope(hidden)
    r.pairs[1] = (silu(hidden) - r.x[...].astype(F32)) * update * (1.0 - update)
    xhat, inverse = standardized(r.first[...])
    r.pairs[0] = xhat
    r.inverse[...] = jnp.broadcast_to(inverse, (ROWS, 128))
    two_sum.finish()

    grad_first = r.cot[...].astype(F32) * valid + norm_back(
        r.grad_two[...], r.pairs[0], r.inverse[:, 0:1], r.prm[66:67]
    )
    r.own_low[...] = (grad_first * r.work[...]).astype(LOW)
    hid_plane = PlaneGather(net, r.own_low, r.hid_all)
    hid_plane.start(last=False)
    grad_update = (grad_first * r.pairs[1]).astype(LOW)
    for s in range(8):
        r.update_part[s] = grad_update[:, s * 128 : (s + 1) * 128]
    upd_plane = ChipSwap(net, r.update_part, r.update_all)
    upd_plane.start()
    hid_plane.start_last()
    r.grad_inputs[...] = grad_first * (1.0 - jax.nn.sigmoid(r.update_pre[...]))
    put_rows(r.sums, 34, r.grad_two[...] * r.pairs[0])
    put_rows(r.sums, 36, r.grad_two[...])

    branch_sum.settle()
    expand_sum.relay()
    scores_plane = PlaneSum(
        net, r.scores_part, r.scores_got, r.scores_sent, r.scores_far, r.scores_sum, r.scores_pairs, r.scores_keep
    )
    mixed_sum = PlaneSum(net, r.part, r.got, r.sent, r.far, r.grad_two, r.pairs, r.work)

    def attend_back(k):
        gate_grad = cols_dot(rows_of(r.hid_all, k), r.wo[...].reshape(256, WIDE))
        pre = rows_of(r.reset_pre, k)
        low_grad = (gate_grad * silu(pre)).astype(LOW)
        low_values = rows_of(r.value_low, k)
        weights = rows_of(r.weights_low, k)
        backs = []
        for h in range(2):
            rows = slice(h * ROWS, (h + 1) * ROWS)
            r.scores_pairs[h] = cols_dot(low_grad[rows], low_values[rows])
            backs.append(rows_dot(weights[rows], low_grad[rows]))
        put(r.value_back, k, jnp.concatenate(backs, axis=0) * silu_slope(rows_of(r.value_pre, k)))
        pair = pair_of(k)
        r.mixture_back[pair, :, 0:128] = r.update_all[pair]
        r.mixture_back[pair, :, 128:384] = (
            (gate_grad * rows_of(r.attended, k) * silu_slope(pre)).astype(LOW).reshape(2, ROWS, 256)
        )
        r.mixture_back[pair, :, 384:512] = r.hid_all[pair, :, cand_cols]
        mixture = rows_of(r.mixture_back, k)
        mixed = cols_dot(mixture, weights_a(256, 768))
        r.pairs[...] = mixed.reshape(2, ROWS, WIDE)

    @pl.loop(0, 4)
    def _(k):
        @pl.when(k > 0)
        def _():
            hid_plane.take_near(k)

        hid_plane.take_twin(k)
        upd_plane.take(k)
        attend_back(k)
        scores_plane.give(k)
        mixed_sum.give(k)

        @pl.when(k > 0)
        def _():
            scores_plane.pair(k - 1)
            mixed_sum.pair(k - 1)

        scores_plane.hold()
        mixed_sum.hold()

    scores_plane.pair(3)
    mixed_sum.pair(3)
    hid_plane.finish()
    upd_plane.finish()
    out_sum = LineSum(net, r.go, r.go_got, r.grad_out)
    attn_sum = LineSum(net, r.ga, r.ga_got, r.ga_sum)

    def attn_grad(zz):
        cols = cols_at(zz, 256)
        r.ga[zz, :, 0:256] = rows_dot(
            r.normed_all[:, :, cols].reshape(tokens, 256), r.value_back[...].reshape(tokens, 256)
        ).astype(LOW)
        r.ga[zz, :, 256:768] = rows_dot(
            r.mixed_all[:, :, cols].reshape(tokens, 256), r.mixture_back[...].reshape(tokens, 512)
        ).astype(LOW)

    attn_sum.run(attn_grad)

    @pl.loop(0, 4)
    def _(t):
        cols = cols_at(t, 256)
        grad = rows_dot(
            r.gated[...].reshape(tokens, 256), r.hid_all[:, :, cols].reshape(tokens, 256)
        ).astype(LOW)
        for zz in range(4):
            r.go[zz, :, cols] = grad[zz * 64 : (zz + 1) * 64]


    reduce_sum.finish()
    stores.put(r.grad_reduce, r.grad_reduce_hbm)
    expand_sum.finish()
    mixed_sum.settle()
    normed_sum = RelayedSum(net, r.part, r.got_c, r.sent_c, r.far_c, r.hidden_pre, r.pairs, r.work)

    def normed_blocks(k):
        normed = cols_dot(rows_of(r.value_back, k), weights_a(0, 256))
        r.pairs[...] = normed.reshape(2, ROWS, WIDE)

    normed_sum.run(normed_blocks)

    scores_plane.settle()
    scores_plane.finish()
    grad_weights = r.scores_sum[...]
    zeta_own_pre = r.zeta_pre[me]
    zeta = silu(zeta_own_pre)
    query_low, key_low, probs = block_scores_of(zeta, r.heads, shift, r.table)
    grad_scores = (probs * (grad_weights - jnp.sum(probs * grad_weights, axis=-1, keepdims=True))).astype(LOW)
    scale = zeta.shape[1] ** (-0.5)
    grad_query = jnp.dot(grad_scores, key_low, preferred_element_type=F32) * scale
    grad_key = rows_dot(grad_scores, query_low) * scale
    skewed = pltpu.roll(
        jnp.dot(grad_scores, mirror_matrix(ROWS), preferred_element_type=F32), 1, 1, stride=1, stride_axis=0
    )
    r.sums[37:40] = jnp.zeros((3, WIDE), F32)
    r.sums[37:38, 0:128] = jnp.sum(grad_query * zeta, axis=0, keepdims=True)
    r.sums[37:38, 128:256] = jnp.sum(grad_key * zeta, axis=0, keepdims=True)
    r.sums[37:38, 256:384] = jnp.sum(grad_query, axis=0, keepdims=True)
    r.sums[37:38, 384:512] = jnp.sum(skewed, axis=0, keepdims=True)
    grad_zeta = grad_query * r.heads[0:1] + grad_key * r.heads[1:2]
    r.zeta_own[...] = (grad_zeta * silu_slope(zeta_own_pre)).astype(LOW)
    zeta_tokens = spread_plane(net, r.zeta_own, r.zeta_all)

    normed_sum.relay()
    branch_sum.relay()
    mixed_sum.finish()
    grad_mixed = r.grad_two[...] + cols_dot(r.zeta_own[...], zeta_weights())
    pull = grad_mixed * silu_slope(r.pre[...])
    lanes_to_rows(pull, r.tall)
    r.pre[...] = pull
    attn_sum.relay()
    ema_backward(r.fac, r.gain, r.nrm, r.tall, r.fac_sum, r.gain_sum, r.tall_out)
    for s in range(8):
        cols = slice(s * 128, (s + 1) * 128)
        r.sums[0:16, cols] = r.fac_sum[:, s, :]
        r.sums[16:32, cols] = r.gain_sum[:, s, :]
        r.sums[33:34, cols] = jnp.sum(r.pre[:, cols] * r.nrm[:, s, :], axis=0, keepdims=True)
    zeta_tokens.finish()
    r.gz[...] = rows_dot(
        r.mixed_all[...].reshape(tokens, WIDE), r.zeta_all[...].reshape(tokens, 128)
    ).reshape(4, 8, 32, 128)
    for zz in range(4):
        r.gz_own[zz] = r.gz[zz, me]
    zeta_grad = swap_line(net, r.gz_own, r.gz_line)
    normed_sum.settle()
    normed_sum.finish()
    for s in range(8):
        cols = slice(s * 128, (s + 1) * 128)
        r.hidden_pre[:, cols] = r.hidden_pre[:, cols] + r.pre[:, cols] * r.prm[65:66, cols] + r.tall_out[:, s, :]
    xhat_one, inverse_one = standardized(r.x[...].astype(F32))
    grad_one = r.hidden_pre[...]
    put_rows(r.sums, 32, grad_one * xhat_one)
    put_rows(r.sums, 35, grad_one)
    r.grad_inputs[...] = r.grad_inputs[...] + norm_back(grad_one, xhat_one, inverse_one, r.prm[64:65])

    stores.put(r.grad_inputs, r.grad_inputs_hbm)

    for s in range(8):
        r.sum_blocks[s] = r.sums[:, s * 128 : (s + 1) * 128]
    small_sum = swap_plane(net, r.sum_blocks, r.sum_parts)
    ge_plane = swap_plane(net, r.ge_sum, r.ge_all)
    small_sum.finish()
    whole = r.sum_parts[0]
    for s in range(1, 8):
        whole = whole + r.sum_parts[s]
    r.sum_rows[z] = whole
    small_rows = spread_line(net, r.sum_rows)
    out_sum.start(last=False)
    branch_sum.finish()
    stream = r.x[...].astype(F32)
    first = r.first[...]
    branch = r.branch[...]
    r.output[...] = ((first + branch) * valid).astype(LOW)
    stores.put(r.output, r.output_hbm)
    r.square_own[...] = jnp.zeros((8, 128), F32)
    for k, item in enumerate((stream, first - stream, branch)):
        squares = jnp.sum(valid * item * item, axis=0, keepdims=True)
        r.square_own[k : k + 1] = jnp.broadcast_to(jnp.sum(squares, axis=1, keepdims=True), (1, 128))
    r.square_own[3:4] = jnp.broadcast_to(jnp.sum(valid, axis=0, keepdims=True), (1, 128))
    square_plane = spread_plane(net, r.square_own, r.square_all)
    attn_sum.finish()
    ga_plane = swap_plane(net, r.ga_sum, r.ga_all)
    small_rows.finish()
    r.sum_cols[...] = (r.sum_rows[0] + r.sum_rows[1]) + (r.sum_rows[2] + r.sum_rows[3])
    small_cols = spread_plane(net, r.sum_cols, r.sums_all)
    out_sum.start_last()
    out_sum.relay()
    square_plane.finish()
    squares = r.square_all[0]
    for s in range(1, 8):
        squares = squares + r.square_all[s]
    r.square_line[z] = squares
    square_rows = spread_line(net, r.square_line)
    ge_plane.finish()
    stores.put(r.ge_all, r.ge_hbm)
    zeta_grad.finish()
    stores.put(r.gz_line, r.gz_hbm)
    ga_plane.finish()
    stores.put(r.ga_all, r.ga_hbm)
    small_cols.finish()
    stores.put(r.sums_all, r.sums_hbm)
    square_rows.finish()
    stores.put(r.square_line, r.square_hbm)
    out_sum.finish()
    stores.put(r.grad_out, r.grad_out_hbm)
    stores.finish()


def layer(*operands):
    return pl.pallas_call(
        layer_kernel,
        name="layer",
        out_shape=[jax.ShapeDtypeStruct(*item) for item in fields(Results).values()],
        in_specs=list(fields(Inputs).values()),
        out_specs=[ANY] * len(fields(Results)),
        scratch_shapes=[pltpu.VMEM(*item) for item in fields(Scratch).values()]
        + [pltpu.SemaphoreType.DMA(item) for item in fields(Lines).values()],
        compiler_params=pltpu.CompilerParams(
            collective_id=1, has_side_effects=True, vmem_limit_bytes=60 << 20
        ),
    )(*operands)


def place_halves(blocks, base, q, out, start):
    lane = lax.broadcasted_iota(jnp.int32, (blocks.shape[1], 128), 1)
    for zz in range(4):
        at = base + (zz // 2) * 128
        left = blocks[2 * q, :, at : at + 128].astype(F32)
        right = blocks[2 * q + 1, :, at : at + 128].astype(F32)
        if zz % 2:
            left = pltpu.roll(left, 64, 1)
        else:
            right = pltpu.roll(right, 64, 1)
        to = start + (zz * 4 + q) * 128
        out[:, to : to + 128] = jnp.where(lane < 64, left, right)


def outputs_kernel(
    output, grad_inputs, grad_out, grad_reduce, ge_all, ga_all, gz_line, sums_all, square_line, ema,
    output_o, grad_inputs_o, values_o, mix_o, out_o, expand_o, reduce_o, ema_o, gains_o, biases_o, heads_o,
    shift_o, position_o, rms_o, turned,
):
    output_o[...] = output[...]
    grad_inputs_o[...] = grad_inputs[...]
    out_o[...] = grad_out[...]
    reduce_o[...] = grad_reduce[...]
    for s in range(8):
        for zz in range(4):
            at = (zz * 8 + s) * 128
            expand_o[:, at : at + 128] = ge_all[s, :, zz * 128 : (zz + 1) * 128].astype(F32)
        mix_o[:, s * 128 : (s + 1) * 128] = ga_all[s, :, 256:384].astype(F32)
        mix_o[:, 3200 + s * 128 : 3328 + s * 128] = ga_all[s, :, 640:768].astype(F32)
    mix_o[:, 1024:1152] = (gz_line[0] + gz_line[1]) + (gz_line[2] + gz_line[3])
    for q in range(4):
        place_halves(ga_all, 0, q, values_o, 0)
        place_halves(ga_all, 384, q, mix_o, 1152)
    mine = sums_all[lax.axis_index("dp")]
    mine = pltpu.roll(mine, (128 - 32 * lax.axis_index("fsdp")) % 128, 1)
    turned[0:40] = mine
    turned[40:128] = jnp.zeros((88, 128), F32)
    gains_o[...] = turned[32:35, 0:32]
    biases_o[...] = turned[35:37, 0:32]
    flipped = turned[...].T
    raw = ema[...].astype(F32)
    damping = jax.nn.sigmoid(raw[:, 0:16])
    mixing = jax.nn.sigmoid(raw[:, 16:32])
    expand = raw[:, 32:48]
    project = raw[:, 48:64]
    by_factor = flipped[0:32, 0:16] * (0.25 * project * mixing * expand)
    by_gain = flipped[0:32, 16:32]
    by_inflow = 0.25 * project * by_gain
    ema_o[:, 0:16] = -by_factor * mixing * damping * (1.0 - damping)
    ema_o[:, 16:32] = (by_inflow * expand - by_factor * damping) * mixing * (1.0 - mixing)
    ema_o[:, 32:48] = by_inflow * mixing
    ema_o[:, 48:64] = 0.25 * mixing * expand * by_gain
    heads_o[0:1] = sums_all[0, 37:38]
    heads_o[1:2] = sums_all[1, 37:38]
    shift_o[...] = sums_all[2, 37]
    position_o[...] = sums_all[3, 37]
    squares = (square_line[0] + square_line[1]) + (square_line[2] + square_line[3])
    roots = [jnp.sqrt(squares[k : k + 1] / (squares[3:4] * WIDE)) for k in range(3)]
    col = lax.broadcasted_iota(jnp.int32, (1, 128), 1)
    line = jnp.where(col == 0, roots[0], jnp.where(col == 1, roots[1], roots[2]))
    rms_o[...] = line[0, 0:3]


def outputs(parts, ema_params):
    shapes = (
        ((ROWS, WIDE), LOW), ((ROWS, WIDE), F32), ((32, 2048), F32), ((32, 4224), F32), ((64, WIDE), F32),
        ((32, 4096), F32), ((ROWS, WIDE), F32), ((32, 64), F32), ((3, 32), F32), ((2, 32), F32), ((2, 128), F32),
        ((128,), F32), ((128,), F32), ((3,), F32),
    )
    return pl.pallas_call(
        outputs_kernel,
        name="outputs",
        out_shape=[jax.ShapeDtypeStruct(shape, dtype) for shape, dtype in shapes],
        in_specs=[VMEM] * 10,
        out_specs=[VMEM] * len(shapes),
        scratch_shapes=[pltpu.VMEM((128, 128), F32)],
    )(*parts, ema_params)


def on_plane(
    inputs, lengths, w_values, w_mix, w_out, w_expand, w_reduce, ema_params,
    norm_gains, norm_biases, head_gains, query_bias, position_bias, cotangent,
):
    parts = layer(
        inputs, cotangent, w_values, w_mix, w_out, w_expand, w_reduce, ema_params, norm_gains, norm_biases,
        head_gains, query_bias, position_bias, lengths,
    )
    done = outputs(parts, ema_params)
    return tuple(done)


def layer_norm(value, gain, shift):
    centre = jnp.mean(value, axis=-1, keepdims=True)
    centered = value - centre
    spread = jnp.mean(centered * centered, axis=-1, keepdims=True)
    return centered * lax.rsqrt(spread + EPS) * gain + shift


def ema_mix(normed, keep, ema_params):
    count = ema_params.shape[1] // 4
    damping = jax.nn.sigmoid(ema_params[:, :count]).T
    mixing = jax.nn.sigmoid(ema_params[:, count : 2 * count]).T
    expand = ema_params[:, 2 * count : 3 * count].T
    project = ema_params[:, 3 * count :].T
    factor = 1.0 - mixing * damping
    inflow = mixing * expand

    def advance(state, item):
        column, flag = item
        state = factor * state * flag[:, None, None] + inflow * column[:, None, :]
        return (state, 0.25 * jnp.sum(project * state, axis=1))

    start = jnp.zeros((normed.shape[0], count, normed.shape[2]), jnp.float32)
    _, smooth = lax.scan(advance, start, (jnp.swapaxes(normed, 0, 1), jnp.swapaxes(keep, 0, 1)))
    return jnp.swapaxes(smooth, 0, 1)


def layout(lengths, rows):
    ends = jnp.cumsum(lengths, axis=1)
    starts = ends - lengths
    place = lax.broadcasted_iota(jnp.int32, (lengths.shape[0], rows), 1)
    begin = jnp.any(place[:, :, None] == starts[:, None, :], axis=2) | (place == ends)
    keep = jnp.where(begin, 0.0, 1.0).astype(jnp.float32)
    valid = jnp.where(place < ends, 1.0, 0.0).astype(jnp.float32)
    return (keep, valid)


def dot_rows(left, right):
    return lax.dot_general(
        left, right, (((0,), (0,)), ((), ())), preferred_element_type=jnp.float32
    )


def dot_cols(left, right):
    return lax.dot_general(
        left, right, (((1,), (1,)), ((), ())), preferred_element_type=jnp.float32
    )


def block_scores(query_low, key_low, position, scale):
    span = query_low.shape[1]
    row = lax.broadcasted_iota(jnp.int32, (span, span), 0)
    col = lax.broadcasted_iota(jnp.int32, (span, span), 1)
    table = position[jnp.clip(row - col, 0, span - 1)]
    scores = (
        jnp.einsum("kiz,kjz->kij", query_low, key_low, preferred_element_type=jnp.float32) * scale
        + table
    )
    return jnp.where(row >= col, scores, NEG)


def diagonal_sums(grid):
    size = grid.shape[0]
    flipped = grid[:, ::-1]
    padded = jnp.pad(flipped, ((0, 0), (0, size)))
    skewed = padded.reshape(-1)[: size * (2 * size - 1)].reshape(size, 2 * size - 1)
    return jnp.sum(skewed, axis=0)[size - 1 :]


def group_rows(value):
    return lax.all_gather(value, "fsdp", axis=0, tiled=True)


def group_total(value):
    return lax.psum_scatter(value, "fsdp", scatter_dimension=0, tiled=True)


def owner_layout(grad, owners):
    return grad.reshape(owners * 8, -1)


def owner_shard(piece, columns):
    return piece.reshape(-1, columns)


def on_device(
    inputs,
    lengths,
    w_values,
    w_mix,
    w_out,
    w_expand,
    w_reduce,
    ema_params,
    norm_gains,
    norm_biases,
    head_gains,
    query_bias,
    position_bias,
    cotangent,
):
    rows, width = inputs.shape
    span = position_bias.shape[0]
    blocks = rows // span
    key_width = head_gains.shape[1]
    scale = key_width ** (-0.5)
    keep, valid = layout(lengths, rows)
    mask = valid[0][:, None]
    gathered = (
        lax.all_gather(w_values, ("dp", "fsdp"), axis=0, tiled=True),
        lax.all_gather(w_mix, ("dp", "fsdp"), axis=0, tiled=True),
        lax.all_gather(w_out, ("dp", "fsdp"), axis=0, tiled=True),
        lax.all_gather(ema_params, ("dp", "fsdp"), axis=0, tiled=True),
        lax.all_gather(norm_gains, ("dp", "fsdp"), axis=1, tiled=True),
        lax.all_gather(norm_biases, ("dp", "fsdp"), axis=1, tiled=True),
    )
    values_full, mix_full, out_full, ema_full, gains_full, biases_full = gathered
    value_width = values_full.shape[1]
    group_size = lax.axis_size("fsdp")
    data_size = lax.axis_size("dp")
    owners = group_size * data_size
    shard_rows = w_expand.shape[0]
    hidden_units = w_expand.shape[1]
    unit_block = hidden_units // (group_size * data_size)
    pieces = w_expand.reshape(shard_rows, data_size, group_size, unit_block)
    swapped = lax.all_to_all(pieces, "fsdp", split_axis=2, concat_axis=0, tiled=True)
    expand_quarter, reduce_use = (
        lax.all_gather(swapped, "dp", axis=0, tiled=True),
        lax.all_gather(w_reduce, "dp", axis=0, tiled=True),
    )
    expand_use = expand_quarter.reshape(expand_quarter.shape[0], data_size * unit_block)
    gains_f = gains_full.astype(jnp.float32)
    biases_f = biases_full.astype(jnp.float32)
    heads_f = head_gains.astype(jnp.float32)
    query_shift = query_bias.astype(jnp.float32)
    position_f = position_bias.astype(jnp.float32)
    stream = inputs.astype(jnp.float32)

    def front(source, gain, shift, omega, params):
        normed_part = layer_norm(source, gain, shift)
        smooth = ema_mix(normed_part[None], keep, params)[0]
        return (normed_part, silu(smooth + omega * normed_part))

    (normed, mixed), front_back = jax.vjp(
        front, stream, gains_f[0], biases_f[0], gains_f[1], ema_full.astype(jnp.float32)
    )
    normed_low = normed.astype(jnp.bfloat16)
    mixed_low = mixed.astype(jnp.bfloat16)
    value_pre = jnp.dot(normed_low, values_full, preferred_element_type=jnp.float32)
    value_low = silu(value_pre).astype(jnp.bfloat16)
    mixture = jnp.dot(mixed_low, mix_full, preferred_element_type=jnp.float32)
    middle = width + key_width
    upper = middle + value_width
    update = jax.nn.sigmoid(mixture[:, :width])
    zeta_pre = mixture[:, width:middle]
    zeta = silu(zeta_pre)
    reset_pre = mixture[:, middle:upper]
    reset = silu(reset_pre)
    candidate = mixture[:, upper:]
    query_low = (
        (zeta * heads_f[0] + query_shift).astype(jnp.bfloat16).reshape(blocks, span, key_width)
    )
    key_low = (zeta * heads_f[1]).astype(jnp.bfloat16).reshape(blocks, span, key_width)
    value_blocks = value_low.reshape(blocks, span, value_width)
    scores = block_scores(query_low, key_low, position_f, scale)
    log_total = jax.nn.logsumexp(scores, axis=-1, keepdims=True)
    weights_low = jnp.exp(scores - log_total).astype(jnp.bfloat16)
    attended = jnp.einsum(
        "kij,kjv->kiv", weights_low, value_blocks, preferred_element_type=jnp.float32
    ).reshape(rows, value_width)
    gated_low = (attended * reset).astype(jnp.bfloat16)
    hidden_pre = candidate + jnp.dot(gated_low, out_full, preferred_element_type=jnp.float32)
    hidden = silu(hidden_pre)
    attn_branch = update * (hidden - stream)
    first = stream + attn_branch
    normed_two, norm_back = jax.vjp(layer_norm, first, gains_f[2], biases_f[1])
    normed_two_low = normed_two.astype(jnp.bfloat16)
    ffn_rows = group_rows(normed_two_low)
    expand_pre = jnp.dot(ffn_rows, expand_use, preferred_element_type=jnp.float32)
    expand_low = silu(expand_pre).astype(jnp.bfloat16)
    branch_part = jnp.dot(expand_low, reduce_use, preferred_element_type=jnp.float32)
    branch = group_total(branch_part)
    output = ((first + branch) * mask).astype(jnp.bfloat16)
    values_back, mix_back, out_back = (
        lax.all_gather(w_values, ("dp", "fsdp"), axis=0, tiled=True),
        lax.all_gather(w_mix, ("dp", "fsdp"), axis=0, tiled=True),
        lax.all_gather(w_out, ("dp", "fsdp"), axis=0, tiled=True),
    )
    grad_out = cotangent.astype(jnp.float32) * mask
    grad_branch = grad_out.astype(jnp.bfloat16)
    grad_rows = group_rows(grad_branch)
    grad_reduce = dot_rows(expand_low, grad_rows)
    grad_expand_out = dot_cols(grad_rows, reduce_use)
    grad_expand_pre = (grad_expand_out * silu_slope(expand_pre)).astype(jnp.bfloat16)
    grad_expand = dot_rows(ffn_rows, grad_expand_pre)
    normed_two_part = dot_cols(grad_expand_pre, expand_use)
    grad_normed_two = group_total(normed_two_part)
    grad_first_norm, grad_gain_two, grad_shift_two = norm_back(grad_normed_two)
    grad_first = grad_out + grad_first_norm
    grad_direct = grad_first * (1.0 - update)
    grad_update = grad_first * (hidden - stream)
    grad_hidden_pre = grad_first * update * silu_slope(hidden_pre)
    grad_hidden_low = grad_hidden_pre.astype(jnp.bfloat16)
    grad_out_proj = dot_rows(gated_low, grad_hidden_low)
    grad_gated = dot_cols(grad_hidden_low, out_back)
    grad_attended = (grad_gated * reset).astype(jnp.bfloat16).reshape(blocks, span, value_width)
    grad_reset = grad_gated * attended
    scores_again = block_scores(query_low, key_low, position_f, scale)
    probs = jnp.exp(scores_again - log_total)
    probs_low = probs.astype(jnp.bfloat16)
    grad_weights = jnp.einsum(
        "kiv,kjv->kij", grad_attended, value_blocks, preferred_element_type=jnp.float32
    )
    grad_value = jnp.einsum(
        "kij,kiv->kjv", probs_low, grad_attended, preferred_element_type=jnp.float32
    ).reshape(rows, value_width)
    inner = jnp.sum(probs * grad_weights, axis=-1, keepdims=True)
    grad_scores = (probs * (grad_weights - inner)).astype(jnp.bfloat16)
    grad_position = diagonal_sums(jnp.sum(grad_scores.astype(jnp.float32), axis=0))
    grad_query = (
        jnp.einsum(
            "kij,kjz->kiz", grad_scores, key_low, preferred_element_type=jnp.float32
        ).reshape(rows, key_width)
        * scale
    )
    grad_key = (
        jnp.einsum(
            "kij,kiz->kjz", grad_scores, query_low, preferred_element_type=jnp.float32
        ).reshape(rows, key_width)
        * scale
    )
    grad_value_pre = (grad_value * silu_slope(value_pre)).astype(jnp.bfloat16)
    grad_values = dot_rows(normed_low, grad_value_pre)
    grad_normed = dot_cols(grad_value_pre, values_back)
    grad_zeta = grad_query * heads_f[0] + grad_key * heads_f[1]
    grad_heads = jnp.stack([jnp.sum(grad_query * zeta, axis=0), jnp.sum(grad_key * zeta, axis=0)])
    grad_query_shift = jnp.sum(grad_query, axis=0)
    grad_mixture = jnp.concatenate(
        [
            grad_update * update * (1.0 - update),
            grad_zeta * silu_slope(zeta_pre),
            grad_reset * silu_slope(reset_pre),
            grad_hidden_pre,
        ],
        axis=1,
    ).astype(jnp.bfloat16)
    grad_mix = dot_rows(mixed_low, grad_mixture)
    grad_mixed = dot_cols(grad_mixture, mix_back)
    grad_source, grad_gain_one, grad_shift_one, grad_omega, grad_ema = front_back(
        (grad_normed, grad_mixed)
    )
    grad_inputs = grad_direct + grad_source
    grad_gains = jnp.stack([grad_gain_one, grad_omega, grad_gain_two])
    grad_shifts = jnp.stack([grad_shift_one, grad_shift_two])
    summed_expand, grad_reduce_dev = (
        lax.psum_scatter(grad_expand, "dp", scatter_dimension=0, tiled=True),
        lax.psum_scatter(grad_reduce, "dp", scatter_dimension=0, tiled=True),
    )
    summed_pieces = summed_expand.reshape(group_size * shard_rows, data_size, 1, unit_block)
    owned = lax.all_to_all(summed_pieces, "fsdp", split_axis=0, concat_axis=2, tiled=True)
    grad_expand_dev = owned.reshape(shard_rows, hidden_units)
    summed_block = (
        lax.psum_scatter(
            owner_layout(grad_values, owners), ("dp", "fsdp"), scatter_dimension=0, tiled=True
        ),
        lax.psum_scatter(
            owner_layout(grad_mix, owners), ("dp", "fsdp"), scatter_dimension=0, tiled=True
        ),
        lax.psum_scatter(grad_out_proj, ("dp", "fsdp"), scatter_dimension=0, tiled=True),
        lax.psum_scatter(
            owner_layout(grad_ema, owners), ("dp", "fsdp"), scatter_dimension=0, tiled=True
        ),
        lax.psum_scatter(grad_gains, ("dp", "fsdp"), scatter_dimension=1, tiled=True),
        lax.psum_scatter(grad_shifts, ("dp", "fsdp"), scatter_dimension=1, tiled=True),
    )
    values_flat, mix_flat, grad_out_dev, ema_flat, grad_gains_dev, grad_shifts_dev = summed_block
    grad_values_dev = owner_shard(values_flat, grad_values.shape[1])
    grad_mix_dev = owner_shard(mix_flat, grad_mix.shape[1])
    grad_ema_dev = owner_shard(ema_flat, grad_ema.shape[1])
    squares = jnp.stack(
        [
            jnp.sum(mask * stream * stream),
            jnp.sum(mask * attn_branch * attn_branch),
            jnp.sum(mask * branch * branch),
        ]
    )
    square_sums, tokens_seen, heads_total, shift_total, position_total = lax.psum(
        (squares, jnp.sum(valid), grad_heads, grad_query_shift, grad_position), ("dp", "fsdp")
    )
    rms = jnp.sqrt(square_sums / (tokens_seen * width))
    return (
        output,
        grad_inputs,
        grad_values_dev,
        grad_mix_dev,
        grad_out_dev,
        grad_expand_dev,
        grad_reduce_dev,
        grad_ema_dev,
        grad_gains_dev,
        grad_shifts_dev,
        heads_total,
        shift_total,
        position_total,
        rms,
    )


def solution(mesh):
    in_specs = (
        P(("dp", "fsdp"), None),
        P(("dp", "fsdp"), None),
        P(("dp", "fsdp"), None),
        P(("dp", "fsdp"), None),
        P(("dp", "fsdp"), None),
        P(("dp", "fsdp"), None),
        P(("dp", "fsdp"), None),
        P(("dp", "fsdp"), None),
        P(None, ("dp", "fsdp")),
        P(None, ("dp", "fsdp")),
        P(),
        P(),
        P(),
        P(("dp", "fsdp"), None),
    )
    out_specs = (
        P(("dp", "fsdp"), None),
        P(("dp", "fsdp"), None),
        P(("dp", "fsdp"), None),
        P(("dp", "fsdp"), None),
        P(("dp", "fsdp"), None),
        P(("dp", "fsdp"), None),
        P(("dp", "fsdp"), None),
        P(("dp", "fsdp"), None),
        P(None, ("dp", "fsdp")),
        P(None, ("dp", "fsdp")),
        P(),
        P(),
        P(),
        P(),
    )
    planes = mesh.shape["dp"] == 8 and mesh.shape["fsdp"] == 4
    return jax.shard_map(
        on_plane if planes else on_device, mesh=mesh, in_specs=in_specs, out_specs=out_specs, check_vma=False
    )
```

```python
import jax
import jax.numpy as jnp
from jax import lax
from jax.experimental import pallas as pl
from jax.experimental.pallas import tpu as pltpu
from jax.sharding import PartitionSpec as P

EPS = 1e-05
NEG = -1e30
F32 = jnp.float32
LOW = jnp.bfloat16
MESH = pl.DeviceIdType.MESH
LINES = 130
STATES = 16


def silu(value):
    return value * jax.nn.sigmoid(value)


def silu_slope(value):
    sigma = jax.nn.sigmoid(value)
    return sigma * (1.0 + value * (1.0 - sigma))


def here():
    dp = lax.axis_index("dp")
    f = lax.axis_index("fsdp")
    return dp // 2, dp % 2, f // 2, f % 2


def device(z, y, x, c):
    return (z * 2 + y, x * 2 + c)


def slot_of(y, x, c):
    return y * 4 + x * 2 + c


def plane_peers(y, x, c):
    peers = []
    for mask in range(1, 8):
        peers.append(
            (
                1 - y if mask & 4 else y,
                1 - x if mask & 2 else x,
                1 - c if mask & 1 else c,
            )
        )
    return peers


def line_peers(z):
    return [z + 1 - 2 * (z % 2), 3 - z, (z + 2) % 4]


def greet(across=True):
    z, y, x, c = here()
    barrier = pltpu.get_barrier_semaphore()
    count = 7
    for peer in plane_peers(y, x, c):
        pl.semaphore_signal(barrier, inc=1, device_id=device(z, *peer), device_id_type=MESH)
    if across:
        count = 10
        for other in line_peers(z):
            pl.semaphore_signal(barrier, inc=1, device_id=device(other, y, x, c), device_id_type=MESH)
    pl.semaphore_wait(barrier, count)


class Net:
    def __init__(self, send, recv):
        self.send = send
        self.recv = recv
        self.used = 0

    def take(self, count):
        self.used += count
        assert self.used <= LINES
        return self.used - count

    def make(self, line, src, dst, target):
        return pltpu.make_async_remote_copy(
            src_ref=src,
            dst_ref=dst,
            send_sem=self.send.at[line],
            recv_sem=self.recv.at[line],
            device_id=target,
            device_id_type=MESH,
        )

    def copy(self, src, dst, target):
        made = self.make(self.take(1), src, dst, target)
        made.start()
        return made


VMEM = pl.BlockSpec(memory_space=pltpu.VMEM)


def rows_dot(left, right):
    return lax.dot_general(left, right, (((0,), (0,)), ((), ())), preferred_element_type=F32)


def cols_dot(left, right):
    return lax.dot_general(left, right, (((1,), (1,)), ((), ())), preferred_element_type=F32)


def lanes_to_rows(wide, tall):
    for s in range(8):
        tall[:, s, :] = wide[:, s * 128 : (s + 1) * 128]


def pick_halves(arr, base, slot, pair):
    one = base + ((2 * pair * 8 + slot) // 2) * 128
    two = base + (((2 * pair + 1) * 8 + slot) // 2) * 128
    left = arr[:, one : one + 128].astype(F32)
    right = arr[:, two : two + 128].astype(F32)
    lane = lax.broadcasted_iota(jnp.int32, left.shape, 1)
    if slot % 2 == 0:
        return jnp.where(lane < 64, left, pltpu.roll(right, 64, 1)).astype(LOW)
    return jnp.where(lane < 64, pltpu.roll(left, 64, 1), right).astype(LOW)


def ema_forward(factor, gain, source, out):
    steps = source.shape[0]

    def step(t, states):
        column = source[t]
        new = []
        terms = []
        for j in range(STATES):
            state = factor[j] * states[j] + column
            new.append(state)
            terms.append(gain[j] * state)
        while len(terms) > 1:
            terms = [terms[i] + terms[i + 1] for i in range(0, len(terms), 2)]
        out[t] = terms[0]
        return tuple(new)

    zero = jnp.zeros(source.shape[1:], F32)
    lax.fori_loop(0, steps, step, (zero,) * STATES)


def ema_backward(fac, gain, nrm, pull_ref, factor_sum, gain_sum, out):
    steps = nrm.shape[0]
    zero = jnp.zeros(nrm.shape[1:], F32)
    group = 4
    for base in range(0, STATES, group):

        def step(t, carry):
            at = steps - 1 - t
            column = nrm[at]
            pull = pull_ref[at]
            new = []
            terms = []
            for k in range(group):
                state, slope, by_factor, by_gain = carry[4 * k : 4 * k + 4]
                f = fac[base + k]
                slope = f * slope + state
                state = f * state + pull
                new += [state, slope, by_factor + column * slope, by_gain + column * state]
                terms.append(gain[base + k] * state)
            total = (terms[0] + terms[1]) + (terms[2] + terms[3])
            out[at] = total if base == 0 else out[at] + total
            return tuple(new)

        done = lax.fori_loop(0, steps, step, (zero,) * (4 * group))
        for k in range(group):
            factor_sum[base + k] = done[4 * k + 2]
            gain_sum[base + k] = done[4 * k + 3]


class PlaneGather:
    def __init__(self, net, src, dst):
        z, y, x, c = here()
        self.net, self.src, self.dst = net, src, dst
        self.base = net.take(7)
        self.me = slot_of(y, x, c)

    def near(self, k):
        z, y, x, c = here()
        yy, xx = chip_of(k)
        return self.net.make(self.base + k - 1, self.src, self.dst.at[self.me], device(z, yy, xx, c))

    def twin(self, k):
        z, y, x, c = here()
        yy, xx = chip_of(k)
        block = self.dst.at[slot_of(yy, xx, c)]
        return self.net.make(self.base + 3 + k, block, block, device(z, y, x, 1 - c))

    def start(self, last=True):
        self.dst[self.me] = self.src[...]
        self.twin(0).start()
        for k in (1, 2, 3) if last else (1, 2):
            self.near(k).start()

    def take_near(self, k):
        self.near(k).wait_recv()
        self.twin(k).start()

    def take_twin(self, k):
        self.twin(k).wait_recv()

    def take_rest(self):
        for k in (1, 2, 3):
            self.take_near(k)
        for k in range(4):
            self.take_twin(k)

    def finish(self):
        for k in (1, 2, 3):
            self.near(k).wait_send()
        for k in range(4):
            self.twin(k).wait_send()


class RelayedGather(PlaneGather):
    def __init__(self, net, src, dst):
        super().__init__(net, src, dst)
        self.relays = net.take(2)

    def pass_on(self, h):
        z, y, x, c = here()
        yy, xx = chip_of(1 + h)
        to_y, to_x = chip_of(2 - h)
        block = self.dst.at[slot_of(yy, xx, c), pl.ds(h * 64, 64)]
        return self.net.make(self.relays + h, block, block, device(z, to_y, to_x, c))

    def take_sides(self):
        for k in (1, 2):
            self.near(k).wait_recv()
            self.pass_on(k - 1).start()
        for k in (1, 2):
            self.twin(k).start()

    def take_last(self):
        for h in range(2):
            self.pass_on(h).wait_recv()
        self.twin(3).start()

    def finish(self):
        for k in (1, 2):
            self.near(k).wait_send()
            self.pass_on(k - 1).wait_send()
        for k in range(4):
            self.twin(k).wait_send()


def chip_of(k):
    z, y, x, c = here()
    return (y + k // 2) % 2, (x + k % 2) % 2


class PlaneSum:
    def __init__(self, net, part, got, sent, far, total, pairs, keep):
        self.net = net
        self.part, self.got, self.sent, self.far, self.total = part, got, sent, far, total
        self.pairs, self.keep = pairs, keep
        self.base = net.take(8)

    def inner(self, k):
        z, y, x, c = here()
        return self.net.make(self.base + k, self.part.at[k], self.got.at[k], device(z, y, x, 1 - c))

    def outer(self, k):
        z, y, x, c = here()
        yy, xx = chip_of(k)
        return self.net.make(self.base + 3 + k, self.sent.at[k - 1], self.far.at[k - 1], device(z, yy, xx, c))

    def give(self, k):
        z, y, x, c = here()
        self.part[k] = self.pairs[1 - c].astype(self.part.dtype)
        self.inner(k).start()

    def hold(self):
        z, y, x, c = here()
        self.keep[...] = self.pairs[c]

    def pair(self, k):
        self.inner(k).wait_recv()
        both = self.keep[...] + self.got[k].astype(F32)

        @pl.when(k == 0)
        def _():
            self.total[...] = both

        @pl.when(k > 0)
        def _():
            self.sent[k - 1] = both.astype(self.sent.dtype)

        self.leave(k)

    def leave(self, k):
        @pl.when(k > 0)
        def _():
            self.outer(k).start()

    def run(self, make):
        @pl.loop(0, 4)
        def _(i):
            make(3 - i)
            self.give(3 - i)

            @pl.when(i > 0)
            def _():
                self.pair(4 - i)

            self.hold()

        self.pair(0)

    def settle(self):
        @pl.loop(0, 4)
        def _(k):
            self.inner(k).wait_send()

    def finish(self):
        @pl.loop(1, 4)
        def _(k):
            self.outer(k).wait()
            self.total[...] = self.total[...] + self.far[k - 1].astype(F32)


class RelayedSum(PlaneSum):
    def half(self, h):
        z, y, x, c = here()
        yy, xx = chip_of(1 + h)
        rows = pl.ds(h * 64, 64)
        return self.net.make(
            self.base + 6 + h, self.sent.at[2, rows], self.far.at[2, rows], device(z, yy, xx, c)
        )

    def leave(self, k):
        @pl.when(k == 3)
        def _():
            self.half(0).start()
            self.half(1).start()

    def relay(self):
        for h in range(2):
            self.half(h).wait_recv()
            at = 1 - h
            rows = slice(h * 64, (h + 1) * 64)
            self.sent[at, rows] = (self.sent[at, rows].astype(F32) + self.far[2, rows].astype(F32)).astype(LOW)
            self.outer(at + 1).start()

    def finish(self):
        for k in (1, 2):
            self.half(k - 1).wait_send()
            self.outer(k).wait()
        self.total[...] = self.total[...] + self.far[0].astype(F32) + self.far[1].astype(F32)


class LineGather:
    def __init__(self, net, buf):
        z, y, x, c = here()
        near, mirror, _ = line_peers(z)
        self.inside = z % 3 > 0
        relayed = (2 * z) % 3 + 3 * (z // 3)
        self.first = net.make(net.take(1), buf.at[z], buf.at[z], device(near, y, x, c))
        self.second = net.make(net.take(1), buf.at[z], buf.at[z], device(mirror, y, x, c))
        self.third = net.make(net.take(1), buf.at[relayed], buf.at[relayed], device((3 * z + 2) % 5, y, x, c))

    def start(self):
        self.first.start()
        self.second.start()

        @pl.when(jnp.logical_not(self.inside))
        def _():
            self.third.start()

    def relay(self):
        @pl.when(self.inside)
        def _():
            self.second.wait_recv()
            self.third.start()

    def finish(self):
        self.first.wait()
        self.second.wait_send()

        @pl.when(jnp.logical_not(self.inside))
        def _():
            self.second.wait_recv()

        self.third.wait()


class LineSum:
    def __init__(self, net, buf, got, out):
        z, y, x, c = here()
        near, mirror, across = line_peers(z)
        self.buf, self.got, self.out = buf, got, out
        self.inside = z % 3 > 0
        self.relayed = (2 * z) % 3 + 3 * (z // 3)
        self.first = net.make(net.take(1), buf.at[across], got.at[0], device((2 * z + 1) % 5, y, x, c))
        self.second = net.make(net.take(1), buf.at[near], got.at[1], device(near, y, x, c))
        self.third = net.make(net.take(1), buf.at[mirror], got.at[2], device(mirror, y, x, c))

    def run(self, make):
        z, y, x, c = here()

        @pl.loop(0, 4)
        def _(i):
            bits = (2 + 3 * i) % 4
            make((z // 2 + bits // 2) % 2 * 2 + (z + bits) % 2)

            @pl.when(i == 0)
            def _():
                self.first.start()

            @pl.when(i == 1)
            def _():
                self.second.start()

        self.start_last()

    def start(self, last=True):
        self.first.start()
        self.second.start()
        if last:
            self.start_last()

    def start_last(self):
        @pl.when(jnp.logical_not(self.inside))
        def _():
            self.third.start()

    def relay(self):
        @pl.when(self.inside)
        def _():
            self.first.wait_recv()
            self.buf[self.relayed] = (self.buf[self.relayed].astype(F32) + self.got[0].astype(F32)).astype(LOW)
            self.third.start()

    def finish(self):
        z, y, x, c = here()
        self.first.wait_send()
        self.second.wait()
        self.third.wait()
        total = self.buf[z].astype(F32) + self.got[1].astype(F32) + self.got[2].astype(F32)
        self.out[...] = total.reshape(self.out.shape).astype(self.out.dtype)

        @pl.when(jnp.logical_not(self.inside))
        def _():
            self.first.wait_recv()
            whole = total + self.got[0].astype(F32)
            self.out[...] = whole.reshape(self.out.shape).astype(self.out.dtype)


class Spread:
    def __init__(self, net, sends, whole):
        self.net, self.whole = net, whole
        self.line = net.take(1)
        for src, dst, target in sends:
            net.make(self.line, src, dst, target).start()

    def finish(self):
        pltpu.make_async_copy(self.whole, self.whole, self.net.recv.at[self.line]).wait()
        pltpu.make_async_copy(self.whole, self.whole, self.net.send.at[self.line]).wait()


def spread_plane(net, src, dst):
    z, y, x, c = here()
    me = slot_of(y, x, c)
    dst[me] = src[...]
    sends = [(src, dst.at[me], device(z, *peer)) for peer in plane_peers(y, x, c)]
    return Spread(net, sends, dst.at[pl.ds(0, 7)])


def spread_column(net, buf):
    z, y, x, c = here()
    block = buf.at[:, slot_of(y, x, c)]
    sends = [(block, block, device(z, *peer)) for peer in plane_peers(y, x, c)]
    return Spread(net, sends, buf.at[:, pl.ds(0, 7)])


def swap_plane(net, src, dst):
    z, y, x, c = here()
    me = slot_of(y, x, c)
    dst[me] = src[me]
    sends = [(src.at[slot_of(*peer)], dst.at[me], device(z, *peer)) for peer in plane_peers(y, x, c)]
    return Spread(net, sends, dst.at[pl.ds(0, 7)])


def spread_line(net, buf, part=None):
    z, y, x, c = here()
    block = buf.at[z] if part is None else buf.at[z, part]
    whole = buf.at[pl.ds(0, 3)] if part is None else buf.at[pl.ds(0, 3), part]
    return Spread(net, [(block, block, device(other, y, x, c)) for other in line_peers(z)], whole)


def swap_line(net, src, dst):
    z, y, x, c = here()
    dst[z] = src[z]
    sends = [(src.at[other], dst.at[z], device(other, y, x, c)) for other in line_peers(z)]
    return Spread(net, sends, dst.at[pl.ds(0, 3)])


class ChipSwap:
    def __init__(self, net, src, dst):
        z, y, x, c = here()
        self.net, self.src, self.dst = net, src, dst
        self.me = slot_of(y, x, c)
        self.base = net.take(8)

    def copy(self, k, twin):
        z, y, x, c = here()
        yy, xx = chip_of(k)
        cc = (c + twin) % 2
        return self.net.make(
            self.base + 2 * k + twin, self.src.at[slot_of(yy, xx, cc)], self.dst.at[self.me], device(z, yy, xx, cc)
        )

    def start(self):
        self.dst[self.me] = self.src[self.me]
        self.copy(0, 1).start()
        for k in (1, 2, 3):
            for twin in range(2):
                self.copy(k, twin).start()

    def take(self, k):
        self.copy(k, 1).wait_recv()

        @pl.when(k > 0)
        def _():
            self.copy(k, 0).wait_recv()

    def finish(self):
        self.copy(0, 1).wait_send()
        for k in (1, 2, 3):
            for twin in range(2):
                self.copy(k, twin).wait_send()


def row_mean(value):
    return jnp.mean(value, axis=-1, keepdims=True)


def standardized(value):
    centred = value - row_mean(value)
    inverse = lax.rsqrt(row_mean(centred * centred) + EPS)
    return centred * inverse, inverse


def norm_back(grad, xhat, inverse, gain):
    scaled = grad * gain
    return inverse * (scaled - row_mean(scaled) - xhat * row_mean(scaled * xhat))


def block_scores_of(zeta, heads, shift, table):
    query_low = (zeta * heads[0:1] + shift).astype(LOW)
    key_low = (zeta * heads[1:2]).astype(LOW)
    scores = cols_dot(query_low, key_low) * (zeta.shape[1] ** (-0.5)) + table[...]
    row = lax.broadcasted_iota(jnp.int32, scores.shape, 0)
    col = lax.broadcasted_iota(jnp.int32, scores.shape, 1)
    scores = jnp.where(row >= col, scores, NEG)
    top = jnp.max(scores, axis=-1, keepdims=True)
    log_total = top + jnp.log(jnp.sum(jnp.exp(scores - top), axis=-1, keepdims=True))
    return query_low, key_low, jnp.exp(scores - log_total)


def mirror_matrix(size):
    row = lax.broadcasted_iota(jnp.int32, (size, size), 0)
    col = lax.broadcasted_iota(jnp.int32, (size, size), 1)
    return jnp.where(row + col == size - 1, 1.0, 0.0).astype(LOW)


def column_of(line):
    size = line.shape[1]
    row = lax.broadcasted_iota(jnp.int32, (size, size), 0)
    col = lax.broadcasted_iota(jnp.int32, (size, size), 1)
    return jnp.sum(jnp.where(row == col, line, 0.0), axis=1, keepdims=True)


def cols_at(index, size):
    return pl.ds(pl.multiple_of(index * size, size), size)


def put_rows(sums, at, wide):
    sums[at : at + 1] = jnp.sum(wide, axis=0, keepdims=True)


ROWS = 128
WIDE = 1024
ALL = (8, ROWS, WIDE)
OWN = (ROWS, WIDE)


ANY = pl.BlockSpec(memory_space=pl.ANY)


class Inputs:
    x_in = ANY
    cot_in = ANY
    wv_in = ANY
    wm_in = ANY
    wo_in = ANY
    we_in = ANY
    wr_in = ANY
    ema = VMEM
    norm_gains = VMEM
    norm_biases = VMEM
    head_gains = VMEM
    query_bias = VMEM
    position_bias = VMEM
    lens = VMEM


class Results:
    output_hbm = (ROWS, WIDE), LOW
    grad_inputs_hbm = (ROWS, WIDE), F32
    grad_out_hbm = (64, WIDE), F32
    grad_reduce_hbm = (ROWS, WIDE), F32
    ge_hbm = (8, 32, 512), LOW
    ga_hbm = (8, 32, 768), LOW
    gz_hbm = (4, 32, 128), F32
    sums_hbm = (8, 40, 128), F32
    square_hbm = (4, 8, 128), F32


class Scratch:
    output = (ROWS, WIDE), LOW
    grad_inputs = (ROWS, WIDE), F32
    grad_out = (64, WIDE), F32
    grad_reduce = (ROWS, WIDE), F32
    ge_all = (8, 32, 512), LOW
    ga_all = (8, 32, 768), LOW
    gz_line = (4, 32, 128), F32
    sums_all = (8, 40, 128), F32
    square_line = (4, 8, 128), F32
    x = OWN, LOW
    cot = OWN, LOW
    wv = (32, 2048), LOW
    wm = (32, 4224), LOW
    we_own = (32, 4096), LOW
    small_wide = (32, 128), F32
    wz = (4, 8, 32, 128), LOW
    inverse = (ROWS, 128), F32
    small_all = (4, 8, 32, 128), LOW
    prm = (72, WIDE), F32
    blocks_a = (8, 32, 768), LOW
    blocks_e = (8, 32, 512), LOW
    wa = (4, 8, 32, 768), LOW
    wo = (4, 64, WIDE), LOW
    we = (4, 8, 32, 512), LOW
    wr = (4, ROWS, WIDE), LOW
    table = (128, 128), F32
    heads = (8, 128), F32
    own_low = OWN, LOW
    normed_all = ALL, LOW
    mixed_all = ALL, LOW
    cot_all = ALL, LOW
    two_all = ALL, LOW
    hid_all = ALL, LOW
    fac = (16, 8, 128), F32
    gain = (16, 8, 128), F32
    fac_sum = (16, 8, 128), F32
    gain_sum = (16, 8, 128), F32
    nrm = (ROWS, 8, 128), F32
    tall = (ROWS, 8, 128), F32
    tall_out = (ROWS, 8, 128), F32
    pre = OWN, F32
    value_pre = (8, ROWS, 256), F32
    value_low = (8, ROWS, 256), LOW
    zeta_pre = (8, ROWS, 128), F32
    weights_low = (8, ROWS, 128), LOW
    attended = (8, ROWS, 256), F32
    reset_pre = (8, ROWS, 256), F32
    gated = (8, ROWS, 256), LOW
    work = OWN, F32
    hidden_pre = OWN, F32
    update_pre = OWN, F32
    first = OWN, F32
    update_part = (8, ROWS, 128), LOW
    update_all = (8, ROWS, 128), LOW
    part = (4, ROWS, WIDE), LOW
    got = (4, ROWS, WIDE), LOW
    sent = (3, ROWS, WIDE), LOW
    far = (3, ROWS, WIDE), LOW
    got_b = (4, ROWS, WIDE), LOW
    sent_b = (3, ROWS, WIDE), LOW
    far_b = (3, ROWS, WIDE), LOW
    got_c = (4, ROWS, WIDE), LOW
    sent_c = (3, ROWS, WIDE), LOW
    far_c = (3, ROWS, WIDE), LOW
    pairs = (2, ROWS, WIDE), F32
    grad_two = OWN, F32
    scores_pairs = (2, ROWS, 128), F32
    scores_keep = (ROWS, 128), F32
    expand_pre = (8, ROWS, 512), F32
    expand_low = (8, ROWS, 512), LOW
    grad_pre = (8, ROWS, 512), LOW
    branch = OWN, F32
    value_back = (8, ROWS, 256), LOW
    mixture_back = (8, ROWS, 512), LOW
    scores_part = (4, ROWS, 128), F32
    scores_got = (4, ROWS, 128), F32
    scores_sent = (3, ROWS, 128), F32
    scores_far = (3, ROWS, 128), F32
    scores_sum = (ROWS, 128), F32
    zeta_own = (ROWS, 128), LOW
    zeta_all = (8, ROWS, 128), LOW
    gr = (4, ROWS, WIDE), LOW
    gr_got = (3, ROWS, WIDE), LOW
    ge = (4, 256, 512), LOW
    ge_got = (3, 256, 512), LOW
    ge_sum = (8, 32, 512), LOW
    go = (4, 64, WIDE), LOW
    go_got = (3, 64, WIDE), LOW
    ga = (4, 256, 768), LOW
    ga_got = (3, 256, 768), LOW
    ga_sum = (8, 32, 768), LOW
    gz = (4, 8, 32, 128), F32
    gz_own = (4, 32, 128), F32
    sums = (40, WIDE), F32
    sum_blocks = (8, 40, 128), F32
    sum_parts = (8, 40, 128), F32
    sum_rows = (4, 40, 128), F32
    sum_cols = (40, 128), F32
    square_own = (8, 128), F32
    square_all = (8, 8, 128), F32


class Lines:
    send = (LINES,)
    recv = (LINES,)
    load = (7,)
    store = (9,)


def fields(group):
    return {name: item for name, item in vars(group).items() if not name.startswith("_")}


class Refs:
    def __init__(self, refs):
        names = [name for group in (Inputs, Results, Scratch, Lines) for name in fields(group)]
        for name, ref in zip(names, refs, strict=True):
            setattr(self, name, ref)


class Stores:
    def __init__(self, sems):
        self.sems, self.made = sems, []

    def put(self, src, dst):
        copy = pltpu.make_async_copy(src, dst, self.sems.at[len(self.made)])
        copy.start()
        self.made.append(copy)

    def finish(self):
        for copy in self.made:
            copy.wait()


def layer_kernel(*refs):
    r = Refs(refs)
    net = Net(r.send, r.recv)
    z, y, x, c = here()
    me = slot_of(y, x, c)
    twin = device(z, y, x, 1 - c)
    tokens = 8 * ROWS
    stores = Stores(r.store)
    loads = [
        pltpu.make_async_copy(src, dst, r.load.at[line])
        for line, (src, dst) in enumerate(
            (
                (r.wm_in, r.wm), (r.wv_in, r.wv), (r.wo_in, r.wo.at[z]), (r.x_in, r.x), (r.we_in, r.we_own),
                (r.wr_in, r.wr.at[z]), (r.cot_in, r.cot),
            )
        )
    ]
    for load in loads:
        load.start()
    greet()
    for load in loads:
        load.wait()

    lane = lax.broadcasted_iota(jnp.int32, (32, 128), 1)
    r.small_wide[...] = jnp.zeros((32, 128), F32)
    r.small_wide[:, 0:64] = r.ema[...].astype(F32)
    small = r.small_wide[...]
    for k in range(5):
        line = r.norm_gains[k : k + 1, :] if k < 3 else r.norm_biases[k - 3 : k - 2, :]
        small = jnp.where(lane == 64 + k, column_of(line.astype(F32)), small)
    r.small_all[z, me] = small.astype(LOW)
    small_line = spread_line(net, r.small_all, me)
    r.wz[z, me] = r.wm[:, 1024:1152]
    zeta_line = spread_line(net, r.wz, me)
    for s in range(8):
        for pair in range(2):
            r.blocks_a[s, :, pair * 128 : (pair + 1) * 128] = pick_halves(r.wv, 0, s, pair)
            r.blocks_a[s, :, 384 + pair * 128 : 512 + pair * 128] = pick_halves(r.wm, 1152, s, pair)
        r.blocks_a[s, :, 256:384] = r.wm[:, s * 128 : (s + 1) * 128]
        r.blocks_a[s, :, 640:768] = r.wm[:, 3200 + s * 128 : 3328 + s * 128]
    attn_plane = swap_plane(net, r.blocks_a, r.wa.at[z])
    out_line = LineGather(net, r.wo)
    out_line.start()
    for s in range(8):
        for zz in range(4):
            r.blocks_e[s, :, zz * 128 : (zz + 1) * 128] = r.we_own[:, (zz * 8 + s) * 128 : (zz * 8 + s + 1) * 128]
    small_line.finish()
    small_plane = spread_column(net, r.small_all)
    near_base = net.take(3)

    def near(k):
        yy, xx = chip_of(k)
        return net.make(near_base + k - 1, r.x, r.mixed_all.at[me], device(z, yy, xx, c))

    for k in (1, 2, 3):
        near(k).start()
    zeta_line.finish()
    zeta_plane = spread_column(net, r.wz)
    expand_plane = swap_plane(net, r.blocks_e, r.we.at[z])
    row = lax.broadcasted_iota(jnp.int32, OWN, 0)
    r.own_low[...] = jnp.where(row < r.lens[...], r.cot[...].astype(F32), 0.0).astype(LOW)
    cot_plane = PlaneGather(net, r.own_low, r.cot_all)
    cot_plane.start()
    r.heads[0:2] = r.head_gains[...].astype(F32)
    r.heads[2:3] = r.query_bias[...].astype(F32).reshape(1, 128)
    wide = jnp.broadcast_to(r.position_bias[...].astype(F32).reshape(1, 128), (128, 128)).astype(LOW)
    turned = jnp.dot(wide, mirror_matrix(128), preferred_element_type=F32)
    r.table[...] = pltpu.roll(turned, 1, 1, stride=1, stride_axis=0)
    out_line.relay()
    attn_plane.finish()
    attn_line = LineGather(net, r.wa)
    attn_line.start()
    small_plane.finish()

    r.prm[...] = r.small_all[...].reshape(WIDE, 128).astype(F32).T[0:72]
    damping = jax.nn.sigmoid(r.prm[0:16])
    mixing = jax.nn.sigmoid(r.prm[16:32])
    lanes_to_rows(1.0 - mixing * damping, r.fac)
    lanes_to_rows(0.25 * r.prm[48:64] * (mixing * r.prm[32:48]), r.gain)
    pair_base = net.take(8)

    def pair_normed(k):
        yy, xx = chip_of(k)
        block = r.normed_all.at[slot_of(yy, xx, c)]
        return net.make(pair_base + k, block, block, twin)

    def pair_mixed(k):
        yy, xx = chip_of(k)
        block = r.mixed_all.at[slot_of(yy, xx, c)]
        return net.make(pair_base + 4 + k, block, block, twin)

    def mix(k, tall, pre):
        yy, xx = chip_of(k)
        slot = slot_of(yy, xx, c)
        source = r.mixed_all[slot]
        xhat, _ = standardized(source.astype(F32))
        normed = xhat * r.prm[64:65] + r.prm[67:68]
        r.normed_all[slot] = normed.astype(LOW)
        pair_normed(k).start()
        lanes_to_rows(normed, tall)
        pre[...] = r.prm[65:66] * normed
        ema_forward(r.fac, r.gain, tall, r.tall_out)
        for s in range(8):
            cols = slice(s * 128, (s + 1) * 128)
            pre[:, cols] = pre[:, cols] + r.tall_out[:, s, :]
        r.mixed_all[slot] = silu(pre[...]).astype(LOW)
        pair_mixed(k).start()

    r.mixed_all[me] = r.x[...]
    mix(0, r.nrm, r.pre)

    @pl.loop(1, 4)
    def _(k):
        near(k).wait_recv()

        @pl.when(k == 3)
        def _():
            attn_line.relay()

        mix(k, r.tall, r.work)

    expand_plane.finish()
    expand_line = LineGather(net, r.we)
    expand_line.start()
    reduce_line = LineGather(net, r.wr)
    reduce_line.start()
    cot_plane.take_rest()
    cot_plane.finish()
    for k in (1, 2, 3):
        near(k).wait_send()
    for k in range(4):
        pair_normed(k).wait()
        pair_mixed(k).wait()
    zeta_plane.finish()
    out_line.finish()
    attn_line.finish()

    cand_cols = cols_at(me, 128)
    shift = r.heads[2:3]

    def weights_a(first, last):
        return r.wa[:, :, :, first:last].reshape(WIDE, last - first)

    def zeta_weights():
        return r.wz[...].reshape(WIDE, 128)

    def pair_of(k):
        yy, xx = chip_of(k)
        return pl.ds((yy * 2 + xx) * 2, 2)

    def rows_of(ref, k):
        return ref[pair_of(k)].reshape(2 * ROWS, ref.shape[2])

    def put(ref, k, value):
        ref[pair_of(k)] = value.reshape(2, ROWS, ref.shape[2]).astype(ref.dtype)

    def attend(k):
        pre = jnp.dot(rows_of(r.normed_all, k), weights_a(0, 256), preferred_element_type=F32)
        put(r.value_pre, k, pre)
        low_values = silu(pre).astype(LOW)
        put(r.value_low, k, low_values)
        mixed = rows_of(r.mixed_all, k)
        mixture = jnp.dot(mixed, weights_a(256, 768), preferred_element_type=F32)
        put(r.update_part, k, mixture[:, 0:128])
        put(r.reset_pre, k, mixture[:, 128:384])
        zeta = jnp.dot(mixed, zeta_weights(), preferred_element_type=F32)
        put(r.zeta_pre, k, zeta)
        zeta = silu(zeta)
        values = []
        weights = []
        for h in range(2):
            rows = slice(h * ROWS, (h + 1) * ROWS)
            _, _, probs = block_scores_of(zeta[rows], r.heads, shift, r.table)
            weights.append(probs.astype(LOW))
            values.append(jnp.dot(weights[h], low_values[rows], preferred_element_type=F32))
        put(r.weights_low, k, jnp.concatenate(weights, axis=0))
        mixed_values = jnp.concatenate(values, axis=0)
        put(r.attended, k, mixed_values)
        gate = (mixed_values * silu(mixture[:, 128:384])).astype(LOW)
        put(r.gated, k, gate)
        hidden = jnp.dot(gate, r.wo[...].reshape(256, WIDE), preferred_element_type=F32)
        r.pairs[...] = hidden.reshape(2, ROWS, WIDE)
        r.pairs[:, :, cand_cols] = r.pairs[:, :, cand_cols] + mixture[:, 384:512].reshape(2, ROWS, 128)

    hidden_sum = PlaneSum(net, r.part, r.got, r.sent, r.far, r.hidden_pre, r.pairs, r.work)
    hidden_sum.run(attend)
    update_plane = swap_plane(net, r.update_part, r.update_all)
    expand_line.relay()
    hidden_sum.settle()
    hidden_sum.finish()
    update_plane.finish()
    for s in range(8):
        r.update_pre[:, s * 128 : (s + 1) * 128] = r.update_all[s].astype(F32)
    stream = r.x[...].astype(F32)
    r.first[...] = stream + jax.nn.sigmoid(r.update_pre[...]) * (silu(r.hidden_pre[...]) - stream)
    xhat, _ = standardized(r.first[...])
    r.own_low[...] = (xhat * r.prm[66:67] + r.prm[68:69]).astype(LOW)
    two_plane = PlaneGather(net, r.own_low, r.two_all)
    two_plane.start()
    reduce_line.relay()
    expand_line.finish()

    def reduce_rows():
        return r.wr[...].reshape(512, WIDE)

    def expand_rows():
        return r.we[...].reshape(WIDE, 512)

    @pl.loop(0, 4)
    def _(k):
        @pl.when(k > 0)
        def _():
            two_plane.take_near(k)

        two_plane.take_twin(k)
        pre = jnp.dot(rows_of(r.two_all, k), expand_rows(), preferred_element_type=F32)
        put(r.expand_pre, k, pre)
        put(r.expand_low, k, silu(pre))

    two_plane.finish()
    reduce_sum = LineSum(net, r.gr, r.gr_got, r.grad_reduce)
    expand_sum = LineSum(net, r.ge, r.ge_got, r.ge_sum)

    def reduce_grad(zz):
        r.gr[zz] = rows_dot(
            r.expand_low[:, :, cols_at(zz, 128)].reshape(tokens, 128), r.cot_all[...].reshape(tokens, WIDE)
        ).astype(LOW)

    reduce_sum.run(reduce_grad)
    reduce_line.finish()

    def expand_back(k):
        grad = (cols_dot(rows_of(r.cot_all, k), reduce_rows()) * silu_slope(rows_of(r.expand_pre, k))).astype(LOW)
        put(r.grad_pre, k, grad)
        r.pairs[...] = cols_dot(grad, expand_rows()).reshape(2, ROWS, WIDE)

    two_sum = PlaneSum(net, r.part, r.got, r.sent, r.far, r.grad_two, r.pairs, r.work)
    two_sum.run(expand_back)

    @pl.loop(0, 4)
    def _(zz):
        r.ge[zz] = rows_dot(
            r.two_all[:, :, cols_at(zz, 256)].reshape(tokens, 256), r.grad_pre[...].reshape(tokens, 512)
        ).astype(LOW)

    expand_sum.start()

    def branch_blocks(k):
        branch = jnp.dot(rows_of(r.expand_low, k), reduce_rows(), preferred_element_type=F32)
        r.pairs[...] = branch.reshape(2, ROWS, WIDE)

    two_sum.settle()
    branch_sum = RelayedSum(net, r.part, r.got_b, r.sent_b, r.far_b, r.branch, r.pairs, r.work)
    branch_sum.run(branch_blocks)
    reduce_sum.relay()
    valid = jnp.where(lax.broadcasted_iota(jnp.int32, (ROWS, 1), 0) < r.lens[...], 1.0, 0.0)
    update = jax.nn.sigmoid(r.update_pre[...])
    hidden = r.hidden_pre[...]
    r.work[...] = update * silu_slope(hidden)
    r.pairs[1] = (silu(hidden) - r.x[...].astype(F32)) * update * (1.0 - update)
    xhat, inverse = standardized(r.first[...])
    r.pairs[0] = xhat
    r.inverse[...] = jnp.broadcast_to(inverse, (ROWS, 128))
    two_sum.finish()

    grad_first = r.cot[...].astype(F32) * valid + norm_back(
        r.grad_two[...], r.pairs[0], r.inverse[:, 0:1], r.prm[66:67]
    )
    r.own_low[...] = (grad_first * r.work[...]).astype(LOW)
    hid_plane = RelayedGather(net, r.own_low, r.hid_all)
    hid_plane.start(last=False)
    grad_update = (grad_first * r.pairs[1]).astype(LOW)
    for s in range(8):
        r.update_part[s] = grad_update[:, s * 128 : (s + 1) * 128]
    upd_plane = ChipSwap(net, r.update_part, r.update_all)
    upd_plane.start()
    r.grad_inputs[...] = grad_first * (1.0 - jax.nn.sigmoid(r.update_pre[...]))
    put_rows(r.sums, 34, r.grad_two[...] * r.pairs[0])
    put_rows(r.sums, 36, r.grad_two[...])

    branch_sum.settle()
    expand_sum.relay()
    scores_plane = PlaneSum(
        net, r.scores_part, r.scores_got, r.scores_sent, r.scores_far, r.scores_sum, r.scores_pairs, r.scores_keep
    )
    mixed_sum = PlaneSum(net, r.part, r.got, r.sent, r.far, r.grad_two, r.pairs, r.work)

    def attend_back(k):
        gate_grad = cols_dot(rows_of(r.hid_all, k), r.wo[...].reshape(256, WIDE))
        pre = rows_of(r.reset_pre, k)
        low_grad = (gate_grad * silu(pre)).astype(LOW)
        low_values = rows_of(r.value_low, k)
        weights = rows_of(r.weights_low, k)
        backs = []
        for h in range(2):
            rows = slice(h * ROWS, (h + 1) * ROWS)
            r.scores_pairs[h] = cols_dot(low_grad[rows], low_values[rows])
            backs.append(rows_dot(weights[rows], low_grad[rows]))
        put(r.value_back, k, jnp.concatenate(backs, axis=0) * silu_slope(rows_of(r.value_pre, k)))
        pair = pair_of(k)
        r.mixture_back[pair, :, 0:128] = r.update_all[pair]
        r.mixture_back[pair, :, 128:384] = (
            (gate_grad * rows_of(r.attended, k) * silu_slope(pre)).astype(LOW).reshape(2, ROWS, 256)
        )
        r.mixture_back[pair, :, 384:512] = r.hid_all[pair, :, cand_cols]
        mixture = rows_of(r.mixture_back, k)
        mixed = cols_dot(mixture, weights_a(256, 768))
        r.pairs[...] = mixed.reshape(2, ROWS, WIDE)

    @pl.loop(0, 4)
    def _(k):
        @pl.when(k == 1)
        def _():
            hid_plane.take_sides()

        @pl.when(k == 3)
        def _():
            hid_plane.take_last()

        hid_plane.take_twin(k)
        upd_plane.take(k)
        attend_back(k)
        scores_plane.give(k)
        mixed_sum.give(k)

        @pl.when(k > 0)
        def _():
            scores_plane.pair(k - 1)
            mixed_sum.pair(k - 1)

        scores_plane.hold()
        mixed_sum.hold()

    scores_plane.pair(3)
    mixed_sum.pair(3)
    hid_plane.finish()
    upd_plane.finish()
    out_sum = LineSum(net, r.go, r.go_got, r.grad_out)
    attn_sum = LineSum(net, r.ga, r.ga_got, r.ga_sum)

    def attn_grad(zz):
        cols = cols_at(zz, 256)
        r.ga[zz, :, 0:256] = rows_dot(
            r.normed_all[:, :, cols].reshape(tokens, 256), r.value_back[...].reshape(tokens, 256)
        ).astype(LOW)
        r.ga[zz, :, 256:768] = rows_dot(
            r.mixed_all[:, :, cols].reshape(tokens, 256), r.mixture_back[...].reshape(tokens, 512)
        ).astype(LOW)

    attn_sum.run(attn_grad)

    @pl.loop(0, 4)
    def _(t):
        cols = cols_at(t, 256)
        grad = rows_dot(
            r.gated[...].reshape(tokens, 256), r.hid_all[:, :, cols].reshape(tokens, 256)
        ).astype(LOW)
        for zz in range(4):
            r.go[zz, :, cols] = grad[zz * 64 : (zz + 1) * 64]


    reduce_sum.finish()
    stores.put(r.grad_reduce, r.grad_reduce_hbm)
    expand_sum.finish()
    mixed_sum.settle()
    normed_sum = RelayedSum(net, r.part, r.got_c, r.sent_c, r.far_c, r.hidden_pre, r.pairs, r.work)

    def normed_blocks(k):
        normed = cols_dot(rows_of(r.value_back, k), weights_a(0, 256))
        r.pairs[...] = normed.reshape(2, ROWS, WIDE)

    normed_sum.run(normed_blocks)

    scores_plane.settle()
    scores_plane.finish()
    grad_weights = r.scores_sum[...]
    zeta_own_pre = r.zeta_pre[me]
    zeta = silu(zeta_own_pre)
    query_low, key_low, probs = block_scores_of(zeta, r.heads, shift, r.table)
    grad_scores = (probs * (grad_weights - jnp.sum(probs * grad_weights, axis=-1, keepdims=True))).astype(LOW)
    scale = zeta.shape[1] ** (-0.5)
    grad_query = jnp.dot(grad_scores, key_low, preferred_element_type=F32) * scale
    grad_key = rows_dot(grad_scores, query_low) * scale
    skewed = pltpu.roll(
        jnp.dot(grad_scores, mirror_matrix(ROWS), preferred_element_type=F32), 1, 1, stride=1, stride_axis=0
    )
    r.sums[37:40] = jnp.zeros((3, WIDE), F32)
    r.sums[37:38, 0:128] = jnp.sum(grad_query * zeta, axis=0, keepdims=True)
    r.sums[37:38, 128:256] = jnp.sum(grad_key * zeta, axis=0, keepdims=True)
    r.sums[37:38, 256:384] = jnp.sum(grad_query, axis=0, keepdims=True)
    r.sums[37:38, 384:512] = jnp.sum(skewed, axis=0, keepdims=True)
    grad_zeta = grad_query * r.heads[0:1] + grad_key * r.heads[1:2]
    r.zeta_own[...] = (grad_zeta * silu_slope(zeta_own_pre)).astype(LOW)
    zeta_tokens = spread_plane(net, r.zeta_own, r.zeta_all)

    normed_sum.relay()
    branch_sum.relay()
    mixed_sum.finish()
    grad_mixed = r.grad_two[...] + cols_dot(r.zeta_own[...], zeta_weights())
    pull = grad_mixed * silu_slope(r.pre[...])
    lanes_to_rows(pull, r.tall)
    r.pre[...] = pull
    attn_sum.relay()
    ema_backward(r.fac, r.gain, r.nrm, r.tall, r.fac_sum, r.gain_sum, r.tall_out)
    for s in range(8):
        cols = slice(s * 128, (s + 1) * 128)
        r.sums[0:16, cols] = r.fac_sum[:, s, :]
        r.sums[16:32, cols] = r.gain_sum[:, s, :]
        r.sums[33:34, cols] = jnp.sum(r.pre[:, cols] * r.nrm[:, s, :], axis=0, keepdims=True)
    zeta_tokens.finish()
    r.gz[...] = rows_dot(
        r.mixed_all[...].reshape(tokens, WIDE), r.zeta_all[...].reshape(tokens, 128)
    ).reshape(4, 8, 32, 128)
    for zz in range(4):
        r.gz_own[zz] = r.gz[zz, me]
    zeta_grad = swap_line(net, r.gz_own, r.gz_line)
    normed_sum.settle()
    normed_sum.finish()
    for s in range(8):
        cols = slice(s * 128, (s + 1) * 128)
        r.hidden_pre[:, cols] = r.hidden_pre[:, cols] + r.pre[:, cols] * r.prm[65:66, cols] + r.tall_out[:, s, :]
    xhat_one, inverse_one = standardized(r.x[...].astype(F32))
    grad_one = r.hidden_pre[...]
    put_rows(r.sums, 32, grad_one * xhat_one)
    put_rows(r.sums, 35, grad_one)
    r.grad_inputs[...] = r.grad_inputs[...] + norm_back(grad_one, xhat_one, inverse_one, r.prm[64:65])

    stores.put(r.grad_inputs, r.grad_inputs_hbm)

    for s in range(8):
        r.sum_blocks[s] = r.sums[:, s * 128 : (s + 1) * 128]
    small_sum = swap_plane(net, r.sum_blocks, r.sum_parts)
    ge_plane = swap_plane(net, r.ge_sum, r.ge_all)
    small_sum.finish()
    whole = r.sum_parts[0]
    for s in range(1, 8):
        whole = whole + r.sum_parts[s]
    r.sum_rows[z] = whole
    small_rows = spread_line(net, r.sum_rows)
    out_sum.start(last=False)
    branch_sum.finish()
    stream = r.x[...].astype(F32)
    first = r.first[...]
    branch = r.branch[...]
    r.output[...] = ((first + branch) * valid).astype(LOW)
    stores.put(r.output, r.output_hbm)
    r.square_own[...] = jnp.zeros((8, 128), F32)
    for k, item in enumerate((stream, first - stream, branch)):
        squares = jnp.sum(valid * item * item, axis=0, keepdims=True)
        r.square_own[k : k + 1] = jnp.broadcast_to(jnp.sum(squares, axis=1, keepdims=True), (1, 128))
    r.square_own[3:4] = jnp.broadcast_to(jnp.sum(valid, axis=0, keepdims=True), (1, 128))
    square_plane = spread_plane(net, r.square_own, r.square_all)
    attn_sum.finish()
    ga_plane = swap_plane(net, r.ga_sum, r.ga_all)
    small_rows.finish()
    r.sum_cols[...] = (r.sum_rows[0] + r.sum_rows[1]) + (r.sum_rows[2] + r.sum_rows[3])
    small_cols = spread_plane(net, r.sum_cols, r.sums_all)
    out_sum.start_last()
    out_sum.relay()
    square_plane.finish()
    squares = r.square_all[0]
    for s in range(1, 8):
        squares = squares + r.square_all[s]
    r.square_line[z] = squares
    square_rows = spread_line(net, r.square_line)
    ge_plane.finish()
    stores.put(r.ge_all, r.ge_hbm)
    zeta_grad.finish()
    stores.put(r.gz_line, r.gz_hbm)
    ga_plane.finish()
    stores.put(r.ga_all, r.ga_hbm)
    small_cols.finish()
    stores.put(r.sums_all, r.sums_hbm)
    square_rows.finish()
    stores.put(r.square_line, r.square_hbm)
    out_sum.finish()
    stores.put(r.grad_out, r.grad_out_hbm)
    stores.finish()


def layer(*operands):
    return pl.pallas_call(
        layer_kernel,
        name="layer",
        out_shape=[jax.ShapeDtypeStruct(*item) for item in fields(Results).values()],
        in_specs=list(fields(Inputs).values()),
        out_specs=[ANY] * len(fields(Results)),
        scratch_shapes=[pltpu.VMEM(*item) for item in fields(Scratch).values()]
        + [pltpu.SemaphoreType.DMA(item) for item in fields(Lines).values()],
        compiler_params=pltpu.CompilerParams(
            collective_id=1, has_side_effects=True, vmem_limit_bytes=60 << 20
        ),
    )(*operands)


def place_halves(blocks, base, q, out, start):
    lane = lax.broadcasted_iota(jnp.int32, (blocks.shape[1], 128), 1)
    for zz in range(4):
        at = base + (zz // 2) * 128
        left = blocks[2 * q, :, at : at + 128].astype(F32)
        right = blocks[2 * q + 1, :, at : at + 128].astype(F32)
        if zz % 2:
            left = pltpu.roll(left, 64, 1)
        else:
            right = pltpu.roll(right, 64, 1)
        to = start + (zz * 4 + q) * 128
        out[:, to : to + 128] = jnp.where(lane < 64, left, right)


def outputs_kernel(
    output, grad_inputs, grad_out, grad_reduce, ge_all, ga_all, gz_line, sums_all, square_line, ema,
    output_o, grad_inputs_o, values_o, mix_o, out_o, expand_o, reduce_o, ema_o, gains_o, biases_o, heads_o,
    shift_o, position_o, rms_o, turned,
):
    output_o[...] = output[...]
    grad_inputs_o[...] = grad_inputs[...]
    out_o[...] = grad_out[...]
    reduce_o[...] = grad_reduce[...]
    for s in range(8):
        for zz in range(4):
            at = (zz * 8 + s) * 128
            expand_o[:, at : at + 128] = ge_all[s, :, zz * 128 : (zz + 1) * 128].astype(F32)
        mix_o[:, s * 128 : (s + 1) * 128] = ga_all[s, :, 256:384].astype(F32)
        mix_o[:, 3200 + s * 128 : 3328 + s * 128] = ga_all[s, :, 640:768].astype(F32)
    mix_o[:, 1024:1152] = (gz_line[0] + gz_line[1]) + (gz_line[2] + gz_line[3])
    for q in range(4):
        place_halves(ga_all, 0, q, values_o, 0)
        place_halves(ga_all, 384, q, mix_o, 1152)
    mine = sums_all[lax.axis_index("dp")]
    mine = pltpu.roll(mine, (128 - 32 * lax.axis_index("fsdp")) % 128, 1)
    turned[0:40] = mine
    turned[40:128] = jnp.zeros((88, 128), F32)
    gains_o[...] = turned[32:35, 0:32]
    biases_o[...] = turned[35:37, 0:32]
    flipped = turned[...].T
    raw = ema[...].astype(F32)
    damping = jax.nn.sigmoid(raw[:, 0:16])
    mixing = jax.nn.sigmoid(raw[:, 16:32])
    expand = raw[:, 32:48]
    project = raw[:, 48:64]
    by_factor = flipped[0:32, 0:16] * (0.25 * project * mixing * expand)
    by_gain = flipped[0:32, 16:32]
    by_inflow = 0.25 * project * by_gain
    ema_o[:, 0:16] = -by_factor * mixing * damping * (1.0 - damping)
    ema_o[:, 16:32] = (by_inflow * expand - by_factor * damping) * mixing * (1.0 - mixing)
    ema_o[:, 32:48] = by_inflow * mixing
    ema_o[:, 48:64] = 0.25 * mixing * expand * by_gain
    heads_o[0:1] = sums_all[0, 37:38]
    heads_o[1:2] = sums_all[1, 37:38]
    shift_o[...] = sums_all[2, 37]
    position_o[...] = sums_all[3, 37]
    squares = (square_line[0] + square_line[1]) + (square_line[2] + square_line[3])
    roots = [jnp.sqrt(squares[k : k + 1] / (squares[3:4] * WIDE)) for k in range(3)]
    col = lax.broadcasted_iota(jnp.int32, (1, 128), 1)
    line = jnp.where(col == 0, roots[0], jnp.where(col == 1, roots[1], roots[2]))
    rms_o[...] = line[0, 0:3]


def outputs(parts, ema_params):
    shapes = (
        ((ROWS, WIDE), LOW), ((ROWS, WIDE), F32), ((32, 2048), F32), ((32, 4224), F32), ((64, WIDE), F32),
        ((32, 4096), F32), ((ROWS, WIDE), F32), ((32, 64), F32), ((3, 32), F32), ((2, 32), F32), ((2, 128), F32),
        ((128,), F32), ((128,), F32), ((3,), F32),
    )
    return pl.pallas_call(
        outputs_kernel,
        name="outputs",
        out_shape=[jax.ShapeDtypeStruct(shape, dtype) for shape, dtype in shapes],
        in_specs=[VMEM] * 10,
        out_specs=[VMEM] * len(shapes),
        scratch_shapes=[pltpu.VMEM((128, 128), F32)],
    )(*parts, ema_params)


def on_plane(
    inputs, lengths, w_values, w_mix, w_out, w_expand, w_reduce, ema_params,
    norm_gains, norm_biases, head_gains, query_bias, position_bias, cotangent,
):
    parts = layer(
        inputs, cotangent, w_values, w_mix, w_out, w_expand, w_reduce, ema_params, norm_gains, norm_biases,
        head_gains, query_bias, position_bias, lengths,
    )
    done = outputs(parts, ema_params)
    return tuple(done)


def layer_norm(value, gain, shift):
    centre = jnp.mean(value, axis=-1, keepdims=True)
    centered = value - centre
    spread = jnp.mean(centered * centered, axis=-1, keepdims=True)
    return centered * lax.rsqrt(spread + EPS) * gain + shift


def ema_mix(normed, keep, ema_params):
    count = ema_params.shape[1] // 4
    damping = jax.nn.sigmoid(ema_params[:, :count]).T
    mixing = jax.nn.sigmoid(ema_params[:, count : 2 * count]).T
    expand = ema_params[:, 2 * count : 3 * count].T
    project = ema_params[:, 3 * count :].T
    factor = 1.0 - mixing * damping
    inflow = mixing * expand

    def advance(state, item):
        column, flag = item
        state = factor * state * flag[:, None, None] + inflow * column[:, None, :]
        return (state, 0.25 * jnp.sum(project * state, axis=1))

    start = jnp.zeros((normed.shape[0], count, normed.shape[2]), jnp.float32)
    _, smooth = lax.scan(advance, start, (jnp.swapaxes(normed, 0, 1), jnp.swapaxes(keep, 0, 1)))
    return jnp.swapaxes(smooth, 0, 1)


def layout(lengths, rows):
    ends = jnp.cumsum(lengths, axis=1)
    starts = ends - lengths
    place = lax.broadcasted_iota(jnp.int32, (lengths.shape[0], rows), 1)
    begin = jnp.any(place[:, :, None] == starts[:, None, :], axis=2) | (place == ends)
    keep = jnp.where(begin, 0.0, 1.0).astype(jnp.float32)
    valid = jnp.where(place < ends, 1.0, 0.0).astype(jnp.float32)
    return (keep, valid)


def dot_rows(left, right):
    return lax.dot_general(
        left, right, (((0,), (0,)), ((), ())), preferred_element_type=jnp.float32
    )


def dot_cols(left, right):
    return lax.dot_general(
        left, right, (((1,), (1,)), ((), ())), preferred_element_type=jnp.float32
    )


def block_scores(query_low, key_low, position, scale):
    span = query_low.shape[1]
    row = lax.broadcasted_iota(jnp.int32, (span, span), 0)
    col = lax.broadcasted_iota(jnp.int32, (span, span), 1)
    table = position[jnp.clip(row - col, 0, span - 1)]
    scores = (
        jnp.einsum("kiz,kjz->kij", query_low, key_low, preferred_element_type=jnp.float32) * scale
        + table
    )
    return jnp.where(row >= col, scores, NEG)


def diagonal_sums(grid):
    size = grid.shape[0]
    flipped = grid[:, ::-1]
    padded = jnp.pad(flipped, ((0, 0), (0, size)))
    skewed = padded.reshape(-1)[: size * (2 * size - 1)].reshape(size, 2 * size - 1)
    return jnp.sum(skewed, axis=0)[size - 1 :]


def group_rows(value):
    return lax.all_gather(value, "fsdp", axis=0, tiled=True)


def group_total(value):
    return lax.psum_scatter(value, "fsdp", scatter_dimension=0, tiled=True)


def owner_layout(grad, owners):
    return grad.reshape(owners * 8, -1)


def owner_shard(piece, columns):
    return piece.reshape(-1, columns)


def on_device(
    inputs,
    lengths,
    w_values,
    w_mix,
    w_out,
    w_expand,
    w_reduce,
    ema_params,
    norm_gains,
    norm_biases,
    head_gains,
    query_bias,
    position_bias,
    cotangent,
):
    rows, width = inputs.shape
    span = position_bias.shape[0]
    blocks = rows // span
    key_width = head_gains.shape[1]
    scale = key_width ** (-0.5)
    keep, valid = layout(lengths, rows)
    mask = valid[0][:, None]
    gathered = (
        lax.all_gather(w_values, ("dp", "fsdp"), axis=0, tiled=True),
        lax.all_gather(w_mix, ("dp", "fsdp"), axis=0, tiled=True),
        lax.all_gather(w_out, ("dp", "fsdp"), axis=0, tiled=True),
        lax.all_gather(ema_params, ("dp", "fsdp"), axis=0, tiled=True),
        lax.all_gather(norm_gains, ("dp", "fsdp"), axis=1, tiled=True),
        lax.all_gather(norm_biases, ("dp", "fsdp"), axis=1, tiled=True),
    )
    values_full, mix_full, out_full, ema_full, gains_full, biases_full = gathered
    value_width = values_full.shape[1]
    group_size = lax.axis_size("fsdp")
    data_size = lax.axis_size("dp")
    owners = group_size * data_size
    shard_rows = w_expand.shape[0]
    hidden_units = w_expand.shape[1]
    unit_block = hidden_units // (group_size * data_size)
    pieces = w_expand.reshape(shard_rows, data_size, group_size, unit_block)
    swapped = lax.all_to_all(pieces, "fsdp", split_axis=2, concat_axis=0, tiled=True)
    expand_quarter, reduce_use = (
        lax.all_gather(swapped, "dp", axis=0, tiled=True),
        lax.all_gather(w_reduce, "dp", axis=0, tiled=True),
    )
    expand_use = expand_quarter.reshape(expand_quarter.shape[0], data_size * unit_block)
    gains_f = gains_full.astype(jnp.float32)
    biases_f = biases_full.astype(jnp.float32)
    heads_f = head_gains.astype(jnp.float32)
    query_shift = query_bias.astype(jnp.float32)
    position_f = position_bias.astype(jnp.float32)
    stream = inputs.astype(jnp.float32)

    def front(source, gain, shift, omega, params):
        normed_part = layer_norm(source, gain, shift)
        smooth = ema_mix(normed_part[None], keep, params)[0]
        return (normed_part, silu(smooth + omega * normed_part))

    (normed, mixed), front_back = jax.vjp(
        front, stream, gains_f[0], biases_f[0], gains_f[1], ema_full.astype(jnp.float32)
    )
    normed_low = normed.astype(jnp.bfloat16)
    mixed_low = mixed.astype(jnp.bfloat16)
    value_pre = jnp.dot(normed_low, values_full, preferred_element_type=jnp.float32)
    value_low = silu(value_pre).astype(jnp.bfloat16)
    mixture = jnp.dot(mixed_low, mix_full, preferred_element_type=jnp.float32)
    middle = width + key_width
    upper = middle + value_width
    update = jax.nn.sigmoid(mixture[:, :width])
    zeta_pre = mixture[:, width:middle]
    zeta = silu(zeta_pre)
    reset_pre = mixture[:, middle:upper]
    reset = silu(reset_pre)
    candidate = mixture[:, upper:]
    query_low = (
        (zeta * heads_f[0] + query_shift).astype(jnp.bfloat16).reshape(blocks, span, key_width)
    )
    key_low = (zeta * heads_f[1]).astype(jnp.bfloat16).reshape(blocks, span, key_width)
    value_blocks = value_low.reshape(blocks, span, value_width)
    scores = block_scores(query_low, key_low, position_f, scale)
    log_total = jax.nn.logsumexp(scores, axis=-1, keepdims=True)
    weights_low = jnp.exp(scores - log_total).astype(jnp.bfloat16)
    attended = jnp.einsum(
        "kij,kjv->kiv", weights_low, value_blocks, preferred_element_type=jnp.float32
    ).reshape(rows, value_width)
    gated_low = (attended * reset).astype(jnp.bfloat16)
    hidden_pre = candidate + jnp.dot(gated_low, out_full, preferred_element_type=jnp.float32)
    hidden = silu(hidden_pre)
    attn_branch = update * (hidden - stream)
    first = stream + attn_branch
    normed_two, norm_back = jax.vjp(layer_norm, first, gains_f[2], biases_f[1])
    normed_two_low = normed_two.astype(jnp.bfloat16)
    ffn_rows = group_rows(normed_two_low)
    expand_pre = jnp.dot(ffn_rows, expand_use, preferred_element_type=jnp.float32)
    expand_low = silu(expand_pre).astype(jnp.bfloat16)
    branch_part = jnp.dot(expand_low, reduce_use, preferred_element_type=jnp.float32)
    branch = group_total(branch_part)
    output = ((first + branch) * mask).astype(jnp.bfloat16)
    values_back, mix_back, out_back = (
        lax.all_gather(w_values, ("dp", "fsdp"), axis=0, tiled=True),
        lax.all_gather(w_mix, ("dp", "fsdp"), axis=0, tiled=True),
        lax.all_gather(w_out, ("dp", "fsdp"), axis=0, tiled=True),
    )
    grad_out = cotangent.astype(jnp.float32) * mask
    grad_branch = grad_out.astype(jnp.bfloat16)
    grad_rows = group_rows(grad_branch)
    grad_reduce = dot_rows(expand_low, grad_rows)
    grad_expand_out = dot_cols(grad_rows, reduce_use)
    grad_expand_pre = (grad_expand_out * silu_slope(expand_pre)).astype(jnp.bfloat16)
    grad_expand = dot_rows(ffn_rows, grad_expand_pre)
    normed_two_part = dot_cols(grad_expand_pre, expand_use)
    grad_normed_two = group_total(normed_two_part)
    grad_first_norm, grad_gain_two, grad_shift_two = norm_back(grad_normed_two)
    grad_first = grad_out + grad_first_norm
    grad_direct = grad_first * (1.0 - update)
    grad_update = grad_first * (hidden - stream)
    grad_hidden_pre = grad_first * update * silu_slope(hidden_pre)
    grad_hidden_low = grad_hidden_pre.astype(jnp.bfloat16)
    grad_out_proj = dot_rows(gated_low, grad_hidden_low)
    grad_gated = dot_cols(grad_hidden_low, out_back)
    grad_attended = (grad_gated * reset).astype(jnp.bfloat16).reshape(blocks, span, value_width)
    grad_reset = grad_gated * attended
    scores_again = block_scores(query_low, key_low, position_f, scale)
    probs = jnp.exp(scores_again - log_total)
    probs_low = probs.astype(jnp.bfloat16)
    grad_weights = jnp.einsum(
        "kiv,kjv->kij", grad_attended, value_blocks, preferred_element_type=jnp.float32
    )
    grad_value = jnp.einsum(
        "kij,kiv->kjv", probs_low, grad_attended, preferred_element_type=jnp.float32
    ).reshape(rows, value_width)
    inner = jnp.sum(probs * grad_weights, axis=-1, keepdims=True)
    grad_scores = (probs * (grad_weights - inner)).astype(jnp.bfloat16)
    grad_position = diagonal_sums(jnp.sum(grad_scores.astype(jnp.float32), axis=0))
    grad_query = (
        jnp.einsum(
            "kij,kjz->kiz", grad_scores, key_low, preferred_element_type=jnp.float32
        ).reshape(rows, key_width)
        * scale
    )
    grad_key = (
        jnp.einsum(
            "kij,kiz->kjz", grad_scores, query_low, preferred_element_type=jnp.float32
        ).reshape(rows, key_width)
        * scale
    )
    grad_value_pre = (grad_value * silu_slope(value_pre)).astype(jnp.bfloat16)
    grad_values = dot_rows(normed_low, grad_value_pre)
    grad_normed = dot_cols(grad_value_pre, values_back)
    grad_zeta = grad_query * heads_f[0] + grad_key * heads_f[1]
    grad_heads = jnp.stack([jnp.sum(grad_query * zeta, axis=0), jnp.sum(grad_key * zeta, axis=0)])
    grad_query_shift = jnp.sum(grad_query, axis=0)
    grad_mixture = jnp.concatenate(
        [
            grad_update * update * (1.0 - update),
            grad_zeta * silu_slope(zeta_pre),
            grad_reset * silu_slope(reset_pre),
            grad_hidden_pre,
        ],
        axis=1,
    ).astype(jnp.bfloat16)
    grad_mix = dot_rows(mixed_low, grad_mixture)
    grad_mixed = dot_cols(grad_mixture, mix_back)
    grad_source, grad_gain_one, grad_shift_one, grad_omega, grad_ema = front_back(
        (grad_normed, grad_mixed)
    )
    grad_inputs = grad_direct + grad_source
    grad_gains = jnp.stack([grad_gain_one, grad_omega, grad_gain_two])
    grad_shifts = jnp.stack([grad_shift_one, grad_shift_two])
    summed_expand, grad_reduce_dev = (
        lax.psum_scatter(grad_expand, "dp", scatter_dimension=0, tiled=True),
        lax.psum_scatter(grad_reduce, "dp", scatter_dimension=0, tiled=True),
    )
    summed_pieces = summed_expand.reshape(group_size * shard_rows, data_size, 1, unit_block)
    owned = lax.all_to_all(summed_pieces, "fsdp", split_axis=0, concat_axis=2, tiled=True)
    grad_expand_dev = owned.reshape(shard_rows, hidden_units)
    summed_block = (
        lax.psum_scatter(
            owner_layout(grad_values, owners), ("dp", "fsdp"), scatter_dimension=0, tiled=True
        ),
        lax.psum_scatter(
            owner_layout(grad_mix, owners), ("dp", "fsdp"), scatter_dimension=0, tiled=True
        ),
        lax.psum_scatter(grad_out_proj, ("dp", "fsdp"), scatter_dimension=0, tiled=True),
        lax.psum_scatter(
            owner_layout(grad_ema, owners), ("dp", "fsdp"), scatter_dimension=0, tiled=True
        ),
        lax.psum_scatter(grad_gains, ("dp", "fsdp"), scatter_dimension=1, tiled=True),
        lax.psum_scatter(grad_shifts, ("dp", "fsdp"), scatter_dimension=1, tiled=True),
    )
    values_flat, mix_flat, grad_out_dev, ema_flat, grad_gains_dev, grad_shifts_dev = summed_block
    grad_values_dev = owner_shard(values_flat, grad_values.shape[1])
    grad_mix_dev = owner_shard(mix_flat, grad_mix.shape[1])
    grad_ema_dev = owner_shard(ema_flat, grad_ema.shape[1])
    squares = jnp.stack(
        [
            jnp.sum(mask * stream * stream),
            jnp.sum(mask * attn_branch * attn_branch),
            jnp.sum(mask * branch * branch),
        ]
    )
    square_sums, tokens_seen, heads_total, shift_total, position_total = lax.psum(
        (squares, jnp.sum(valid), grad_heads, grad_query_shift, grad_position), ("dp", "fsdp")
    )
    rms = jnp.sqrt(square_sums / (tokens_seen * width))
    return (
        output,
        grad_inputs,
        grad_values_dev,
        grad_mix_dev,
        grad_out_dev,
        grad_expand_dev,
        grad_reduce_dev,
        grad_ema_dev,
        grad_gains_dev,
        grad_shifts_dev,
        heads_total,
        shift_total,
        position_total,
        rms,
    )


def solution(mesh):
    in_specs = (
        P(("dp", "fsdp"), None),
        P(("dp", "fsdp"), None),
        P(("dp", "fsdp"), None),
        P(("dp", "fsdp"), None),
        P(("dp", "fsdp"), None),
        P(("dp", "fsdp"), None),
        P(("dp", "fsdp"), None),
        P(("dp", "fsdp"), None),
        P(None, ("dp", "fsdp")),
        P(None, ("dp", "fsdp")),
        P(),
        P(),
        P(),
        P(("dp", "fsdp"), None),
    )
    out_specs = (
        P(("dp", "fsdp"), None),
        P(("dp", "fsdp"), None),
        P(("dp", "fsdp"), None),
        P(("dp", "fsdp"), None),
        P(("dp", "fsdp"), None),
        P(("dp", "fsdp"), None),
        P(("dp", "fsdp"), None),
        P(("dp", "fsdp"), None),
        P(None, ("dp", "fsdp")),
        P(None, ("dp", "fsdp")),
        P(),
        P(),
        P(),
        P(),
    )
    planes = mesh.shape["dp"] == 8 and mesh.shape["fsdp"] == 4
    return jax.shard_map(
        on_plane if planes else on_device, mesh=mesh, in_specs=in_specs, out_specs=out_specs, check_vma=False
    )
```

```python
import jax
import jax.numpy as jnp
from jax import lax
from jax.experimental import pallas as pl
from jax.experimental.pallas import tpu as pltpu
from jax.sharding import PartitionSpec as P

EPS = 1e-05
NEG = -1e30
F32 = jnp.float32
LOW = jnp.bfloat16
MESH = pl.DeviceIdType.MESH
LINES = 132
STATES = 16


def silu(value):
    return value * jax.nn.sigmoid(value)


def silu_slope(value):
    sigma = jax.nn.sigmoid(value)
    return sigma * (1.0 + value * (1.0 - sigma))


def here():
    dp = lax.axis_index("dp")
    f = lax.axis_index("fsdp")
    return dp // 2, dp % 2, f // 2, f % 2


def device(z, y, x, c):
    return (z * 2 + y, x * 2 + c)


def slot_of(y, x, c):
    return y * 4 + x * 2 + c


def plane_peers(y, x, c):
    peers = []
    for mask in range(1, 8):
        peers.append(
            (
                1 - y if mask & 4 else y,
                1 - x if mask & 2 else x,
                1 - c if mask & 1 else c,
            )
        )
    return peers


def line_peers(z):
    return [z + 1 - 2 * (z % 2), 3 - z, (z + 2) % 4]


def greet(across=True):
    z, y, x, c = here()
    barrier = pltpu.get_barrier_semaphore()
    count = 7
    for peer in plane_peers(y, x, c):
        pl.semaphore_signal(barrier, inc=1, device_id=device(z, *peer), device_id_type=MESH)
    if across:
        count = 10
        for other in line_peers(z):
            pl.semaphore_signal(barrier, inc=1, device_id=device(other, y, x, c), device_id_type=MESH)
    pl.semaphore_wait(barrier, count)


class Net:
    def __init__(self, send, recv):
        self.send = send
        self.recv = recv
        self.used = 0

    def take(self, count):
        self.used += count
        assert self.used <= LINES
        return self.used - count

    def make(self, line, src, dst, target):
        return pltpu.make_async_remote_copy(
            src_ref=src,
            dst_ref=dst,
            send_sem=self.send.at[line],
            recv_sem=self.recv.at[line],
            device_id=target,
            device_id_type=MESH,
        )

    def copy(self, src, dst, target):
        made = self.make(self.take(1), src, dst, target)
        made.start()
        return made


VMEM = pl.BlockSpec(memory_space=pltpu.VMEM)


def rows_dot(left, right):
    return lax.dot_general(left, right, (((0,), (0,)), ((), ())), preferred_element_type=F32)


def cols_dot(left, right):
    return lax.dot_general(left, right, (((1,), (1,)), ((), ())), preferred_element_type=F32)


def lanes_to_rows(wide, tall):
    for s in range(8):
        tall[:, s, :] = wide[:, s * 128 : (s + 1) * 128]


def pick_halves(arr, base, slot, pair):
    one = base + ((2 * pair * 8 + slot) // 2) * 128
    two = base + (((2 * pair + 1) * 8 + slot) // 2) * 128
    left = arr[:, one : one + 128].astype(F32)
    right = arr[:, two : two + 128].astype(F32)
    lane = lax.broadcasted_iota(jnp.int32, left.shape, 1)
    if slot % 2 == 0:
        return jnp.where(lane < 64, left, pltpu.roll(right, 64, 1)).astype(LOW)
    return jnp.where(lane < 64, pltpu.roll(left, 64, 1), right).astype(LOW)


def ema_forward(factor, gain, source, out):
    steps = source.shape[0]

    def step(t, states):
        column = source[t]
        new = []
        terms = []
        for j in range(STATES):
            state = factor[j] * states[j] + column
            new.append(state)
            terms.append(gain[j] * state)
        while len(terms) > 1:
            terms = [terms[i] + terms[i + 1] for i in range(0, len(terms), 2)]
        out[t] = terms[0]
        return tuple(new)

    zero = jnp.zeros(source.shape[1:], F32)
    lax.fori_loop(0, steps, step, (zero,) * STATES)


def ema_backward(fac, gain, nrm, pull_ref, factor_sum, gain_sum, out):
    steps = nrm.shape[0]
    zero = jnp.zeros(nrm.shape[1:], F32)
    group = 4
    for base in range(0, STATES, group):

        def step(t, carry):
            at = steps - 1 - t
            column = nrm[at]
            pull = pull_ref[at]
            new = []
            terms = []
            for k in range(group):
                state, slope, by_factor, by_gain = carry[4 * k : 4 * k + 4]
                f = fac[base + k]
                slope = f * slope + state
                state = f * state + pull
                new += [state, slope, by_factor + column * slope, by_gain + column * state]
                terms.append(gain[base + k] * state)
            total = (terms[0] + terms[1]) + (terms[2] + terms[3])
            out[at] = total if base == 0 else out[at] + total
            return tuple(new)

        done = lax.fori_loop(0, steps, step, (zero,) * (4 * group))
        for k in range(group):
            factor_sum[base + k] = done[4 * k + 2]
            gain_sum[base + k] = done[4 * k + 3]


class PlaneGather:
    def __init__(self, net, src, dst):
        z, y, x, c = here()
        self.net, self.src, self.dst = net, src, dst
        self.base = net.take(7)
        self.me = slot_of(y, x, c)

    def near(self, k):
        z, y, x, c = here()
        yy, xx = chip_of(k)
        return self.net.make(self.base + k - 1, self.src, self.dst.at[self.me], device(z, yy, xx, c))

    def twin(self, k):
        z, y, x, c = here()
        yy, xx = chip_of(k)
        block = self.dst.at[slot_of(yy, xx, c)]
        return self.net.make(self.base + 3 + k, block, block, device(z, y, x, 1 - c))

    def start(self, last=True):
        self.dst[self.me] = self.src[...]
        self.twin(0).start()
        for k in (1, 2, 3) if last else (1, 2):
            self.near(k).start()

    def take_near(self, k):
        self.near(k).wait_recv()
        self.twin(k).start()

    def take_twin(self, k):
        self.twin(k).wait_recv()

    def take_rest(self):
        for k in (1, 2, 3):
            self.take_near(k)
        for k in range(4):
            self.take_twin(k)

    def finish(self):
        for k in (1, 2, 3):
            self.near(k).wait_send()
        for k in range(4):
            self.twin(k).wait_send()


class RelayedGather(PlaneGather):
    def __init__(self, net, src, dst):
        super().__init__(net, src, dst)
        self.relays = net.take(2)

    def pass_on(self, h):
        z, y, x, c = here()
        yy, xx = chip_of(1 + h)
        to_y, to_x = chip_of(2 - h)
        block = self.dst.at[slot_of(yy, xx, c), pl.ds(h * 64, 64)]
        return self.net.make(self.relays + h, block, block, device(z, to_y, to_x, c))

    def take_sides(self):
        for k in (1, 2):
            self.near(k).wait_recv()
            self.pass_on(k - 1).start()
        for k in (1, 2):
            self.twin(k).start()

    def take_last(self):
        for h in range(2):
            self.pass_on(h).wait_recv()
        self.twin(3).start()

    def finish(self):
        for k in (1, 2):
            self.near(k).wait_send()
            self.pass_on(k - 1).wait_send()
        for k in range(4):
            self.twin(k).wait_send()


def chip_of(k):
    z, y, x, c = here()
    return (y + k // 2) % 2, (x + k % 2) % 2


class PlaneSum:
    def __init__(self, net, part, got, sent, far, total, pairs, keep):
        self.net = net
        self.part, self.got, self.sent, self.far, self.total = part, got, sent, far, total
        self.pairs, self.keep = pairs, keep
        self.base = net.take(8)

    def inner(self, k):
        z, y, x, c = here()
        return self.net.make(self.base + k, self.part.at[k], self.got.at[k], device(z, y, x, 1 - c))

    def outer(self, k):
        z, y, x, c = here()
        yy, xx = chip_of(k)
        return self.net.make(self.base + 3 + k, self.sent.at[k - 1], self.far.at[k - 1], device(z, yy, xx, c))

    def give(self, k):
        z, y, x, c = here()
        self.part[k] = self.pairs[1 - c].astype(self.part.dtype)
        self.inner(k).start()

    def hold(self):
        z, y, x, c = here()
        self.keep[...] = self.pairs[c]

    def pair(self, k):
        self.inner(k).wait_recv()
        both = self.keep[...] + self.got[k].astype(F32)

        @pl.when(k == 0)
        def _():
            self.total[...] = both

        @pl.when(k > 0)
        def _():
            self.sent[k - 1] = both.astype(self.sent.dtype)

        self.leave(k)

    def leave(self, k):
        @pl.when(k > 0)
        def _():
            self.outer(k).start()

    def run(self, make):
        @pl.loop(0, 4)
        def _(i):
            make(3 - i)
            self.give(3 - i)

            @pl.when(i > 0)
            def _():
                self.pair(4 - i)

            self.hold()

        self.pair(0)

    def settle(self):
        @pl.loop(0, 4)
        def _(k):
            self.inner(k).wait_send()

    def finish(self):
        @pl.loop(1, 4)
        def _(k):
            self.outer(k).wait()
            self.total[...] = self.total[...] + self.far[k - 1].astype(F32)


class RelayedSum(PlaneSum):
    def half(self, h):
        z, y, x, c = here()
        yy, xx = chip_of(1 + h)
        rows = pl.ds(h * 64, 64)
        return self.net.make(
            self.base + 6 + h, self.sent.at[2, rows], self.far.at[2, rows], device(z, yy, xx, c)
        )

    def leave(self, k):
        @pl.when(k == 3)
        def _():
            self.half(0).start()
            self.half(1).start()

    def relay(self):
        for h in range(2):
            self.half(h).wait_recv()
            at = 1 - h
            rows = slice(h * 64, (h + 1) * 64)
            self.sent[at, rows] = (self.sent[at, rows].astype(F32) + self.far[2, rows].astype(F32)).astype(LOW)
            self.outer(at + 1).start()

    def finish(self):
        for k in (1, 2):
            self.half(k - 1).wait_send()
            self.outer(k).wait()
        self.total[...] = self.total[...] + self.far[0].astype(F32) + self.far[1].astype(F32)


class LineGather:
    def __init__(self, net, buf):
        z, y, x, c = here()
        near, mirror, _ = line_peers(z)
        self.inside = z % 3 > 0
        relayed = (2 * z) % 3 + 3 * (z // 3)
        self.first = net.make(net.take(1), buf.at[z], buf.at[z], device(near, y, x, c))
        self.second = net.make(net.take(1), buf.at[z], buf.at[z], device(mirror, y, x, c))
        self.third = net.make(net.take(1), buf.at[relayed], buf.at[relayed], device((3 * z + 2) % 5, y, x, c))

    def start(self):
        self.first.start()
        self.second.start()

        @pl.when(jnp.logical_not(self.inside))
        def _():
            self.third.start()

    def relay(self):
        @pl.when(self.inside)
        def _():
            self.second.wait_recv()
            self.third.start()

    def finish(self):
        self.first.wait()
        self.second.wait_send()

        @pl.when(jnp.logical_not(self.inside))
        def _():
            self.second.wait_recv()

        self.third.wait()


class LineSum:
    def __init__(self, net, buf, got, out):
        z, y, x, c = here()
        near, mirror, across = line_peers(z)
        self.buf, self.got, self.out = buf, got, out
        self.inside = z % 3 > 0
        self.relayed = (2 * z) % 3 + 3 * (z // 3)
        self.first = net.make(net.take(1), buf.at[across], got.at[0], device((2 * z + 1) % 5, y, x, c))
        self.second = net.make(net.take(1), buf.at[near], got.at[1], device(near, y, x, c))
        self.third = net.make(net.take(1), buf.at[mirror], got.at[2], device(mirror, y, x, c))

    def run(self, make):
        z, y, x, c = here()

        @pl.loop(0, 4)
        def _(i):
            bits = (2 + 3 * i) % 4
            make((z // 2 + bits // 2) % 2 * 2 + (z + bits) % 2)

            @pl.when(i == 0)
            def _():
                self.first.start()

            @pl.when(i == 1)
            def _():
                self.second.start()

        self.start_last()

    def start(self, last=True):
        self.first.start()
        self.second.start()
        if last:
            self.start_last()

    def start_last(self):
        @pl.when(jnp.logical_not(self.inside))
        def _():
            self.third.start()

    def relay(self):
        @pl.when(self.inside)
        def _():
            self.first.wait_recv()
            self.buf[self.relayed] = (self.buf[self.relayed].astype(F32) + self.got[0].astype(F32)).astype(LOW)
            self.third.start()

    def finish(self):
        z, y, x, c = here()
        self.first.wait_send()
        self.second.wait()
        self.third.wait()
        total = self.buf[z].astype(F32) + self.got[1].astype(F32) + self.got[2].astype(F32)
        self.out[...] = total.reshape(self.out.shape).astype(self.out.dtype)

        @pl.when(jnp.logical_not(self.inside))
        def _():
            self.first.wait_recv()
            whole = total + self.got[0].astype(F32)
            self.out[...] = whole.reshape(self.out.shape).astype(self.out.dtype)


class Spread:
    def __init__(self, net, sends, whole):
        self.net, self.whole = net, whole
        self.line = net.take(1)
        for src, dst, target in sends:
            net.make(self.line, src, dst, target).start()

    def finish(self):
        pltpu.make_async_copy(self.whole, self.whole, self.net.recv.at[self.line]).wait()
        pltpu.make_async_copy(self.whole, self.whole, self.net.send.at[self.line]).wait()


def spread_plane(net, src, dst):
    z, y, x, c = here()
    me = slot_of(y, x, c)
    dst[me] = src[...]
    sends = [(src, dst.at[me], device(z, *peer)) for peer in plane_peers(y, x, c)]
    return Spread(net, sends, dst.at[pl.ds(0, 7)])


def spread_column(net, buf):
    z, y, x, c = here()
    block = buf.at[:, slot_of(y, x, c)]
    sends = [(block, block, device(z, *peer)) for peer in plane_peers(y, x, c)]
    return Spread(net, sends, buf.at[:, pl.ds(0, 7)])


def swap_plane(net, src, dst):
    z, y, x, c = here()
    me = slot_of(y, x, c)
    dst[me] = src[me]
    sends = [(src.at[slot_of(*peer)], dst.at[me], device(z, *peer)) for peer in plane_peers(y, x, c)]
    return Spread(net, sends, dst.at[pl.ds(0, 7)])


def spread_line(net, buf, part=None):
    z, y, x, c = here()
    block = buf.at[z] if part is None else buf.at[z, part]
    whole = buf.at[pl.ds(0, 3)] if part is None else buf.at[pl.ds(0, 3), part]
    return Spread(net, [(block, block, device(other, y, x, c)) for other in line_peers(z)], whole)


def swap_line(net, src, dst):
    z, y, x, c = here()
    dst[z] = src[z]
    sends = [(src.at[other], dst.at[z], device(other, y, x, c)) for other in line_peers(z)]
    return Spread(net, sends, dst.at[pl.ds(0, 3)])


class ChipSwap:
    def __init__(self, net, src, dst):
        z, y, x, c = here()
        self.net, self.src, self.dst = net, src, dst
        self.me = slot_of(y, x, c)
        self.base = net.take(8)

    def copy(self, k, twin):
        z, y, x, c = here()
        yy, xx = chip_of(k)
        cc = (c + twin) % 2
        return self.net.make(
            self.base + 2 * k + twin, self.src.at[slot_of(yy, xx, cc)], self.dst.at[self.me], device(z, yy, xx, cc)
        )

    def start(self):
        self.dst[self.me] = self.src[self.me]
        self.copy(0, 1).start()
        for k in (1, 2, 3):
            for twin in range(2):
                self.copy(k, twin).start()

    def take(self, k):
        self.copy(k, 1).wait_recv()

        @pl.when(k > 0)
        def _():
            self.copy(k, 0).wait_recv()

    def finish(self):
        self.copy(0, 1).wait_send()
        for k in (1, 2, 3):
            for twin in range(2):
                self.copy(k, twin).wait_send()


def row_mean(value):
    return jnp.mean(value, axis=-1, keepdims=True)


def standardized(value):
    centred = value - row_mean(value)
    inverse = lax.rsqrt(row_mean(centred * centred) + EPS)
    return centred * inverse, inverse


def norm_back(grad, xhat, inverse, gain):
    scaled = grad * gain
    return inverse * (scaled - row_mean(scaled) - xhat * row_mean(scaled * xhat))


def block_scores_of(zeta, heads, shift, table):
    query_low = (zeta * heads[0:1] + shift).astype(LOW)
    key_low = (zeta * heads[1:2]).astype(LOW)
    scores = cols_dot(query_low, key_low) * (zeta.shape[1] ** (-0.5)) + table[...]
    row = lax.broadcasted_iota(jnp.int32, scores.shape, 0)
    col = lax.broadcasted_iota(jnp.int32, scores.shape, 1)
    scores = jnp.where(row >= col, scores, NEG)
    top = jnp.max(scores, axis=-1, keepdims=True)
    log_total = top + jnp.log(jnp.sum(jnp.exp(scores - top), axis=-1, keepdims=True))
    return query_low, key_low, jnp.exp(scores - log_total)


def mirror_matrix(size):
    row = lax.broadcasted_iota(jnp.int32, (size, size), 0)
    col = lax.broadcasted_iota(jnp.int32, (size, size), 1)
    return jnp.where(row + col == size - 1, 1.0, 0.0).astype(LOW)


def column_of(line):
    size = line.shape[1]
    row = lax.broadcasted_iota(jnp.int32, (size, size), 0)
    col = lax.broadcasted_iota(jnp.int32, (size, size), 1)
    return jnp.sum(jnp.where(row == col, line, 0.0), axis=1, keepdims=True)


def cols_at(index, size):
    return pl.ds(pl.multiple_of(index * size, size), size)


def put_rows(sums, at, wide):
    sums[at : at + 1] = jnp.sum(wide, axis=0, keepdims=True)


ROWS = 128
WIDE = 1024
ALL = (8, ROWS, WIDE)
OWN = (ROWS, WIDE)


ANY = pl.BlockSpec(memory_space=pl.ANY)


class Inputs:
    x_in = ANY
    cot_in = ANY
    wv_in = ANY
    wm_in = ANY
    wo_in = ANY
    we_in = ANY
    wr_in = ANY
    ema = VMEM
    norm_gains = VMEM
    norm_biases = VMEM
    head_gains = VMEM
    query_bias = VMEM
    position_bias = VMEM
    lens = VMEM


class Results:
    output_hbm = (ROWS, WIDE), LOW
    grad_inputs_hbm = (ROWS, WIDE), F32
    grad_out_hbm = (64, WIDE), F32
    grad_reduce_hbm = (ROWS, WIDE), F32
    ge_hbm = (8, 32, 512), LOW
    ga_hbm = (8, 32, 768), LOW
    gz_hbm = (4, 32, 128), F32
    sums_hbm = (8, 40, 128), F32
    square_hbm = (4, 8, 128), F32


class Scratch:
    output = (ROWS, WIDE), LOW
    grad_inputs = (ROWS, WIDE), F32
    grad_out = (64, WIDE), F32
    grad_reduce = (ROWS, WIDE), F32
    ge_all = (8, 32, 512), LOW
    ga_all = (8, 32, 768), LOW
    gz_line = (4, 32, 128), F32
    sums_all = (8, 40, 128), F32
    square_line = (4, 8, 128), F32
    x = OWN, LOW
    cot = OWN, LOW
    wv = (32, 2048), LOW
    wm = (32, 4224), LOW
    we_own = (32, 4096), LOW
    small_wide = (32, 128), F32
    wz = (4, 8, 32, 128), LOW
    inverse = (ROWS, 128), F32
    small_all = (4, 8, 32, 128), LOW
    prm = (72, WIDE), F32
    blocks_a = (8, 32, 768), LOW
    blocks_e = (8, 32, 512), LOW
    wa = (4, 8, 32, 768), LOW
    wo = (4, 64, WIDE), LOW
    we = (4, 8, 32, 512), LOW
    wr = (4, ROWS, WIDE), LOW
    table = (128, 128), F32
    heads = (8, 128), F32
    own_low = OWN, LOW
    normed_all = ALL, LOW
    mixed_all = ALL, LOW
    cot_all = ALL, LOW
    two_all = ALL, LOW
    hid_all = ALL, LOW
    fac = (16, 8, 128), F32
    gain = (16, 8, 128), F32
    fac_sum = (16, 8, 128), F32
    gain_sum = (16, 8, 128), F32
    nrm = (ROWS, 8, 128), F32
    tall = (ROWS, 8, 128), F32
    tall_out = (ROWS, 8, 128), F32
    pre = OWN, F32
    value_pre = (8, ROWS, 256), F32
    value_low = (8, ROWS, 256), LOW
    zeta_pre = (8, ROWS, 128), F32
    weights_low = (8, ROWS, 128), LOW
    attended = (8, ROWS, 256), F32
    reset_pre = (8, ROWS, 256), F32
    gated = (8, ROWS, 256), LOW
    work = OWN, F32
    hidden_pre = OWN, F32
    update_pre = OWN, F32
    first = OWN, F32
    update_part = (8, ROWS, 128), LOW
    update_all = (8, ROWS, 128), LOW
    part = (4, ROWS, WIDE), LOW
    got = (4, ROWS, WIDE), LOW
    sent = (3, ROWS, WIDE), LOW
    far = (3, ROWS, WIDE), LOW
    got_b = (4, ROWS, WIDE), LOW
    sent_b = (3, ROWS, WIDE), LOW
    far_b = (3, ROWS, WIDE), LOW
    got_c = (4, ROWS, WIDE), LOW
    sent_c = (3, ROWS, WIDE), LOW
    far_c = (3, ROWS, WIDE), LOW
    pairs = (2, ROWS, WIDE), F32
    grad_two = OWN, F32
    scores_pairs = (2, ROWS, 128), F32
    scores_keep = (ROWS, 128), F32
    expand_pre = (8, ROWS, 512), F32
    expand_low = (8, ROWS, 512), LOW
    grad_pre = (8, ROWS, 512), LOW
    branch = OWN, F32
    value_back = (8, ROWS, 256), LOW
    mixture_back = (8, ROWS, 512), LOW
    scores_part = (4, ROWS, 128), F32
    scores_got = (4, ROWS, 128), F32
    scores_sent = (3, ROWS, 128), F32
    scores_far = (3, ROWS, 128), F32
    scores_sum = (ROWS, 128), F32
    zeta_own = (ROWS, 128), LOW
    zeta_all = (8, ROWS, 128), LOW
    gr = (4, ROWS, WIDE), LOW
    gr_got = (3, ROWS, WIDE), LOW
    ge = (4, 256, 512), LOW
    ge_got = (3, 256, 512), LOW
    ge_sum = (8, 32, 512), LOW
    go = (4, 64, WIDE), LOW
    go_got = (3, 64, WIDE), LOW
    ga = (4, 256, 768), LOW
    ga_got = (3, 256, 768), LOW
    ga_sum = (8, 32, 768), LOW
    gz = (4, 8, 32, 128), F32
    gz_own = (4, 32, 128), F32
    sums = (40, WIDE), F32
    sum_blocks = (8, 40, 128), F32
    sum_parts = (8, 40, 128), F32
    sum_rows = (4, 40, 128), F32
    sum_cols = (40, 128), F32
    square_own = (8, 128), F32
    square_all = (8, 8, 128), F32


class Lines:
    send = (LINES,)
    recv = (LINES,)
    load = (7,)
    store = (9,)


def fields(group):
    return {name: item for name, item in vars(group).items() if not name.startswith("_")}


class Refs:
    def __init__(self, refs):
        names = [name for group in (Inputs, Results, Scratch, Lines) for name in fields(group)]
        for name, ref in zip(names, refs, strict=True):
            setattr(self, name, ref)


class Stores:
    def __init__(self, sems):
        self.sems, self.made = sems, []

    def put(self, src, dst):
        copy = pltpu.make_async_copy(src, dst, self.sems.at[len(self.made)])
        copy.start()
        self.made.append(copy)

    def finish(self):
        for copy in self.made:
            copy.wait()


def layer_kernel(*refs):
    r = Refs(refs)
    net = Net(r.send, r.recv)
    z, y, x, c = here()
    me = slot_of(y, x, c)
    twin = device(z, y, x, 1 - c)
    tokens = 8 * ROWS
    stores = Stores(r.store)
    loads = [
        pltpu.make_async_copy(src, dst, r.load.at[line])
        for line, (src, dst) in enumerate(
            (
                (r.wm_in, r.wm), (r.wv_in, r.wv), (r.wo_in, r.wo.at[z]), (r.x_in, r.x), (r.we_in, r.we_own),
                (r.wr_in, r.wr.at[z]), (r.cot_in, r.cot),
            )
        )
    ]
    for load in loads:
        load.start()
    greet()
    for load in loads:
        load.wait()

    lane = lax.broadcasted_iota(jnp.int32, (32, 128), 1)
    r.small_wide[...] = jnp.zeros((32, 128), F32)
    r.small_wide[:, 0:64] = r.ema[...].astype(F32)
    small = r.small_wide[...]
    for k in range(5):
        line = r.norm_gains[k : k + 1, :] if k < 3 else r.norm_biases[k - 3 : k - 2, :]
        small = jnp.where(lane == 64 + k, column_of(line.astype(F32)), small)
    r.small_all[z, me] = small.astype(LOW)
    small_line = spread_line(net, r.small_all, me)
    r.wz[z, me] = r.wm[:, 1024:1152]
    zeta_line = spread_line(net, r.wz, me)
    for s in range(8):
        for pair in range(2):
            r.blocks_a[s, :, pair * 128 : (pair + 1) * 128] = pick_halves(r.wv, 0, s, pair)
            r.blocks_a[s, :, 384 + pair * 128 : 512 + pair * 128] = pick_halves(r.wm, 1152, s, pair)
        r.blocks_a[s, :, 256:384] = r.wm[:, s * 128 : (s + 1) * 128]
        r.blocks_a[s, :, 640:768] = r.wm[:, 3200 + s * 128 : 3328 + s * 128]
    attn_plane = swap_plane(net, r.blocks_a, r.wa.at[z])
    out_line = LineGather(net, r.wo)
    out_line.start()
    for s in range(8):
        for zz in range(4):
            r.blocks_e[s, :, zz * 128 : (zz + 1) * 128] = r.we_own[:, (zz * 8 + s) * 128 : (zz * 8 + s + 1) * 128]
    small_line.finish()
    small_plane = spread_column(net, r.small_all)
    near_base = net.take(3)

    def near(k):
        yy, xx = chip_of(k)
        return net.make(near_base + k - 1, r.x, r.mixed_all.at[me], device(z, yy, xx, c))

    for k in (1, 2, 3):
        near(k).start()
    zeta_line.finish()
    zeta_plane = spread_column(net, r.wz)
    expand_plane = swap_plane(net, r.blocks_e, r.we.at[z])
    row = lax.broadcasted_iota(jnp.int32, OWN, 0)
    r.own_low[...] = jnp.where(row < r.lens[...], r.cot[...].astype(F32), 0.0).astype(LOW)
    cot_plane = PlaneGather(net, r.own_low, r.cot_all)
    cot_plane.start()
    r.heads[0:2] = r.head_gains[...].astype(F32)
    r.heads[2:3] = r.query_bias[...].astype(F32).reshape(1, 128)
    wide = jnp.broadcast_to(r.position_bias[...].astype(F32).reshape(1, 128), (128, 128)).astype(LOW)
    turned = jnp.dot(wide, mirror_matrix(128), preferred_element_type=F32)
    r.table[...] = pltpu.roll(turned, 1, 1, stride=1, stride_axis=0)
    out_line.relay()
    attn_plane.finish()
    attn_line = LineGather(net, r.wa)
    attn_line.start()
    small_plane.finish()

    r.prm[...] = r.small_all[...].reshape(WIDE, 128).astype(F32).T[0:72]
    damping = jax.nn.sigmoid(r.prm[0:16])
    mixing = jax.nn.sigmoid(r.prm[16:32])
    lanes_to_rows(1.0 - mixing * damping, r.fac)
    lanes_to_rows(0.25 * r.prm[48:64] * (mixing * r.prm[32:48]), r.gain)
    pair_base = net.take(8)

    def pair_normed(k):
        yy, xx = chip_of(k)
        block = r.normed_all.at[slot_of(yy, xx, c)]
        return net.make(pair_base + k, block, block, twin)

    def pair_mixed(k):
        yy, xx = chip_of(k)
        block = r.mixed_all.at[slot_of(yy, xx, c)]
        return net.make(pair_base + 4 + k, block, block, twin)

    def mix(k, tall, pre):
        yy, xx = chip_of(k)
        slot = slot_of(yy, xx, c)
        source = r.mixed_all[slot]
        xhat, _ = standardized(source.astype(F32))
        normed = xhat * r.prm[64:65] + r.prm[67:68]
        r.normed_all[slot] = normed.astype(LOW)
        pair_normed(k).start()
        lanes_to_rows(normed, tall)
        pre[...] = r.prm[65:66] * normed
        ema_forward(r.fac, r.gain, tall, r.tall_out)
        for s in range(8):
            cols = slice(s * 128, (s + 1) * 128)
            pre[:, cols] = pre[:, cols] + r.tall_out[:, s, :]
        r.mixed_all[slot] = silu(pre[...]).astype(LOW)
        pair_mixed(k).start()

    r.mixed_all[me] = r.x[...]
    mix(0, r.nrm, r.pre)

    @pl.loop(1, 4)
    def _(k):
        near(k).wait_recv()

        @pl.when(k == 3)
        def _():
            attn_line.relay()

        mix(k, r.tall, r.work)

    expand_plane.finish()
    expand_line = LineGather(net, r.we)
    expand_line.start()
    reduce_line = LineGather(net, r.wr)
    reduce_line.start()
    cot_plane.take_rest()
    cot_plane.finish()
    for k in (1, 2, 3):
        near(k).wait_send()
    for k in range(4):
        pair_normed(k).wait()
        pair_mixed(k).wait()
    zeta_plane.finish()
    out_line.finish()
    attn_line.finish()

    cand_cols = cols_at(me, 128)
    shift = r.heads[2:3]

    def weights_a(first, last):
        return r.wa[:, :, :, first:last].reshape(WIDE, last - first)

    def zeta_weights():
        return r.wz[...].reshape(WIDE, 128)

    def pair_of(k):
        yy, xx = chip_of(k)
        return pl.ds((yy * 2 + xx) * 2, 2)

    def rows_of(ref, k):
        return ref[pair_of(k)].reshape(2 * ROWS, ref.shape[2])

    def put(ref, k, value):
        ref[pair_of(k)] = value.reshape(2, ROWS, ref.shape[2]).astype(ref.dtype)

    def attend(k):
        pre = jnp.dot(rows_of(r.normed_all, k), weights_a(0, 256), preferred_element_type=F32)
        put(r.value_pre, k, pre)
        low_values = silu(pre).astype(LOW)
        put(r.value_low, k, low_values)
        mixed = rows_of(r.mixed_all, k)
        mixture = jnp.dot(mixed, weights_a(256, 768), preferred_element_type=F32)
        put(r.update_part, k, mixture[:, 0:128])
        put(r.reset_pre, k, mixture[:, 128:384])
        zeta = jnp.dot(mixed, zeta_weights(), preferred_element_type=F32)
        put(r.zeta_pre, k, zeta)
        zeta = silu(zeta)
        values = []
        weights = []
        for h in range(2):
            rows = slice(h * ROWS, (h + 1) * ROWS)
            _, _, probs = block_scores_of(zeta[rows], r.heads, shift, r.table)
            weights.append(probs.astype(LOW))
            values.append(jnp.dot(weights[h], low_values[rows], preferred_element_type=F32))
        put(r.weights_low, k, jnp.concatenate(weights, axis=0))
        mixed_values = jnp.concatenate(values, axis=0)
        put(r.attended, k, mixed_values)
        gate = (mixed_values * silu(mixture[:, 128:384])).astype(LOW)
        put(r.gated, k, gate)
        hidden = jnp.dot(gate, r.wo[...].reshape(256, WIDE), preferred_element_type=F32)
        r.pairs[...] = hidden.reshape(2, ROWS, WIDE)
        r.pairs[:, :, cand_cols] = r.pairs[:, :, cand_cols] + mixture[:, 384:512].reshape(2, ROWS, 128)

    hidden_sum = PlaneSum(net, r.part, r.got, r.sent, r.far, r.hidden_pre, r.pairs, r.work)
    hidden_sum.run(attend)
    update_plane = swap_plane(net, r.update_part, r.update_all)
    expand_line.relay()
    hidden_sum.settle()
    hidden_sum.finish()
    update_plane.finish()
    for s in range(8):
        r.update_pre[:, s * 128 : (s + 1) * 128] = r.update_all[s].astype(F32)
    stream = r.x[...].astype(F32)
    r.first[...] = stream + jax.nn.sigmoid(r.update_pre[...]) * (silu(r.hidden_pre[...]) - stream)
    xhat, _ = standardized(r.first[...])
    r.own_low[...] = (xhat * r.prm[66:67] + r.prm[68:69]).astype(LOW)
    two_plane = RelayedGather(net, r.own_low, r.two_all)
    two_plane.start(last=False)
    reduce_line.relay()
    expand_line.finish()

    def reduce_rows():
        return r.wr[...].reshape(512, WIDE)

    def expand_rows():
        return r.we[...].reshape(WIDE, 512)

    @pl.loop(0, 4)
    def _(k):
        @pl.when(k == 1)
        def _():
            two_plane.take_sides()

        @pl.when(k == 3)
        def _():
            two_plane.take_last()

        two_plane.take_twin(k)
        pre = jnp.dot(rows_of(r.two_all, k), expand_rows(), preferred_element_type=F32)
        put(r.expand_pre, k, pre)
        put(r.expand_low, k, silu(pre))

    two_plane.finish()
    reduce_sum = LineSum(net, r.gr, r.gr_got, r.grad_reduce)
    expand_sum = LineSum(net, r.ge, r.ge_got, r.ge_sum)

    def reduce_grad(zz):
        r.gr[zz] = rows_dot(
            r.expand_low[:, :, cols_at(zz, 128)].reshape(tokens, 128), r.cot_all[...].reshape(tokens, WIDE)
        ).astype(LOW)

    reduce_sum.run(reduce_grad)
    reduce_line.finish()

    def expand_back(k):
        grad = (cols_dot(rows_of(r.cot_all, k), reduce_rows()) * silu_slope(rows_of(r.expand_pre, k))).astype(LOW)
        put(r.grad_pre, k, grad)
        r.pairs[...] = cols_dot(grad, expand_rows()).reshape(2, ROWS, WIDE)

    two_sum = PlaneSum(net, r.part, r.got, r.sent, r.far, r.grad_two, r.pairs, r.work)
    two_sum.run(expand_back)

    @pl.loop(0, 4)
    def _(zz):
        r.ge[zz] = rows_dot(
            r.two_all[:, :, cols_at(zz, 256)].reshape(tokens, 256), r.grad_pre[...].reshape(tokens, 512)
        ).astype(LOW)

    expand_sum.start()

    def branch_blocks(k):
        branch = jnp.dot(rows_of(r.expand_low, k), reduce_rows(), preferred_element_type=F32)
        r.pairs[...] = branch.reshape(2, ROWS, WIDE)

    two_sum.settle()
    branch_sum = RelayedSum(net, r.part, r.got_b, r.sent_b, r.far_b, r.branch, r.pairs, r.work)
    branch_sum.run(branch_blocks)
    reduce_sum.relay()
    valid = jnp.where(lax.broadcasted_iota(jnp.int32, (ROWS, 1), 0) < r.lens[...], 1.0, 0.0)
    update = jax.nn.sigmoid(r.update_pre[...])
    hidden = r.hidden_pre[...]
    r.work[...] = update * silu_slope(hidden)
    r.pairs[1] = (silu(hidden) - r.x[...].astype(F32)) * update * (1.0 - update)
    xhat, inverse = standardized(r.first[...])
    r.pairs[0] = xhat
    r.inverse[...] = jnp.broadcast_to(inverse, (ROWS, 128))
    two_sum.finish()

    grad_first = r.cot[...].astype(F32) * valid + norm_back(
        r.grad_two[...], r.pairs[0], r.inverse[:, 0:1], r.prm[66:67]
    )
    r.own_low[...] = (grad_first * r.work[...]).astype(LOW)
    hid_plane = RelayedGather(net, r.own_low, r.hid_all)
    hid_plane.start(last=False)
    grad_update = (grad_first * r.pairs[1]).astype(LOW)
    for s in range(8):
        r.update_part[s] = grad_update[:, s * 128 : (s + 1) * 128]
    upd_plane = ChipSwap(net, r.update_part, r.update_all)
    upd_plane.start()
    r.grad_inputs[...] = grad_first * (1.0 - jax.nn.sigmoid(r.update_pre[...]))
    put_rows(r.sums, 34, r.grad_two[...] * r.pairs[0])
    put_rows(r.sums, 36, r.grad_two[...])

    branch_sum.settle()
    expand_sum.relay()
    scores_plane = PlaneSum(
        net, r.scores_part, r.scores_got, r.scores_sent, r.scores_far, r.scores_sum, r.scores_pairs, r.scores_keep
    )
    mixed_sum = PlaneSum(net, r.part, r.got, r.sent, r.far, r.grad_two, r.pairs, r.work)

    def attend_back(k):
        gate_grad = cols_dot(rows_of(r.hid_all, k), r.wo[...].reshape(256, WIDE))
        pre = rows_of(r.reset_pre, k)
        low_grad = (gate_grad * silu(pre)).astype(LOW)
        low_values = rows_of(r.value_low, k)
        weights = rows_of(r.weights_low, k)
        backs = []
        for h in range(2):
            rows = slice(h * ROWS, (h + 1) * ROWS)
            r.scores_pairs[h] = cols_dot(low_grad[rows], low_values[rows])
            backs.append(rows_dot(weights[rows], low_grad[rows]))
        put(r.value_back, k, jnp.concatenate(backs, axis=0) * silu_slope(rows_of(r.value_pre, k)))
        pair = pair_of(k)
        r.mixture_back[pair, :, 0:128] = r.update_all[pair]
        r.mixture_back[pair, :, 128:384] = (
            (gate_grad * rows_of(r.attended, k) * silu_slope(pre)).astype(LOW).reshape(2, ROWS, 256)
        )
        r.mixture_back[pair, :, 384:512] = r.hid_all[pair, :, cand_cols]
        mixture = rows_of(r.mixture_back, k)
        mixed = cols_dot(mixture, weights_a(256, 768))
        r.pairs[...] = mixed.reshape(2, ROWS, WIDE)

    @pl.loop(0, 4)
    def _(k):
        @pl.when(k == 1)
        def _():
            hid_plane.take_sides()

        @pl.when(k == 3)
        def _():
            hid_plane.take_last()

        hid_plane.take_twin(k)
        upd_plane.take(k)
        attend_back(k)
        scores_plane.give(k)
        mixed_sum.give(k)

        @pl.when(k > 0)
        def _():
            scores_plane.pair(k - 1)
            mixed_sum.pair(k - 1)

        scores_plane.hold()
        mixed_sum.hold()

    scores_plane.pair(3)
    mixed_sum.pair(3)
    hid_plane.finish()
    upd_plane.finish()
    out_sum = LineSum(net, r.go, r.go_got, r.grad_out)
    attn_sum = LineSum(net, r.ga, r.ga_got, r.ga_sum)

    def attn_grad(zz):
        cols = cols_at(zz, 256)
        r.ga[zz, :, 0:256] = rows_dot(
            r.normed_all[:, :, cols].reshape(tokens, 256), r.value_back[...].reshape(tokens, 256)
        ).astype(LOW)
        r.ga[zz, :, 256:768] = rows_dot(
            r.mixed_all[:, :, cols].reshape(tokens, 256), r.mixture_back[...].reshape(tokens, 512)
        ).astype(LOW)

    attn_sum.run(attn_grad)

    @pl.loop(0, 4)
    def _(t):
        cols = cols_at(t, 256)
        grad = rows_dot(
            r.gated[...].reshape(tokens, 256), r.hid_all[:, :, cols].reshape(tokens, 256)
        ).astype(LOW)
        for zz in range(4):
            r.go[zz, :, cols] = grad[zz * 64 : (zz + 1) * 64]

    out_sum.start(last=False)


    reduce_sum.finish()
    stores.put(r.grad_reduce, r.grad_reduce_hbm)
    expand_sum.finish()
    mixed_sum.settle()
    normed_sum = RelayedSum(net, r.part, r.got_c, r.sent_c, r.far_c, r.hidden_pre, r.pairs, r.work)

    def normed_blocks(k):
        normed = cols_dot(rows_of(r.value_back, k), weights_a(0, 256))
        r.pairs[...] = normed.reshape(2, ROWS, WIDE)

    normed_sum.run(normed_blocks)

    scores_plane.settle()
    scores_plane.finish()
    grad_weights = r.scores_sum[...]
    zeta_own_pre = r.zeta_pre[me]
    zeta = silu(zeta_own_pre)
    query_low, key_low, probs = block_scores_of(zeta, r.heads, shift, r.table)
    grad_scores = (probs * (grad_weights - jnp.sum(probs * grad_weights, axis=-1, keepdims=True))).astype(LOW)
    scale = zeta.shape[1] ** (-0.5)
    grad_query = jnp.dot(grad_scores, key_low, preferred_element_type=F32) * scale
    grad_key = rows_dot(grad_scores, query_low) * scale
    skewed = pltpu.roll(
        jnp.dot(grad_scores, mirror_matrix(ROWS), preferred_element_type=F32), 1, 1, stride=1, stride_axis=0
    )
    r.sums[37:40] = jnp.zeros((3, WIDE), F32)
    r.sums[37:38, 0:128] = jnp.sum(grad_query * zeta, axis=0, keepdims=True)
    r.sums[37:38, 128:256] = jnp.sum(grad_key * zeta, axis=0, keepdims=True)
    r.sums[37:38, 256:384] = jnp.sum(grad_query, axis=0, keepdims=True)
    r.sums[37:38, 384:512] = jnp.sum(skewed, axis=0, keepdims=True)
    grad_zeta = grad_query * r.heads[0:1] + grad_key * r.heads[1:2]
    r.zeta_own[...] = (grad_zeta * silu_slope(zeta_own_pre)).astype(LOW)
    zeta_tokens = spread_plane(net, r.zeta_own, r.zeta_all)

    normed_sum.relay()
    branch_sum.relay()
    mixed_sum.finish()
    grad_mixed = r.grad_two[...] + cols_dot(r.zeta_own[...], zeta_weights())
    pull = grad_mixed * silu_slope(r.pre[...])
    lanes_to_rows(pull, r.tall)
    r.pre[...] = pull
    attn_sum.relay()
    ema_backward(r.fac, r.gain, r.nrm, r.tall, r.fac_sum, r.gain_sum, r.tall_out)
    for s in range(8):
        cols = slice(s * 128, (s + 1) * 128)
        r.sums[0:16, cols] = r.fac_sum[:, s, :]
        r.sums[16:32, cols] = r.gain_sum[:, s, :]
        r.sums[33:34, cols] = jnp.sum(r.pre[:, cols] * r.nrm[:, s, :], axis=0, keepdims=True)
    zeta_tokens.finish()
    r.gz[...] = rows_dot(
        r.mixed_all[...].reshape(tokens, WIDE), r.zeta_all[...].reshape(tokens, 128)
    ).reshape(4, 8, 32, 128)
    for zz in range(4):
        r.gz_own[zz] = r.gz[zz, me]
    zeta_grad = swap_line(net, r.gz_own, r.gz_line)
    normed_sum.settle()
    normed_sum.finish()
    for s in range(8):
        cols = slice(s * 128, (s + 1) * 128)
        r.hidden_pre[:, cols] = r.hidden_pre[:, cols] + r.pre[:, cols] * r.prm[65:66, cols] + r.tall_out[:, s, :]
    xhat_one, inverse_one = standardized(r.x[...].astype(F32))
    grad_one = r.hidden_pre[...]
    put_rows(r.sums, 32, grad_one * xhat_one)
    put_rows(r.sums, 35, grad_one)
    r.grad_inputs[...] = r.grad_inputs[...] + norm_back(grad_one, xhat_one, inverse_one, r.prm[64:65])

    stores.put(r.grad_inputs, r.grad_inputs_hbm)

    for s in range(8):
        r.sum_blocks[s] = r.sums[:, s * 128 : (s + 1) * 128]
    small_sum = swap_plane(net, r.sum_blocks, r.sum_parts)
    ge_plane = swap_plane(net, r.ge_sum, r.ge_all)
    small_sum.finish()
    whole = r.sum_parts[0]
    for s in range(1, 8):
        whole = whole + r.sum_parts[s]
    r.sum_rows[z] = whole
    small_rows = spread_line(net, r.sum_rows)
    branch_sum.finish()
    stream = r.x[...].astype(F32)
    first = r.first[...]
    branch = r.branch[...]
    r.output[...] = ((first + branch) * valid).astype(LOW)
    stores.put(r.output, r.output_hbm)
    r.square_own[...] = jnp.zeros((8, 128), F32)
    for k, item in enumerate((stream, first - stream, branch)):
        squares = jnp.sum(valid * item * item, axis=0, keepdims=True)
        r.square_own[k : k + 1] = jnp.broadcast_to(jnp.sum(squares, axis=1, keepdims=True), (1, 128))
    r.square_own[3:4] = jnp.broadcast_to(jnp.sum(valid, axis=0, keepdims=True), (1, 128))
    square_plane = spread_plane(net, r.square_own, r.square_all)
    attn_sum.finish()
    ga_plane = swap_plane(net, r.ga_sum, r.ga_all)
    small_rows.finish()
    r.sum_cols[...] = (r.sum_rows[0] + r.sum_rows[1]) + (r.sum_rows[2] + r.sum_rows[3])
    small_cols = spread_plane(net, r.sum_cols, r.sums_all)
    out_sum.start_last()
    out_sum.relay()
    square_plane.finish()
    squares = r.square_all[0]
    for s in range(1, 8):
        squares = squares + r.square_all[s]
    r.square_line[z] = squares
    square_rows = spread_line(net, r.square_line)
    ge_plane.finish()
    stores.put(r.ge_all, r.ge_hbm)
    zeta_grad.finish()
    stores.put(r.gz_line, r.gz_hbm)
    ga_plane.finish()
    stores.put(r.ga_all, r.ga_hbm)
    small_cols.finish()
    stores.put(r.sums_all, r.sums_hbm)
    square_rows.finish()
    stores.put(r.square_line, r.square_hbm)
    out_sum.finish()
    stores.put(r.grad_out, r.grad_out_hbm)
    stores.finish()


def layer(*operands):
    return pl.pallas_call(
        layer_kernel,
        name="layer",
        out_shape=[jax.ShapeDtypeStruct(*item) for item in fields(Results).values()],
        in_specs=list(fields(Inputs).values()),
        out_specs=[ANY] * len(fields(Results)),
        scratch_shapes=[pltpu.VMEM(*item) for item in fields(Scratch).values()]
        + [pltpu.SemaphoreType.DMA(item) for item in fields(Lines).values()],
        compiler_params=pltpu.CompilerParams(
            collective_id=1, has_side_effects=True, vmem_limit_bytes=60 << 20
        ),
    )(*operands)


def place_halves(blocks, base, q, out, start):
    lane = lax.broadcasted_iota(jnp.int32, (blocks.shape[1], 128), 1)
    for zz in range(4):
        at = base + (zz // 2) * 128
        left = blocks[2 * q, :, at : at + 128].astype(F32)
        right = blocks[2 * q + 1, :, at : at + 128].astype(F32)
        if zz % 2:
            left = pltpu.roll(left, 64, 1)
        else:
            right = pltpu.roll(right, 64, 1)
        to = start + (zz * 4 + q) * 128
        out[:, to : to + 128] = jnp.where(lane < 64, left, right)


def outputs_kernel(
    output, grad_inputs, grad_out, grad_reduce, ge_all, ga_all, gz_line, sums_all, square_line, ema,
    output_o, grad_inputs_o, values_o, mix_o, out_o, expand_o, reduce_o, ema_o, gains_o, biases_o, heads_o,
    shift_o, position_o, rms_o, turned,
):
    output_o[...] = output[...]
    grad_inputs_o[...] = grad_inputs[...]
    out_o[...] = grad_out[...]
    reduce_o[...] = grad_reduce[...]
    for s in range(8):
        for zz in range(4):
            at = (zz * 8 + s) * 128
            expand_o[:, at : at + 128] = ge_all[s, :, zz * 128 : (zz + 1) * 128].astype(F32)
        mix_o[:, s * 128 : (s + 1) * 128] = ga_all[s, :, 256:384].astype(F32)
        mix_o[:, 3200 + s * 128 : 3328 + s * 128] = ga_all[s, :, 640:768].astype(F32)
    mix_o[:, 1024:1152] = (gz_line[0] + gz_line[1]) + (gz_line[2] + gz_line[3])
    for q in range(4):
        place_halves(ga_all, 0, q, values_o, 0)
        place_halves(ga_all, 384, q, mix_o, 1152)
    mine = sums_all[lax.axis_index("dp")]
    mine = pltpu.roll(mine, (128 - 32 * lax.axis_index("fsdp")) % 128, 1)
    turned[0:40] = mine
    turned[40:128] = jnp.zeros((88, 128), F32)
    gains_o[...] = turned[32:35, 0:32]
    biases_o[...] = turned[35:37, 0:32]
    flipped = turned[...].T
    raw = ema[...].astype(F32)
    damping = jax.nn.sigmoid(raw[:, 0:16])
    mixing = jax.nn.sigmoid(raw[:, 16:32])
    expand = raw[:, 32:48]
    project = raw[:, 48:64]
    by_factor = flipped[0:32, 0:16] * (0.25 * project * mixing * expand)
    by_gain = flipped[0:32, 16:32]
    by_inflow = 0.25 * project * by_gain
    ema_o[:, 0:16] = -by_factor * mixing * damping * (1.0 - damping)
    ema_o[:, 16:32] = (by_inflow * expand - by_factor * damping) * mixing * (1.0 - mixing)
    ema_o[:, 32:48] = by_inflow * mixing
    ema_o[:, 48:64] = 0.25 * mixing * expand * by_gain
    heads_o[0:1] = sums_all[0, 37:38]
    heads_o[1:2] = sums_all[1, 37:38]
    shift_o[...] = sums_all[2, 37]
    position_o[...] = sums_all[3, 37]
    squares = (square_line[0] + square_line[1]) + (square_line[2] + square_line[3])
    roots = [jnp.sqrt(squares[k : k + 1] / (squares[3:4] * WIDE)) for k in range(3)]
    col = lax.broadcasted_iota(jnp.int32, (1, 128), 1)
    line = jnp.where(col == 0, roots[0], jnp.where(col == 1, roots[1], roots[2]))
    rms_o[...] = line[0, 0:3]


def outputs(parts, ema_params):
    shapes = (
        ((ROWS, WIDE), LOW), ((ROWS, WIDE), F32), ((32, 2048), F32), ((32, 4224), F32), ((64, WIDE), F32),
        ((32, 4096), F32), ((ROWS, WIDE), F32), ((32, 64), F32), ((3, 32), F32), ((2, 32), F32), ((2, 128), F32),
        ((128,), F32), ((128,), F32), ((3,), F32),
    )
    return pl.pallas_call(
        outputs_kernel,
        name="outputs",
        out_shape=[jax.ShapeDtypeStruct(shape, dtype) for shape, dtype in shapes],
        in_specs=[VMEM] * 10,
        out_specs=[VMEM] * len(shapes),
        scratch_shapes=[pltpu.VMEM((128, 128), F32)],
    )(*parts, ema_params)


def on_plane(
    inputs, lengths, w_values, w_mix, w_out, w_expand, w_reduce, ema_params,
    norm_gains, norm_biases, head_gains, query_bias, position_bias, cotangent,
):
    parts = layer(
        inputs, cotangent, w_values, w_mix, w_out, w_expand, w_reduce, ema_params, norm_gains, norm_biases,
        head_gains, query_bias, position_bias, lengths,
    )
    done = outputs(parts, ema_params)
    return tuple(done)


def layer_norm(value, gain, shift):
    centre = jnp.mean(value, axis=-1, keepdims=True)
    centered = value - centre
    spread = jnp.mean(centered * centered, axis=-1, keepdims=True)
    return centered * lax.rsqrt(spread + EPS) * gain + shift


def ema_mix(normed, keep, ema_params):
    count = ema_params.shape[1] // 4
    damping = jax.nn.sigmoid(ema_params[:, :count]).T
    mixing = jax.nn.sigmoid(ema_params[:, count : 2 * count]).T
    expand = ema_params[:, 2 * count : 3 * count].T
    project = ema_params[:, 3 * count :].T
    factor = 1.0 - mixing * damping
    inflow = mixing * expand

    def advance(state, item):
        column, flag = item
        state = factor * state * flag[:, None, None] + inflow * column[:, None, :]
        return (state, 0.25 * jnp.sum(project * state, axis=1))

    start = jnp.zeros((normed.shape[0], count, normed.shape[2]), jnp.float32)
    _, smooth = lax.scan(advance, start, (jnp.swapaxes(normed, 0, 1), jnp.swapaxes(keep, 0, 1)))
    return jnp.swapaxes(smooth, 0, 1)


def layout(lengths, rows):
    ends = jnp.cumsum(lengths, axis=1)
    starts = ends - lengths
    place = lax.broadcasted_iota(jnp.int32, (lengths.shape[0], rows), 1)
    begin = jnp.any(place[:, :, None] == starts[:, None, :], axis=2) | (place == ends)
    keep = jnp.where(begin, 0.0, 1.0).astype(jnp.float32)
    valid = jnp.where(place < ends, 1.0, 0.0).astype(jnp.float32)
    return (keep, valid)


def dot_rows(left, right):
    return lax.dot_general(
        left, right, (((0,), (0,)), ((), ())), preferred_element_type=jnp.float32
    )


def dot_cols(left, right):
    return lax.dot_general(
        left, right, (((1,), (1,)), ((), ())), preferred_element_type=jnp.float32
    )


def block_scores(query_low, key_low, position, scale):
    span = query_low.shape[1]
    row = lax.broadcasted_iota(jnp.int32, (span, span), 0)
    col = lax.broadcasted_iota(jnp.int32, (span, span), 1)
    table = position[jnp.clip(row - col, 0, span - 1)]
    scores = (
        jnp.einsum("kiz,kjz->kij", query_low, key_low, preferred_element_type=jnp.float32) * scale
        + table
    )
    return jnp.where(row >= col, scores, NEG)


def diagonal_sums(grid):
    size = grid.shape[0]
    flipped = grid[:, ::-1]
    padded = jnp.pad(flipped, ((0, 0), (0, size)))
    skewed = padded.reshape(-1)[: size * (2 * size - 1)].reshape(size, 2 * size - 1)
    return jnp.sum(skewed, axis=0)[size - 1 :]


def group_rows(value):
    return lax.all_gather(value, "fsdp", axis=0, tiled=True)


def group_total(value):
    return lax.psum_scatter(value, "fsdp", scatter_dimension=0, tiled=True)


def owner_layout(grad, owners):
    return grad.reshape(owners * 8, -1)


def owner_shard(piece, columns):
    return piece.reshape(-1, columns)


def on_device(
    inputs,
    lengths,
    w_values,
    w_mix,
    w_out,
    w_expand,
    w_reduce,
    ema_params,
    norm_gains,
    norm_biases,
    head_gains,
    query_bias,
    position_bias,
    cotangent,
):
    rows, width = inputs.shape
    span = position_bias.shape[0]
    blocks = rows // span
    key_width = head_gains.shape[1]
    scale = key_width ** (-0.5)
    keep, valid = layout(lengths, rows)
    mask = valid[0][:, None]
    gathered = (
        lax.all_gather(w_values, ("dp", "fsdp"), axis=0, tiled=True),
        lax.all_gather(w_mix, ("dp", "fsdp"), axis=0, tiled=True),
        lax.all_gather(w_out, ("dp", "fsdp"), axis=0, tiled=True),
        lax.all_gather(ema_params, ("dp", "fsdp"), axis=0, tiled=True),
        lax.all_gather(norm_gains, ("dp", "fsdp"), axis=1, tiled=True),
        lax.all_gather(norm_biases, ("dp", "fsdp"), axis=1, tiled=True),
    )
    values_full, mix_full, out_full, ema_full, gains_full, biases_full = gathered
    value_width = values_full.shape[1]
    group_size = lax.axis_size("fsdp")
    data_size = lax.axis_size("dp")
    owners = group_size * data_size
    shard_rows = w_expand.shape[0]
    hidden_units = w_expand.shape[1]
    unit_block = hidden_units // (group_size * data_size)
    pieces = w_expand.reshape(shard_rows, data_size, group_size, unit_block)
    swapped = lax.all_to_all(pieces, "fsdp", split_axis=2, concat_axis=0, tiled=True)
    expand_quarter, reduce_use = (
        lax.all_gather(swapped, "dp", axis=0, tiled=True),
        lax.all_gather(w_reduce, "dp", axis=0, tiled=True),
    )
    expand_use = expand_quarter.reshape(expand_quarter.shape[0], data_size * unit_block)
    gains_f = gains_full.astype(jnp.float32)
    biases_f = biases_full.astype(jnp.float32)
    heads_f = head_gains.astype(jnp.float32)
    query_shift = query_bias.astype(jnp.float32)
    position_f = position_bias.astype(jnp.float32)
    stream = inputs.astype(jnp.float32)

    def front(source, gain, shift, omega, params):
        normed_part = layer_norm(source, gain, shift)
        smooth = ema_mix(normed_part[None], keep, params)[0]
        return (normed_part, silu(smooth + omega * normed_part))

    (normed, mixed), front_back = jax.vjp(
        front, stream, gains_f[0], biases_f[0], gains_f[1], ema_full.astype(jnp.float32)
    )
    normed_low = normed.astype(jnp.bfloat16)
    mixed_low = mixed.astype(jnp.bfloat16)
    value_pre = jnp.dot(normed_low, values_full, preferred_element_type=jnp.float32)
    value_low = silu(value_pre).astype(jnp.bfloat16)
    mixture = jnp.dot(mixed_low, mix_full, preferred_element_type=jnp.float32)
    middle = width + key_width
    upper = middle + value_width
    update = jax.nn.sigmoid(mixture[:, :width])
    zeta_pre = mixture[:, width:middle]
    zeta = silu(zeta_pre)
    reset_pre = mixture[:, middle:upper]
    reset = silu(reset_pre)
    candidate = mixture[:, upper:]
    query_low = (
        (zeta * heads_f[0] + query_shift).astype(jnp.bfloat16).reshape(blocks, span, key_width)
    )
    key_low = (zeta * heads_f[1]).astype(jnp.bfloat16).reshape(blocks, span, key_width)
    value_blocks = value_low.reshape(blocks, span, value_width)
    scores = block_scores(query_low, key_low, position_f, scale)
    log_total = jax.nn.logsumexp(scores, axis=-1, keepdims=True)
    weights_low = jnp.exp(scores - log_total).astype(jnp.bfloat16)
    attended = jnp.einsum(
        "kij,kjv->kiv", weights_low, value_blocks, preferred_element_type=jnp.float32
    ).reshape(rows, value_width)
    gated_low = (attended * reset).astype(jnp.bfloat16)
    hidden_pre = candidate + jnp.dot(gated_low, out_full, preferred_element_type=jnp.float32)
    hidden = silu(hidden_pre)
    attn_branch = update * (hidden - stream)
    first = stream + attn_branch
    normed_two, norm_back = jax.vjp(layer_norm, first, gains_f[2], biases_f[1])
    normed_two_low = normed_two.astype(jnp.bfloat16)
    ffn_rows = group_rows(normed_two_low)
    expand_pre = jnp.dot(ffn_rows, expand_use, preferred_element_type=jnp.float32)
    expand_low = silu(expand_pre).astype(jnp.bfloat16)
    branch_part = jnp.dot(expand_low, reduce_use, preferred_element_type=jnp.float32)
    branch = group_total(branch_part)
    output = ((first + branch) * mask).astype(jnp.bfloat16)
    values_back, mix_back, out_back = (
        lax.all_gather(w_values, ("dp", "fsdp"), axis=0, tiled=True),
        lax.all_gather(w_mix, ("dp", "fsdp"), axis=0, tiled=True),
        lax.all_gather(w_out, ("dp", "fsdp"), axis=0, tiled=True),
    )
    grad_out = cotangent.astype(jnp.float32) * mask
    grad_branch = grad_out.astype(jnp.bfloat16)
    grad_rows = group_rows(grad_branch)
    grad_reduce = dot_rows(expand_low, grad_rows)
    grad_expand_out = dot_cols(grad_rows, reduce_use)
    grad_expand_pre = (grad_expand_out * silu_slope(expand_pre)).astype(jnp.bfloat16)
    grad_expand = dot_rows(ffn_rows, grad_expand_pre)
    normed_two_part = dot_cols(grad_expand_pre, expand_use)
    grad_normed_two = group_total(normed_two_part)
    grad_first_norm, grad_gain_two, grad_shift_two = norm_back(grad_normed_two)
    grad_first = grad_out + grad_first_norm
    grad_direct = grad_first * (1.0 - update)
    grad_update = grad_first * (hidden - stream)
    grad_hidden_pre = grad_first * update * silu_slope(hidden_pre)
    grad_hidden_low = grad_hidden_pre.astype(jnp.bfloat16)
    grad_out_proj = dot_rows(gated_low, grad_hidden_low)
    grad_gated = dot_cols(grad_hidden_low, out_back)
    grad_attended = (grad_gated * reset).astype(jnp.bfloat16).reshape(blocks, span, value_width)
    grad_reset = grad_gated * attended
    scores_again = block_scores(query_low, key_low, position_f, scale)
    probs = jnp.exp(scores_again - log_total)
    probs_low = probs.astype(jnp.bfloat16)
    grad_weights = jnp.einsum(
        "kiv,kjv->kij", grad_attended, value_blocks, preferred_element_type=jnp.float32
    )
    grad_value = jnp.einsum(
        "kij,kiv->kjv", probs_low, grad_attended, preferred_element_type=jnp.float32
    ).reshape(rows, value_width)
    inner = jnp.sum(probs * grad_weights, axis=-1, keepdims=True)
    grad_scores = (probs * (grad_weights - inner)).astype(jnp.bfloat16)
    grad_position = diagonal_sums(jnp.sum(grad_scores.astype(jnp.float32), axis=0))
    grad_query = (
        jnp.einsum(
            "kij,kjz->kiz", grad_scores, key_low, preferred_element_type=jnp.float32
        ).reshape(rows, key_width)
        * scale
    )
    grad_key = (
        jnp.einsum(
            "kij,kiz->kjz", grad_scores, query_low, preferred_element_type=jnp.float32
        ).reshape(rows, key_width)
        * scale
    )
    grad_value_pre = (grad_value * silu_slope(value_pre)).astype(jnp.bfloat16)
    grad_values = dot_rows(normed_low, grad_value_pre)
    grad_normed = dot_cols(grad_value_pre, values_back)
    grad_zeta = grad_query * heads_f[0] + grad_key * heads_f[1]
    grad_heads = jnp.stack([jnp.sum(grad_query * zeta, axis=0), jnp.sum(grad_key * zeta, axis=0)])
    grad_query_shift = jnp.sum(grad_query, axis=0)
    grad_mixture = jnp.concatenate(
        [
            grad_update * update * (1.0 - update),
            grad_zeta * silu_slope(zeta_pre),
            grad_reset * silu_slope(reset_pre),
            grad_hidden_pre,
        ],
        axis=1,
    ).astype(jnp.bfloat16)
    grad_mix = dot_rows(mixed_low, grad_mixture)
    grad_mixed = dot_cols(grad_mixture, mix_back)
    grad_source, grad_gain_one, grad_shift_one, grad_omega, grad_ema = front_back(
        (grad_normed, grad_mixed)
    )
    grad_inputs = grad_direct + grad_source
    grad_gains = jnp.stack([grad_gain_one, grad_omega, grad_gain_two])
    grad_shifts = jnp.stack([grad_shift_one, grad_shift_two])
    summed_expand, grad_reduce_dev = (
        lax.psum_scatter(grad_expand, "dp", scatter_dimension=0, tiled=True),
        lax.psum_scatter(grad_reduce, "dp", scatter_dimension=0, tiled=True),
    )
    summed_pieces = summed_expand.reshape(group_size * shard_rows, data_size, 1, unit_block)
    owned = lax.all_to_all(summed_pieces, "fsdp", split_axis=0, concat_axis=2, tiled=True)
    grad_expand_dev = owned.reshape(shard_rows, hidden_units)
    summed_block = (
        lax.psum_scatter(
            owner_layout(grad_values, owners), ("dp", "fsdp"), scatter_dimension=0, tiled=True
        ),
        lax.psum_scatter(
            owner_layout(grad_mix, owners), ("dp", "fsdp"), scatter_dimension=0, tiled=True
        ),
        lax.psum_scatter(grad_out_proj, ("dp", "fsdp"), scatter_dimension=0, tiled=True),
        lax.psum_scatter(
            owner_layout(grad_ema, owners), ("dp", "fsdp"), scatter_dimension=0, tiled=True
        ),
        lax.psum_scatter(grad_gains, ("dp", "fsdp"), scatter_dimension=1, tiled=True),
        lax.psum_scatter(grad_shifts, ("dp", "fsdp"), scatter_dimension=1, tiled=True),
    )
    values_flat, mix_flat, grad_out_dev, ema_flat, grad_gains_dev, grad_shifts_dev = summed_block
    grad_values_dev = owner_shard(values_flat, grad_values.shape[1])
    grad_mix_dev = owner_shard(mix_flat, grad_mix.shape[1])
    grad_ema_dev = owner_shard(ema_flat, grad_ema.shape[1])
    squares = jnp.stack(
        [
            jnp.sum(mask * stream * stream),
            jnp.sum(mask * attn_branch * attn_branch),
            jnp.sum(mask * branch * branch),
        ]
    )
    square_sums, tokens_seen, heads_total, shift_total, position_total = lax.psum(
        (squares, jnp.sum(valid), grad_heads, grad_query_shift, grad_position), ("dp", "fsdp")
    )
    rms = jnp.sqrt(square_sums / (tokens_seen * width))
    return (
        output,
        grad_inputs,
        grad_values_dev,
        grad_mix_dev,
        grad_out_dev,
        grad_expand_dev,
        grad_reduce_dev,
        grad_ema_dev,
        grad_gains_dev,
        grad_shifts_dev,
        heads_total,
        shift_total,
        position_total,
        rms,
    )


def solution(mesh):
    in_specs = (
        P(("dp", "fsdp"), None),
        P(("dp", "fsdp"), None),
        P(("dp", "fsdp"), None),
        P(("dp", "fsdp"), None),
        P(("dp", "fsdp"), None),
        P(("dp", "fsdp"), None),
        P(("dp", "fsdp"), None),
        P(("dp", "fsdp"), None),
        P(None, ("dp", "fsdp")),
        P(None, ("dp", "fsdp")),
        P(),
        P(),
        P(),
        P(("dp", "fsdp"), None),
    )
    out_specs = (
        P(("dp", "fsdp"), None),
        P(("dp", "fsdp"), None),
        P(("dp", "fsdp"), None),
        P(("dp", "fsdp"), None),
        P(("dp", "fsdp"), None),
        P(("dp", "fsdp"), None),
        P(("dp", "fsdp"), None),
        P(("dp", "fsdp"), None),
        P(None, ("dp", "fsdp")),
        P(None, ("dp", "fsdp")),
        P(),
        P(),
        P(),
        P(),
    )
    planes = mesh.shape["dp"] == 8 and mesh.shape["fsdp"] == 4
    return jax.shard_map(
        on_plane if planes else on_device, mesh=mesh, in_specs=in_specs, out_specs=out_specs, check_vma=False
    )
```

```python
import jax
import jax.numpy as jnp
from jax import lax
from jax.experimental import pallas as pl
from jax.experimental.pallas import tpu as pltpu
from jax.sharding import PartitionSpec as P

EPS = 1e-05
NEG = -1e30
F32 = jnp.float32
LOW = jnp.bfloat16
MESH = pl.DeviceIdType.MESH
LINES = 132
STATES = 16


def silu(value):
    return value * jax.nn.sigmoid(value)


def silu_slope(value):
    sigma = jax.nn.sigmoid(value)
    return sigma * (1.0 + value * (1.0 - sigma))


def here():
    dp = lax.axis_index("dp")
    f = lax.axis_index("fsdp")
    return dp // 2, dp % 2, f // 2, f % 2


def device(z, y, x, c):
    return (z * 2 + y, x * 2 + c)


def slot_of(y, x, c):
    return y * 4 + x * 2 + c


def plane_peers(y, x, c):
    peers = []
    for mask in range(1, 8):
        peers.append(
            (
                1 - y if mask & 4 else y,
                1 - x if mask & 2 else x,
                1 - c if mask & 1 else c,
            )
        )
    return peers


def line_peers(z):
    return [z + 1 - 2 * (z % 2), 3 - z, (z + 2) % 4]


def greet(across=True):
    z, y, x, c = here()
    barrier = pltpu.get_barrier_semaphore()
    count = 7
    for peer in plane_peers(y, x, c):
        pl.semaphore_signal(barrier, inc=1, device_id=device(z, *peer), device_id_type=MESH)
    if across:
        count = 10
        for other in line_peers(z):
            pl.semaphore_signal(barrier, inc=1, device_id=device(other, y, x, c), device_id_type=MESH)
    pl.semaphore_wait(barrier, count)


class Net:
    def __init__(self, send, recv):
        self.send = send
        self.recv = recv
        self.used = 0

    def take(self, count):
        self.used += count
        assert self.used <= LINES
        return self.used - count

    def make(self, line, src, dst, target):
        return pltpu.make_async_remote_copy(
            src_ref=src,
            dst_ref=dst,
            send_sem=self.send.at[line],
            recv_sem=self.recv.at[line],
            device_id=target,
            device_id_type=MESH,
        )

    def copy(self, src, dst, target):
        made = self.make(self.take(1), src, dst, target)
        made.start()
        return made


VMEM = pl.BlockSpec(memory_space=pltpu.VMEM)


def rows_dot(left, right):
    return lax.dot_general(left, right, (((0,), (0,)), ((), ())), preferred_element_type=F32)


def cols_dot(left, right):
    return lax.dot_general(left, right, (((1,), (1,)), ((), ())), preferred_element_type=F32)


def lanes_to_rows(wide, tall):
    for s in range(8):
        tall[:, s, :] = wide[:, s * 128 : (s + 1) * 128]


def pick_halves(arr, base, slot, pair):
    one = base + ((2 * pair * 8 + slot) // 2) * 128
    two = base + (((2 * pair + 1) * 8 + slot) // 2) * 128
    left = arr[:, one : one + 128].astype(F32)
    right = arr[:, two : two + 128].astype(F32)
    lane = lax.broadcasted_iota(jnp.int32, left.shape, 1)
    if slot % 2 == 0:
        return jnp.where(lane < 64, left, pltpu.roll(right, 64, 1)).astype(LOW)
    return jnp.where(lane < 64, pltpu.roll(left, 64, 1), right).astype(LOW)


def ema_forward(factor, gain, source, out):
    steps = source.shape[0]

    def step(t, states):
        column = source[t]
        new = []
        terms = []
        for j in range(STATES):
            state = factor[j] * states[j] + column
            new.append(state)
            terms.append(gain[j] * state)
        while len(terms) > 1:
            terms = [terms[i] + terms[i + 1] for i in range(0, len(terms), 2)]
        out[t] = terms[0]
        return tuple(new)

    zero = jnp.zeros(source.shape[1:], F32)
    lax.fori_loop(0, steps, step, (zero,) * STATES)


def ema_backward(fac, gain, nrm, pull_ref, factor_sum, gain_sum, out):
    steps = nrm.shape[0]
    zero = jnp.zeros(nrm.shape[1:], F32)
    group = 4
    for base in range(0, STATES, group):

        def step(t, carry):
            at = steps - 1 - t
            column = nrm[at]
            pull = pull_ref[at]
            new = []
            terms = []
            for k in range(group):
                state, slope, by_factor, by_gain = carry[4 * k : 4 * k + 4]
                f = fac[base + k]
                slope = f * slope + state
                state = f * state + pull
                new += [state, slope, by_factor + column * slope, by_gain + column * state]
                terms.append(gain[base + k] * state)
            total = (terms[0] + terms[1]) + (terms[2] + terms[3])
            out[at] = total if base == 0 else out[at] + total
            return tuple(new)

        done = lax.fori_loop(0, steps, step, (zero,) * (4 * group))
        for k in range(group):
            factor_sum[base + k] = done[4 * k + 2]
            gain_sum[base + k] = done[4 * k + 3]


class PlaneGather:
    def __init__(self, net, src, dst):
        z, y, x, c = here()
        self.net, self.src, self.dst = net, src, dst
        self.base = net.take(7)
        self.me = slot_of(y, x, c)

    def near(self, k):
        z, y, x, c = here()
        yy, xx = chip_of(k)
        return self.net.make(self.base + k - 1, self.src, self.dst.at[self.me], device(z, yy, xx, c))

    def twin(self, k):
        z, y, x, c = here()
        yy, xx = chip_of(k)
        block = self.dst.at[slot_of(yy, xx, c)]
        return self.net.make(self.base + 3 + k, block, block, device(z, y, x, 1 - c))

    def start(self, last=True):
        self.dst[self.me] = self.src[...]
        self.twin(0).start()
        for k in (1, 2, 3) if last else (1, 2):
            self.near(k).start()

    def take_near(self, k):
        self.near(k).wait_recv()
        self.twin(k).start()

    def take_twin(self, k):
        self.twin(k).wait_recv()

    def take_rest(self):
        for k in (1, 2, 3):
            self.take_near(k)
        for k in range(4):
            self.take_twin(k)

    def finish(self):
        for k in (1, 2, 3):
            self.near(k).wait_send()
        for k in range(4):
            self.twin(k).wait_send()


class RelayedGather(PlaneGather):
    def __init__(self, net, src, dst):
        super().__init__(net, src, dst)
        self.relays = net.take(2)

    def pass_on(self, h):
        z, y, x, c = here()
        yy, xx = chip_of(1 + h)
        to_y, to_x = chip_of(2 - h)
        block = self.dst.at[slot_of(yy, xx, c), pl.ds(h * 64, 64)]
        return self.net.make(self.relays + h, block, block, device(z, to_y, to_x, c))

    def take_sides(self):
        for k in (1, 2):
            self.near(k).wait_recv()
            self.pass_on(k - 1).start()
        for k in (1, 2):
            self.twin(k).start()

    def take_last(self):
        for h in range(2):
            self.pass_on(h).wait_recv()
        self.twin(3).start()

    def finish(self):
        for k in (1, 2):
            self.near(k).wait_send()
            self.pass_on(k - 1).wait_send()
        for k in range(4):
            self.twin(k).wait_send()


def chip_of(k):
    z, y, x, c = here()
    return (y + k // 2) % 2, (x + k % 2) % 2


class PlaneSum:
    def __init__(self, net, part, got, sent, far, total, pairs, keep):
        self.net = net
        self.part, self.got, self.sent, self.far, self.total = part, got, sent, far, total
        self.pairs, self.keep = pairs, keep
        self.base = net.take(8)

    def inner(self, k):
        z, y, x, c = here()
        return self.net.make(self.base + k, self.part.at[k], self.got.at[k], device(z, y, x, 1 - c))

    def outer(self, k):
        z, y, x, c = here()
        yy, xx = chip_of(k)
        return self.net.make(self.base + 3 + k, self.sent.at[k - 1], self.far.at[k - 1], device(z, yy, xx, c))

    def give(self, k):
        z, y, x, c = here()
        self.part[k] = self.pairs[1 - c].astype(self.part.dtype)
        self.inner(k).start()

    def hold(self):
        z, y, x, c = here()
        self.keep[...] = self.pairs[c]

    def pair(self, k):
        self.inner(k).wait_recv()
        both = self.keep[...] + self.got[k].astype(F32)

        @pl.when(k == 0)
        def _():
            self.total[...] = both

        @pl.when(k > 0)
        def _():
            self.sent[k - 1] = both.astype(self.sent.dtype)

        self.leave(k)

    def leave(self, k):
        @pl.when(k > 0)
        def _():
            self.outer(k).start()

    def run(self, make):
        @pl.loop(0, 4)
        def _(i):
            make(3 - i)
            self.give(3 - i)

            @pl.when(i > 0)
            def _():
                self.pair(4 - i)

            self.hold()

        self.pair(0)

    def settle(self):
        @pl.loop(0, 4)
        def _(k):
            self.inner(k).wait_send()

    def finish(self):
        @pl.loop(1, 4)
        def _(k):
            self.outer(k).wait()
            self.total[...] = self.total[...] + self.far[k - 1].astype(F32)


class RelayedSum(PlaneSum):
    def half(self, h):
        z, y, x, c = here()
        yy, xx = chip_of(1 + h)
        rows = pl.ds(h * 64, 64)
        return self.net.make(
            self.base + 6 + h, self.sent.at[2, rows], self.far.at[2, rows], device(z, yy, xx, c)
        )

    def leave(self, k):
        @pl.when(k == 3)
        def _():
            self.half(0).start()
            self.half(1).start()

    def relay(self):
        for h in range(2):
            self.half(h).wait_recv()
            at = 1 - h
            rows = slice(h * 64, (h + 1) * 64)
            self.sent[at, rows] = (self.sent[at, rows].astype(F32) + self.far[2, rows].astype(F32)).astype(LOW)
            self.outer(at + 1).start()

    def finish(self):
        for k in (1, 2):
            self.half(k - 1).wait_send()
            self.outer(k).wait()
        self.total[...] = self.total[...] + self.far[0].astype(F32) + self.far[1].astype(F32)


class LineGather:
    def __init__(self, net, buf):
        z, y, x, c = here()
        near, mirror, _ = line_peers(z)
        self.inside = z % 3 > 0
        relayed = (2 * z) % 3 + 3 * (z // 3)
        self.first = net.make(net.take(1), buf.at[z], buf.at[z], device(near, y, x, c))
        self.second = net.make(net.take(1), buf.at[z], buf.at[z], device(mirror, y, x, c))
        self.third = net.make(net.take(1), buf.at[relayed], buf.at[relayed], device((3 * z + 2) % 5, y, x, c))

    def start(self):
        self.first.start()
        self.second.start()

        @pl.when(jnp.logical_not(self.inside))
        def _():
            self.third.start()

    def relay(self):
        @pl.when(self.inside)
        def _():
            self.second.wait_recv()
            self.third.start()

    def finish(self):
        self.first.wait()
        self.second.wait_send()

        @pl.when(jnp.logical_not(self.inside))
        def _():
            self.second.wait_recv()

        self.third.wait()


class LineSum:
    def __init__(self, net, buf, got, out):
        z, y, x, c = here()
        near, mirror, across = line_peers(z)
        self.buf, self.got, self.out = buf, got, out
        self.inside = z % 3 > 0
        self.relayed = (2 * z) % 3 + 3 * (z // 3)
        self.first = net.make(net.take(1), buf.at[across], got.at[0], device((2 * z + 1) % 5, y, x, c))
        self.second = net.make(net.take(1), buf.at[near], got.at[1], device(near, y, x, c))
        self.third = net.make(net.take(1), buf.at[mirror], got.at[2], device(mirror, y, x, c))

    def run(self, make):
        z, y, x, c = here()

        @pl.loop(0, 4)
        def _(i):
            bits = (2 + 3 * i) % 4
            make((z // 2 + bits // 2) % 2 * 2 + (z + bits) % 2)

            @pl.when(i == 0)
            def _():
                self.first.start()

            @pl.when(i == 1)
            def _():
                self.second.start()

        self.start_last()

    def start(self, last=True):
        self.first.start()
        self.second.start()
        if last:
            self.start_last()

    def start_last(self):
        @pl.when(jnp.logical_not(self.inside))
        def _():
            self.third.start()

    def relay(self):
        @pl.when(self.inside)
        def _():
            self.first.wait_recv()
            self.buf[self.relayed] = (self.buf[self.relayed].astype(F32) + self.got[0].astype(F32)).astype(LOW)
            self.third.start()

    def finish(self):
        z, y, x, c = here()
        self.first.wait_send()
        self.second.wait()
        self.third.wait()
        total = self.buf[z].astype(F32) + self.got[1].astype(F32) + self.got[2].astype(F32)
        self.out[...] = total.reshape(self.out.shape).astype(self.out.dtype)

        @pl.when(jnp.logical_not(self.inside))
        def _():
            self.first.wait_recv()
            whole = total + self.got[0].astype(F32)
            self.out[...] = whole.reshape(self.out.shape).astype(self.out.dtype)


class Spread:
    def __init__(self, net, sends, whole):
        self.net, self.whole = net, whole
        self.line = net.take(1)
        for src, dst, target in sends:
            net.make(self.line, src, dst, target).start()

    def finish(self):
        pltpu.make_async_copy(self.whole, self.whole, self.net.recv.at[self.line]).wait()
        pltpu.make_async_copy(self.whole, self.whole, self.net.send.at[self.line]).wait()


def spread_plane(net, src, dst):
    z, y, x, c = here()
    me = slot_of(y, x, c)
    dst[me] = src[...]
    sends = [(src, dst.at[me], device(z, *peer)) for peer in plane_peers(y, x, c)]
    return Spread(net, sends, dst.at[pl.ds(0, 7)])


def spread_column(net, buf):
    z, y, x, c = here()
    block = buf.at[:, slot_of(y, x, c)]
    sends = [(block, block, device(z, *peer)) for peer in plane_peers(y, x, c)]
    return Spread(net, sends, buf.at[:, pl.ds(0, 7)])


def swap_plane(net, src, dst):
    z, y, x, c = here()
    me = slot_of(y, x, c)
    dst[me] = src[me]
    sends = [(src.at[slot_of(*peer)], dst.at[me], device(z, *peer)) for peer in plane_peers(y, x, c)]
    return Spread(net, sends, dst.at[pl.ds(0, 7)])


def spread_line(net, buf, part=None):
    z, y, x, c = here()
    block = buf.at[z] if part is None else buf.at[z, part]
    whole = buf.at[pl.ds(0, 3)] if part is None else buf.at[pl.ds(0, 3), part]
    return Spread(net, [(block, block, device(other, y, x, c)) for other in line_peers(z)], whole)


def swap_line(net, src, dst):
    z, y, x, c = here()
    dst[z] = src[z]
    sends = [(src.at[other], dst.at[z], device(other, y, x, c)) for other in line_peers(z)]
    return Spread(net, sends, dst.at[pl.ds(0, 3)])


class ChipSwap:
    def __init__(self, net, src, dst):
        z, y, x, c = here()
        self.net, self.src, self.dst = net, src, dst
        self.me = slot_of(y, x, c)
        self.base = net.take(8)

    def copy(self, k, twin):
        z, y, x, c = here()
        yy, xx = chip_of(k)
        cc = (c + twin) % 2
        return self.net.make(
            self.base + 2 * k + twin, self.src.at[slot_of(yy, xx, cc)], self.dst.at[self.me], device(z, yy, xx, cc)
        )

    def start(self):
        self.dst[self.me] = self.src[self.me]
        self.copy(0, 1).start()
        for k in (1, 2, 3):
            for twin in range(2):
                self.copy(k, twin).start()

    def take(self, k):
        self.copy(k, 1).wait_recv()

        @pl.when(k > 0)
        def _():
            self.copy(k, 0).wait_recv()

    def finish(self):
        self.copy(0, 1).wait_send()
        for k in (1, 2, 3):
            for twin in range(2):
                self.copy(k, twin).wait_send()


def row_mean(value):
    return jnp.mean(value, axis=-1, keepdims=True)


def standardized(value):
    centred = value - row_mean(value)
    inverse = lax.rsqrt(row_mean(centred * centred) + EPS)
    return centred * inverse, inverse


def norm_back(grad, xhat, inverse, gain):
    scaled = grad * gain
    return inverse * (scaled - row_mean(scaled) - xhat * row_mean(scaled * xhat))


def block_scores_of(zeta, heads, shift, table):
    query_low = (zeta * heads[0:1] + shift).astype(LOW)
    key_low = (zeta * heads[1:2]).astype(LOW)
    scores = cols_dot(query_low, key_low) * (zeta.shape[1] ** (-0.5)) + table[...]
    row = lax.broadcasted_iota(jnp.int32, scores.shape, 0)
    col = lax.broadcasted_iota(jnp.int32, scores.shape, 1)
    scores = jnp.where(row >= col, scores, NEG)
    top = jnp.max(scores, axis=-1, keepdims=True)
    log_total = top + jnp.log(jnp.sum(jnp.exp(scores - top), axis=-1, keepdims=True))
    return query_low, key_low, jnp.exp(scores - log_total)


def mirror_matrix(size):
    row = lax.broadcasted_iota(jnp.int32, (size, size), 0)
    col = lax.broadcasted_iota(jnp.int32, (size, size), 1)
    return jnp.where(row + col == size - 1, 1.0, 0.0).astype(LOW)


def column_of(line):
    size = line.shape[1]
    row = lax.broadcasted_iota(jnp.int32, (size, size), 0)
    col = lax.broadcasted_iota(jnp.int32, (size, size), 1)
    return jnp.sum(jnp.where(row == col, line, 0.0), axis=1, keepdims=True)


def cols_at(index, size):
    return pl.ds(pl.multiple_of(index * size, size), size)


def put_rows(sums, at, wide):
    sums[at : at + 1] = jnp.sum(wide, axis=0, keepdims=True)


ROWS = 128
WIDE = 1024
ALL = (8, ROWS, WIDE)
OWN = (ROWS, WIDE)


ANY = pl.BlockSpec(memory_space=pl.ANY)


class Inputs:
    x_in = ANY
    cot_in = ANY
    wv_in = ANY
    wm_in = ANY
    wo_in = ANY
    we_in = ANY
    wr_in = ANY
    ema = VMEM
    norm_gains = VMEM
    norm_biases = VMEM
    head_gains = VMEM
    query_bias = VMEM
    position_bias = VMEM
    lens = VMEM


class Results:
    output_hbm = (ROWS, WIDE), LOW
    grad_inputs_hbm = (ROWS, WIDE), F32
    grad_out_hbm = (64, WIDE), F32
    grad_reduce_hbm = (ROWS, WIDE), F32
    ge_hbm = (8, 32, 512), LOW
    ga_hbm = (8, 32, 768), LOW
    gz_hbm = (4, 32, 128), F32
    sums_hbm = (8, 40, 128), F32
    square_hbm = (4, 8, 128), F32


class Scratch:
    output = (ROWS, WIDE), LOW
    grad_inputs = (ROWS, WIDE), F32
    grad_out = (64, WIDE), F32
    grad_reduce = (ROWS, WIDE), F32
    ge_all = (8, 32, 512), LOW
    ga_all = (8, 32, 768), LOW
    gz_line = (4, 32, 128), F32
    sums_all = (8, 40, 128), F32
    square_line = (4, 8, 128), F32
    x = OWN, LOW
    cot = OWN, LOW
    wv = (32, 2048), LOW
    wm = (32, 4224), LOW
    we_own = (32, 4096), LOW
    small_wide = (32, 128), F32
    wz = (4, 8, 32, 128), LOW
    inverse = (ROWS, 128), F32
    small_all = (4, 8, 32, 128), LOW
    prm = (72, WIDE), F32
    blocks_a = (8, 32, 768), LOW
    blocks_e = (8, 32, 512), LOW
    wa = (4, 8, 32, 768), LOW
    wo = (4, 64, WIDE), LOW
    we = (4, 8, 32, 512), LOW
    wr = (4, ROWS, WIDE), LOW
    table = (128, 128), F32
    heads = (8, 128), F32
    own_low = OWN, LOW
    normed_all = ALL, LOW
    mixed_all = ALL, LOW
    cot_all = ALL, LOW
    two_all = ALL, LOW
    hid_all = ALL, LOW
    fac = (16, 8, 128), F32
    gain = (16, 8, 128), F32
    fac_sum = (16, 8, 128), F32
    gain_sum = (16, 8, 128), F32
    nrm = (ROWS, 8, 128), F32
    tall = (ROWS, 8, 128), F32
    tall_out = (ROWS, 8, 128), F32
    pre = OWN, F32
    value_pre = (8, ROWS, 256), F32
    value_low = (8, ROWS, 256), LOW
    zeta_pre = (8, ROWS, 128), F32
    weights_low = (8, ROWS, 128), LOW
    attended = (8, ROWS, 256), F32
    reset_pre = (8, ROWS, 256), F32
    gated = (8, ROWS, 256), LOW
    work = OWN, F32
    hidden_pre = OWN, F32
    update_pre = OWN, F32
    first = OWN, F32
    update_part = (8, ROWS, 128), LOW
    update_all = (8, ROWS, 128), LOW
    part = (4, ROWS, WIDE), LOW
    got = (4, ROWS, WIDE), LOW
    sent = (3, ROWS, WIDE), LOW
    far = (3, ROWS, WIDE), LOW
    got_b = (4, ROWS, WIDE), LOW
    sent_b = (3, ROWS, WIDE), LOW
    far_b = (3, ROWS, WIDE), LOW
    got_c = (4, ROWS, WIDE), LOW
    sent_c = (3, ROWS, WIDE), LOW
    far_c = (3, ROWS, WIDE), LOW
    pairs = (2, ROWS, WIDE), F32
    grad_two = OWN, F32
    scores_pairs = (2, ROWS, 128), F32
    scores_keep = (ROWS, 128), F32
    expand_pre = (8, ROWS, 512), F32
    expand_low = (8, ROWS, 512), LOW
    grad_pre = (8, ROWS, 512), LOW
    branch = OWN, F32
    value_back = (8, ROWS, 256), LOW
    mixture_back = (8, ROWS, 512), LOW
    scores_part = (4, ROWS, 128), F32
    scores_got = (4, ROWS, 128), F32
    scores_sent = (3, ROWS, 128), F32
    scores_far = (3, ROWS, 128), F32
    scores_sum = (ROWS, 128), F32
    zeta_own = (ROWS, 128), LOW
    zeta_all = (8, ROWS, 128), LOW
    gr = (4, ROWS, WIDE), LOW
    gr_got = (3, ROWS, WIDE), LOW
    ge = (4, 256, 512), LOW
    ge_got = (3, 256, 512), LOW
    ge_sum = (8, 32, 512), LOW
    go = (4, 64, WIDE), LOW
    go_got = (3, 64, WIDE), LOW
    ga = (4, 256, 768), LOW
    ga_got = (3, 256, 768), LOW
    ga_sum = (8, 32, 768), LOW
    gz = (4, 8, 32, 128), F32
    gz_own = (4, 32, 128), F32
    sums = (40, WIDE), F32
    sum_blocks = (8, 40, 128), F32
    sum_parts = (8, 40, 128), F32
    sum_rows = (4, 40, 128), F32
    sum_cols = (40, 128), F32
    square_own = (8, 128), F32
    square_all = (8, 8, 128), F32


class Lines:
    send = (LINES,)
    recv = (LINES,)
    load = (7,)
    store = (9,)


def fields(group):
    return {name: item for name, item in vars(group).items() if not name.startswith("_")}


class Refs:
    def __init__(self, refs):
        names = [name for group in (Inputs, Results, Scratch, Lines) for name in fields(group)]
        for name, ref in zip(names, refs, strict=True):
            setattr(self, name, ref)


class Stores:
    def __init__(self, sems):
        self.sems, self.made = sems, []

    def put(self, src, dst):
        copy = pltpu.make_async_copy(src, dst, self.sems.at[len(self.made)])
        copy.start()
        self.made.append(copy)

    def finish(self):
        for copy in self.made:
            copy.wait()


def layer_kernel(*refs):
    r = Refs(refs)
    net = Net(r.send, r.recv)
    z, y, x, c = here()
    me = slot_of(y, x, c)
    twin = device(z, y, x, 1 - c)
    tokens = 8 * ROWS
    stores = Stores(r.store)
    loads = [
        pltpu.make_async_copy(src, dst, r.load.at[line])
        for line, (src, dst) in enumerate(
            (
                (r.wm_in, r.wm), (r.wv_in, r.wv), (r.wo_in, r.wo.at[z]), (r.x_in, r.x), (r.we_in, r.we_own),
                (r.wr_in, r.wr.at[z]), (r.cot_in, r.cot),
            )
        )
    ]
    for load in loads:
        load.start()
    greet()
    for load in loads:
        load.wait()

    lane = lax.broadcasted_iota(jnp.int32, (32, 128), 1)
    r.small_wide[...] = jnp.zeros((32, 128), F32)
    r.small_wide[:, 0:64] = r.ema[...].astype(F32)
    small = r.small_wide[...]
    for k in range(5):
        line = r.norm_gains[k : k + 1, :] if k < 3 else r.norm_biases[k - 3 : k - 2, :]
        small = jnp.where(lane == 64 + k, column_of(line.astype(F32)), small)
    r.small_all[z, me] = small.astype(LOW)
    small_line = spread_line(net, r.small_all, me)
    r.wz[z, me] = r.wm[:, 1024:1152]
    zeta_line = spread_line(net, r.wz, me)
    for s in range(8):
        for pair in range(2):
            r.blocks_a[s, :, pair * 128 : (pair + 1) * 128] = pick_halves(r.wv, 0, s, pair)
            r.blocks_a[s, :, 384 + pair * 128 : 512 + pair * 128] = pick_halves(r.wm, 1152, s, pair)
        r.blocks_a[s, :, 256:384] = r.wm[:, s * 128 : (s + 1) * 128]
        r.blocks_a[s, :, 640:768] = r.wm[:, 3200 + s * 128 : 3328 + s * 128]
    attn_plane = swap_plane(net, r.blocks_a, r.wa.at[z])
    out_line = LineGather(net, r.wo)
    out_line.start()
    for s in range(8):
        for zz in range(4):
            r.blocks_e[s, :, zz * 128 : (zz + 1) * 128] = r.we_own[:, (zz * 8 + s) * 128 : (zz * 8 + s + 1) * 128]
    small_line.finish()
    small_plane = spread_column(net, r.small_all)
    near_base = net.take(3)

    def near(k):
        yy, xx = chip_of(k)
        return net.make(near_base + k - 1, r.x, r.mixed_all.at[me], device(z, yy, xx, c))

    for k in (1, 2, 3):
        near(k).start()
    zeta_line.finish()
    zeta_plane = spread_column(net, r.wz)
    expand_plane = swap_plane(net, r.blocks_e, r.we.at[z])
    row = lax.broadcasted_iota(jnp.int32, OWN, 0)
    r.own_low[...] = jnp.where(row < r.lens[...], r.cot[...].astype(F32), 0.0).astype(LOW)
    cot_plane = PlaneGather(net, r.own_low, r.cot_all)
    cot_plane.start()
    r.heads[0:2] = r.head_gains[...].astype(F32)
    r.heads[2:3] = r.query_bias[...].astype(F32).reshape(1, 128)
    wide = jnp.broadcast_to(r.position_bias[...].astype(F32).reshape(1, 128), (128, 128)).astype(LOW)
    turned = jnp.dot(wide, mirror_matrix(128), preferred_element_type=F32)
    r.table[...] = pltpu.roll(turned, 1, 1, stride=1, stride_axis=0)
    out_line.relay()
    attn_plane.finish()
    attn_line = LineGather(net, r.wa)
    attn_line.start()
    small_plane.finish()

    r.prm[...] = r.small_all[...].reshape(WIDE, 128).astype(F32).T[0:72]
    damping = jax.nn.sigmoid(r.prm[0:16])
    mixing = jax.nn.sigmoid(r.prm[16:32])
    lanes_to_rows(1.0 - mixing * damping, r.fac)
    lanes_to_rows(0.25 * r.prm[48:64] * (mixing * r.prm[32:48]), r.gain)
    pair_base = net.take(8)

    def pair_normed(k):
        yy, xx = chip_of(k)
        block = r.normed_all.at[slot_of(yy, xx, c)]
        return net.make(pair_base + k, block, block, twin)

    def pair_mixed(k):
        yy, xx = chip_of(k)
        block = r.mixed_all.at[slot_of(yy, xx, c)]
        return net.make(pair_base + 4 + k, block, block, twin)

    def mix(k, tall, pre):
        yy, xx = chip_of(k)
        slot = slot_of(yy, xx, c)
        source = r.mixed_all[slot]
        xhat, _ = standardized(source.astype(F32))
        normed = xhat * r.prm[64:65] + r.prm[67:68]
        r.normed_all[slot] = normed.astype(LOW)
        pair_normed(k).start()
        lanes_to_rows(normed, tall)
        pre[...] = r.prm[65:66] * normed
        ema_forward(r.fac, r.gain, tall, r.tall_out)
        for s in range(8):
            cols = slice(s * 128, (s + 1) * 128)
            pre[:, cols] = pre[:, cols] + r.tall_out[:, s, :]
        r.mixed_all[slot] = silu(pre[...]).astype(LOW)
        pair_mixed(k).start()

    r.mixed_all[me] = r.x[...]
    mix(0, r.nrm, r.pre)

    @pl.loop(1, 4)
    def _(k):
        near(k).wait_recv()

        @pl.when(k == 3)
        def _():
            attn_line.relay()

        mix(k, r.tall, r.work)

    expand_plane.finish()
    expand_line = LineGather(net, r.we)
    expand_line.start()
    reduce_line = LineGather(net, r.wr)
    reduce_line.start()
    cot_plane.take_rest()
    cot_plane.finish()
    for k in (1, 2, 3):
        near(k).wait_send()
    for k in range(4):
        pair_normed(k).wait()
        pair_mixed(k).wait()
    zeta_plane.finish()
    out_line.finish()
    attn_line.finish()

    cand_cols = cols_at(me, 128)
    shift = r.heads[2:3]

    def weights_a(first, last):
        return r.wa[:, :, :, first:last].reshape(WIDE, last - first)

    def zeta_weights():
        return r.wz[...].reshape(WIDE, 128)

    def pair_of(k):
        yy, xx = chip_of(k)
        return pl.ds((yy * 2 + xx) * 2, 2)

    def rows_of(ref, k):
        return ref[pair_of(k)].reshape(2 * ROWS, ref.shape[2])

    def put(ref, k, value):
        ref[pair_of(k)] = value.reshape(2, ROWS, ref.shape[2]).astype(ref.dtype)

    def attend(k):
        pre = jnp.dot(rows_of(r.normed_all, k), weights_a(0, 256), preferred_element_type=F32)
        put(r.value_pre, k, pre)
        low_values = silu(pre).astype(LOW)
        put(r.value_low, k, low_values)
        mixed = rows_of(r.mixed_all, k)
        mixture = jnp.dot(mixed, weights_a(256, 768), preferred_element_type=F32)
        put(r.update_part, k, mixture[:, 0:128])
        put(r.reset_pre, k, mixture[:, 128:384])
        zeta = jnp.dot(mixed, zeta_weights(), preferred_element_type=F32)
        put(r.zeta_pre, k, zeta)
        zeta = silu(zeta)
        values = []
        weights = []
        for h in range(2):
            rows = slice(h * ROWS, (h + 1) * ROWS)
            _, _, probs = block_scores_of(zeta[rows], r.heads, shift, r.table)
            weights.append(probs.astype(LOW))
            values.append(jnp.dot(weights[h], low_values[rows], preferred_element_type=F32))
        put(r.weights_low, k, jnp.concatenate(weights, axis=0))
        mixed_values = jnp.concatenate(values, axis=0)
        put(r.attended, k, mixed_values)
        gate = (mixed_values * silu(mixture[:, 128:384])).astype(LOW)
        put(r.gated, k, gate)
        hidden = jnp.dot(gate, r.wo[...].reshape(256, WIDE), preferred_element_type=F32)
        r.pairs[...] = hidden.reshape(2, ROWS, WIDE)
        r.pairs[:, :, cand_cols] = r.pairs[:, :, cand_cols] + mixture[:, 384:512].reshape(2, ROWS, 128)

    hidden_sum = PlaneSum(net, r.part, r.got, r.sent, r.far, r.hidden_pre, r.pairs, r.work)
    hidden_sum.run(attend)
    update_plane = swap_plane(net, r.update_part, r.update_all)
    expand_line.relay()
    hidden_sum.settle()
    hidden_sum.finish()
    update_plane.finish()
    for s in range(8):
        r.update_pre[:, s * 128 : (s + 1) * 128] = r.update_all[s].astype(F32)
    stream = r.x[...].astype(F32)
    r.first[...] = stream + jax.nn.sigmoid(r.update_pre[...]) * (silu(r.hidden_pre[...]) - stream)
    xhat, _ = standardized(r.first[...])
    r.own_low[...] = (xhat * r.prm[66:67] + r.prm[68:69]).astype(LOW)
    two_plane = RelayedGather(net, r.own_low, r.two_all)
    two_plane.start(last=False)
    reduce_line.relay()
    expand_line.finish()

    def reduce_rows():
        return r.wr[...].reshape(512, WIDE)

    def expand_rows():
        return r.we[...].reshape(WIDE, 512)

    @pl.loop(0, 4)
    def _(k):
        @pl.when(k == 1)
        def _():
            two_plane.take_sides()

        @pl.when(k == 3)
        def _():
            two_plane.take_last()

        two_plane.take_twin(k)
        pre = jnp.dot(rows_of(r.two_all, k), expand_rows(), preferred_element_type=F32)
        put(r.expand_pre, k, pre)
        put(r.expand_low, k, silu(pre))

    two_plane.finish()
    reduce_sum = LineSum(net, r.gr, r.gr_got, r.grad_reduce)
    expand_sum = LineSum(net, r.ge, r.ge_got, r.ge_sum)

    def reduce_grad(zz):
        r.gr[zz] = rows_dot(
            r.expand_low[:, :, cols_at(zz, 128)].reshape(tokens, 128), r.cot_all[...].reshape(tokens, WIDE)
        ).astype(LOW)

    reduce_sum.run(reduce_grad)
    reduce_line.finish()

    def expand_back(k):
        grad = (cols_dot(rows_of(r.cot_all, k), reduce_rows()) * silu_slope(rows_of(r.expand_pre, k))).astype(LOW)
        put(r.grad_pre, k, grad)
        r.pairs[...] = cols_dot(grad, expand_rows()).reshape(2, ROWS, WIDE)

    two_sum = PlaneSum(net, r.part, r.got, r.sent, r.far, r.grad_two, r.pairs, r.work)
    two_sum.run(expand_back)

    @pl.loop(0, 4)
    def _(zz):
        r.ge[zz] = rows_dot(
            r.two_all[:, :, cols_at(zz, 256)].reshape(tokens, 256), r.grad_pre[...].reshape(tokens, 512)
        ).astype(LOW)

    expand_sum.start()

    def branch_blocks(k):
        branch = jnp.dot(rows_of(r.expand_low, k), reduce_rows(), preferred_element_type=F32)
        r.pairs[...] = branch.reshape(2, ROWS, WIDE)

    two_sum.settle()
    branch_sum = RelayedSum(net, r.part, r.got_b, r.sent_b, r.far_b, r.branch, r.pairs, r.work)
    branch_sum.run(branch_blocks)
    reduce_sum.relay()
    valid = jnp.where(lax.broadcasted_iota(jnp.int32, (ROWS, 1), 0) < r.lens[...], 1.0, 0.0)
    update = jax.nn.sigmoid(r.update_pre[...])
    hidden = r.hidden_pre[...]
    r.work[...] = update * silu_slope(hidden)
    r.pairs[1] = (silu(hidden) - r.x[...].astype(F32)) * update * (1.0 - update)
    xhat, inverse = standardized(r.first[...])
    r.pairs[0] = xhat
    r.inverse[...] = jnp.broadcast_to(inverse, (ROWS, 128))
    two_sum.finish()

    grad_first = r.cot[...].astype(F32) * valid + norm_back(
        r.grad_two[...], r.pairs[0], r.inverse[:, 0:1], r.prm[66:67]
    )
    r.own_low[...] = (grad_first * r.work[...]).astype(LOW)
    hid_plane = RelayedGather(net, r.own_low, r.hid_all)
    hid_plane.start(last=False)
    grad_update = (grad_first * r.pairs[1]).astype(LOW)
    for s in range(8):
        r.update_part[s] = grad_update[:, s * 128 : (s + 1) * 128]
    upd_plane = ChipSwap(net, r.update_part, r.update_all)
    upd_plane.start()
    r.grad_inputs[...] = grad_first * (1.0 - jax.nn.sigmoid(r.update_pre[...]))
    put_rows(r.sums, 34, r.grad_two[...] * r.pairs[0])
    put_rows(r.sums, 36, r.grad_two[...])

    branch_sum.settle()
    expand_sum.relay()
    scores_plane = PlaneSum(
        net, r.scores_part, r.scores_got, r.scores_sent, r.scores_far, r.scores_sum, r.scores_pairs, r.scores_keep
    )
    mixed_sum = PlaneSum(net, r.part, r.got, r.sent, r.far, r.grad_two, r.pairs, r.work)

    def attend_back(k):
        gate_grad = cols_dot(rows_of(r.hid_all, k), r.wo[...].reshape(256, WIDE))
        pre = rows_of(r.reset_pre, k)
        low_grad = (gate_grad * silu(pre)).astype(LOW)
        low_values = rows_of(r.value_low, k)
        weights = rows_of(r.weights_low, k)
        backs = []
        for h in range(2):
            rows = slice(h * ROWS, (h + 1) * ROWS)
            r.scores_pairs[h] = cols_dot(low_grad[rows], low_values[rows])
            backs.append(rows_dot(weights[rows], low_grad[rows]))
        put(r.value_back, k, jnp.concatenate(backs, axis=0) * silu_slope(rows_of(r.value_pre, k)))
        pair = pair_of(k)
        r.mixture_back[pair, :, 0:128] = r.update_all[pair]
        r.mixture_back[pair, :, 128:384] = (
            (gate_grad * rows_of(r.attended, k) * silu_slope(pre)).astype(LOW).reshape(2, ROWS, 256)
        )
        r.mixture_back[pair, :, 384:512] = r.hid_all[pair, :, cand_cols]
        mixture = rows_of(r.mixture_back, k)
        mixed = cols_dot(mixture, weights_a(256, 768))
        r.pairs[...] = mixed.reshape(2, ROWS, WIDE)

    @pl.loop(0, 4)
    def _(k):
        @pl.when(k == 1)
        def _():
            hid_plane.take_sides()

        @pl.when(k == 3)
        def _():
            hid_plane.take_last()

        hid_plane.take_twin(k)
        upd_plane.take(k)
        attend_back(k)
        scores_plane.give(k)
        mixed_sum.give(k)

        @pl.when(k > 0)
        def _():
            scores_plane.pair(k - 1)
            mixed_sum.pair(k - 1)

        scores_plane.hold()
        mixed_sum.hold()

    scores_plane.pair(3)
    mixed_sum.pair(3)
    hid_plane.finish()
    upd_plane.finish()
    out_sum = LineSum(net, r.go, r.go_got, r.grad_out)
    attn_sum = LineSum(net, r.ga, r.ga_got, r.ga_sum)

    def attn_grad(zz):
        cols = cols_at(zz, 256)
        r.ga[zz, :, 0:256] = rows_dot(
            r.normed_all[:, :, cols].reshape(tokens, 256), r.value_back[...].reshape(tokens, 256)
        ).astype(LOW)
        r.ga[zz, :, 256:768] = rows_dot(
            r.mixed_all[:, :, cols].reshape(tokens, 256), r.mixture_back[...].reshape(tokens, 512)
        ).astype(LOW)

    attn_sum.run(attn_grad)

    @pl.loop(0, 4)
    def _(t):
        cols = cols_at(t, 256)
        grad = rows_dot(
            r.gated[...].reshape(tokens, 256), r.hid_all[:, :, cols].reshape(tokens, 256)
        ).astype(LOW)
        for zz in range(4):
            r.go[zz, :, cols] = grad[zz * 64 : (zz + 1) * 64]

    out_sum.start(last=False)


    reduce_sum.finish()
    stores.put(r.grad_reduce, r.grad_reduce_hbm)
    expand_sum.finish()
    mixed_sum.settle()
    normed_sum = RelayedSum(net, r.part, r.got_c, r.sent_c, r.far_c, r.hidden_pre, r.pairs, r.work)

    def normed_blocks(k):
        normed = cols_dot(rows_of(r.value_back, k), weights_a(0, 256))
        r.pairs[...] = normed.reshape(2, ROWS, WIDE)

    normed_sum.run(normed_blocks)

    scores_plane.settle()
    scores_plane.finish()
    grad_weights = r.scores_sum[...]
    zeta_own_pre = r.zeta_pre[me]
    zeta = silu(zeta_own_pre)
    query_low, key_low, probs = block_scores_of(zeta, r.heads, shift, r.table)
    grad_scores = (probs * (grad_weights - jnp.sum(probs * grad_weights, axis=-1, keepdims=True))).astype(LOW)
    scale = zeta.shape[1] ** (-0.5)
    grad_query = jnp.dot(grad_scores, key_low, preferred_element_type=F32) * scale
    grad_key = rows_dot(grad_scores, query_low) * scale
    skewed = pltpu.roll(
        jnp.dot(grad_scores, mirror_matrix(ROWS), preferred_element_type=F32), 1, 1, stride=1, stride_axis=0
    )
    r.sums[37:40] = jnp.zeros((3, WIDE), F32)
    r.sums[37:38, 0:128] = jnp.sum(grad_query * zeta, axis=0, keepdims=True)
    r.sums[37:38, 128:256] = jnp.sum(grad_key * zeta, axis=0, keepdims=True)
    r.sums[37:38, 256:384] = jnp.sum(grad_query, axis=0, keepdims=True)
    r.sums[37:38, 384:512] = jnp.sum(skewed, axis=0, keepdims=True)
    grad_zeta = grad_query * r.heads[0:1] + grad_key * r.heads[1:2]
    r.zeta_own[...] = (grad_zeta * silu_slope(zeta_own_pre)).astype(LOW)

    normed_sum.relay()
    zeta_tokens = spread_plane(net, r.zeta_own, r.zeta_all)
    branch_sum.relay()
    mixed_sum.finish()
    grad_mixed = r.grad_two[...] + cols_dot(r.zeta_own[...], zeta_weights())
    pull = grad_mixed * silu_slope(r.pre[...])
    lanes_to_rows(pull, r.tall)
    r.pre[...] = pull
    attn_sum.relay()
    ema_backward(r.fac, r.gain, r.nrm, r.tall, r.fac_sum, r.gain_sum, r.tall_out)
    for s in range(8):
        cols = slice(s * 128, (s + 1) * 128)
        r.sums[0:16, cols] = r.fac_sum[:, s, :]
        r.sums[16:32, cols] = r.gain_sum[:, s, :]
        r.sums[33:34, cols] = jnp.sum(r.pre[:, cols] * r.nrm[:, s, :], axis=0, keepdims=True)
    normed_sum.settle()
    normed_sum.finish()
    for s in range(8):
        cols = slice(s * 128, (s + 1) * 128)
        r.hidden_pre[:, cols] = r.hidden_pre[:, cols] + r.pre[:, cols] * r.prm[65:66, cols] + r.tall_out[:, s, :]
    xhat_one, inverse_one = standardized(r.x[...].astype(F32))
    grad_one = r.hidden_pre[...]
    put_rows(r.sums, 32, grad_one * xhat_one)
    put_rows(r.sums, 35, grad_one)
    r.grad_inputs[...] = r.grad_inputs[...] + norm_back(grad_one, xhat_one, inverse_one, r.prm[64:65])

    stores.put(r.grad_inputs, r.grad_inputs_hbm)

    for s in range(8):
        r.sum_blocks[s] = r.sums[:, s * 128 : (s + 1) * 128]
    small_sum = swap_plane(net, r.sum_blocks, r.sum_parts)
    ge_plane = swap_plane(net, r.ge_sum, r.ge_all)
    zeta_tokens.finish()
    r.gz[...] = rows_dot(
        r.mixed_all[...].reshape(tokens, WIDE), r.zeta_all[...].reshape(tokens, 128)
    ).reshape(4, 8, 32, 128)
    for zz in range(4):
        r.gz_own[zz] = r.gz[zz, me]
    zeta_grad = swap_line(net, r.gz_own, r.gz_line)
    small_sum.finish()
    whole = r.sum_parts[0]
    for s in range(1, 8):
        whole = whole + r.sum_parts[s]
    r.sum_rows[z] = whole
    small_rows = spread_line(net, r.sum_rows)
    branch_sum.finish()
    stream = r.x[...].astype(F32)
    first = r.first[...]
    branch = r.branch[...]
    r.output[...] = ((first + branch) * valid).astype(LOW)
    stores.put(r.output, r.output_hbm)
    r.square_own[...] = jnp.zeros((8, 128), F32)
    for k, item in enumerate((stream, first - stream, branch)):
        squares = jnp.sum(valid * item * item, axis=0, keepdims=True)
        r.square_own[k : k + 1] = jnp.broadcast_to(jnp.sum(squares, axis=1, keepdims=True), (1, 128))
    r.square_own[3:4] = jnp.broadcast_to(jnp.sum(valid, axis=0, keepdims=True), (1, 128))
    square_plane = spread_plane(net, r.square_own, r.square_all)
    attn_sum.finish()
    ga_plane = swap_plane(net, r.ga_sum, r.ga_all)
    small_rows.finish()
    r.sum_cols[...] = (r.sum_rows[0] + r.sum_rows[1]) + (r.sum_rows[2] + r.sum_rows[3])
    small_cols = spread_plane(net, r.sum_cols, r.sums_all)
    out_sum.start_last()
    out_sum.relay()
    square_plane.finish()
    squares = r.square_all[0]
    for s in range(1, 8):
        squares = squares + r.square_all[s]
    r.square_line[z] = squares
    square_rows = spread_line(net, r.square_line)
    ge_plane.finish()
    stores.put(r.ge_all, r.ge_hbm)
    zeta_grad.finish()
    stores.put(r.gz_line, r.gz_hbm)
    ga_plane.finish()
    stores.put(r.ga_all, r.ga_hbm)
    small_cols.finish()
    stores.put(r.sums_all, r.sums_hbm)
    square_rows.finish()
    stores.put(r.square_line, r.square_hbm)
    out_sum.finish()
    stores.put(r.grad_out, r.grad_out_hbm)
    stores.finish()


def layer(*operands):
    return pl.pallas_call(
        layer_kernel,
        name="layer",
        out_shape=[jax.ShapeDtypeStruct(*item) for item in fields(Results).values()],
        in_specs=list(fields(Inputs).values()),
        out_specs=[ANY] * len(fields(Results)),
        scratch_shapes=[pltpu.VMEM(*item) for item in fields(Scratch).values()]
        + [pltpu.SemaphoreType.DMA(item) for item in fields(Lines).values()],
        compiler_params=pltpu.CompilerParams(
            collective_id=1, has_side_effects=True, vmem_limit_bytes=60 << 20
        ),
    )(*operands)


def place_halves(blocks, base, q, out, start):
    lane = lax.broadcasted_iota(jnp.int32, (blocks.shape[1], 128), 1)
    for zz in range(4):
        at = base + (zz // 2) * 128
        left = blocks[2 * q, :, at : at + 128].astype(F32)
        right = blocks[2 * q + 1, :, at : at + 128].astype(F32)
        if zz % 2:
            left = pltpu.roll(left, 64, 1)
        else:
            right = pltpu.roll(right, 64, 1)
        to = start + (zz * 4 + q) * 128
        out[:, to : to + 128] = jnp.where(lane < 64, left, right)


def outputs_kernel(
    output, grad_inputs, grad_out, grad_reduce, ge_all, ga_all, gz_line, sums_all, square_line, ema,
    output_o, grad_inputs_o, values_o, mix_o, out_o, expand_o, reduce_o, ema_o, gains_o, biases_o, heads_o,
    shift_o, position_o, rms_o, turned,
):
    output_o[...] = output[...]
    grad_inputs_o[...] = grad_inputs[...]
    out_o[...] = grad_out[...]
    reduce_o[...] = grad_reduce[...]
    for s in range(8):
        for zz in range(4):
            at = (zz * 8 + s) * 128
            expand_o[:, at : at + 128] = ge_all[s, :, zz * 128 : (zz + 1) * 128].astype(F32)
        mix_o[:, s * 128 : (s + 1) * 128] = ga_all[s, :, 256:384].astype(F32)
        mix_o[:, 3200 + s * 128 : 3328 + s * 128] = ga_all[s, :, 640:768].astype(F32)
    mix_o[:, 1024:1152] = (gz_line[0] + gz_line[1]) + (gz_line[2] + gz_line[3])
    for q in range(4):
        place_halves(ga_all, 0, q, values_o, 0)
        place_halves(ga_all, 384, q, mix_o, 1152)
    mine = sums_all[lax.axis_index("dp")]
    mine = pltpu.roll(mine, (128 - 32 * lax.axis_index("fsdp")) % 128, 1)
    turned[0:40] = mine
    turned[40:128] = jnp.zeros((88, 128), F32)
    gains_o[...] = turned[32:35, 0:32]
    biases_o[...] = turned[35:37, 0:32]
    flipped = turned[...].T
    raw = ema[...].astype(F32)
    damping = jax.nn.sigmoid(raw[:, 0:16])
    mixing = jax.nn.sigmoid(raw[:, 16:32])
    expand = raw[:, 32:48]
    project = raw[:, 48:64]
    by_factor = flipped[0:32, 0:16] * (0.25 * project * mixing * expand)
    by_gain = flipped[0:32, 16:32]
    by_inflow = 0.25 * project * by_gain
    ema_o[:, 0:16] = -by_factor * mixing * damping * (1.0 - damping)
    ema_o[:, 16:32] = (by_inflow * expand - by_factor * damping) * mixing * (1.0 - mixing)
    ema_o[:, 32:48] = by_inflow * mixing
    ema_o[:, 48:64] = 0.25 * mixing * expand * by_gain
    heads_o[0:1] = sums_all[0, 37:38]
    heads_o[1:2] = sums_all[1, 37:38]
    shift_o[...] = sums_all[2, 37]
    position_o[...] = sums_all[3, 37]
    squares = (square_line[0] + square_line[1]) + (square_line[2] + square_line[3])
    roots = [jnp.sqrt(squares[k : k + 1] / (squares[3:4] * WIDE)) for k in range(3)]
    col = lax.broadcasted_iota(jnp.int32, (1, 128), 1)
    line = jnp.where(col == 0, roots[0], jnp.where(col == 1, roots[1], roots[2]))
    rms_o[...] = line[0, 0:3]


def outputs(parts, ema_params):
    shapes = (
        ((ROWS, WIDE), LOW), ((ROWS, WIDE), F32), ((32, 2048), F32), ((32, 4224), F32), ((64, WIDE), F32),
        ((32, 4096), F32), ((ROWS, WIDE), F32), ((32, 64), F32), ((3, 32), F32), ((2, 32), F32), ((2, 128), F32),
        ((128,), F32), ((128,), F32), ((3,), F32),
    )
    return pl.pallas_call(
        outputs_kernel,
        name="outputs",
        out_shape=[jax.ShapeDtypeStruct(shape, dtype) for shape, dtype in shapes],
        in_specs=[VMEM] * 10,
        out_specs=[VMEM] * len(shapes),
        scratch_shapes=[pltpu.VMEM((128, 128), F32)],
    )(*parts, ema_params)


def on_plane(
    inputs, lengths, w_values, w_mix, w_out, w_expand, w_reduce, ema_params,
    norm_gains, norm_biases, head_gains, query_bias, position_bias, cotangent,
):
    parts = layer(
        inputs, cotangent, w_values, w_mix, w_out, w_expand, w_reduce, ema_params, norm_gains, norm_biases,
        head_gains, query_bias, position_bias, lengths,
    )
    done = outputs(parts, ema_params)
    return tuple(done)


def layer_norm(value, gain, shift):
    centre = jnp.mean(value, axis=-1, keepdims=True)
    centered = value - centre
    spread = jnp.mean(centered * centered, axis=-1, keepdims=True)
    return centered * lax.rsqrt(spread + EPS) * gain + shift


def ema_mix(normed, keep, ema_params):
    count = ema_params.shape[1] // 4
    damping = jax.nn.sigmoid(ema_params[:, :count]).T
    mixing = jax.nn.sigmoid(ema_params[:, count : 2 * count]).T
    expand = ema_params[:, 2 * count : 3 * count].T
    project = ema_params[:, 3 * count :].T
    factor = 1.0 - mixing * damping
    inflow = mixing * expand

    def advance(state, item):
        column, flag = item
        state = factor * state * flag[:, None, None] + inflow * column[:, None, :]
        return (state, 0.25 * jnp.sum(project * state, axis=1))

    start = jnp.zeros((normed.shape[0], count, normed.shape[2]), jnp.float32)
    _, smooth = lax.scan(advance, start, (jnp.swapaxes(normed, 0, 1), jnp.swapaxes(keep, 0, 1)))
    return jnp.swapaxes(smooth, 0, 1)


def layout(lengths, rows):
    ends = jnp.cumsum(lengths, axis=1)
    starts = ends - lengths
    place = lax.broadcasted_iota(jnp.int32, (lengths.shape[0], rows), 1)
    begin = jnp.any(place[:, :, None] == starts[:, None, :], axis=2) | (place == ends)
    keep = jnp.where(begin, 0.0, 1.0).astype(jnp.float32)
    valid = jnp.where(place < ends, 1.0, 0.0).astype(jnp.float32)
    return (keep, valid)


def dot_rows(left, right):
    return lax.dot_general(
        left, right, (((0,), (0,)), ((), ())), preferred_element_type=jnp.float32
    )


def dot_cols(left, right):
    return lax.dot_general(
        left, right, (((1,), (1,)), ((), ())), preferred_element_type=jnp.float32
    )


def block_scores(query_low, key_low, position, scale):
    span = query_low.shape[1]
    row = lax.broadcasted_iota(jnp.int32, (span, span), 0)
    col = lax.broadcasted_iota(jnp.int32, (span, span), 1)
    table = position[jnp.clip(row - col, 0, span - 1)]
    scores = (
        jnp.einsum("kiz,kjz->kij", query_low, key_low, preferred_element_type=jnp.float32) * scale
        + table
    )
    return jnp.where(row >= col, scores, NEG)


def diagonal_sums(grid):
    size = grid.shape[0]
    flipped = grid[:, ::-1]
    padded = jnp.pad(flipped, ((0, 0), (0, size)))
    skewed = padded.reshape(-1)[: size * (2 * size - 1)].reshape(size, 2 * size - 1)
    return jnp.sum(skewed, axis=0)[size - 1 :]


def group_rows(value):
    return lax.all_gather(value, "fsdp", axis=0, tiled=True)


def group_total(value):
    return lax.psum_scatter(value, "fsdp", scatter_dimension=0, tiled=True)


def owner_layout(grad, owners):
    return grad.reshape(owners * 8, -1)


def owner_shard(piece, columns):
    return piece.reshape(-1, columns)


def on_device(
    inputs,
    lengths,
    w_values,
    w_mix,
    w_out,
    w_expand,
    w_reduce,
    ema_params,
    norm_gains,
    norm_biases,
    head_gains,
    query_bias,
    position_bias,
    cotangent,
):
    rows, width = inputs.shape
    span = position_bias.shape[0]
    blocks = rows // span
    key_width = head_gains.shape[1]
    scale = key_width ** (-0.5)
    keep, valid = layout(lengths, rows)
    mask = valid[0][:, None]
    gathered = (
        lax.all_gather(w_values, ("dp", "fsdp"), axis=0, tiled=True),
        lax.all_gather(w_mix, ("dp", "fsdp"), axis=0, tiled=True),
        lax.all_gather(w_out, ("dp", "fsdp"), axis=0, tiled=True),
        lax.all_gather(ema_params, ("dp", "fsdp"), axis=0, tiled=True),
        lax.all_gather(norm_gains, ("dp", "fsdp"), axis=1, tiled=True),
        lax.all_gather(norm_biases, ("dp", "fsdp"), axis=1, tiled=True),
    )
    values_full, mix_full, out_full, ema_full, gains_full, biases_full = gathered
    value_width = values_full.shape[1]
    group_size = lax.axis_size("fsdp")
    data_size = lax.axis_size("dp")
    owners = group_size * data_size
    shard_rows = w_expand.shape[0]
    hidden_units = w_expand.shape[1]
    unit_block = hidden_units // (group_size * data_size)
    pieces = w_expand.reshape(shard_rows, data_size, group_size, unit_block)
    swapped = lax.all_to_all(pieces, "fsdp", split_axis=2, concat_axis=0, tiled=True)
    expand_quarter, reduce_use = (
        lax.all_gather(swapped, "dp", axis=0, tiled=True),
        lax.all_gather(w_reduce, "dp", axis=0, tiled=True),
    )
    expand_use = expand_quarter.reshape(expand_quarter.shape[0], data_size * unit_block)
    gains_f = gains_full.astype(jnp.float32)
    biases_f = biases_full.astype(jnp.float32)
    heads_f = head_gains.astype(jnp.float32)
    query_shift = query_bias.astype(jnp.float32)
    position_f = position_bias.astype(jnp.float32)
    stream = inputs.astype(jnp.float32)

    def front(source, gain, shift, omega, params):
        normed_part = layer_norm(source, gain, shift)
        smooth = ema_mix(normed_part[None], keep, params)[0]
        return (normed_part, silu(smooth + omega * normed_part))

    (normed, mixed), front_back = jax.vjp(
        front, stream, gains_f[0], biases_f[0], gains_f[1], ema_full.astype(jnp.float32)
    )
    normed_low = normed.astype(jnp.bfloat16)
    mixed_low = mixed.astype(jnp.bfloat16)
    value_pre = jnp.dot(normed_low, values_full, preferred_element_type=jnp.float32)
    value_low = silu(value_pre).astype(jnp.bfloat16)
    mixture = jnp.dot(mixed_low, mix_full, preferred_element_type=jnp.float32)
    middle = width + key_width
    upper = middle + value_width
    update = jax.nn.sigmoid(mixture[:, :width])
    zeta_pre = mixture[:, width:middle]
    zeta = silu(zeta_pre)
    reset_pre = mixture[:, middle:upper]
    reset = silu(reset_pre)
    candidate = mixture[:, upper:]
    query_low = (
        (zeta * heads_f[0] + query_shift).astype(jnp.bfloat16).reshape(blocks, span, key_width)
    )
    key_low = (zeta * heads_f[1]).astype(jnp.bfloat16).reshape(blocks, span, key_width)
    value_blocks = value_low.reshape(blocks, span, value_width)
    scores = block_scores(query_low, key_low, position_f, scale)
    log_total = jax.nn.logsumexp(scores, axis=-1, keepdims=True)
    weights_low = jnp.exp(scores - log_total).astype(jnp.bfloat16)
    attended = jnp.einsum(
        "kij,kjv->kiv", weights_low, value_blocks, preferred_element_type=jnp.float32
    ).reshape(rows, value_width)
    gated_low = (attended * reset).astype(jnp.bfloat16)
    hidden_pre = candidate + jnp.dot(gated_low, out_full, preferred_element_type=jnp.float32)
    hidden = silu(hidden_pre)
    attn_branch = update * (hidden - stream)
    first = stream + attn_branch
    normed_two, norm_back = jax.vjp(layer_norm, first, gains_f[2], biases_f[1])
    normed_two_low = normed_two.astype(jnp.bfloat16)
    ffn_rows = group_rows(normed_two_low)
    expand_pre = jnp.dot(ffn_rows, expand_use, preferred_element_type=jnp.float32)
    expand_low = silu(expand_pre).astype(jnp.bfloat16)
    branch_part = jnp.dot(expand_low, reduce_use, preferred_element_type=jnp.float32)
    branch = group_total(branch_part)
    output = ((first + branch) * mask).astype(jnp.bfloat16)
    values_back, mix_back, out_back = (
        lax.all_gather(w_values, ("dp", "fsdp"), axis=0, tiled=True),
        lax.all_gather(w_mix, ("dp", "fsdp"), axis=0, tiled=True),
        lax.all_gather(w_out, ("dp", "fsdp"), axis=0, tiled=True),
    )
    grad_out = cotangent.astype(jnp.float32) * mask
    grad_branch = grad_out.astype(jnp.bfloat16)
    grad_rows = group_rows(grad_branch)
    grad_reduce = dot_rows(expand_low, grad_rows)
    grad_expand_out = dot_cols(grad_rows, reduce_use)
    grad_expand_pre = (grad_expand_out * silu_slope(expand_pre)).astype(jnp.bfloat16)
    grad_expand = dot_rows(ffn_rows, grad_expand_pre)
    normed_two_part = dot_cols(grad_expand_pre, expand_use)
    grad_normed_two = group_total(normed_two_part)
    grad_first_norm, grad_gain_two, grad_shift_two = norm_back(grad_normed_two)
    grad_first = grad_out + grad_first_norm
    grad_direct = grad_first * (1.0 - update)
    grad_update = grad_first * (hidden - stream)
    grad_hidden_pre = grad_first * update * silu_slope(hidden_pre)
    grad_hidden_low = grad_hidden_pre.astype(jnp.bfloat16)
    grad_out_proj = dot_rows(gated_low, grad_hidden_low)
    grad_gated = dot_cols(grad_hidden_low, out_back)
    grad_attended = (grad_gated * reset).astype(jnp.bfloat16).reshape(blocks, span, value_width)
    grad_reset = grad_gated * attended
    scores_again = block_scores(query_low, key_low, position_f, scale)
    probs = jnp.exp(scores_again - log_total)
    probs_low = probs.astype(jnp.bfloat16)
    grad_weights = jnp.einsum(
        "kiv,kjv->kij", grad_attended, value_blocks, preferred_element_type=jnp.float32
    )
    grad_value = jnp.einsum(
        "kij,kiv->kjv", probs_low, grad_attended, preferred_element_type=jnp.float32
    ).reshape(rows, value_width)
    inner = jnp.sum(probs * grad_weights, axis=-1, keepdims=True)
    grad_scores = (probs * (grad_weights - inner)).astype(jnp.bfloat16)
    grad_position = diagonal_sums(jnp.sum(grad_scores.astype(jnp.float32), axis=0))
    grad_query = (
        jnp.einsum(
            "kij,kjz->kiz", grad_scores, key_low, preferred_element_type=jnp.float32
        ).reshape(rows, key_width)
        * scale
    )
    grad_key = (
        jnp.einsum(
            "kij,kiz->kjz", grad_scores, query_low, preferred_element_type=jnp.float32
        ).reshape(rows, key_width)
        * scale
    )
    grad_value_pre = (grad_value * silu_slope(value_pre)).astype(jnp.bfloat16)
    grad_values = dot_rows(normed_low, grad_value_pre)
    grad_normed = dot_cols(grad_value_pre, values_back)
    grad_zeta = grad_query * heads_f[0] + grad_key * heads_f[1]
    grad_heads = jnp.stack([jnp.sum(grad_query * zeta, axis=0), jnp.sum(grad_key * zeta, axis=0)])
    grad_query_shift = jnp.sum(grad_query, axis=0)
    grad_mixture = jnp.concatenate(
        [
            grad_update * update * (1.0 - update),
            grad_zeta * silu_slope(zeta_pre),
            grad_reset * silu_slope(reset_pre),
            grad_hidden_pre,
        ],
        axis=1,
    ).astype(jnp.bfloat16)
    grad_mix = dot_rows(mixed_low, grad_mixture)
    grad_mixed = dot_cols(grad_mixture, mix_back)
    grad_source, grad_gain_one, grad_shift_one, grad_omega, grad_ema = front_back(
        (grad_normed, grad_mixed)
    )
    grad_inputs = grad_direct + grad_source
    grad_gains = jnp.stack([grad_gain_one, grad_omega, grad_gain_two])
    grad_shifts = jnp.stack([grad_shift_one, grad_shift_two])
    summed_expand, grad_reduce_dev = (
        lax.psum_scatter(grad_expand, "dp", scatter_dimension=0, tiled=True),
        lax.psum_scatter(grad_reduce, "dp", scatter_dimension=0, tiled=True),
    )
    summed_pieces = summed_expand.reshape(group_size * shard_rows, data_size, 1, unit_block)
    owned = lax.all_to_all(summed_pieces, "fsdp", split_axis=0, concat_axis=2, tiled=True)
    grad_expand_dev = owned.reshape(shard_rows, hidden_units)
    summed_block = (
        lax.psum_scatter(
            owner_layout(grad_values, owners), ("dp", "fsdp"), scatter_dimension=0, tiled=True
        ),
        lax.psum_scatter(
            owner_layout(grad_mix, owners), ("dp", "fsdp"), scatter_dimension=0, tiled=True
        ),
        lax.psum_scatter(grad_out_proj, ("dp", "fsdp"), scatter_dimension=0, tiled=True),
        lax.psum_scatter(
            owner_layout(grad_ema, owners), ("dp", "fsdp"), scatter_dimension=0, tiled=True
        ),
        lax.psum_scatter(grad_gains, ("dp", "fsdp"), scatter_dimension=1, tiled=True),
        lax.psum_scatter(grad_shifts, ("dp", "fsdp"), scatter_dimension=1, tiled=True),
    )
    values_flat, mix_flat, grad_out_dev, ema_flat, grad_gains_dev, grad_shifts_dev = summed_block
    grad_values_dev = owner_shard(values_flat, grad_values.shape[1])
    grad_mix_dev = owner_shard(mix_flat, grad_mix.shape[1])
    grad_ema_dev = owner_shard(ema_flat, grad_ema.shape[1])
    squares = jnp.stack(
        [
            jnp.sum(mask * stream * stream),
            jnp.sum(mask * attn_branch * attn_branch),
            jnp.sum(mask * branch * branch),
        ]
    )
    square_sums, tokens_seen, heads_total, shift_total, position_total = lax.psum(
        (squares, jnp.sum(valid), grad_heads, grad_query_shift, grad_position), ("dp", "fsdp")
    )
    rms = jnp.sqrt(square_sums / (tokens_seen * width))
    return (
        output,
        grad_inputs,
        grad_values_dev,
        grad_mix_dev,
        grad_out_dev,
        grad_expand_dev,
        grad_reduce_dev,
        grad_ema_dev,
        grad_gains_dev,
        grad_shifts_dev,
        heads_total,
        shift_total,
        position_total,
        rms,
    )


def solution(mesh):
    in_specs = (
        P(("dp", "fsdp"), None),
        P(("dp", "fsdp"), None),
        P(("dp", "fsdp"), None),
        P(("dp", "fsdp"), None),
        P(("dp", "fsdp"), None),
        P(("dp", "fsdp"), None),
        P(("dp", "fsdp"), None),
        P(("dp", "fsdp"), None),
        P(None, ("dp", "fsdp")),
        P(None, ("dp", "fsdp")),
        P(),
        P(),
        P(),
        P(("dp", "fsdp"), None),
    )
    out_specs = (
        P(("dp", "fsdp"), None),
        P(("dp", "fsdp"), None),
        P(("dp", "fsdp"), None),
        P(("dp", "fsdp"), None),
        P(("dp", "fsdp"), None),
        P(("dp", "fsdp"), None),
        P(("dp", "fsdp"), None),
        P(("dp", "fsdp"), None),
        P(None, ("dp", "fsdp")),
        P(None, ("dp", "fsdp")),
        P(),
        P(),
        P(),
        P(),
    )
    planes = mesh.shape["dp"] == 8 and mesh.shape["fsdp"] == 4
    return jax.shard_map(
        on_plane if planes else on_device, mesh=mesh, in_specs=in_specs, out_specs=out_specs, check_vma=False
    )
```
